32 devices in a mesh: narrow: 8 (over y, x, core), wide: 4 (over z).
Axes of the slice: x: 2, y: 2, z: 4, core: 2. Of those that a mesh axis runs over, the one named last changes fastest.
Arguments:
- block_input: bfloat16 [8192, 2048], P(('narrow', 'wide')), may hold values from -6 to 6
- cotangent: bfloat16 [8192, 2048], P(('narrow', 'wide')), may hold values from -6 to 6
- query_weight: bfloat16 [2048, 1536], P('narrow'), may hold values from -0.125 to 0.125
- key_weight: bfloat16 [2048, 384], P('narrow'), may hold values from -0.125 to 0.125
- value_weight: bfloat16 [2048, 384], P('narrow'), may hold values from -0.125 to 0.125
- project_weight: bfloat16 [1536, 2048], P(None, 'narrow'), may hold values from -0.625 to 0.625
- prenorm_gain: bfloat16 [2048], P('narrow'), may hold values from 0.5 to 1.5
- midnorm_gain: bfloat16 [2048], P('narrow'), may hold values from 0.5 to 1.5
- gate_weight: bfloat16 [2048, 4608], P(None, 'wide'), may hold values from -0.125 to 0.125
- up_weight: bfloat16 [2048, 4608], P(None, 'wide'), may hold values from -0.125 to 0.125
- down_weight: bfloat16 [4608, 2048], P('wide'), may hold values from -0.125 to 0.125
- doc_lengths: int32 [32, 4], P(('narrow', 'wide')), may hold values from 1 to 128, 256 in all within a row
- tile_counts: int32 [4], replicated, may hold values from 1 to 9, as said below
Outputs:
- block_output: bfloat16 [8192, 2048], P(('narrow', 'wide'))
- input_grad: bfloat16 [8192, 2048], P(('narrow', 'wide'))
- query_grad: float32 [2048, 1536], P('narrow')
- key_grad: float32 [2048, 384], P('narrow')
- value_grad: float32 [2048, 384], P('narrow')
- project_grad: float32 [1536, 2048], P(None, 'narrow')
- prenorm_grad: float32 [2048], P('narrow')
- midnorm_grad: float32 [2048], P('narrow')
- gate_grad: float32 [2048, 4608], P(None, 'wide')
- up_grad: float32 [2048, 4608], P(None, 'wide')
- down_grad: float32 [4608, 2048], P('wide')
The draws below stay inside these ranges and needn't reach their ends.
Inputs may be any that keep to these rules, and one draw needn't show every extreme that they name: `doc_lengths`: each row's 4 lengths sum to 256, and the longest of every row has 128 tokens. `tile_counts`: the counts sum to 34, and one index of wide holds 9.
All inputs are finite; a program needn't handle non-finite values.
Results may differ from the reference program's by a relative error of at most 0.02.
Values may be sent and summed in bfloat16 or wider, within the bound.
A program may use at most 192 MiB of HBM per device.

```python
import math
import jax
import jax.numpy as jnp
import numpy as np
from jax import lax

D = 2048
HEADS = 24
KV_HEADS = 6
HEAD_DIM = 64
TILES = 34
TILE = 128
TOK_DEV = 256
DOCS = 4
DOC_MOST = 128
FF = 4352
SLOTS = 9
COLS_DEV = 1152
FF_PAD = 4608
ROWS = 32
TOKENS = 8192
N_NARROW = 8
N_WIDE = 4


def draw_tile_counts(key, part):
    order = jax.random.permutation(jax.random.fold_in(key, 1), N_WIDE)
    index = jnp.arange(N_WIDE, dtype=jnp.int32)
    counts = jnp.where(index == 0, SLOTS, 1).astype(jnp.int32)
    remain = TILES - SLOTS - (N_WIDE - 1)
    for unit in range(remain):
        scores = jax.random.randint(jax.random.fold_in(key, 100 + unit), (N_WIDE,), 0, 1 << 20).astype(jnp.int32)
        scores = scores * N_WIDE + index
        scores = jnp.where(counts < SLOTS, scores, -1)
        pick = jnp.argmax(scores).astype(jnp.int32)
        counts = counts + (index == pick).astype(jnp.int32)
    return counts[order].astype(jnp.int32)


def strengthened(entries, stream_key, source, target, blocks, factor):
    owner, partner = [(jnp.arange(entries.shape[dim]) // (entries.shape[dim] // blocks)).reshape([-1 if axis == dim else 1 for axis in range(entries.ndim)]) for dim in (source, target)]
    chosen = jax.random.permutation(stream_key, blocks)[partner]
    strong = (owner == chosen) | (owner == (partner + blocks // 2) % blocks)
    return jnp.where(strong, factor * entries, entries)


def block_scale(rng, dims, cuts, least, top_value):
    def one(dim, shards_of):
        steps = jax.random.uniform(jax.random.fold_in(jax.random.fold_in(rng, 6), dim), (shards_of,), jnp.float32, least / len(cuts), top_value / len(cuts))
        return jnp.repeat(jnp.exp(steps), dims[dim] // shards_of).reshape((-1,) + (1,) * (len(dims) - dim - 1))

    factor_of = one(*cuts[0])
    for cut in cuts[1:]:
        factor_of = factor_of * one(*cut)
    return factor_of


def length_profile(number_of, total, bound, skew):
    portions = [(1 << 20) // math.isqrt(grade ** skew) + 1 for grade in range(2, number_of + 1)]
    spare, given = total - bound - (number_of - 1), [1] * (number_of - 1)
    while spare > 0:
        movable = [i for i in range(number_of - 1) if given[i] < bound]
        pool, left = sum([portions[i] for i in movable]), spare
        for i in movable:
            extra = min(bound - given[i], max(1, left * portions[i] // pool), spare)
            given[i] = given[i] + extra
            spare = spare - extra
    return np.array([bound] + given)


def ragged(key, number_of, total, bound, slope):
    if number_of == 2:
        one = jax.random.randint(key, (), max(1, total - bound), min(bound, total - 1) + 1)
        return jnp.stack([one, total - one])
    sizes = jnp.asarray(length_profile(number_of, total, bound, slope), jnp.int32)
    pairs = (number_of - 1) // 2
    donor, sink = sizes[1:1 + 2 * pairs:2], sizes[2:2 + 2 * pairs:2]
    room = jnp.minimum(donor - 1, bound - sink)
    shifted = jax.random.randint(jax.random.fold_in(key, 1), (pairs,), 0, 1 << 20) % (room + 1)
    sizes = sizes.at[1:1 + 2 * pairs:2].set(donor - shifted).at[2:2 + 2 * pairs:2].set(sink + shifted)
    return sizes[jax.random.permutation(jax.random.fold_in(key, 2), number_of)]


def scatter_about(rng, extent, width, bound, shards=(), kind=jnp.bfloat16):
    values = jax.random.normal(rng, extent, jnp.float32) * width
    if len(shards) > 0:
        values = block_scale(rng, extent, shards, -0.22, 0.18) * values
    return jnp.clip(values, min=-bound, max=bound).astype(kind)


def bell_draw_with(rng, dims, deviation, most, split, heavy, kind=jnp.bfloat16):
    values = deviation * jax.random.normal(rng, dims, jnp.float32)
    if split:
        values = values * block_scale(rng, dims, split, -0.22, 0.18)
    return jnp.clip(strengthened(values, jax.random.fold_in(rng, 3), *heavy), -most, most).astype(kind)


def setup_inputs(seed: int = 0) -> dict:
    key_of = jax.random.split(jax.random.key(seed), 14)
    block_input = scatter_about(key_of[0], (TOKENS, D), 1.0, 6.0, ((0, 32),))
    cotangent = bell_draw_with(key_of[1], (TOKENS, D), 1.0, 6.0, ((0, 32),), (0, 1, 32, 2.75))
    query_weight = scatter_about(key_of[2], (D, HEADS * HEAD_DIM), D ** -0.5, 0.125, ((0, 8),))
    key_weight = scatter_about(key_of[3], (D, KV_HEADS * HEAD_DIM), D ** -0.5, 0.125, ((0, 8),))
    value_weight = scatter_about(key_of[4], (D, KV_HEADS * HEAD_DIM), D ** -0.5, 0.125, ((0, 8),))
    project_weight = scatter_about(key_of[5], (HEADS * HEAD_DIM, D), (HEADS * HEAD_DIM // 16) ** -0.5, 0.625, ((1, 8),))
    prenorm_gain = jnp.clip(1.0 + 0.1 * jax.random.normal(key_of[6], (D,), jnp.float32), 0.5, 1.5).astype(jnp.bfloat16)
    midnorm_gain = jnp.clip(1.0 + 0.1 * jax.random.normal(key_of[7], (D,), jnp.float32), 0.5, 1.5).astype(jnp.bfloat16)
    gate_weight = scatter_about(key_of[8], (D, FF_PAD), D ** -0.5, 0.125, ((1, 4),))
    up_weight = scatter_about(key_of[9], (D, FF_PAD), D ** -0.5, 0.125, ((1, 4),))
    down_weight = scatter_about(key_of[10], (FF_PAD, D), (FF // 2) ** -0.5, 0.125, ((0, 4),))
    doc_lengths = jax.vmap(lambda own: ragged(own, DOCS, TOK_DEV, DOC_MOST, 1))(jax.random.split(key_of[11], ROWS)).reshape((ROWS, DOCS)).astype(jnp.int32)
    tile_counts = draw_tile_counts(jax.random.fold_in(key_of[13], 71), 0)
    return dict(block_input=block_input, cotangent=cotangent, query_weight=query_weight, key_weight=key_weight, value_weight=value_weight, project_weight=project_weight, prenorm_gain=prenorm_gain, midnorm_gain=midnorm_gain, gate_weight=gate_weight, up_weight=up_weight, down_weight=down_weight, doc_lengths=doc_lengths, tile_counts=tile_counts)


@jax.custom_vjp
def low(v):
    return lax.optimization_barrier(v.astype(jnp.bfloat16)).astype(jnp.float32)

@jax.custom_vjp
def low_back(v):
    return v

def low_keep(v):
    return (low(v), None)

def low_pass(kept, grad):
    return (grad,)

def back_keep(v):
    return (v, None)

def back_low(kept, grad):
    return (low(grad),)
low.defvjp(low_keep, low_pass)
low_back.defvjp(back_keep, back_low)
EPSILON = 1e-06

def precise_dot(left, right):
    return jnp.dot(left, right, precision=lax.Precision.HIGHEST, preferred_element_type=jnp.float32)

def rms_scale(rows, gain):
    factor = lax.rsqrt(lax.optimization_barrier(jnp.mean(rows * rows, axis=-1, keepdims=True)) + EPSILON)
    return rows * factor * gain

def reference(block_input, cotangent, query_weight, key_weight, value_weight, project_weight, prenorm_gain, midnorm_gain, gate_weight, up_weight, down_weight, doc_lengths, tile_counts):
    rows_count = N_NARROW * N_WIDE
    group = HEADS // KV_HEADS
    scale = HEAD_DIM ** (-0.5)
    position = jnp.arange(TOK_DEV, dtype=jnp.int32)
    ends = jnp.cumsum(doc_lengths, axis=1).astype(jnp.int32)
    segment = lax.optimization_barrier(jnp.sum((position[None, :, None] >= ends[:, None, :]).astype(jnp.int32), axis=2))
    column = jnp.arange(FF_PAD, dtype=jnp.int32)
    owner = column // COLS_DEV
    slot = column % COLS_DEV // TILE
    owner_count = lax.optimization_barrier(jnp.sum(jnp.where(owner[:, None] == jnp.arange(N_WIDE, dtype=jnp.int32)[None, :], tile_counts[None, :], 0), axis=1))
    live = (slot < owner_count).astype(jnp.float32)
    per_group = math.gcd(rows_count, max(1, 4096 // TOK_DEV))
    groups = rows_count // per_group
    causal = position[None, :] <= position[:, None]

    def attend(pieces):
        query_block, key_block, value_block, segment_block = pieces
        raw = jnp.einsum('rqcgd,rkcd->rcgqk', query_block, key_block, precision=lax.Precision.HIGHEST)
        scores = low_back(raw * scale)
        allowed = (segment_block[:, :, None] == segment_block[:, None, :]) & causal[None]
        masked = jnp.where(allowed[:, None, None], scores, -1e+30)
        peak = lax.optimization_barrier(jnp.max(masked, axis=-1, keepdims=True))
        expo = jnp.exp(masked - peak)
        probs = expo / lax.optimization_barrier(jnp.sum(expo, axis=-1, keepdims=True))
        probs_low = low(probs)
        return jnp.einsum('rcgqk,rkcd->rqcgd', probs_low, value_block, precision=lax.Precision.HIGHEST)

    def forward(inputs, qweight, kweight, vweight, pweight, first_gain, second_gain, gweight, uweight, dweight):
        normed = low(rms_scale(inputs, first_gain))
        query_rows = low_back(low(precise_dot(normed, qweight)))
        key_rows = low_back(low(precise_dot(normed, kweight)))
        value_rows = low_back(low(precise_dot(normed, vweight)))
        query_block = query_rows.reshape(groups, per_group, TOK_DEV, KV_HEADS, group, HEAD_DIM)
        key_block = key_rows.reshape(groups, per_group, TOK_DEV, KV_HEADS, HEAD_DIM)
        value_block = value_rows.reshape(groups, per_group, TOK_DEV, KV_HEADS, HEAD_DIM)
        segment_block = segment.reshape(groups, per_group, TOK_DEV)
        attended = lax.map(jax.checkpoint(attend), (query_block, key_block, value_block, segment_block))
        attended = low_back(low(attended.reshape(TOKENS, HEADS * HEAD_DIM)))
        branch = low_back(precise_dot(attended, pweight))
        middle = inputs + branch
        mixed_in = low(rms_scale(middle, second_gain))
        gate_pre = low_back(precise_dot(mixed_in, gweight))
        up_pre = low_back(precise_dot(mixed_in, uweight))
        hidden = low(jax.nn.silu(gate_pre) * up_pre * live)
        feed = low_back(precise_dot(hidden, dweight))
        return middle + feed
    primals = (block_input.astype(jnp.float32), query_weight.astype(jnp.float32), key_weight.astype(jnp.float32), value_weight.astype(jnp.float32), project_weight.astype(jnp.float32), prenorm_gain.astype(jnp.float32), midnorm_gain.astype(jnp.float32), gate_weight.astype(jnp.float32), up_weight.astype(jnp.float32), down_weight.astype(jnp.float32))
    result, backward = jax.vjp(forward, *primals)
    grads = backward(cotangent.astype(jnp.float32))
    return (result.astype(jnp.bfloat16), grads[0].astype(jnp.bfloat16), grads[1], grads[2], grads[3], grads[4], grads[5], grads[6], grads[7], grads[8], grads[9])
```

```python
import functools

import jax
import jax.numpy as jnp
from jax import lax
from jax.experimental import pallas as pl
from jax.experimental.pallas import tpu as pltpu
from jax.sharding import PartitionSpec as P

HEADS = 24
KV_HEADS = 6
HEAD_DIM = 64
TILE = 128


EPSILON = 1e-06

BF = jnp.bfloat16
F32 = jnp.float32


def rms_scale(rows, gain):
    factor = lax.rsqrt(jnp.mean(rows * rows, axis=-1, keepdims=True) + EPSILON)
    return rows * factor * gain


def contract_rows(left, right):
    return lax.dot_general(
        left, right, (((0,), (0,)), ((), ())), preferred_element_type=jnp.float32
    )


def contract_cols(left, right):
    return lax.dot_general(
        left, right, (((1,), (1,)), ((), ())), preferred_element_type=jnp.float32
    )


def flip(n, bit):
    return n + bit - 2 * bit * lax.rem(n // bit, 2)


def at(n, w):
    return {"narrow": n, "wide": w}


def send(src, dst, ssem, rsem, n, w):
    return pltpu.make_async_remote_copy(
        src_ref=src,
        dst_ref=dst,
        send_sem=ssem,
        recv_sem=rsem,
        device_id=at(n, w),
        device_id_type=pl.DeviceIdType.MESH,
    )


def greet(narrow_peers, n, w, line):
    barrier = pltpu.get_barrier_semaphore()
    for peer in narrow_peers:
        pl.semaphore_signal(
            barrier, inc=1, device_id=at(peer, w), device_id_type=pl.DeviceIdType.MESH
        )
    if not line:
        pl.semaphore_wait(barrier, len(narrow_peers))
    if line:
        pl.semaphore_signal(
            barrier, inc=1, device_id=at(n, flip(w, 2)), device_id_type=pl.DeviceIdType.MESH
        )

        @pl.when(w > 0)
        def _():
            pl.semaphore_signal(
                barrier, inc=1, device_id=at(n, w - 1), device_id_type=pl.DeviceIdType.MESH
            )

        @pl.when(w < 3)
        def _():
            pl.semaphore_signal(
                barrier, inc=1, device_id=at(n, w + 1), device_id_type=pl.DeviceIdType.MESH
            )

        @pl.when((w == 0) | (w == 3))
        def _():
            pl.semaphore_wait(barrier, len(narrow_peers) + 2)

        @pl.when((w == 1) | (w == 2))
        def _():
            pl.semaphore_wait(barrier, len(narrow_peers) + 3)


class LineGather:
    KINDS = 4

    def __init__(self, n, w, own, whole, ssem, rsem, chunks):
        self.n, self.w, self.own, self.whole = n, w, own, whole
        self.ssem, self.rsem, self.chunks = ssem, rsem, chunks
        self.rows = own.shape[0] // chunks

    def part(self, shard, i):
        return self.whole.at[shard, pl.ds(i * self.rows, self.rows), :]

    def mine(self, i):
        return self.own.at[pl.ds(i * self.rows, self.rows), :]

    def copy(self, kind, i, src, shard, w):
        k = kind * self.chunks + i
        return send(src, self.part(shard, i), self.ssem.at[k], self.rsem.at[k], self.n, w)

    def far(self, i):
        return self.copy(0, i, self.mine(i), self.w, flip(self.w, 2))

    def left(self, i):
        return self.copy(1, i, self.mine(i), self.w, jnp.maximum(self.w - 1, 0))

    def right(self, i):
        return self.copy(2, i, self.mine(i), self.w, jnp.minimum(self.w + 1, 3))

    def onward(self, i):
        shard = flip(self.w, 2)
        return self.copy(3, i, self.part(shard, i), shard, 3 * (self.w // 2))

    def middle(self):
        return (self.w == 1) | (self.w == 2)

    def start(self):
        for i in range(self.chunks):
            self.far(i).start()

        @pl.when(self.w > 0)
        def _():
            for i in range(self.chunks):
                self.left(i).start()

        @pl.when(self.w < 3)
        def _():
            for i in range(self.chunks):
                self.right(i).start()

    def forward(self, i):
        self.far(i).wait_recv()

        @pl.when(self.middle())
        def _():
            self.onward(i).start()

    def finish(self):
        for i in range(self.chunks):
            self.far(i).wait_send()

        @pl.when(self.w > 0)
        def _():
            for i in range(self.chunks):
                self.left(i).wait_send()
                self.right(i).wait_recv()

        @pl.when(self.w < 3)
        def _():
            for i in range(self.chunks):
                self.right(i).wait_send()
                self.left(i).wait_recv()

        @pl.when(self.middle())
        def _():
            for i in range(self.chunks):
                self.onward(i).wait_send()

        @pl.when((self.w == 0) | (self.w == 3))
        def _():
            for i in range(self.chunks):
                self.onward(i).wait_recv()


def first_kernel(
    q_ref,
    k_ref,
    v_ref,
    p_ref,
    g_ref,
    c_ref,
    qkv_full,
    p_full,
    g_full,
    c_full,
    q_buf,
    k_buf,
    v_buf,
    p_buf,
    g_buf,
    c_buf,
    in_sem,
    out_sem,
    ssem,
    rsem,
    gs_sem,
    gr_sem,
    zs_sem,
    zr_sem,
):
    n, w = lax.axis_index("narrow"), lax.axis_index("wide")
    x, y, c, d = flip(n, 2), flip(n, 4), flip(n, 1), flip(flip(n, 2), 4)
    others = [lax.rem(n + i, 8) for i in range(1, 8)]
    rows = q_ref.shape[0]
    half = rows // 2
    depth = p_ref.shape[0]
    qc, kc = q_ref.shape[1], k_ref.shape[1]
    cols = ((0, qc), (qc, kc), (qc + kc, kc))

    locals_in = []
    for i, (src, dst) in enumerate(
        ((q_ref, q_buf), (k_ref, k_buf), (v_ref, v_buf), (p_ref, p_buf), (g_ref, g_buf), (c_ref, c_buf))
    ):
        cp = pltpu.make_async_copy(src, dst, in_sem.at[i])
        cp.start()
        locals_in.append(cp)

    greet(others, n, w, True)

    def region(t, block, h):
        if t == 3:
            r = pl.ds(0, depth) if h == 2 else pl.ds(h * (depth // 2), depth // 2)
            return p_full.at[r, pl.ds(pl.multiple_of(block * rows, rows), rows)]
        r = pl.ds(block * rows, rows) if h == 2 else pl.ds(block * rows + h * half, half)
        return qkv_full.at[r, pl.ds(cols[t][0], cols[t][1])]

    def own(t, h):
        ref = (q_ref, k_ref, v_ref, p_ref)[t]
        if h == 2:
            return ref
        size = ref.shape[0] // 2
        return ref.at[pl.ds(h * size, size), :]

    def msg(t, kind, src, block, h, peer):
        k = t * 10 + kind
        return send(src, region(t, block, h), ssem.at[k], rsem.at[k], peer, w)

    def to_x(t, h):
        return msg(t, h, own(t, h), n, h, x)

    def to_y(t, h):
        return msg(t, 2 + h, own(t, h), n, h, y)

    def on_x(t):
        return msg(t, 4, region(t, y, 0), y, 0, x)

    def on_y(t):
        return msg(t, 5, region(t, x, 1), x, 1, y)

    def to_c(t, which):
        block = (n, x, y, d)[which]
        src = own(t, 2) if which == 0 else region(t, block, 2)
        return msg(t, 6 + which, src, block, 2, c)

    line = LineGather(n, w, c_ref, c_full, zs_sem, zr_sem, 4)
    for t in range(4):
        to_x(t, 1).start()
        to_y(t, 0).start()
        to_x(t, 0).start()
        to_y(t, 1).start()
        if t == 0:
            line.start()
    for t in range(4):
        to_c(t, 0).start()
    for i, peer in enumerate(others):
        send(g_ref, g_full.at[n], gs_sem.at[i], gr_sem.at[i], peer, w).start()

    outs = (
        (q_buf, region(0, n, 2)),
        (k_buf, region(1, n, 2)),
        (v_buf, region(2, n, 2)),
        (p_buf, region(3, n, 2)),
        (g_buf, g_full.at[n]),
        (c_buf, c_full.at[w]),
    )
    locals_out = []
    for i, (src, dst) in enumerate(outs):
        locals_in[i].wait()
        cp = pltpu.make_async_copy(src, dst, out_sem.at[i])
        cp.start()
        locals_out.append(cp)

    def relay(t):
        to_y(t, 0).wait_recv()
        on_x(t).start()
        to_x(t, 1).wait_recv()
        on_y(t).start()
        to_x(t, 0).wait_recv()
        to_c(t, 1).start()
        to_y(t, 1).wait_recv()
        to_c(t, 2).start()

    def corner(t):
        on_x(t).wait_recv()
        on_y(t).wait_recv()
        to_c(t, 3).start()

    line.forward(0)
    relay(0)
    line.forward(1)
    relay(1)
    relay(2)
    line.forward(2)
    relay(3)
    line.forward(3)
    for t in range(4):
        corner(t)
    for t in range(4):
        for h in range(2):
            to_x(t, h).wait_send()
            to_y(t, h).wait_send()
        on_x(t).wait_send()
        on_y(t).wait_send()
        for which in range(4):
            to_c(t, which).wait()
    for i, peer in enumerate(others):
        send(g_ref, g_full.at[n], gs_sem.at[i], gr_sem.at[i], peer, w).wait()
    line.finish()
    for cp in locals_out:
        cp.wait()


def gather_first(query, key, value, project, gains, cotangent):
    rows = query.shape[0]
    width = query.shape[1] + 2 * key.shape[1]
    spec = pl.BlockSpec(memory_space=pl.ANY)
    return pl.pallas_call(
        first_kernel,
        name="gather_first",
        out_shape=(
            jax.ShapeDtypeStruct((8 * rows, width), BF),
            jax.ShapeDtypeStruct((project.shape[0], 8 * rows), BF),
            jax.ShapeDtypeStruct((8,) + gains.shape, gains.dtype),
            jax.ShapeDtypeStruct((4,) + cotangent.shape, BF),
        ),
        in_specs=[spec] * 6,
        out_specs=[spec] * 4,
        scratch_shapes=[
            pltpu.VMEM(query.shape, BF),
            pltpu.VMEM(key.shape, BF),
            pltpu.VMEM(value.shape, BF),
            pltpu.VMEM(project.shape, BF),
            pltpu.VMEM(gains.shape, gains.dtype),
            pltpu.VMEM(cotangent.shape, BF),
            pltpu.SemaphoreType.DMA((6,)),
            pltpu.SemaphoreType.DMA((6,)),
            pltpu.SemaphoreType.DMA((40,)),
            pltpu.SemaphoreType.DMA((40,)),
            pltpu.SemaphoreType.DMA((7,)),
            pltpu.SemaphoreType.DMA((7,)),
            pltpu.SemaphoreType.DMA((16,)),
            pltpu.SemaphoreType.DMA((16,)),
        ],
        compiler_params=pltpu.CompilerParams(collective_id=1, has_side_effects=True),
    )(query, key, value, project, gains, cotangent)


def line_gather_kernel(x_ref, whole, buf, in_sem, out_sem, ssem, rsem):
    n, w = lax.axis_index("narrow"), lax.axis_index("wide")
    cp = pltpu.make_async_copy(x_ref, buf, in_sem)
    cp.start()
    greet([], n, w, True)
    line = LineGather(n, w, x_ref, whole, ssem, rsem, 4)
    line.start()
    cp.wait()
    cp = pltpu.make_async_copy(buf, whole.at[w], out_sem)
    cp.start()
    for i in range(4):
        line.forward(i)
    line.finish()
    cp.wait()


def line_gather(rows):
    spec = pl.BlockSpec(memory_space=pl.ANY)
    return pl.pallas_call(
        line_gather_kernel,
        name="line_gather",
        out_shape=jax.ShapeDtypeStruct((4,) + rows.shape, BF),
        in_specs=[spec],
        out_specs=spec,
        scratch_shapes=[
            pltpu.VMEM(rows.shape, BF),
            pltpu.SemaphoreType.DMA,
            pltpu.SemaphoreType.DMA,
            pltpu.SemaphoreType.DMA((16,)),
            pltpu.SemaphoreType.DMA((16,)),
        ],
        compiler_params=pltpu.CompilerParams(collective_id=2, has_side_effects=True),
    )(rows)


class LineScatter:
    def __init__(self, n, w, terms, bufs, ssem, rsem, chunks):
        self.n, self.w, self.terms = n, w, terms
        self.from_left, self.from_right, self.from_far, self.relayed, self.total = bufs
        self.ssem, self.rsem, self.chunks = ssem, rsem, chunks
        self.rows = terms.shape[1] // chunks

    def cut(self, ref, i):
        return ref.at[pl.ds(i * self.rows, self.rows), :]

    def term(self, d, i):
        return self.terms.at[d, pl.ds(i * self.rows, self.rows), :]

    def copy(self, kind, i, src, dst, w):
        k = kind * self.chunks + i
        return send(src, self.cut(dst, i), self.ssem.at[k], self.rsem.at[k], self.n, w)

    def relay(self, i):
        end = 3 - 3 * (self.w // 2)
        return self.copy(0, i, self.term(end, i), self.relayed, 1 + self.w // 3)

    def far(self, i):
        d = flip(self.w, 2)
        return self.copy(1, i, self.term(d, i), self.from_far, d)

    def far_sum(self, i):
        return self.copy(1, i, self.cut(self.total, i), self.from_far, flip(self.w, 2))

    def left(self, i):
        d = jnp.maximum(self.w - 1, 0)
        return self.copy(2, i, self.term(d, i), self.from_right, d)

    def right(self, i):
        d = jnp.minimum(self.w + 1, 3)
        return self.copy(3, i, self.term(d, i), self.from_left, d)

    def middle(self):
        return (self.w == 1) | (self.w == 2)

    def end(self):
        return (self.w == 0) | (self.w == 3)

    def start(self):
        @pl.when(self.end())
        def _():
            for i in range(self.chunks):
                self.relay(i).start()
            for i in range(self.chunks):
                self.far(i).start()

        @pl.when(self.w > 0)
        def _():
            for i in range(self.chunks):
                self.left(i).start()

        @pl.when(self.w < 3)
        def _():
            for i in range(self.chunks):
                self.right(i).start()

    def pass_on(self, i, mine):
        @pl.when(self.middle())
        def _():
            self.relay(i).wait_recv()
            rows = pl.ds(i * self.rows, self.rows)
            self.total[rows, :] = (
                mine[rows, :].astype(F32) + self.relayed[rows, :].astype(F32)
            ).astype(BF)
            self.far_sum(i).start()

    def finish(self, i, mine, out):
        rows = pl.ds(i * self.rows, self.rows)
        self.far(i).wait_recv()

        @pl.when(self.w > 0)
        def _():
            self.right(i).wait_recv()

        @pl.when(self.w < 3)
        def _():
            self.left(i).wait_recv()

        @pl.when(self.w == 0)
        def _():
            out[rows, :] = (
                mine[rows, :].astype(F32)
                + self.from_far[rows, :].astype(F32)
                + self.from_right[rows, :].astype(F32)
            ).astype(out.dtype)

        @pl.when(self.w == 3)
        def _():
            out[rows, :] = (
                mine[rows, :].astype(F32)
                + self.from_far[rows, :].astype(F32)
                + self.from_left[rows, :].astype(F32)
            ).astype(out.dtype)

        @pl.when(self.middle())
        def _():
            out[rows, :] = (
                mine[rows, :].astype(F32)
                + self.from_far[rows, :].astype(F32)
                + self.from_left[rows, :].astype(F32)
                + self.from_right[rows, :].astype(F32)
            ).astype(out.dtype)

    def drain(self):
        for i in range(self.chunks):
            self.far(i).wait_send()

        @pl.when(self.end())
        def _():
            for i in range(self.chunks):
                self.relay(i).wait_send()

        @pl.when(self.w > 0)
        def _():
            for i in range(self.chunks):
                self.left(i).wait_send()

        @pl.when(self.w < 3)
        def _():
            for i in range(self.chunks):
                self.right(i).wait_send()


def line_scatter_kernel(terms, out, mine, away, fl, fr, ff, rl, tot, in_sem, ssem, rsem):
    n, w = lax.axis_index("narrow"), lax.axis_index("wide")
    cps = [
        pltpu.make_async_copy(terms.at[w], mine, in_sem.at[0]),
        pltpu.make_async_copy(terms.at[flip(w, 2)], away, in_sem.at[1]),
    ]
    for cp in cps:
        cp.start()
    greet([], n, w, True)
    line = LineScatter(n, w, terms, (fl, fr, ff, rl, tot), ssem, rsem, 4)
    line.start()
    for cp in cps:
        cp.wait()
    for i in range(4):
        line.pass_on(i, away)
    for i in range(4):
        line.finish(i, mine, out)
    line.drain()


def line_scatter(terms):
    shape = terms.shape[1:]
    return pl.pallas_call(
        line_scatter_kernel,
        name="line_scatter",
        out_shape=jax.ShapeDtypeStruct(shape, F32),
        in_specs=[pl.BlockSpec(memory_space=pl.ANY)],
        out_specs=pl.BlockSpec(memory_space=pltpu.VMEM),
        scratch_shapes=[pltpu.VMEM(shape, BF)] * 7
        + [
            pltpu.SemaphoreType.DMA((2,)),
            pltpu.SemaphoreType.DMA((16,)),
            pltpu.SemaphoreType.DMA((16,)),
        ],
        compiler_params=pltpu.CompilerParams(collective_id=3, has_side_effects=True),
    )(terms)


def per_device(
    fast,
    block_input,
    cotangent,
    query_weight,
    key_weight,
    value_weight,
    project_weight,
    prenorm_gain,
    midnorm_gain,
    gate_weight,
    up_weight,
    down_weight,
    doc_lengths,
    tile_counts,
):
    tokens_here, model = block_input.shape
    if fast:
        gains = jnp.stack([prenorm_gain, midnorm_gain]).astype(F32).reshape(1, -1)
        qkv_full, project_full, gains_full, grad_rows = gather_first(
            query_weight, key_weight, value_weight, project_weight, gains, cotangent
        )
        grad_rows = grad_rows.reshape(-1, model)
        gains_full = gains_full.reshape(8, 2, -1)
        first_gain = gains_full[:, 0].reshape(-1)
        second_gain = gains_full[:, 1].reshape(-1)
    else:
        qkv_full = jnp.concatenate(
            [
                lax.all_gather(query_weight, "narrow", axis=0, tiled=True),
                lax.all_gather(key_weight, "narrow", axis=0, tiled=True),
                lax.all_gather(value_weight, "narrow", axis=0, tiled=True),
            ],
            axis=1,
        )
        project_full = lax.all_gather(project_weight, "narrow", axis=1, tiled=True)
        first_gain = lax.all_gather(prenorm_gain, "narrow", axis=0, tiled=True).astype(F32)
        second_gain = lax.all_gather(midnorm_gain, "narrow", axis=0, tiled=True).astype(F32)
        grad_rows = lax.all_gather(cotangent, "wide", axis=0, tiled=True)
    group = HEADS // KV_HEADS
    scale = HEAD_DIM ** (-0.5)
    q_cols, k_cols = HEADS * HEAD_DIM, KV_HEADS * HEAD_DIM
    inputs_f = block_input.astype(jnp.float32)
    normed = rms_scale(inputs_f, first_gain).astype(jnp.bfloat16)
    qkv = jnp.dot(normed, qkv_full, preferred_element_type=jnp.float32).astype(jnp.bfloat16)
    query_rows = qkv[:, :q_cols].reshape(tokens_here, KV_HEADS, group, HEAD_DIM)
    key_rows = qkv[:, q_cols : q_cols + k_cols].reshape(tokens_here, KV_HEADS, HEAD_DIM)
    value_rows = qkv[:, q_cols + k_cols :].reshape(tokens_here, KV_HEADS, HEAD_DIM)
    ends = jnp.cumsum(doc_lengths[0])
    position = jnp.arange(tokens_here, dtype=jnp.int32)
    segment = jnp.sum((position[:, None] >= ends[None, :]).astype(jnp.int32), axis=1)
    allowed = (segment[:, None] == segment[None, :]) & (position[None, :] <= position[:, None])
    scores = (
        jnp.einsum("qcgd,kcd->cgqk", query_rows, key_rows, preferred_element_type=jnp.float32)
        * scale
    )
    masked = jnp.where(allowed, scores, -1e30)
    peak = jnp.max(masked, axis=-1, keepdims=True)
    expo = jnp.exp(masked - peak)
    total = jnp.sum(expo, axis=-1, keepdims=True)
    probs_low = (expo / total).astype(jnp.bfloat16)
    logsum = peak + jnp.log(total)
    attended = (
        jnp.einsum("cgqk,kcd->qcgd", probs_low, value_rows, preferred_element_type=jnp.float32)
        .astype(jnp.bfloat16)
        .reshape(tokens_here, HEADS * HEAD_DIM)
    )
    branch = jnp.dot(attended, project_full, preferred_element_type=jnp.float32)
    middle = inputs_f + branch
    mixed_in = rms_scale(middle, second_gain).astype(jnp.bfloat16)
    if fast:
        gathered = line_gather(mixed_in).reshape(-1, model)
    else:
        gathered = lax.all_gather(mixed_in, "wide", axis=0, tiled=True)
    width = gate_weight.shape[1]
    wide_index = lax.axis_index("wide")
    my_count = jnp.sum(
        jnp.where(jnp.arange(tile_counts.shape[0], dtype=jnp.int32) == wide_index, tile_counts, 0)
    )
    live = (jnp.arange(width, dtype=jnp.int32) // TILE < my_count).astype(jnp.float32)
    gate_pre = jnp.dot(gathered, gate_weight, preferred_element_type=jnp.float32)
    up_pre = jnp.dot(gathered, up_weight, preferred_element_type=jnp.float32)
    hidden_back = contract_cols(grad_rows, down_weight)
    sigma = jax.nn.sigmoid(gate_pre)
    hidden = (gate_pre * sigma * up_pre * live).astype(jnp.bfloat16)
    gate_back = (hidden_back * up_pre * live * sigma * (1.0 + gate_pre * (1.0 - sigma))).astype(
        jnp.bfloat16
    )
    up_back = (hidden_back * gate_pre * sigma * live).astype(jnp.bfloat16)
    mixed_terms = (
        contract_cols(gate_back, gate_weight) + contract_cols(up_back, up_weight)
    ).astype(jnp.bfloat16)
    if fast:
        mixed_back = line_scatter(mixed_terms.reshape(4, tokens_here, model))
    else:
        mixed_back = lax.psum_scatter(
            mixed_terms, "wide", scatter_dimension=0, tiled=True
        ).astype(F32)
    partial_rows = jnp.dot(hidden, down_weight, preferred_element_type=jnp.float32)
    feed = lax.psum_scatter(
        partial_rows.astype(jnp.bfloat16), "wide", scatter_dimension=0, tiled=True
    ).astype(jnp.float32)
    block_output = (middle + feed).astype(jnp.bfloat16)
    out_grad = cotangent.astype(jnp.float32)
    down_part = contract_rows(hidden, grad_rows)
    gate_part = contract_rows(gathered, gate_back)
    up_part = contract_rows(gathered, up_back)
    unused_second, second_backward = jax.vjp(rms_scale, middle, second_gain)
    middle_norm_back, second_gain_part = second_backward(mixed_back)
    middle_back = out_grad + middle_norm_back
    branch_back = middle_back.astype(jnp.bfloat16)
    project_part = contract_rows(attended, branch_back)
    attended_back = (
        contract_cols(branch_back, project_full)
        .astype(jnp.bfloat16)
        .reshape(tokens_here, KV_HEADS, group, HEAD_DIM)
    )
    scores_again = (
        jnp.einsum("qcgd,kcd->cgqk", query_rows, key_rows, preferred_element_type=jnp.float32)
        * scale
    )
    probs_again = jnp.where(allowed, jnp.exp(scores_again - logsum), 0.0)
    probs_again_low = probs_again.astype(jnp.bfloat16)
    value_back = (
        jnp.einsum(
            "cgqk,qcgd->kcd", probs_again_low, attended_back, preferred_element_type=jnp.float32
        )
        .astype(jnp.bfloat16)
        .reshape(tokens_here, KV_HEADS * HEAD_DIM)
    )
    probs_back = jnp.einsum(
        "qcgd,kcd->cgqk", attended_back, value_rows, preferred_element_type=jnp.float32
    )
    scores_back = (
        probs_again * (probs_back - jnp.sum(probs_again * probs_back, axis=-1, keepdims=True))
    ).astype(jnp.bfloat16)
    query_back = (
        (
            jnp.einsum("cgqk,kcd->qcgd", scores_back, key_rows, preferred_element_type=jnp.float32)
            * scale
        )
        .astype(jnp.bfloat16)
        .reshape(tokens_here, HEADS * HEAD_DIM)
    )
    key_back = (
        (
            jnp.einsum(
                "cgqk,qcgd->kcd", scores_back, query_rows, preferred_element_type=jnp.float32
            )
            * scale
        )
        .astype(jnp.bfloat16)
        .reshape(tokens_here, KV_HEADS * HEAD_DIM)
    )
    qkv_back = jnp.concatenate([query_back, key_back, value_back], axis=1)
    qkv_part = contract_rows(normed, qkv_back)
    normed_back = contract_cols(qkv_back, qkv_full)
    unused_first, first_backward = jax.vjp(rms_scale, inputs_f, first_gain)
    input_norm_back, first_gain_part = first_backward(normed_back)
    input_grad = (middle_back + input_norm_back).astype(jnp.bfloat16)

    def owned(part, axis):
        share = lax.psum_scatter(
            part.astype(jnp.bfloat16), "narrow", scatter_dimension=axis, tiled=True
        )
        return lax.psum(share, "wide").astype(jnp.float32)

    qkv_total = owned(qkv_part, 0)
    project_total = owned(project_part, 1)
    first_total = owned(first_gain_part, 0)
    second_total = owned(second_gain_part, 0)
    gate_total, up_total, down_total = (
        lax.psum(gate_part.astype(jnp.bfloat16), "narrow").astype(jnp.float32),
        lax.psum(up_part.astype(jnp.bfloat16), "narrow").astype(jnp.float32),
        lax.psum(down_part.astype(jnp.bfloat16), "narrow").astype(jnp.float32),
    )
    return (
        block_output,
        input_grad,
        qkv_total[:, :q_cols],
        qkv_total[:, q_cols : q_cols + k_cols],
        qkv_total[:, q_cols + k_cols :],
        project_total,
        first_total,
        second_total,
        gate_total,
        up_total,
        down_total,
    )


def solution(mesh):
    fast = mesh.shape["narrow"] == 8 and mesh.shape["wide"] == 4
    placed = (
        P(("narrow", "wide"), None),
        P(("narrow", "wide"), None),
        P("narrow", None),
        P("narrow", None),
        P("narrow", None),
        P(None, "narrow"),
        P("narrow"),
        P("narrow"),
        P(None, "wide"),
        P(None, "wide"),
        P("wide", None),
        P(("narrow", "wide"), None),
        P(),
    )
    return jax.shard_map(
        functools.partial(per_device, fast),
        mesh=mesh,
        in_specs=placed,
        out_specs=(
            P(("narrow", "wide"), None),
            P(("narrow", "wide"), None),
            P("narrow", None),
            P("narrow", None),
            P("narrow", None),
            P(None, "narrow"),
            P("narrow"),
            P("narrow"),
            P(None, "wide"),
            P(None, "wide"),
            P("wide", None),
        ),
        check_vma=False,
    )
```

```python
import functools

import jax
import jax.numpy as jnp
from jax import lax
from jax.experimental import pallas as pl
from jax.experimental.pallas import tpu as pltpu
from jax.sharding import PartitionSpec as P

HEADS = 24
KV_HEADS = 6
HEAD_DIM = 64
TILE = 128


EPSILON = 1e-06

BF = jnp.bfloat16
F32 = jnp.float32


def rms_scale(rows, gain):
    factor = lax.rsqrt(jnp.mean(rows * rows, axis=-1, keepdims=True) + EPSILON)
    return rows * factor * gain


def contract_rows(left, right):
    return lax.dot_general(
        left, right, (((0,), (0,)), ((), ())), preferred_element_type=jnp.float32
    )


def contract_cols(left, right):
    return lax.dot_general(
        left, right, (((1,), (1,)), ((), ())), preferred_element_type=jnp.float32
    )


def flip(n, bit):
    return n + bit - 2 * bit * lax.rem(n // bit, 2)


def at(n, w):
    return {"narrow": n, "wide": w}


def send(src, dst, ssem, rsem, n, w):
    return pltpu.make_async_remote_copy(
        src_ref=src,
        dst_ref=dst,
        send_sem=ssem,
        recv_sem=rsem,
        device_id=at(n, w),
        device_id_type=pl.DeviceIdType.MESH,
    )


def greet(narrow_peers, n, w, line):
    barrier = pltpu.get_barrier_semaphore()
    for peer in narrow_peers:
        pl.semaphore_signal(
            barrier, inc=1, device_id=at(peer, w), device_id_type=pl.DeviceIdType.MESH
        )
    if not line:
        pl.semaphore_wait(barrier, len(narrow_peers))
    if line:
        pl.semaphore_signal(
            barrier, inc=1, device_id=at(n, flip(w, 2)), device_id_type=pl.DeviceIdType.MESH
        )

        @pl.when(w > 0)
        def _():
            pl.semaphore_signal(
                barrier, inc=1, device_id=at(n, w - 1), device_id_type=pl.DeviceIdType.MESH
            )

        @pl.when(w < 3)
        def _():
            pl.semaphore_signal(
                barrier, inc=1, device_id=at(n, w + 1), device_id_type=pl.DeviceIdType.MESH
            )

        @pl.when((w == 0) | (w == 3))
        def _():
            pl.semaphore_wait(barrier, len(narrow_peers) + 2)

        @pl.when((w == 1) | (w == 2))
        def _():
            pl.semaphore_wait(barrier, len(narrow_peers) + 3)


class LineGather:
    KINDS = 4

    def __init__(self, n, w, own, whole, ssem, rsem, chunks):
        self.n, self.w, self.own, self.whole = n, w, own, whole
        self.ssem, self.rsem, self.chunks = ssem, rsem, chunks
        self.rows = own.shape[0] // chunks

    def part(self, shard, i):
        return self.whole.at[shard, pl.ds(i * self.rows, self.rows), :]

    def mine(self, i):
        return self.own.at[pl.ds(i * self.rows, self.rows), :]

    def copy(self, kind, i, src, shard, w):
        k = kind * self.chunks + i
        return send(src, self.part(shard, i), self.ssem.at[k], self.rsem.at[k], self.n, w)

    def far(self, i):
        return self.copy(0, i, self.mine(i), self.w, flip(self.w, 2))

    def left(self, i):
        return self.copy(1, i, self.mine(i), self.w, jnp.maximum(self.w - 1, 0))

    def right(self, i):
        return self.copy(2, i, self.mine(i), self.w, jnp.minimum(self.w + 1, 3))

    def onward(self, i):
        shard = flip(self.w, 2)
        return self.copy(3, i, self.part(shard, i), shard, 3 * (self.w // 2))

    def middle(self):
        return (self.w == 1) | (self.w == 2)

    def start(self):
        for i in range(self.chunks):
            self.far(i).start()

        @pl.when(self.w > 0)
        def _():
            for i in range(self.chunks):
                self.left(i).start()

        @pl.when(self.w < 3)
        def _():
            for i in range(self.chunks):
                self.right(i).start()

    def forward(self, i):
        self.far(i).wait_recv()

        @pl.when(self.middle())
        def _():
            self.onward(i).start()

    def finish(self):
        for i in range(self.chunks):
            self.far(i).wait_send()

        @pl.when(self.w > 0)
        def _():
            for i in range(self.chunks):
                self.left(i).wait_send()
                self.right(i).wait_recv()

        @pl.when(self.w < 3)
        def _():
            for i in range(self.chunks):
                self.right(i).wait_send()
                self.left(i).wait_recv()

        @pl.when(self.middle())
        def _():
            for i in range(self.chunks):
                self.onward(i).wait_send()

        @pl.when((self.w == 0) | (self.w == 3))
        def _():
            for i in range(self.chunks):
                self.onward(i).wait_recv()


def first_kernel(
    q_ref,
    k_ref,
    v_ref,
    p_ref,
    g_ref,
    c_ref,
    qkv_full,
    p_full,
    g_full,
    c_full,
    q_buf,
    k_buf,
    v_buf,
    p_buf,
    g_buf,
    c_buf,
    in_sem,
    out_sem,
    ssem,
    rsem,
    gs_sem,
    gr_sem,
    zs_sem,
    zr_sem,
):
    n, w = lax.axis_index("narrow"), lax.axis_index("wide")
    x, y, c, d = flip(n, 2), flip(n, 4), flip(n, 1), flip(flip(n, 2), 4)
    others = [lax.rem(n + i, 8) for i in range(1, 8)]
    rows = q_ref.shape[0]
    half = rows // 2
    depth = p_ref.shape[0]
    qc, kc = q_ref.shape[1], k_ref.shape[1]
    cols = ((0, qc), (qc, kc), (qc + kc, kc))

    locals_in = []
    for i, (src, dst) in enumerate(
        ((q_ref, q_buf), (k_ref, k_buf), (v_ref, v_buf), (p_ref, p_buf), (g_ref, g_buf), (c_ref, c_buf))
    ):
        cp = pltpu.make_async_copy(src, dst, in_sem.at[i])
        cp.start()
        locals_in.append(cp)

    greet(others, n, w, True)

    def region(t, block, h):
        if t == 3:
            r = pl.ds(0, depth) if h == 2 else pl.ds(h * (depth // 2), depth // 2)
            return p_full.at[r, pl.ds(pl.multiple_of(block * rows, rows), rows)]
        r = pl.ds(block * rows, rows) if h == 2 else pl.ds(block * rows + h * half, half)
        return qkv_full.at[r, pl.ds(cols[t][0], cols[t][1])]

    def own(t, h):
        ref = (q_ref, k_ref, v_ref, p_ref)[t]
        if h == 2:
            return ref
        size = ref.shape[0] // 2
        return ref.at[pl.ds(h * size, size), :]

    def msg(t, kind, src, block, h, peer):
        k = t * 10 + kind
        return send(src, region(t, block, h), ssem.at[k], rsem.at[k], peer, w)

    def to_x(t, h):
        return msg(t, h, own(t, h), n, h, x)

    def to_y(t, h):
        return msg(t, 2 + h, own(t, h), n, h, y)

    def on_x(t):
        return msg(t, 4, region(t, y, 0), y, 0, x)

    def on_y(t):
        return msg(t, 5, region(t, x, 1), x, 1, y)

    def to_c(t, which):
        block = (n, x, y, d)[which]
        src = own(t, 2) if which == 0 else region(t, block, 2)
        return msg(t, 6 + which, src, block, 2, c)

    line = LineGather(n, w, c_ref, c_full, zs_sem, zr_sem, 4)
    for t in range(4):
        to_x(t, 1).start()
        to_y(t, 0).start()
        to_x(t, 0).start()
        to_y(t, 1).start()
        if t == 0:
            line.start()
    for t in range(4):
        to_c(t, 0).start()
    for i, peer in enumerate(others):
        send(g_ref, g_full.at[n], gs_sem.at[i], gr_sem.at[i], peer, w).start()

    outs = (
        (q_buf, region(0, n, 2)),
        (k_buf, region(1, n, 2)),
        (v_buf, region(2, n, 2)),
        (p_buf, region(3, n, 2)),
        (g_buf, g_full.at[n]),
        (c_buf, c_full.at[w]),
    )
    locals_out = []
    for i, (src, dst) in enumerate(outs):
        locals_in[i].wait()
        cp = pltpu.make_async_copy(src, dst, out_sem.at[i])
        cp.start()
        locals_out.append(cp)

    def relay(t):
        to_y(t, 0).wait_recv()
        on_x(t).start()
        to_x(t, 1).wait_recv()
        on_y(t).start()
        to_x(t, 0).wait_recv()
        to_c(t, 1).start()
        to_y(t, 1).wait_recv()
        to_c(t, 2).start()

    def corner(t):
        on_x(t).wait_recv()
        on_y(t).wait_recv()
        to_c(t, 3).start()

    line.forward(0)
    relay(0)
    line.forward(1)
    relay(1)
    relay(2)
    line.forward(2)
    relay(3)
    line.forward(3)
    for t in range(4):
        corner(t)
    for t in range(4):
        for h in range(2):
            to_x(t, h).wait_send()
            to_y(t, h).wait_send()
        on_x(t).wait_send()
        on_y(t).wait_send()
        for which in range(4):
            to_c(t, which).wait()
    for i, peer in enumerate(others):
        send(g_ref, g_full.at[n], gs_sem.at[i], gr_sem.at[i], peer, w).wait()
    line.finish()
    for cp in locals_out:
        cp.wait()


def gather_first(query, key, value, project, gains, cotangent):
    rows = query.shape[0]
    width = query.shape[1] + 2 * key.shape[1]
    spec = pl.BlockSpec(memory_space=pl.ANY)
    return pl.pallas_call(
        first_kernel,
        name="gather_first",
        out_shape=(
            jax.ShapeDtypeStruct((8 * rows, width), BF),
            jax.ShapeDtypeStruct((project.shape[0], 8 * rows), BF),
            jax.ShapeDtypeStruct((8,) + gains.shape, gains.dtype),
            jax.ShapeDtypeStruct((4,) + cotangent.shape, BF),
        ),
        in_specs=[spec] * 6,
        out_specs=[spec] * 4,
        scratch_shapes=[
            pltpu.VMEM(query.shape, BF),
            pltpu.VMEM(key.shape, BF),
            pltpu.VMEM(value.shape, BF),
            pltpu.VMEM(project.shape, BF),
            pltpu.VMEM(gains.shape, gains.dtype),
            pltpu.VMEM(cotangent.shape, BF),
            pltpu.SemaphoreType.DMA((6,)),
            pltpu.SemaphoreType.DMA((6,)),
            pltpu.SemaphoreType.DMA((40,)),
            pltpu.SemaphoreType.DMA((40,)),
            pltpu.SemaphoreType.DMA((7,)),
            pltpu.SemaphoreType.DMA((7,)),
            pltpu.SemaphoreType.DMA((16,)),
            pltpu.SemaphoreType.DMA((16,)),
        ],
        compiler_params=pltpu.CompilerParams(collective_id=1, has_side_effects=True),
    )(query, key, value, project, gains, cotangent)


def line_gather_kernel(x_ref, whole, buf, in_sem, out_sem, ssem, rsem):
    n, w = lax.axis_index("narrow"), lax.axis_index("wide")
    cp = pltpu.make_async_copy(x_ref, buf, in_sem)
    cp.start()
    greet([], n, w, True)
    line = LineGather(n, w, x_ref, whole, ssem, rsem, 4)
    line.start()
    cp.wait()
    cp = pltpu.make_async_copy(buf, whole.at[w], out_sem)
    cp.start()
    for i in range(4):
        line.forward(i)
    line.finish()
    cp.wait()


def line_gather(rows):
    spec = pl.BlockSpec(memory_space=pl.ANY)
    return pl.pallas_call(
        line_gather_kernel,
        name="line_gather",
        out_shape=jax.ShapeDtypeStruct((4,) + rows.shape, BF),
        in_specs=[spec],
        out_specs=spec,
        scratch_shapes=[
            pltpu.VMEM(rows.shape, BF),
            pltpu.SemaphoreType.DMA,
            pltpu.SemaphoreType.DMA,
            pltpu.SemaphoreType.DMA((16,)),
            pltpu.SemaphoreType.DMA((16,)),
        ],
        compiler_params=pltpu.CompilerParams(collective_id=2, has_side_effects=True),
    )(rows)


class LineScatter:
    def __init__(self, n, w, terms, bufs, ssem, rsem, chunks):
        self.n, self.w, self.terms = n, w, terms
        self.from_left, self.from_right, self.from_far, self.relayed, self.total = bufs
        self.ssem, self.rsem, self.chunks = ssem, rsem, chunks
        self.rows = terms.shape[1] // chunks

    def cut(self, ref, i):
        return ref.at[pl.ds(i * self.rows, self.rows), :]

    def term(self, d, i):
        return self.terms.at[d, pl.ds(i * self.rows, self.rows), :]

    def copy(self, kind, i, src, dst, w):
        k = kind * self.chunks + i
        return send(src, self.cut(dst, i), self.ssem.at[k], self.rsem.at[k], self.n, w)

    def relay(self, i):
        end = 3 - 3 * (self.w // 2)
        return self.copy(0, i, self.term(end, i), self.relayed, 1 + self.w // 3)

    def far(self, i):
        d = flip(self.w, 2)
        return self.copy(1, i, self.term(d, i), self.from_far, d)

    def far_sum(self, i):
        return self.copy(1, i, self.cut(self.total, i), self.from_far, flip(self.w, 2))

    def left(self, i):
        d = jnp.maximum(self.w - 1, 0)
        return self.copy(2, i, self.term(d, i), self.from_right, d)

    def right(self, i):
        d = jnp.minimum(self.w + 1, 3)
        return self.copy(3, i, self.term(d, i), self.from_left, d)

    def middle(self):
        return (self.w == 1) | (self.w == 2)

    def end(self):
        return (self.w == 0) | (self.w == 3)

    def start(self):
        @pl.when(self.end())
        def _():
            for i in range(self.chunks):
                self.relay(i).start()
            for i in range(self.chunks):
                self.far(i).start()

        @pl.when(self.w > 0)
        def _():
            for i in range(self.chunks):
                self.left(i).start()

        @pl.when(self.w < 3)
        def _():
            for i in range(self.chunks):
                self.right(i).start()

    def pass_on(self, i, mine):
        @pl.when(self.middle())
        def _():
            self.relay(i).wait_recv()
            rows = pl.ds(i * self.rows, self.rows)
            self.total[rows, :] = (
                mine[rows, :].astype(F32) + self.relayed[rows, :].astype(F32)
            ).astype(BF)
            self.far_sum(i).start()

    def finish(self, i, mine, out):
        rows = pl.ds(i * self.rows, self.rows)
        self.far(i).wait_recv()

        @pl.when(self.w > 0)
        def _():
            self.right(i).wait_recv()

        @pl.when(self.w < 3)
        def _():
            self.left(i).wait_recv()

        @pl.when(self.w == 0)
        def _():
            out[rows, :] = (
                mine[rows, :].astype(F32)
                + self.from_far[rows, :].astype(F32)
                + self.from_right[rows, :].astype(F32)
            ).astype(out.dtype)

        @pl.when(self.w == 3)
        def _():
            out[rows, :] = (
                mine[rows, :].astype(F32)
                + self.from_far[rows, :].astype(F32)
                + self.from_left[rows, :].astype(F32)
            ).astype(out.dtype)

        @pl.when(self.middle())
        def _():
            out[rows, :] = (
                mine[rows, :].astype(F32)
                + self.from_far[rows, :].astype(F32)
                + self.from_left[rows, :].astype(F32)
                + self.from_right[rows, :].astype(F32)
            ).astype(out.dtype)

    def drain(self):
        for i in range(self.chunks):
            self.far(i).wait_send()

        @pl.when(self.end())
        def _():
            for i in range(self.chunks):
                self.relay(i).wait_send()

        @pl.when(self.w > 0)
        def _():
            for i in range(self.chunks):
                self.left(i).wait_send()

        @pl.when(self.w < 3)
        def _():
            for i in range(self.chunks):
                self.right(i).wait_send()


def line_scatter_kernel(terms, out, mine, away, fl, fr, ff, rl, tot, in_sem, ssem, rsem):
    n, w = lax.axis_index("narrow"), lax.axis_index("wide")
    cps = [
        pltpu.make_async_copy(terms.at[w], mine, in_sem.at[0]),
        pltpu.make_async_copy(terms.at[flip(w, 2)], away, in_sem.at[1]),
    ]
    for cp in cps:
        cp.start()
    greet([], n, w, True)
    line = LineScatter(n, w, terms, (fl, fr, ff, rl, tot), ssem, rsem, 4)
    line.start()
    for cp in cps:
        cp.wait()
    for i in range(4):
        line.pass_on(i, away)
    for i in range(4):
        line.finish(i, mine, out)
    line.drain()


def line_scatter(terms):
    shape = terms.shape[1:]
    return pl.pallas_call(
        line_scatter_kernel,
        name="line_scatter",
        out_shape=jax.ShapeDtypeStruct(shape, F32),
        in_specs=[pl.BlockSpec(memory_space=pl.ANY)],
        out_specs=pl.BlockSpec(memory_space=pltpu.VMEM),
        scratch_shapes=[pltpu.VMEM(shape, BF)] * 7
        + [
            pltpu.SemaphoreType.DMA((2,)),
            pltpu.SemaphoreType.DMA((16,)),
            pltpu.SemaphoreType.DMA((16,)),
        ],
        compiler_params=pltpu.CompilerParams(collective_id=3, has_side_effects=True),
    )(terms)


class Reduce:
    def __init__(self, me, part, cols, x_first, bufs, sems, k):
        self.n, self.w, self.y, self.x, self.core = me
        self.part, self.cols, self.x_first = part, pl.ds(*cols), x_first
        self.sum, self.pair, self.one, self.two = bufs
        self.sems, self.k = sems, k
        self.rows = part.shape[3]
        self.near = flip(self.n, 2) if x_first else flip(self.n, 4)
        self.next = flip(self.n, 4) if x_first else flip(self.n, 2)

    def load(self):
        return pltpu.make_async_copy(
            self.part.at[:, :, self.core, :, self.cols], self.sum, self.sems[0].at[self.k]
        )

    def swap(self):
        return send(
            self.part.at[:, :, 1 - self.core, :, self.cols],
            self.pair,
            self.sems[1].at[self.k],
            self.sems[2].at[self.k],
            flip(self.n, 1),
            self.w,
        )

    def block(self, first, second):
        return (second, first) if self.x_first else (first, second)

    def axes(self):
        return (self.x, self.y) if self.x_first else (self.y, self.x)

    def stage(self, s):
        a, b = self.axes()
        if s == 1:
            src = self.sum.at[:, 1 - a] if self.x_first else self.sum.at[1 - a]
            dst, peer = self.one, self.near
        else:
            src = self.sum.at[self.block(a, 1 - b)]
            dst, peer = self.two, self.next
        k = 2 * self.k + s - 1
        return send(src, dst, self.sems[3].at[k], self.sems[4].at[k], peer, self.w)

    def add(self, block, other):
        step = 64 if self.rows % 64 == 0 else 48

        @pl.loop(0, self.rows // step)
        def _(i):
            r = pl.ds(pl.multiple_of(i * step, step), step)
            self.sum[block[0], block[1], r, :] = (
                self.sum[block[0], block[1], r, :] + other[r, :]
            )

    def after_swap(self):
        a, b = self.axes()
        self.swap().wait_recv()
        self.load().wait()
        for first in (1 - a, a):
            for second in (1 - b, b):
                block = self.block(first, second)
                self.add(block, self.pair.at[block])

    def after_one(self):
        a, b = self.axes()
        self.stage(1).wait()
        self.add(self.block(a, 1 - b), self.one.at[1 - b])
        self.stage(2).start()
        self.add(self.block(a, b), self.one.at[b])

    def after_two(self):
        a, b = self.axes()
        self.stage(2).wait()
        self.add(self.block(a, b), self.two)

    def result(self):
        return self.sum.at[self.y, self.x]


class Spread:
    def __init__(self, item, full, sems, k):
        self.item, self.full, self.sems, self.k = item, full, sems, k
        n = item.n
        self.blocks = (n, flip(n, 2), flip(n, 4), flip(flip(n, 2), 4))

    def region(self, block):
        return self.full.at[block, :, self.item.cols]

    def copy(self, kind, src, block, peer):
        k = 7 * self.k + kind
        return send(
            src, self.region(block), self.sems[0].at[k], self.sems[1].at[k], peer, self.item.w
        )

    def own(self, kind):
        n = self.item.n
        return self.copy(kind, self.item.result(), n, (flip(n, 2), flip(n, 4), flip(n, 1))[kind])

    def corner(self):
        n, b = self.item.n, self.blocks
        if self.item.x_first:
            return self.copy(3, self.region(b[2]), b[2], flip(n, 2))
        return self.copy(3, self.region(b[1]), b[1], flip(n, 4))

    def to_core(self, which):
        block = self.blocks[which]
        return self.copy(3 + which, self.region(block), block, flip(self.item.n, 1))

    def keep(self):
        return pltpu.make_async_copy(
            self.item.result(), self.region(self.item.n), self.sems[2].at[self.k]
        )

    def start(self):
        order = (1, 0, 2) if self.item.x_first else (0, 1, 2)
        for kind in order:
            self.own(kind).start()
        self.keep().start()

    def relay(self):
        first, second = (1, 0) if self.item.x_first else (0, 1)
        self.own(first).wait_recv()
        self.corner().start()
        self.to_core(1 + first).start()
        self.own(second).wait_recv()
        self.to_core(1 + second).start()

    def last(self):
        self.corner().wait_recv()
        self.to_core(3).start()

    def finish(self):
        for kind in range(2):
            self.own(kind).wait_send()
        self.own(2).wait()
        self.corner().wait_send()
        for which in range(1, 4):
            self.to_core(which).wait()
        self.keep().wait()


class Rows:
    def __init__(self, ref):
        self.ref = ref
        self.shape = (4, ref.shape[0] // 4, ref.shape[1])

    @property
    def at(self):
        return self

    def __getitem__(self, index):
        d, r, _ = index
        return self.ref.at[pl.ds(d * self.shape[1] + r.start, r.size), :]


def last_kernel(items, n_attn, *refs):
    refs = list(refs)

    def take(count):
        out = refs[:count]
        del refs[:count]
        return out

    parts = take(5)
    feed_terms, gain_parts = take(2)
    outs = take(n_attn)
    full = take(3)
    feed_out, gain_out = take(2)
    bufs = [take(4) for _ in items]
    line_bufs = [take(6) for _ in range(n_attn)]
    feed_bufs = take(7)
    gain_in, gain_sum, gain_line = take(3)
    load_sem, swap_s, swap_r, st_s, st_r = take(5)
    sp_s, sp_r, sp_l = take(3)
    lr_s, lr_r, lg_s, lg_r, lg_l = take(5)
    fd_s, fd_r, fd_l = take(3)
    gn_s, gn_r, gz_s, gz_r = take(4)

    n, w = lax.axis_index("narrow"), lax.axis_index("wide")
    me = (n, w, n // 4, lax.rem(n // 2, 2), lax.rem(n, 2))
    red = [
        Reduce(me, parts[p], cols, xf, bufs[k], (load_sem, swap_s, swap_r, st_s, st_r), k)
        for k, (p, cols, xf) in enumerate(items)
    ]
    attn, ffn = red[:n_attn], red[n_attn:]
    spread = [
        Spread(item, full[items[n_attn + k][0] - 2], (sp_s, sp_r, sp_l), k)
        for k, item in enumerate(ffn)
    ]
    for item in red:
        item.load().start()
    mine, away = feed_bufs[0], feed_bufs[1]
    feed_loads = [
        pltpu.make_async_copy(feed_terms.at[w], mine, fd_l.at[0]),
        pltpu.make_async_copy(feed_terms.at[flip(w, 2)], away, fd_l.at[1]),
    ]
    for cp in feed_loads:
        cp.start()

    barrier = pltpu.get_barrier_semaphore()
    narrow_peers = [lax.rem(n + i, 8) for i in range(1, 8)]
    wide_peers = [lax.rem(w + i, 4) for i in range(1, 4)]
    for peer in narrow_peers:
        pl.semaphore_signal(
            barrier, inc=1, device_id=at(peer, w), device_id_type=pl.DeviceIdType.MESH
        )
    for peer in wide_peers:
        pl.semaphore_signal(
            barrier, inc=1, device_id=at(n, peer), device_id_type=pl.DeviceIdType.MESH
        )
    pl.semaphore_wait(barrier, 10)

    for item in red:
        item.swap().start()
    feed = LineScatter(n, w, feed_terms, feed_bufs[2:], fd_s, fd_r, 4)
    feed.start()

    def gain_narrow(i):
        peer = narrow_peers[i]
        return send(gain_parts.at[peer], gain_in.at[i], gn_s.at[i], gn_r.at[i], peer, w)

    def gain_wide(i):
        return send(gain_sum, gain_line.at[i], gz_s.at[i], gz_r.at[i], n, wide_peers[i])

    for i in range(7):
        gain_narrow(i).start()

    for item in attn:
        item.after_swap()
        item.stage(1).start()
    for cp in feed_loads:
        cp.wait()
    feed.pass_on(0, away)
    for item in ffn[:2]:
        item.after_swap()
    feed.pass_on(1, away)
    for item in attn[:2]:
        item.after_one()
    for item in ffn[:2]:
        item.stage(1).start()
    feed.pass_on(2, away)
    for item in ffn[2:]:
        item.after_swap()
    feed.pass_on(3, away)
    for item in attn[2:]:
        item.after_one()
    for item in ffn[2:]:
        item.stage(1).start()

    for i in range(7):
        gain_narrow(i).wait()
    total = gain_parts[n]
    for i in range(7):
        total = total + gain_in[i]
    gain_sum[...] = total
    for i in range(3):
        gain_wide(i).start()

    scatters, gathers = [], []
    for k, item in enumerate(attn):
        own = line_bufs[k][5]
        scatters.append(
            LineScatter(n, w, Rows(item.result()), line_bufs[k][:5], lr_s.at[k], lr_r.at[k], 1)
        )
        gathers.append(LineGather(n, w, own, outs[k], lg_s.at[k], lg_r.at[k], 1))

    def quarter(item, d):
        return item.result().at[pl.ds(d * (item.rows // 4), item.rows // 4), :]

    def line_pass(k):
        scatters[k].pass_on(0, quarter(attn[k], flip(w, 2)))

    def keep(k):
        return pltpu.make_async_copy(line_bufs[k][5], outs[k].at[w], lg_l.at[k])

    def line_turn(k):
        scatters[k].finish(0, quarter(attn[k], w), line_bufs[k][5])
        gathers[k].start()
        keep(k).start()

    for k in (0, 1):
        attn[k].after_two()
        scatters[k].start()
    for i in range(4):
        feed.finish(i, mine, feed_out)
    for k in (2, 3):
        attn[k].after_two()
        scatters[k].start()
    for k in (0, 1):
        line_pass(k)
    for item in ffn[:2]:
        item.after_one()
    for k in (2, 3):
        line_pass(k)
    for k in (0, 1):
        line_turn(k)
    for item in ffn[2:]:
        item.after_one()
    for k in (2, 3):
        line_turn(k)
    for k in (0, 1):
        gathers[k].forward(0)
    for k in (0, 1):
        ffn[k].after_two()
        spread[k].start()
    for k in (2, 3):
        gathers[k].forward(0)
    for k in (2, 3):
        ffn[k].after_two()
        spread[k].start()
    for i in range(3):
        gain_wide(i).wait()
    gain_out[...] = ((gain_sum[...] + gain_line[0]) + (gain_line[1] + gain_line[2]))
    for s in spread:
        s.relay()
    for s in spread:
        s.last()
    for s in spread:
        s.finish()
    for item in red:
        item.swap().wait_send()
    for k in range(n_attn):
        scatters[k].drain()
        gathers[k].finish()
        keep(k).wait()
    feed.drain()


def reduce_last(qkv_part, project_part, gate_part, up_part, down_part, feed_terms, gain_parts):
    whole = [qkv_part, project_part, gate_part, up_part, down_part]
    parts = [p.reshape(2, 2, 2, p.shape[0] // 8, p.shape[1]) for p in whole]
    items = []
    for p, xf in ((0, True), (0, False), (1, True), (1, False)):
        half = parts[p].shape[4] // 2
        items.append((p, (0 if xf else half, half), xf))
    n_attn = len(items)
    items.append((2, (0, gate_part.shape[1]), True))
    items.append((3, (0, up_part.shape[1]), False))
    half = down_part.shape[1] // 2
    items.append((4, (0, half), True))
    items.append((4, (half, half), False))
    scratch = []
    for p, (_, cols), _ in items:
        rows = parts[p].shape[3]
        scratch += [
            pltpu.VMEM((2, 2, rows, cols), BF),
            pltpu.VMEM((2, 2, rows, cols), BF),
            pltpu.VMEM((2, rows, cols), BF),
            pltpu.VMEM((rows, cols), BF),
        ]
    outs = []
    for p, (_, cols), _ in items[:n_attn]:
        quarter = (parts[p].shape[3] // 4, cols)
        scratch += [pltpu.VMEM(quarter, BF)] * 6
        outs.append(jax.ShapeDtypeStruct((4,) + quarter, BF))
    for part in parts[2:]:
        outs.append(jax.ShapeDtypeStruct((8,) + part.shape[3:], BF))
    outs.append(jax.ShapeDtypeStruct(feed_terms.shape[1:], F32))
    outs.append(jax.ShapeDtypeStruct(gain_parts.shape[1:], F32))
    scratch += [pltpu.VMEM(feed_terms.shape[1:], BF)] * 7
    scratch += [
        pltpu.VMEM((7,) + gain_parts.shape[1:], F32),
        pltpu.VMEM(gain_parts.shape[1:], F32),
        pltpu.VMEM((3,) + gain_parts.shape[1:], F32),
    ]
    dma = pltpu.SemaphoreType.DMA
    k, f = len(items), len(items) - n_attn
    scratch += [dma((k,)), dma((k,)), dma((k,)), dma((2 * k,)), dma((2 * k,))]
    scratch += [dma((7 * f,)), dma((7 * f,)), dma((f,))]
    scratch += [dma((n_attn, 4))] * 4 + [dma((n_attn,))]
    scratch += [dma((16,)), dma((16,)), dma((2,))]
    scratch += [dma((7,)), dma((7,)), dma((3,)), dma((3,))]
    hbm, vmem = pl.BlockSpec(memory_space=pl.ANY), pl.BlockSpec(memory_space=pltpu.VMEM)
    out = pl.pallas_call(
        functools.partial(last_kernel, items, n_attn),
        name="reduce_last",
        out_shape=tuple(outs),
        in_specs=[hbm] * 6 + [vmem],
        out_specs=[hbm] * (n_attn + 3) + [vmem] * 2,
        scratch_shapes=scratch,
        compiler_params=pltpu.CompilerParams(
            collective_id=4, has_side_effects=True, vmem_limit_bytes=64 * 1024 * 1024 - 65536
        ),
    )(*parts, feed_terms, gain_parts)
    rows = parts[0].shape[3]
    qkv = jnp.concatenate([out[0].reshape(rows, -1), out[1].reshape(rows, -1)], axis=1)
    project = jnp.concatenate([out[2].reshape(rows, -1), out[3].reshape(rows, -1)], axis=1)
    ffn = [o.reshape(-1, o.shape[2]) for o in out[n_attn : n_attn + 3]]
    return qkv, project, ffn, out[n_attn + 3], out[n_attn + 4]


def per_device(
    fast,
    block_input,
    cotangent,
    query_weight,
    key_weight,
    value_weight,
    project_weight,
    prenorm_gain,
    midnorm_gain,
    gate_weight,
    up_weight,
    down_weight,
    doc_lengths,
    tile_counts,
):
    tokens_here, model = block_input.shape
    if fast:
        gains = jnp.stack([prenorm_gain, midnorm_gain]).astype(F32).reshape(1, -1)
        qkv_full, project_full, gains_full, grad_rows = gather_first(
            query_weight, key_weight, value_weight, project_weight, gains, cotangent
        )
        grad_rows = grad_rows.reshape(-1, model)
        gains_full = gains_full.reshape(8, 2, -1)
        first_gain = gains_full[:, 0].reshape(-1)
        second_gain = gains_full[:, 1].reshape(-1)
    else:
        qkv_full = jnp.concatenate(
            [
                lax.all_gather(query_weight, "narrow", axis=0, tiled=True),
                lax.all_gather(key_weight, "narrow", axis=0, tiled=True),
                lax.all_gather(value_weight, "narrow", axis=0, tiled=True),
            ],
            axis=1,
        )
        project_full = lax.all_gather(project_weight, "narrow", axis=1, tiled=True)
        first_gain = lax.all_gather(prenorm_gain, "narrow", axis=0, tiled=True).astype(F32)
        second_gain = lax.all_gather(midnorm_gain, "narrow", axis=0, tiled=True).astype(F32)
        grad_rows = lax.all_gather(cotangent, "wide", axis=0, tiled=True)
    group = HEADS // KV_HEADS
    scale = HEAD_DIM ** (-0.5)
    q_cols, k_cols = HEADS * HEAD_DIM, KV_HEADS * HEAD_DIM
    inputs_f = block_input.astype(jnp.float32)
    normed = rms_scale(inputs_f, first_gain).astype(jnp.bfloat16)
    qkv = jnp.dot(normed, qkv_full, preferred_element_type=jnp.float32).astype(jnp.bfloat16)
    query_rows = qkv[:, :q_cols].reshape(tokens_here, KV_HEADS, group, HEAD_DIM)
    key_rows = qkv[:, q_cols : q_cols + k_cols].reshape(tokens_here, KV_HEADS, HEAD_DIM)
    value_rows = qkv[:, q_cols + k_cols :].reshape(tokens_here, KV_HEADS, HEAD_DIM)
    ends = jnp.cumsum(doc_lengths[0])
    position = jnp.arange(tokens_here, dtype=jnp.int32)
    segment = jnp.sum((position[:, None] >= ends[None, :]).astype(jnp.int32), axis=1)
    allowed = (segment[:, None] == segment[None, :]) & (position[None, :] <= position[:, None])
    scores = (
        jnp.einsum("qcgd,kcd->cgqk", query_rows, key_rows, preferred_element_type=jnp.float32)
        * scale
    )
    masked = jnp.where(allowed, scores, -1e30)
    peak = jnp.max(masked, axis=-1, keepdims=True)
    expo = jnp.exp(masked - peak)
    total = jnp.sum(expo, axis=-1, keepdims=True)
    probs_low = (expo / total).astype(jnp.bfloat16)
    logsum = peak + jnp.log(total)
    attended = (
        jnp.einsum("cgqk,kcd->qcgd", probs_low, value_rows, preferred_element_type=jnp.float32)
        .astype(jnp.bfloat16)
        .reshape(tokens_here, HEADS * HEAD_DIM)
    )
    branch = jnp.dot(attended, project_full, preferred_element_type=jnp.float32)
    middle = inputs_f + branch
    mixed_in = rms_scale(middle, second_gain).astype(jnp.bfloat16)
    if fast:
        gathered = line_gather(mixed_in).reshape(-1, model)
    else:
        gathered = lax.all_gather(mixed_in, "wide", axis=0, tiled=True)
    width = gate_weight.shape[1]
    wide_index = lax.axis_index("wide")
    my_count = jnp.sum(
        jnp.where(jnp.arange(tile_counts.shape[0], dtype=jnp.int32) == wide_index, tile_counts, 0)
    )
    live = (jnp.arange(width, dtype=jnp.int32) // TILE < my_count).astype(jnp.float32)
    gate_pre = jnp.dot(gathered, gate_weight, preferred_element_type=jnp.float32)
    up_pre = jnp.dot(gathered, up_weight, preferred_element_type=jnp.float32)
    hidden_back = contract_cols(grad_rows, down_weight)
    sigma = jax.nn.sigmoid(gate_pre)
    hidden = (gate_pre * sigma * up_pre * live).astype(jnp.bfloat16)
    gate_back = (hidden_back * up_pre * live * sigma * (1.0 + gate_pre * (1.0 - sigma))).astype(
        jnp.bfloat16
    )
    up_back = (hidden_back * gate_pre * sigma * live).astype(jnp.bfloat16)
    mixed_terms = (
        contract_cols(gate_back, gate_weight) + contract_cols(up_back, up_weight)
    ).astype(jnp.bfloat16)
    if fast:
        mixed_back = line_scatter(mixed_terms.reshape(4, tokens_here, model))
    else:
        mixed_back = lax.psum_scatter(
            mixed_terms, "wide", scatter_dimension=0, tiled=True
        ).astype(F32)
    partial_rows = jnp.dot(hidden, down_weight, preferred_element_type=jnp.float32)
    out_grad = cotangent.astype(jnp.float32)
    down_part = contract_rows(hidden, grad_rows)
    gate_part = contract_rows(gathered, gate_back)
    up_part = contract_rows(gathered, up_back)
    unused_second, second_backward = jax.vjp(rms_scale, middle, second_gain)
    middle_norm_back, second_gain_part = second_backward(mixed_back)
    middle_back = out_grad + middle_norm_back
    branch_back = middle_back.astype(jnp.bfloat16)
    project_part = contract_rows(branch_back, attended)
    attended_back = (
        contract_cols(branch_back, project_full)
        .astype(jnp.bfloat16)
        .reshape(tokens_here, KV_HEADS, group, HEAD_DIM)
    )
    scores_again = (
        jnp.einsum("qcgd,kcd->cgqk", query_rows, key_rows, preferred_element_type=jnp.float32)
        * scale
    )
    probs_again = jnp.where(allowed, jnp.exp(scores_again - logsum), 0.0)
    probs_again_low = probs_again.astype(jnp.bfloat16)
    value_back = (
        jnp.einsum(
            "cgqk,qcgd->kcd", probs_again_low, attended_back, preferred_element_type=jnp.float32
        )
        .astype(jnp.bfloat16)
        .reshape(tokens_here, KV_HEADS * HEAD_DIM)
    )
    probs_back = jnp.einsum(
        "qcgd,kcd->cgqk", attended_back, value_rows, preferred_element_type=jnp.float32
    )
    scores_back = (
        probs_again * (probs_back - jnp.sum(probs_again * probs_back, axis=-1, keepdims=True))
    ).astype(jnp.bfloat16)
    query_back = (
        (
            jnp.einsum("cgqk,kcd->qcgd", scores_back, key_rows, preferred_element_type=jnp.float32)
            * scale
        )
        .astype(jnp.bfloat16)
        .reshape(tokens_here, HEADS * HEAD_DIM)
    )
    key_back = (
        (
            jnp.einsum(
                "cgqk,qcgd->kcd", scores_back, query_rows, preferred_element_type=jnp.float32
            )
            * scale
        )
        .astype(jnp.bfloat16)
        .reshape(tokens_here, KV_HEADS * HEAD_DIM)
    )
    qkv_back = jnp.concatenate([query_back, key_back, value_back], axis=1)
    qkv_part = contract_rows(normed, qkv_back)
    normed_back = contract_cols(qkv_back, qkv_full)
    unused_first, first_backward = jax.vjp(rms_scale, inputs_f, first_gain)
    input_norm_back, first_gain_part = first_backward(normed_back)
    input_grad = (middle_back + input_norm_back).astype(jnp.bfloat16)

    if fast:
        gain_parts = jnp.stack(
            [first_gain_part.reshape(8, -1), second_gain_part.reshape(8, -1)], axis=1
        ).reshape(8, 1, -1)
        qkv_total, project_total, ffn_totals, feed, gain_total = reduce_last(
            qkv_part.astype(BF),
            project_part.astype(BF),
            gate_part.astype(BF),
            up_part.astype(BF),
            down_part.astype(BF),
            partial_rows.astype(BF).reshape(4, tokens_here, model),
            gain_parts,
        )
        gain_total = gain_total.reshape(2, -1)
        first_total, second_total = gain_total[0], gain_total[1]
        qkv_total = qkv_total.astype(F32)
        project_total = project_total.T.astype(F32)
        gate_total, up_total, down_total = [t.astype(F32) for t in ffn_totals]
    else:

        def owned(part):
            share = lax.psum_scatter(part.astype(BF), "narrow", scatter_dimension=0, tiled=True)
            return lax.psum(share, "wide").astype(F32)

        qkv_total = owned(qkv_part)
        project_total = owned(project_part).T
        first_total = owned(first_gain_part)
        second_total = owned(second_gain_part)
        gate_total, up_total, down_total = (
            lax.psum(gate_part.astype(BF), "narrow").astype(F32),
            lax.psum(up_part.astype(BF), "narrow").astype(F32),
            lax.psum(down_part.astype(BF), "narrow").astype(F32),
        )
        feed = lax.psum_scatter(
            partial_rows.astype(BF), "wide", scatter_dimension=0, tiled=True
        ).astype(F32)
    block_output = (middle + feed).astype(BF)
    return (
        block_output,
        input_grad,
        qkv_total[:, :q_cols],
        qkv_total[:, q_cols : q_cols + k_cols],
        qkv_total[:, q_cols + k_cols :],
        project_total,
        first_total,
        second_total,
        gate_total,
        up_total,
        down_total,
    )


def solution(mesh):
    fast = mesh.shape["narrow"] == 8 and mesh.shape["wide"] == 4
    placed = (
        P(("narrow", "wide"), None),
        P(("narrow", "wide"), None),
        P("narrow", None),
        P("narrow", None),
        P("narrow", None),
        P(None, "narrow"),
        P("narrow"),
        P("narrow"),
        P(None, "wide"),
        P(None, "wide"),
        P("wide", None),
        P(("narrow", "wide"), None),
        P(),
    )
    return jax.shard_map(
        functools.partial(per_device, fast),
        mesh=mesh,
        in_specs=placed,
        out_specs=(
            P(("narrow", "wide"), None),
            P(("narrow", "wide"), None),
            P("narrow", None),
            P("narrow", None),
            P("narrow", None),
            P(None, "narrow"),
            P("narrow"),
            P("narrow"),
            P(None, "wide"),
            P(None, "wide"),
            P("wide", None),
        ),
        check_vma=False,
    )
```

```python
import functools

import jax
import jax.numpy as jnp
from jax import lax
from jax.experimental import pallas as pl
from jax.experimental.pallas import tpu as pltpu
from jax.sharding import PartitionSpec as P

HEADS = 24
KV_HEADS = 6
HEAD_DIM = 64
TILE = 128


EPSILON = 1e-06

BF = jnp.bfloat16
F32 = jnp.float32


def rms_scale(rows, gain):
    factor = lax.rsqrt(jnp.mean(rows * rows, axis=-1, keepdims=True) + EPSILON)
    return rows * factor * gain


def contract_rows(left, right):
    return lax.dot_general(
        left, right, (((0,), (0,)), ((), ())), preferred_element_type=jnp.float32
    )


def contract_cols(left, right):
    return lax.dot_general(
        left, right, (((1,), (1,)), ((), ())), preferred_element_type=jnp.float32
    )


def flip(n, bit):
    return n + bit - 2 * bit * lax.rem(n // bit, 2)


def at(n, w):
    return {"narrow": n, "wide": w}


def send(src, dst, ssem, rsem, n, w):
    return pltpu.make_async_remote_copy(
        src_ref=src,
        dst_ref=dst,
        send_sem=ssem,
        recv_sem=rsem,
        device_id=at(n, w),
        device_id_type=pl.DeviceIdType.MESH,
    )


def greet(narrow_peers, n, w, line):
    barrier = pltpu.get_barrier_semaphore()
    for peer in narrow_peers:
        pl.semaphore_signal(
            barrier, inc=1, device_id=at(peer, w), device_id_type=pl.DeviceIdType.MESH
        )
    if not line:
        pl.semaphore_wait(barrier, len(narrow_peers))
    if line:
        pl.semaphore_signal(
            barrier, inc=1, device_id=at(n, flip(w, 2)), device_id_type=pl.DeviceIdType.MESH
        )

        @pl.when(w > 0)
        def _():
            pl.semaphore_signal(
                barrier, inc=1, device_id=at(n, w - 1), device_id_type=pl.DeviceIdType.MESH
            )

        @pl.when(w < 3)
        def _():
            pl.semaphore_signal(
                barrier, inc=1, device_id=at(n, w + 1), device_id_type=pl.DeviceIdType.MESH
            )

        @pl.when((w == 0) | (w == 3))
        def _():
            pl.semaphore_wait(barrier, len(narrow_peers) + 2)

        @pl.when((w == 1) | (w == 2))
        def _():
            pl.semaphore_wait(barrier, len(narrow_peers) + 3)


class LineGather:
    KINDS = 4

    def __init__(self, n, w, own, whole, ssem, rsem, chunks):
        self.n, self.w, self.own, self.whole = n, w, own, whole
        self.ssem, self.rsem, self.chunks = ssem, rsem, chunks
        self.rows = own.shape[0] // chunks

    def span(self, i):
        return pl.ds(pl.multiple_of(i * self.rows, self.rows), self.rows)

    def part(self, shard, i):
        return self.whole.at[shard, self.span(i), :]

    def mine(self, i):
        return self.own.at[self.span(i), :]

    def copy(self, kind, i, src, shard, w):
        k = kind * self.chunks + i
        return send(src, self.part(shard, i), self.ssem.at[k], self.rsem.at[k], self.n, w)

    def far(self, i):
        return self.copy(0, i, self.mine(i), self.w, flip(self.w, 2))

    def left(self, i):
        return self.copy(1, i, self.mine(i), self.w, jnp.maximum(self.w - 1, 0))

    def right(self, i):
        return self.copy(2, i, self.mine(i), self.w, jnp.minimum(self.w + 1, 3))

    def onward(self, i):
        shard = flip(self.w, 2)
        return self.copy(3, i, self.part(shard, i), shard, 3 * (self.w // 2))

    def middle(self):
        return (self.w == 1) | (self.w == 2)

    def start_chunk(self, i):
        self.far(i).start()

        @pl.when(self.w > 0)
        def _():
            self.left(i).start()

        @pl.when(self.w < 3)
        def _():
            self.right(i).start()

    def start(self):
        for i in range(self.chunks):
            self.start_chunk(i)

    def forward(self, i):
        self.far(i).wait_recv()

        @pl.when(self.middle())
        def _():
            self.onward(i).start()

    def ready(self, i):
        @pl.when(self.w > 0)
        def _():
            self.right(i).wait_recv()

        @pl.when(self.w < 3)
        def _():
            self.left(i).wait_recv()

        @pl.when((self.w == 0) | (self.w == 3))
        def _():
            self.onward(i).wait_recv()

    def finish_sends(self):
        for i in range(self.chunks):
            self.far(i).wait_send()

        @pl.when(self.w > 0)
        def _():
            for i in range(self.chunks):
                self.left(i).wait_send()

        @pl.when(self.w < 3)
        def _():
            for i in range(self.chunks):
                self.right(i).wait_send()

        @pl.when(self.middle())
        def _():
            for i in range(self.chunks):
                self.onward(i).wait_send()

    def finish(self):
        for i in range(self.chunks):
            self.ready(i)
        self.finish_sends()


def first_kernel(
    q_ref,
    k_ref,
    v_ref,
    p_ref,
    g_ref,
    c_ref,
    qkv_full,
    p_full,
    g_full,
    c_full,
    q_buf,
    k_buf,
    v_buf,
    p_buf,
    g_buf,
    c_buf,
    in_sem,
    out_sem,
    ssem,
    rsem,
    gs_sem,
    gr_sem,
    zs_sem,
    zr_sem,
):
    n, w = lax.axis_index("narrow"), lax.axis_index("wide")
    x, y, c, d = flip(n, 2), flip(n, 4), flip(n, 1), flip(flip(n, 2), 4)
    others = [lax.rem(n + i, 8) for i in range(1, 8)]
    rows = q_ref.shape[0]
    half = rows // 2
    depth = p_ref.shape[0]
    qc, kc = q_ref.shape[1], k_ref.shape[1]
    cols = ((0, qc), (qc, kc), (qc + kc, kc))

    locals_in = []
    for i, (src, dst) in enumerate(
        ((q_ref, q_buf), (k_ref, k_buf), (v_ref, v_buf), (p_ref, p_buf), (g_ref, g_buf), (c_ref, c_buf))
    ):
        cp = pltpu.make_async_copy(src, dst, in_sem.at[i])
        cp.start()
        locals_in.append(cp)

    greet(others, n, w, True)

    def region(t, block, h):
        if t == 3:
            r = pl.ds(0, depth) if h == 2 else pl.ds(h * (depth // 2), depth // 2)
            return p_full.at[r, pl.ds(pl.multiple_of(block * rows, rows), rows)]
        r = pl.ds(block * rows, rows) if h == 2 else pl.ds(block * rows + h * half, half)
        return qkv_full.at[r, pl.ds(cols[t][0], cols[t][1])]

    def own(t, h):
        ref = (q_ref, k_ref, v_ref, p_ref)[t]
        if h == 2:
            return ref
        size = ref.shape[0] // 2
        return ref.at[pl.ds(h * size, size), :]

    def msg(t, kind, src, block, h, peer):
        k = t * 10 + kind
        return send(src, region(t, block, h), ssem.at[k], rsem.at[k], peer, w)

    def to_x(t, h):
        return msg(t, h, own(t, h), n, h, x)

    def to_y(t, h):
        return msg(t, 2 + h, own(t, h), n, h, y)

    def on_x(t):
        return msg(t, 4, region(t, y, 0), y, 0, x)

    def on_y(t):
        return msg(t, 5, region(t, x, 1), x, 1, y)

    def to_c(t, which):
        block = (n, x, y, d)[which]
        src = own(t, 2) if which == 0 else region(t, block, 2)
        return msg(t, 6 + which, src, block, 2, c)

    line = LineGather(n, w, c_ref, c_full, zs_sem, zr_sem, 4)
    for t in range(4):
        to_x(t, 1).start()
        to_y(t, 0).start()
        to_x(t, 0).start()
        to_y(t, 1).start()
        if t == 0:
            line.start()
    for t in range(4):
        to_c(t, 0).start()
    for i, peer in enumerate(others):
        send(g_ref, g_full.at[n], gs_sem.at[i], gr_sem.at[i], peer, w).start()

    outs = (
        (q_buf, region(0, n, 2)),
        (k_buf, region(1, n, 2)),
        (v_buf, region(2, n, 2)),
        (p_buf, region(3, n, 2)),
        (g_buf, g_full.at[n]),
        (c_buf, c_full.at[w]),
    )
    locals_out = []
    for i, (src, dst) in enumerate(outs):
        locals_in[i].wait()
        cp = pltpu.make_async_copy(src, dst, out_sem.at[i])
        cp.start()
        locals_out.append(cp)

    def relay(t):
        to_y(t, 0).wait_recv()
        on_x(t).start()
        to_x(t, 1).wait_recv()
        on_y(t).start()
        to_x(t, 0).wait_recv()
        to_c(t, 1).start()
        to_y(t, 1).wait_recv()
        to_c(t, 2).start()

    def corner(t):
        on_x(t).wait_recv()
        on_y(t).wait_recv()
        to_c(t, 3).start()

    line.forward(0)
    relay(0)
    line.forward(1)
    relay(1)
    relay(2)
    line.forward(2)
    relay(3)
    line.forward(3)
    for t in range(4):
        corner(t)
    for t in range(4):
        for h in range(2):
            to_x(t, h).wait_send()
            to_y(t, h).wait_send()
        on_x(t).wait_send()
        on_y(t).wait_send()
        for which in range(4):
            to_c(t, which).wait()
    for i, peer in enumerate(others):
        send(g_ref, g_full.at[n], gs_sem.at[i], gr_sem.at[i], peer, w).wait()
    line.finish()
    for cp in locals_out:
        cp.wait()


def gather_first(query, key, value, project, gains, cotangent):
    rows = query.shape[0]
    width = query.shape[1] + 2 * key.shape[1]
    spec = pl.BlockSpec(memory_space=pl.ANY)
    return pl.pallas_call(
        first_kernel,
        name="gather_first",
        out_shape=(
            jax.ShapeDtypeStruct((8 * rows, width), BF),
            jax.ShapeDtypeStruct((project.shape[0], 8 * rows), BF),
            jax.ShapeDtypeStruct((8,) + gains.shape, gains.dtype),
            jax.ShapeDtypeStruct((4,) + cotangent.shape, BF),
        ),
        in_specs=[spec] * 6,
        out_specs=[spec] * 4,
        scratch_shapes=[
            pltpu.VMEM(query.shape, BF),
            pltpu.VMEM(key.shape, BF),
            pltpu.VMEM(value.shape, BF),
            pltpu.VMEM(project.shape, BF),
            pltpu.VMEM(gains.shape, gains.dtype),
            pltpu.VMEM(cotangent.shape, BF),
            pltpu.SemaphoreType.DMA((6,)),
            pltpu.SemaphoreType.DMA((6,)),
            pltpu.SemaphoreType.DMA((40,)),
            pltpu.SemaphoreType.DMA((40,)),
            pltpu.SemaphoreType.DMA((7,)),
            pltpu.SemaphoreType.DMA((7,)),
            pltpu.SemaphoreType.DMA((16,)),
            pltpu.SemaphoreType.DMA((16,)),
        ],
        compiler_params=pltpu.CompilerParams(collective_id=1, has_side_effects=True),
    )(query, key, value, project, gains, cotangent)


class LineScatter:
    def __init__(self, n, w, terms, bufs, ssem, rsem, chunks):
        self.n, self.w, self.terms = n, w, terms
        self.from_left, self.from_right, self.from_far, self.relayed, self.total = bufs
        self.ssem, self.rsem, self.chunks = ssem, rsem, chunks
        self.rows = terms.shape[1] // chunks

    def span(self, i):
        return pl.ds(pl.multiple_of(i * self.rows, self.rows), self.rows)

    def cut(self, ref, i):
        return ref.at[self.span(i), :]

    def term(self, d, i):
        return self.terms.at[d, self.span(i), :]

    def copy(self, kind, i, src, dst, w):
        k = kind * self.chunks + i
        return send(src, self.cut(dst, i), self.ssem.at[k], self.rsem.at[k], self.n, w)

    def relay(self, i):
        end = 3 - 3 * (self.w // 2)
        return self.copy(0, i, self.term(end, i), self.relayed, 1 + self.w // 3)

    def far(self, i):
        d = flip(self.w, 2)
        return self.copy(1, i, self.term(d, i), self.from_far, d)

    def far_sum(self, i):
        return self.copy(1, i, self.cut(self.total, i), self.from_far, flip(self.w, 2))

    def left(self, i):
        d = jnp.maximum(self.w - 1, 0)
        return self.copy(2, i, self.term(d, i), self.from_right, d)

    def right(self, i):
        d = jnp.minimum(self.w + 1, 3)
        return self.copy(3, i, self.term(d, i), self.from_left, d)

    def middle(self):
        return (self.w == 1) | (self.w == 2)

    def end(self):
        return (self.w == 0) | (self.w == 3)

    def start_chunk(self, i):
        @pl.when(self.end())
        def _():
            self.relay(i).start()
            self.far(i).start()

        @pl.when(self.w > 0)
        def _():
            self.left(i).start()

        @pl.when(self.w < 3)
        def _():
            self.right(i).start()

    def start(self):
        for i in range(self.chunks):
            self.start_chunk(i)

    def pass_on(self, i, mine):
        @pl.when(self.middle())
        def _():
            self.relay(i).wait_recv()
            rows = self.span(i)
            own = self.terms[flip(self.w, 2), rows, :] if mine is None else mine[rows, :]
            self.total[rows, :] = (own.astype(F32) + self.relayed[rows, :].astype(F32)).astype(BF)
            self.far_sum(i).start()

    def finish(self, i, mine, out):
        rows = self.span(i)
        self.far(i).wait_recv()

        @pl.when(self.w > 0)
        def _():
            self.right(i).wait_recv()

        @pl.when(self.w < 3)
        def _():
            self.left(i).wait_recv()

        def put(*bufs):
            own = self.terms[self.w, rows, :] if mine is None else mine[rows, :]
            total = own.astype(F32)
            for buf in bufs:
                total = total + buf[rows, :].astype(F32)
            out[rows, :] = total.astype(out.dtype)

        @pl.when(self.w == 0)
        def _():
            put(self.from_far, self.from_right)

        @pl.when(self.w == 3)
        def _():
            put(self.from_far, self.from_left)

        @pl.when(self.middle())
        def _():
            put(self.from_far, self.from_left, self.from_right)

    def drain(self):
        for i in range(self.chunks):
            self.far(i).wait_send()

        @pl.when(self.end())
        def _():
            for i in range(self.chunks):
                self.relay(i).wait_send()

        @pl.when(self.w > 0)
        def _():
            for i in range(self.chunks):
                self.left(i).wait_send()

        @pl.when(self.w < 3)
        def _():
            for i in range(self.chunks):
                self.right(i).wait_send()


def middle_kernel(
    mixed,
    cot,
    wg,
    wu,
    wd,
    live,
    back_out,
    partial_out,
    gate_go,
    gate_stay,
    up_go,
    up_stay,
    low_go,
    low_stay,
    high_go,
    high_stay,
    x_all,
    cot_v,
    wg_v,
    wu_v,
    wd_v,
    gate_f,
    up_f,
    back_f,
    hid,
    gb,
    ub,
    terms,
    from_left,
    from_right,
    from_far,
    relayed,
    total,
    part_buf,
    gate_k,
    up_k,
    down_k,
    in_sem,
    ag_s,
    ag_r,
    rs_s,
    rs_r,
    part_sem,
    sw_s,
    sw_r,
    out_sem,
    ready,
):
    n, w = lax.axis_index("narrow"), lax.axis_index("wide")
    y, x, core = n // 4, lax.rem(n // 2, 2), lax.rem(n, 2)
    mate = flip(n, 1)
    chunks = 4
    rows = mixed.shape[0] // chunks
    tokens, model = 4 * mixed.shape[0], mixed.shape[1]
    width = wg.shape[1]
    batch = 4 * rows
    loads = [
        pltpu.make_async_copy(src, dst, in_sem.at[k])
        for k, (src, dst) in enumerate(
            ((mixed, x_all.at[w]), (wg, wg_v), (wu, wu_v), (cot, cot_v), (wd, wd_v))
        )
    ]
    for cp in loads:
        cp.start()
    greet([mate], n, w, True)

    gather = LineGather(n, w, mixed, x_all, ag_s, ag_r, chunks)
    scatter = LineScatter(
        n, w, terms, (from_left, from_right, from_far, relayed, total), rs_s, rs_r, chunks
    )
    for i in range(chunks):
        gather.start_chunk(i)
    gather.forward(0)
    for cp in loads:
        cp.wait()

    def rows_of(ref, i):
        r = pl.ds(pl.multiple_of(i * rows, rows), rows)
        return ref[:, r, :].reshape(batch, ref.shape[2])

    def store(i):
        return pltpu.make_async_copy(
            part_buf.at[lax.rem(i, 2)],
            partial_out.at[:, pl.ds(pl.multiple_of(i * rows, rows), rows), :],
            part_sem.at[lax.rem(i, 2)],
        )

    @pl.loop(0, chunks)
    def _(i):
        r = pl.ds(pl.multiple_of(i * rows, rows), rows)
        gather.ready(i)
        xs = rows_of(x_all, i)
        gate_f[...] = jnp.dot(xs, wg_v[...], preferred_element_type=F32)
        up_f[...] = jnp.dot(xs, wu_v[...], preferred_element_type=F32)

        @pl.when(i < chunks - 1)
        def _():
            gather.forward(i + 1)

        back_f[...] = contract_cols(rows_of(cot_v, i), wd_v[...])
        step = 16

        @pl.loop(0, batch // step)
        def _(t):
            s = pl.ds(pl.multiple_of(t * step, step), step)
            d = t // (rows // step)
            into = pl.ds(
                pl.multiple_of(i * rows + lax.rem(t, rows // step) * step, step), step
            )
            gate, up = gate_f[s, :], up_f[s, :] * live[...]
            sigma = jax.nn.sigmoid(gate)
            silu = gate * sigma
            hid[d, into, :] = (silu * up).astype(BF)
            back = back_f[s, :]
            gb[d, into, :] = (back * up * sigma * (1.0 + gate * (1.0 - sigma))).astype(BF)
            ub[d, into, :] = (back * silu * live[...]).astype(BF)

        @pl.when(i > 0)
        def _():
            scatter.pass_on(i - 1, None)

        terms[:, r, :] = (
            (contract_cols(rows_of(gb, i), wg_v[...]) + contract_cols(rows_of(ub, i), wu_v[...]))
            .astype(BF)
            .reshape(4, rows, model)
        )
        scatter.start_chunk(i)

        @pl.when(i > 1)
        def _():
            store(i - 2).wait()

        part_buf[lax.rem(i, 2)] = (
            jnp.dot(rows_of(hid, i), wd_v[...], preferred_element_type=F32)
            .astype(BF)
            .reshape(4, rows, model)
        )
        store(i).start()

    pl.semaphore_signal(
        ready, inc=1, device_id=at(mate, w), device_id_type=pl.DeviceIdType.MESH
    )
    scatter.pass_on(chunks - 1, None)

    def row_grad(back, block):
        cols = pl.ds(pl.multiple_of(block * (model // 8), model // 8), model // 8)
        return contract_rows(
            x_all[:, :, cols].reshape(tokens, model // 8), back[...].reshape(tokens, width)
        )

    def col_grad(block):
        cols = pl.ds(pl.multiple_of(block * (model // 8), model // 8), model // 8)
        return contract_rows(
            hid[...].reshape(tokens, width), cot_v[:, :, cols].reshape(tokens, model // 8)
        )

    eighth, half = model // 8, model // 2

    def place(j, base):
        return pl.ds(pl.multiple_of(base + j * eighth, eighth), eighth)

    swaps = [
        send(buf.at[pl.ds(half, half), :], buf.at[pl.ds(0, half), :], sw_s.at[k], sw_r.at[k], mate, w)
        for k, buf in enumerate((wg_v, wu_v))
    ]
    swaps.append(
        send(
            wd_v.at[:, pl.ds(half, half)], wd_v.at[:, pl.ds(0, half)], sw_s.at[2], sw_r.at[2], mate, w
        )
    )

    @pl.loop(0, 4)
    def _(j):
        wg_v[place(j, half), :] = row_grad(gb, 2 * j + 1 - core).astype(BF)

    pl.semaphore_wait(ready, 1)
    swaps[0].start()

    @pl.loop(0, 4)
    def _(j):
        wu_v[place(j, half), :] = row_grad(ub, 2 * j + 1 - core).astype(BF)

    swaps[1].start()

    @pl.loop(0, 4)
    def _(j):
        wd_v[:, place(j, half)] = col_grad(2 * j + 1 - core).astype(BF)

    swaps[2].start()

    swaps[0].wait_recv()

    @pl.loop(0, 4)
    def _(j):
        gate_k[j // 2, lax.rem(j, 2)] = (
            row_grad(gb, 2 * j + core) + wg_v[place(j, 0), :].astype(F32)
        ).astype(BF)

    cut = width // 2
    pieces = (
        (gate_k.at[:, 1 - x], gate_go),
        (gate_k.at[:, x], gate_stay),
        (up_k.at[1 - y], up_go),
        (up_k.at[y], up_stay),
        (down_k.at[:, 1 - x, pl.ds(0, cut), :], low_go),
        (down_k.at[:, x, pl.ds(0, cut), :], low_stay),
        (down_k.at[1 - y, :, pl.ds(cut, cut), :], high_go),
        (down_k.at[y, :, pl.ds(cut, cut), :], high_stay),
    )
    puts = [
        pltpu.make_async_copy(src, dst, out_sem.at[k]) for k, (src, dst) in enumerate(pieces)
    ]
    for k in (0, 1):
        puts[k].start()
    swaps[1].wait_recv()

    @pl.loop(0, 4)
    def _(j):
        up_k[j // 2, lax.rem(j, 2)] = (
            row_grad(ub, 2 * j + core) + wu_v[place(j, 0), :].astype(F32)
        ).astype(BF)

    for k in (2, 3):
        puts[k].start()
    swaps[2].wait_recv()

    @pl.loop(0, 4)
    def _(j):
        down_k[j // 2, lax.rem(j, 2)] = (
            col_grad(2 * j + core) + wd_v[:, place(j, 0)].astype(F32)
        ).astype(BF)

    for k in (4, 5, 6, 7):
        puts[k].start()
    for i in range(chunks):
        scatter.finish(i, None, back_out)
    scatter.drain()
    gather.finish_sends()
    for k in range(3):
        swaps[k].wait_send()
    store(chunks - 2).wait()
    store(chunks - 1).wait()
    for cp in puts:
        cp.wait()


def feed_forward(mixed, cot, gate_weight, up_weight, down_weight, live):
    tokens_here, model = mixed.shape
    width = gate_weight.shape[1]
    rows, eighth, cut = tokens_here // 4, model // 8, width // 2
    hbm, vmem = pl.BlockSpec(memory_space=pl.ANY), pl.BlockSpec(memory_space=pltpu.VMEM)
    row_piece = jax.ShapeDtypeStruct((2, eighth, width), BF)
    col_piece = jax.ShapeDtypeStruct((2, cut, eighth), BF)
    dma = pltpu.SemaphoreType.DMA
    acc = pltpu.VMEM((4 * rows, width), F32)
    act = pltpu.VMEM((4, tokens_here, width), BF)
    tok = pltpu.VMEM((4, tokens_here, model), BF)
    own = pltpu.VMEM((tokens_here, model), BF)
    return pl.pallas_call(
        middle_kernel,
        name="feed_forward",
        out_shape=(
            jax.ShapeDtypeStruct(mixed.shape, F32),
            jax.ShapeDtypeStruct((4,) + mixed.shape, BF),
        )
        + (row_piece,) * 4
        + (col_piece,) * 4,
        in_specs=[hbm] * 5 + [vmem],
        out_specs=[vmem] + [hbm] * 9,
        scratch_shapes=[
            tok,
            tok,
            pltpu.VMEM(gate_weight.shape, BF),
            pltpu.VMEM(up_weight.shape, BF),
            pltpu.VMEM(down_weight.shape, BF),
            acc,
            acc,
            acc,
            act,
            act,
            act,
            tok,
            own,
            own,
            own,
            own,
            own,
            pltpu.VMEM((2, 4, rows, model), BF),
            pltpu.VMEM((2, 2, eighth, width), BF),
            pltpu.VMEM((2, 2, eighth, width), BF),
            pltpu.VMEM((2, 2, width, eighth), BF),
            dma((5,)),
            dma((16,)),
            dma((16,)),
            dma((16,)),
            dma((16,)),
            dma((2,)),
            dma((3,)),
            dma((3,)),
            dma((8,)),
            pltpu.SemaphoreType.REGULAR,
        ],
        compiler_params=pltpu.CompilerParams(
            collective_id=5, has_side_effects=True, vmem_limit_bytes=64 * 1024 * 1024 - 65536
        ),
    )(mixed, cot, gate_weight, up_weight, down_weight, live)


class Reduce:
    def __init__(self, me, part, cols, x_first, bufs, sems, k):
        self.n, self.w, self.y, self.x, self.core = me
        self.part, self.cols, self.x_first = part, pl.ds(*cols), x_first
        self.sum, self.pair, self.one, self.two = bufs
        self.sems, self.k = sems, k
        self.rows = part.shape[3]
        self.near = flip(self.n, 2) if x_first else flip(self.n, 4)
        self.next = flip(self.n, 4) if x_first else flip(self.n, 2)

    def load(self):
        return pltpu.make_async_copy(
            self.part.at[:, :, self.core, :, self.cols], self.sum, self.sems[0].at[self.k]
        )

    def swap(self):
        return send(
            self.part.at[:, :, 1 - self.core, :, self.cols],
            self.pair,
            self.sems[1].at[self.k],
            self.sems[2].at[self.k],
            flip(self.n, 1),
            self.w,
        )

    def block(self, first, second):
        return (second, first) if self.x_first else (first, second)

    def axes(self):
        return (self.x, self.y) if self.x_first else (self.y, self.x)

    def stage(self, s):
        a, b = self.axes()
        if s == 1:
            src = self.sum.at[:, 1 - a] if self.x_first else self.sum.at[1 - a]
            dst, peer = self.one, self.near
        else:
            src = self.sum.at[self.block(a, 1 - b)]
            dst, peer = self.two, self.next
        k = 2 * self.k + s - 1
        return send(src, dst, self.sems[3].at[k], self.sems[4].at[k], peer, self.w)

    def add(self, block, other):
        step = 64 if self.rows % 64 == 0 else 48

        @pl.loop(0, self.rows // step)
        def _(i):
            r = pl.ds(pl.multiple_of(i * step, step), step)
            self.sum[block[0], block[1], r, :] = (
                self.sum[block[0], block[1], r, :] + other[r, :]
            )

    def after_swap(self):
        a, b = self.axes()
        self.swap().wait_recv()
        self.load().wait()
        for first in (1 - a, a):
            for second in (1 - b, b):
                block = self.block(first, second)
                self.add(block, self.pair.at[block])
            if first is not a:
                self.stage(1).start()

    def after_one(self):
        a, b = self.axes()
        self.stage(1).wait()
        self.add(self.block(a, 1 - b), self.one.at[1 - b])
        self.stage(2).start()
        self.add(self.block(a, b), self.one.at[b])

    def after_two(self):
        a, b = self.axes()
        self.stage(2).wait()
        self.add(self.block(a, b), self.two)

    def result(self):
        return self.sum.at[self.y, self.x]


class Half:
    def __init__(self, me, kept, came, x_first, bufs, sems, k):
        self.n, self.w, self.y, self.x, self.core = me
        self.kept, self.came, self.x_first = kept, came, x_first
        self.sum, self.one, self.two = bufs
        self.sems, self.k = sems, k
        self.rows = kept.shape[1]
        self.next = flip(self.n, 4) if x_first else flip(self.n, 2)
        self.here = self.y if x_first else self.x

    def loads(self):
        return [
            pltpu.make_async_copy(self.kept, self.sum, self.sems[0].at[2 * self.k]),
            pltpu.make_async_copy(self.came, self.one, self.sems[0].at[2 * self.k + 1]),
        ]

    def stage(self):
        return send(
            self.sum.at[1 - self.here],
            self.two,
            self.sems[1].at[self.k],
            self.sems[2].at[self.k],
            self.next,
            self.w,
        )

    def add(self, block, other):
        @pl.loop(0, self.rows // 64)
        def _(i):
            r = pl.ds(pl.multiple_of(i * 64, 64), 64)
            self.sum[block, r, :] = self.sum[block, r, :] + other[r, :]

    def after_one(self):
        for cp in self.loads():
            cp.wait()
        self.add(1 - self.here, self.one.at[1 - self.here])
        self.stage().start()
        self.add(self.here, self.one.at[self.here])

    def after_two(self):
        self.stage().wait()
        self.add(self.here, self.two)

    def result(self):
        return self.sum.at[self.here]


class Spread:
    def __init__(self, item, region, sems, k):
        self.item, self.region, self.sems, self.k = item, region, sems, k
        n = item.n
        self.blocks = (n, flip(n, 2), flip(n, 4), flip(flip(n, 2), 4))

    def copy(self, kind, src, block, peer):
        k = 7 * self.k + kind
        return send(
            src, self.region(block), self.sems[0].at[k], self.sems[1].at[k], peer, self.item.w
        )

    def own(self, kind):
        n = self.item.n
        return self.copy(kind, self.item.result(), n, (flip(n, 2), flip(n, 4), flip(n, 1))[kind])

    def corner(self):
        n, b = self.item.n, self.blocks
        if self.item.x_first:
            return self.copy(3, self.region(b[2]), b[2], flip(n, 2))
        return self.copy(3, self.region(b[1]), b[1], flip(n, 4))

    def to_core(self, which):
        block = self.blocks[which]
        return self.copy(3 + which, self.region(block), block, flip(self.item.n, 1))

    def keep(self):
        return pltpu.make_async_copy(
            self.item.result(), self.region(self.item.n), self.sems[2].at[self.k]
        )

    def start(self):
        order = (1, 0, 2) if self.item.x_first else (0, 1, 2)
        for kind in order:
            self.own(kind).start()
        self.keep().start()

    def relay(self):
        first, second = (1, 0) if self.item.x_first else (0, 1)
        self.own(first).wait_recv()
        self.corner().start()
        self.to_core(1 + first).start()
        self.own(second).wait_recv()
        self.to_core(1 + second).start()

    def last(self):
        self.corner().wait_recv()
        self.to_core(3).start()

    def finish(self):
        for kind in range(2):
            self.own(kind).wait_send()
        self.own(2).wait()
        self.corner().wait_send()
        for which in range(1, 4):
            self.to_core(which).wait()
        self.keep().wait()


class Rows:
    def __init__(self, ref):
        self.ref = ref
        self.shape = (4, ref.shape[0] // 4, ref.shape[1])

    @property
    def at(self):
        return self

    def __getitem__(self, index):
        d, r, _ = index
        return self.ref.at[pl.ds(d * self.shape[1] + r.start, r.size), :]


def last_kernel(items, *refs):
    refs = list(refs)

    def take(count):
        out = refs[:count]
        del refs[:count]
        return out

    parts = take(2)
    stays, comes = take(4), take(4)
    feed_terms, gain_parts = take(2)
    outs = take(4)
    gate_full, up_full, down_full = take(3)
    feed_out, gain_out = take(2)
    attn_bufs = [take(4) for _ in range(4)]
    ffn_bufs = [take(3) for _ in range(4)]
    line_bufs = [take(6) for _ in range(4)]
    feed_bufs = take(7)
    gain_in, gain_sum, gain_line = take(3)
    load_sem, swap_s, swap_r, st_s, st_r = take(5)
    half_sems = take(3)
    sp_sems = take(3)
    lr_s, lr_r, lg_s, lg_r, lg_l = take(5)
    fd_s, fd_r, fd_l = take(3)
    gn_s, gn_r, gz_s, gz_r = take(4)

    n, w = lax.axis_index("narrow"), lax.axis_index("wide")
    me = (n, w, n // 4, lax.rem(n // 2, 2), lax.rem(n, 2))
    attn = [
        Reduce(me, parts[p], cols, xf, attn_bufs[k], (load_sem, swap_s, swap_r, st_s, st_r), k)
        for k, (p, cols, xf) in enumerate(items)
    ]
    ffn = [
        Half(me, stays[k], comes[k], k % 2 == 0, ffn_bufs[k], half_sems, k) for k in range(4)
    ]
    cut, eighth = stays[2].shape[1], stays[2].shape[2]

    def down_region(k):
        return lambda block: down_full.at[
            pl.ds(k * cut, cut), pl.ds(pl.multiple_of(block * eighth, eighth), eighth)
        ]

    regions = (
        lambda block: gate_full.at[block],
        lambda block: up_full.at[block],
        down_region(0),
        down_region(1),
    )
    spread = [Spread(ffn[k], regions[k], sp_sems, k) for k in range(4)]
    for item in ffn:
        for cp in item.loads():
            cp.start()
    for item in attn:
        item.load().start()
    mine, away = feed_bufs[0], feed_bufs[1]
    feed_loads = [
        pltpu.make_async_copy(feed_terms.at[w], mine, fd_l.at[0]),
        pltpu.make_async_copy(feed_terms.at[flip(w, 2)], away, fd_l.at[1]),
    ]
    for cp in feed_loads:
        cp.start()

    barrier = pltpu.get_barrier_semaphore()
    narrow_peers = [lax.rem(n + i, 8) for i in range(1, 8)]
    wide_peers = [lax.rem(w + i, 4) for i in range(1, 4)]
    for peer in narrow_peers:
        pl.semaphore_signal(
            barrier, inc=1, device_id=at(peer, w), device_id_type=pl.DeviceIdType.MESH
        )
    for peer in wide_peers:
        pl.semaphore_signal(
            barrier, inc=1, device_id=at(n, peer), device_id_type=pl.DeviceIdType.MESH
        )
    pl.semaphore_wait(barrier, 10)

    for item in attn:
        item.swap().start()
    feed = LineScatter(n, w, feed_terms, feed_bufs[2:], fd_s, fd_r, 4)
    feed.start()

    def gain_narrow(i):
        peer = narrow_peers[i]
        return send(gain_parts.at[peer], gain_in.at[i], gn_s.at[i], gn_r.at[i], peer, w)

    def gain_wide(i):
        return send(gain_sum, gain_line.at[i], gz_s.at[i], gz_r.at[i], n, wide_peers[i])

    for i in range(7):
        gain_narrow(i).start()

    for item in ffn:
        item.after_one()
    for cp in feed_loads:
        cp.wait()
    feed.pass_on(0, away)
    for item in attn:
        item.after_swap()
    feed.pass_on(1, away)
    for i in range(7):
        gain_narrow(i).wait()
    total = gain_parts[n]
    for i in range(7):
        total = total + gain_in[i]
    gain_sum[...] = total
    for i in range(3):
        gain_wide(i).start()
    feed.pass_on(2, away)
    for item in attn[:2]:
        item.after_one()
    feed.pass_on(3, away)
    for item in attn[2:]:
        item.after_one()
    for k in range(4):
        ffn[k].after_two()
        spread[k].start()

    scatters, gathers = [], []
    for k, item in enumerate(attn):
        own = line_bufs[k][5]
        scatters.append(
            LineScatter(n, w, Rows(item.result()), line_bufs[k][:5], lr_s.at[k], lr_r.at[k], 1)
        )
        gathers.append(LineGather(n, w, own, outs[k], lg_s.at[k], lg_r.at[k], 1))

    def quarter(item, d):
        return item.result().at[pl.ds(d * (item.rows // 4), item.rows // 4), :]

    def line_pass(k):
        scatters[k].pass_on(0, quarter(attn[k], flip(w, 2)))

    def keep(k):
        return pltpu.make_async_copy(line_bufs[k][5], outs[k].at[w], lg_l.at[k])

    def line_turn(k):
        scatters[k].finish(0, quarter(attn[k], w), line_bufs[k][5])
        gathers[k].start()
        keep(k).start()

    for k in (0, 1):
        attn[k].after_two()
        scatters[k].start()
    for i in range(4):
        feed.finish(i, mine, feed_out)
    for k in (2, 3):
        attn[k].after_two()
        scatters[k].start()
    for k in (0, 1, 2, 3):
        line_pass(k)
    for k in (0, 1, 2, 3):
        line_turn(k)
    for s in spread[:2]:
        s.relay()
    for k in (0, 1, 2, 3):
        gathers[k].forward(0)
    for s in spread[2:]:
        s.relay()
    for i in range(3):
        gain_wide(i).wait()
    gain_out[...] = (gain_sum[...] + gain_line[0]) + (gain_line[1] + gain_line[2])
    for s in spread:
        s.last()
    for s in spread:
        s.finish()
    for item in attn:
        item.swap().wait_send()
    for k in range(4):
        scatters[k].drain()
        gathers[k].finish()
        keep(k).wait()
    feed.drain()


def reduce_last(qkv_part, project_part, stays, comes, feed_terms, gain_parts):
    parts = [p.reshape(2, 2, 2, p.shape[0] // 8, p.shape[1]) for p in (qkv_part, project_part)]
    rows = parts[0].shape[3]
    items = []
    for p, xf in ((0, True), (0, False), (1, True), (1, False)):
        half = parts[p].shape[4] // 2
        items.append((p, (0 if xf else half, half), xf))
    scratch = []
    for _, (_, cols), _ in items:
        scratch += [
            pltpu.VMEM((2, 2, rows, cols), BF),
            pltpu.VMEM((2, 2, rows, cols), BF),
            pltpu.VMEM((2, rows, cols), BF),
            pltpu.VMEM((rows, cols), BF),
        ]
    for stay in stays:
        scratch += [
            pltpu.VMEM(stay.shape, BF),
            pltpu.VMEM(stay.shape, BF),
            pltpu.VMEM(stay.shape[1:], BF),
        ]
    outs = []
    for _, (_, cols), _ in items:
        scratch += [pltpu.VMEM((rows // 4, cols), BF)] * 6
        outs.append(jax.ShapeDtypeStruct((4, rows // 4, cols), BF))
    outs.append(jax.ShapeDtypeStruct((8,) + stays[0].shape[1:], BF))
    outs.append(jax.ShapeDtypeStruct((8,) + stays[1].shape[1:], BF))
    outs.append(jax.ShapeDtypeStruct((2 * stays[2].shape[1], 8 * stays[2].shape[2]), BF))
    outs.append(jax.ShapeDtypeStruct(feed_terms.shape[1:], F32))
    outs.append(jax.ShapeDtypeStruct(gain_parts.shape[1:], F32))
    scratch += [pltpu.VMEM(feed_terms.shape[1:], BF)] * 7
    scratch += [
        pltpu.VMEM((7,) + gain_parts.shape[1:], F32),
        pltpu.VMEM(gain_parts.shape[1:], F32),
        pltpu.VMEM((3,) + gain_parts.shape[1:], F32),
    ]
    dma = pltpu.SemaphoreType.DMA
    scratch += [dma((4,)), dma((4,)), dma((4,)), dma((8,)), dma((8,))]
    scratch += [dma((8,)), dma((4,)), dma((4,))]
    scratch += [dma((28,)), dma((28,)), dma((4,))]
    scratch += [dma((4, 4))] * 4 + [dma((4,))]
    scratch += [dma((16,)), dma((16,)), dma((2,))]
    scratch += [dma((7,)), dma((7,)), dma((3,)), dma((3,))]
    hbm, vmem = pl.BlockSpec(memory_space=pl.ANY), pl.BlockSpec(memory_space=pltpu.VMEM)
    out = pl.pallas_call(
        functools.partial(last_kernel, items),
        name="reduce_last",
        out_shape=tuple(outs),
        in_specs=[hbm] * 11 + [vmem],
        out_specs=[hbm] * 7 + [vmem] * 2,
        scratch_shapes=scratch,
        compiler_params=pltpu.CompilerParams(
            collective_id=4, has_side_effects=True, vmem_limit_bytes=64 * 1024 * 1024 - 65536
        ),
    )(*parts, *stays, *comes, feed_terms, gain_parts)
    qkv = jnp.concatenate([out[0].reshape(rows, -1), out[1].reshape(rows, -1)], axis=1)
    project = jnp.concatenate([out[2].reshape(rows, -1), out[3].reshape(rows, -1)], axis=1)
    width = out[4].shape[2]
    ffn = [out[4].reshape(-1, width), out[5].reshape(-1, width), out[6]]
    return qkv, project, ffn, out[7], out[8]


def per_device(
    fast,
    block_input,
    cotangent,
    query_weight,
    key_weight,
    value_weight,
    project_weight,
    prenorm_gain,
    midnorm_gain,
    gate_weight,
    up_weight,
    down_weight,
    doc_lengths,
    tile_counts,
):
    tokens_here, model = block_input.shape
    if fast:
        gains = jnp.stack([prenorm_gain, midnorm_gain]).astype(F32).reshape(1, -1)
        qkv_full, project_full, gains_full, grad_rows = gather_first(
            query_weight, key_weight, value_weight, project_weight, gains, cotangent
        )
        gains_full = gains_full.reshape(8, 2, -1)
        first_gain = gains_full[:, 0].reshape(-1)
        second_gain = gains_full[:, 1].reshape(-1)
    else:
        qkv_full = jnp.concatenate(
            [
                lax.all_gather(query_weight, "narrow", axis=0, tiled=True),
                lax.all_gather(key_weight, "narrow", axis=0, tiled=True),
                lax.all_gather(value_weight, "narrow", axis=0, tiled=True),
            ],
            axis=1,
        )
        project_full = lax.all_gather(project_weight, "narrow", axis=1, tiled=True)
        first_gain = lax.all_gather(prenorm_gain, "narrow", axis=0, tiled=True).astype(F32)
        second_gain = lax.all_gather(midnorm_gain, "narrow", axis=0, tiled=True).astype(F32)
        grad_rows = lax.all_gather(cotangent, "wide", axis=0, tiled=True)
    group = HEADS // KV_HEADS
    scale = HEAD_DIM ** (-0.5)
    q_cols, k_cols = HEADS * HEAD_DIM, KV_HEADS * HEAD_DIM
    inputs_f = block_input.astype(jnp.float32)
    normed = rms_scale(inputs_f, first_gain).astype(jnp.bfloat16)
    qkv = jnp.dot(normed, qkv_full, preferred_element_type=jnp.float32).astype(jnp.bfloat16)
    query_rows = qkv[:, :q_cols].reshape(tokens_here, KV_HEADS, group, HEAD_DIM)
    key_rows = qkv[:, q_cols : q_cols + k_cols].reshape(tokens_here, KV_HEADS, HEAD_DIM)
    value_rows = qkv[:, q_cols + k_cols :].reshape(tokens_here, KV_HEADS, HEAD_DIM)
    ends = jnp.cumsum(doc_lengths[0])
    position = jnp.arange(tokens_here, dtype=jnp.int32)
    segment = jnp.sum((position[:, None] >= ends[None, :]).astype(jnp.int32), axis=1)
    allowed = (segment[:, None] == segment[None, :]) & (position[None, :] <= position[:, None])
    scores = (
        jnp.einsum("qcgd,kcd->cgqk", query_rows, key_rows, preferred_element_type=jnp.float32)
        * scale
    )
    masked = jnp.where(allowed, scores, -1e30)
    peak = jnp.max(masked, axis=-1, keepdims=True)
    expo = jnp.exp(masked - peak)
    total = jnp.sum(expo, axis=-1, keepdims=True)
    probs_low = (expo / total).astype(jnp.bfloat16)
    logsum = peak + jnp.log(total)
    attended = (
        jnp.einsum("cgqk,kcd->qcgd", probs_low, value_rows, preferred_element_type=jnp.float32)
        .astype(jnp.bfloat16)
        .reshape(tokens_here, HEADS * HEAD_DIM)
    )
    branch = jnp.dot(attended, project_full, preferred_element_type=jnp.float32)
    middle = inputs_f + branch
    mixed_in = rms_scale(middle, second_gain).astype(jnp.bfloat16)
    width = gate_weight.shape[1]
    wide_index = lax.axis_index("wide")
    my_count = jnp.sum(
        jnp.where(jnp.arange(tile_counts.shape[0], dtype=jnp.int32) == wide_index, tile_counts, 0)
    )
    live = (jnp.arange(width, dtype=jnp.int32) // TILE < my_count).astype(jnp.float32)
    if fast:
        mixed_back, feed_terms, *pieces = feed_forward(
            mixed_in, grad_rows, gate_weight, up_weight, down_weight, live.reshape(1, -1)
        )
        stays = pieces[1::2]
        comes = [
            lax.ppermute(piece, "narrow", [(i, i ^ bit) for i in range(8)])
            for piece, bit in zip(pieces[0::2], (2, 4, 2, 4))
        ]
    else:
        gathered = lax.all_gather(mixed_in, "wide", axis=0, tiled=True)
        gate_pre = jnp.dot(gathered, gate_weight, preferred_element_type=jnp.float32)
        up_pre = jnp.dot(gathered, up_weight, preferred_element_type=jnp.float32)
        hidden_back = contract_cols(grad_rows, down_weight)
        sigma = jax.nn.sigmoid(gate_pre)
        hidden = (gate_pre * sigma * up_pre * live).astype(BF)
        gate_back = (
            hidden_back * up_pre * live * sigma * (1.0 + gate_pre * (1.0 - sigma))
        ).astype(BF)
        up_back = (hidden_back * gate_pre * sigma * live).astype(BF)
        mixed_terms = (
            contract_cols(gate_back, gate_weight) + contract_cols(up_back, up_weight)
        ).astype(BF)
        mixed_back = lax.psum_scatter(
            mixed_terms, "wide", scatter_dimension=0, tiled=True
        ).astype(F32)
        partial_rows = jnp.dot(hidden, down_weight, preferred_element_type=jnp.float32)
        down_part = contract_rows(hidden, grad_rows)
        gate_part = contract_rows(gathered, gate_back)
        up_part = contract_rows(gathered, up_back)
    out_grad = cotangent.astype(jnp.float32)
    unused_second, second_backward = jax.vjp(rms_scale, middle, second_gain)
    middle_norm_back, second_gain_part = second_backward(mixed_back)
    middle_back = out_grad + middle_norm_back
    branch_back = middle_back.astype(jnp.bfloat16)
    project_part = contract_rows(branch_back, attended)
    attended_back = (
        contract_cols(branch_back, project_full)
        .astype(jnp.bfloat16)
        .reshape(tokens_here, KV_HEADS, group, HEAD_DIM)
    )
    scores_again = (
        jnp.einsum("qcgd,kcd->cgqk", query_rows, key_rows, preferred_element_type=jnp.float32)
        * scale
    )
    probs_again = jnp.where(allowed, jnp.exp(scores_again - logsum), 0.0)
    probs_again_low = probs_again.astype(jnp.bfloat16)
    value_back = (
        jnp.einsum(
            "cgqk,qcgd->kcd", probs_again_low, attended_back, preferred_element_type=jnp.float32
        )
        .astype(jnp.bfloat16)
        .reshape(tokens_here, KV_HEADS * HEAD_DIM)
    )
    probs_back = jnp.einsum(
        "qcgd,kcd->cgqk", attended_back, value_rows, preferred_element_type=jnp.float32
    )
    scores_back = (
        probs_again * (probs_back - jnp.sum(probs_again * probs_back, axis=-1, keepdims=True))
    ).astype(jnp.bfloat16)
    query_back = (
        (
            jnp.einsum("cgqk,kcd->qcgd", scores_back, key_rows, preferred_element_type=jnp.float32)
            * scale
        )
        .astype(jnp.bfloat16)
        .reshape(tokens_here, HEADS * HEAD_DIM)
    )
    key_back = (
        (
            jnp.einsum(
                "cgqk,qcgd->kcd", scores_back, query_rows, preferred_element_type=jnp.float32
            )
            * scale
        )
        .astype(jnp.bfloat16)
        .reshape(tokens_here, KV_HEADS * HEAD_DIM)
    )
    qkv_back = jnp.concatenate([query_back, key_back, value_back], axis=1)
    qkv_part = contract_rows(normed, qkv_back)
    normed_back = contract_cols(qkv_back, qkv_full)
    unused_first, first_backward = jax.vjp(rms_scale, inputs_f, first_gain)
    input_norm_back, first_gain_part = first_backward(normed_back)
    input_grad = (middle_back + input_norm_back).astype(jnp.bfloat16)

    if fast:
        gain_parts = jnp.stack(
            [first_gain_part.reshape(8, -1), second_gain_part.reshape(8, -1)], axis=1
        ).reshape(8, 1, -1)
        qkv_total, project_total, ffn_totals, feed, gain_total = reduce_last(
            qkv_part.astype(BF),
            project_part.astype(BF),
            stays,
            comes,
            feed_terms,
            gain_parts,
        )
        gain_total = gain_total.reshape(2, -1)
        first_total, second_total = gain_total[0], gain_total[1]
        qkv_total = qkv_total.astype(F32)
        project_total = project_total.T.astype(F32)
        gate_total, up_total, down_total = [t.astype(F32) for t in ffn_totals]
    else:

        def owned(part):
            share = lax.psum_scatter(part.astype(BF), "narrow", scatter_dimension=0, tiled=True)
            return lax.psum(share, "wide").astype(F32)

        qkv_total = owned(qkv_part)
        project_total = owned(project_part).T
        first_total = owned(first_gain_part)
        second_total = owned(second_gain_part)
        gate_total, up_total, down_total = (
            lax.psum(gate_part.astype(BF), "narrow").astype(F32),
            lax.psum(up_part.astype(BF), "narrow").astype(F32),
            lax.psum(down_part.astype(BF), "narrow").astype(F32),
        )
        feed = lax.psum_scatter(
            partial_rows.astype(BF), "wide", scatter_dimension=0, tiled=True
        ).astype(F32)
    block_output = (middle + feed).astype(BF)
    return (
        block_output,
        input_grad,
        qkv_total[:, :q_cols],
        qkv_total[:, q_cols : q_cols + k_cols],
        qkv_total[:, q_cols + k_cols :],
        project_total,
        first_total,
        second_total,
        gate_total,
        up_total,
        down_total,
    )


def solution(mesh):
    fast = mesh.shape["narrow"] == 8 and mesh.shape["wide"] == 4
    placed = (
        P(("narrow", "wide"), None),
        P(("narrow", "wide"), None),
        P("narrow", None),
        P("narrow", None),
        P("narrow", None),
        P(None, "narrow"),
        P("narrow"),
        P("narrow"),
        P(None, "wide"),
        P(None, "wide"),
        P("wide", None),
        P(("narrow", "wide"), None),
        P(),
    )
    return jax.shard_map(
        functools.partial(per_device, fast),
        mesh=mesh,
        in_specs=placed,
        out_specs=(
            P(("narrow", "wide"), None),
            P(("narrow", "wide"), None),
            P("narrow", None),
            P("narrow", None),
            P("narrow", None),
            P(None, "narrow"),
            P("narrow"),
            P("narrow"),
            P(None, "wide"),
            P(None, "wide"),
            P("wide", None),
        ),
        check_vma=False,
    )
```

```python
import functools

import jax
import jax.numpy as jnp
from jax import lax
from jax.experimental import pallas as pl
from jax.experimental.pallas import tpu as pltpu
from jax.sharding import PartitionSpec as P

HEADS = 24
KV_HEADS = 6
HEAD_DIM = 64
TILE = 128


EPSILON = 1e-06

BF = jnp.bfloat16
F32 = jnp.float32


def rms_scale(rows, gain):
    factor = lax.rsqrt(jnp.mean(rows * rows, axis=-1, keepdims=True) + EPSILON)
    return rows * factor * gain


def contract_rows(left, right):
    return lax.dot_general(
        left, right, (((0,), (0,)), ((), ())), preferred_element_type=jnp.float32
    )


def contract_cols(left, right):
    return lax.dot_general(
        left, right, (((1,), (1,)), ((), ())), preferred_element_type=jnp.float32
    )


def flip(n, bit):
    return n + bit - 2 * bit * lax.rem(n // bit, 2)


def at(n, w):
    return {"narrow": n, "wide": w}


def send(src, dst, ssem, rsem, n, w):
    return pltpu.make_async_remote_copy(
        src_ref=src,
        dst_ref=dst,
        send_sem=ssem,
        recv_sem=rsem,
        device_id=at(n, w),
        device_id_type=pl.DeviceIdType.MESH,
    )


def greet(narrow_peers, n, w, line):
    barrier = pltpu.get_barrier_semaphore()
    for peer in narrow_peers:
        pl.semaphore_signal(
            barrier, inc=1, device_id=at(peer, w), device_id_type=pl.DeviceIdType.MESH
        )
    if not line:
        pl.semaphore_wait(barrier, len(narrow_peers))
    if line:

        @pl.when(w > 0)
        def _():
            pl.semaphore_signal(
                barrier, inc=1, device_id=at(n, w - 1), device_id_type=pl.DeviceIdType.MESH
            )

        @pl.when(w < 3)
        def _():
            pl.semaphore_signal(
                barrier, inc=1, device_id=at(n, w + 1), device_id_type=pl.DeviceIdType.MESH
            )

        @pl.when((w == 0) | (w == 3))
        def _():
            pl.semaphore_wait(barrier, len(narrow_peers) + 1)

        @pl.when((w == 1) | (w == 2))
        def _():
            pl.semaphore_wait(barrier, len(narrow_peers) + 2)


class LineGather:
    def __init__(self, n, w, own, whole, ssem, rsem, chunks):
        self.n, self.w, self.own, self.whole = n, w, own, whole
        self.ssem, self.rsem, self.chunks = ssem, rsem, chunks
        self.rows = own.shape[0] // chunks

    def span(self, i):
        return pl.ds(pl.multiple_of(i * self.rows, self.rows), self.rows)

    def part(self, shard, i):
        return self.whole.at[shard, self.span(i), :]

    def put(self, way, here, shard, i):
        src = self.own.at[self.span(i), :] if shard is here else self.part(shard, i)
        to = here + 1 - 2 * way
        s = (way * 4 + shard) * self.chunks + i
        r = shard * self.chunks + i
        return send(src, self.part(shard, i), self.ssem.at[s], self.rsem.at[r], self.n, to)

    def came(self, shard, i):
        self.put(0, 0, shard, i).wait_recv()

    def start_chunk(self, i):
        @pl.when(self.w < 3)
        def _():
            self.put(0, self.w, self.w, i).start()

        @pl.when(self.w > 0)
        def _():
            self.put(1, self.w, self.w, i).start()

    def start(self):
        for i in range(self.chunks):
            self.start_chunk(i)

    def near(self, i):
        @pl.when(self.w == 1)
        def _():
            self.came(0, i)
            self.put(0, 1, 0, i).start()
            self.came(2, i)
            self.put(1, 1, 2, i).start()

        @pl.when(self.w == 2)
        def _():
            self.came(3, i)
            self.put(1, 2, 3, i).start()
            self.came(1, i)
            self.put(0, 2, 1, i).start()

    def far(self, i):
        @pl.when(self.w == 1)
        def _():
            self.came(3, i)
            self.put(1, 1, 3, i).start()

        @pl.when(self.w == 2)
        def _():
            self.came(0, i)
            self.put(0, 2, 0, i).start()

    def ready(self, i):
        @pl.when(self.w == 0)
        def _():
            for shard in (1, 2, 3):
                self.came(shard, i)

        @pl.when(self.w == 3)
        def _():
            for shard in (2, 1, 0):
                self.came(shard, i)

    def finish_sends(self):
        for here in range(4):

            @pl.when(self.w == here)
            def _():
                for i in range(self.chunks):
                    if here < 3:
                        for shard in range(here + 1):
                            self.put(0, here, shard, i).wait_send()
                    if here > 0:
                        for shard in range(here, 4):
                            self.put(1, here, shard, i).wait_send()

    def finish(self):
        for i in range(self.chunks):
            self.ready(i)
        self.finish_sends()


def first_kernel(
    q_ref,
    k_ref,
    v_ref,
    p_ref,
    g_ref,
    c_ref,
    qkv_full,
    p_full,
    g_full,
    c_full,
    q_buf,
    k_buf,
    v_buf,
    p_buf,
    g_buf,
    c_buf,
    in_sem,
    out_sem,
    ssem,
    rsem,
    gs_sem,
    gr_sem,
    zs_sem,
    zr_sem,
):
    n, w = lax.axis_index("narrow"), lax.axis_index("wide")
    x, y, c, d = flip(n, 2), flip(n, 4), flip(n, 1), flip(flip(n, 2), 4)
    others = [lax.rem(n + i, 8) for i in range(1, 8)]
    rows = q_ref.shape[0]
    half = rows // 2
    depth = p_ref.shape[0]
    qc, kc = q_ref.shape[1], k_ref.shape[1]
    cols = ((0, qc), (qc, kc), (qc + kc, kc))

    locals_in = []
    for i, (src, dst) in enumerate(
        ((q_ref, q_buf), (k_ref, k_buf), (v_ref, v_buf), (p_ref, p_buf), (g_ref, g_buf), (c_ref, c_buf))
    ):
        cp = pltpu.make_async_copy(src, dst, in_sem.at[i])
        cp.start()
        locals_in.append(cp)

    greet(others, n, w, True)

    def region(t, block, h):
        if t == 3:
            r = pl.ds(0, depth) if h == 2 else pl.ds(h * (depth // 2), depth // 2)
            return p_full.at[r, pl.ds(pl.multiple_of(block * rows, rows), rows)]
        r = pl.ds(block * rows, rows) if h == 2 else pl.ds(block * rows + h * half, half)
        return qkv_full.at[r, pl.ds(cols[t][0], cols[t][1])]

    def own(t, h):
        ref = (q_ref, k_ref, v_ref, p_ref)[t]
        if h == 2:
            return ref
        size = ref.shape[0] // 2
        return ref.at[pl.ds(h * size, size), :]

    def msg(t, kind, src, block, h, peer):
        k = t * 10 + kind
        return send(src, region(t, block, h), ssem.at[k], rsem.at[k], peer, w)

    def to_x(t, h):
        return msg(t, h, own(t, h), n, h, x)

    def to_y(t, h):
        return msg(t, 2 + h, own(t, h), n, h, y)

    def on_x(t):
        return msg(t, 4, region(t, y, 0), y, 0, x)

    def on_y(t):
        return msg(t, 5, region(t, x, 1), x, 1, y)

    def to_c(t, which):
        block = (n, x, y, d)[which]
        src = own(t, 2) if which == 0 else region(t, block, 2)
        return msg(t, 6 + which, src, block, 2, c)

    line = LineGather(n, w, c_ref, c_full, zs_sem, zr_sem, 4)
    for t in range(4):
        to_x(t, 1).start()
        to_y(t, 0).start()
        to_x(t, 0).start()
        to_y(t, 1).start()
        if t == 0:
            line.start()
    for t in range(4):
        to_c(t, 0).start()
    for i, peer in enumerate(others):
        send(g_ref, g_full.at[n], gs_sem.at[i], gr_sem.at[i], peer, w).start()

    outs = (
        (q_buf, region(0, n, 2)),
        (k_buf, region(1, n, 2)),
        (v_buf, region(2, n, 2)),
        (p_buf, region(3, n, 2)),
        (g_buf, g_full.at[n]),
        (c_buf, c_full.at[w]),
    )
    locals_out = []
    for i, (src, dst) in enumerate(outs):
        locals_in[i].wait()
        cp = pltpu.make_async_copy(src, dst, out_sem.at[i])
        cp.start()
        locals_out.append(cp)

    def relay(t):
        to_y(t, 0).wait_recv()
        on_x(t).start()
        to_x(t, 1).wait_recv()
        on_y(t).start()
        to_x(t, 0).wait_recv()
        to_c(t, 1).start()
        to_y(t, 1).wait_recv()
        to_c(t, 2).start()

    def corner(t):
        on_x(t).wait_recv()
        on_y(t).wait_recv()
        to_c(t, 3).start()

    for i in range(3):
        line.near(i)
    relay(0)
    line.near(3)
    relay(1)
    relay(2)
    for i in range(3):
        line.far(i)
    relay(3)
    line.far(3)
    for t in range(4):
        corner(t)
    for t in range(4):
        for h in range(2):
            to_x(t, h).wait_send()
            to_y(t, h).wait_send()
        on_x(t).wait_send()
        on_y(t).wait_send()
        for which in range(4):
            to_c(t, which).wait()
    for i, peer in enumerate(others):
        send(g_ref, g_full.at[n], gs_sem.at[i], gr_sem.at[i], peer, w).wait()
    line.finish()
    for cp in locals_out:
        cp.wait()


def gather_first(query, key, value, project, gains, cotangent):
    rows = query.shape[0]
    width = query.shape[1] + 2 * key.shape[1]
    spec = pl.BlockSpec(memory_space=pl.ANY)
    return pl.pallas_call(
        first_kernel,
        name="gather_first",
        out_shape=(
            jax.ShapeDtypeStruct((8 * rows, width), BF),
            jax.ShapeDtypeStruct((project.shape[0], 8 * rows), BF),
            jax.ShapeDtypeStruct((8,) + gains.shape, gains.dtype),
            jax.ShapeDtypeStruct((4,) + cotangent.shape, BF),
        ),
        in_specs=[spec] * 6,
        out_specs=[spec] * 4,
        scratch_shapes=[
            pltpu.VMEM(query.shape, BF),
            pltpu.VMEM(key.shape, BF),
            pltpu.VMEM(value.shape, BF),
            pltpu.VMEM(project.shape, BF),
            pltpu.VMEM(gains.shape, gains.dtype),
            pltpu.VMEM(cotangent.shape, BF),
            pltpu.SemaphoreType.DMA((6,)),
            pltpu.SemaphoreType.DMA((6,)),
            pltpu.SemaphoreType.DMA((40,)),
            pltpu.SemaphoreType.DMA((40,)),
            pltpu.SemaphoreType.DMA((7,)),
            pltpu.SemaphoreType.DMA((7,)),
            pltpu.SemaphoreType.DMA((32,)),
            pltpu.SemaphoreType.DMA((16,)),
        ],
        compiler_params=pltpu.CompilerParams(collective_id=1, has_side_effects=True),
    )(query, key, value, project, gains, cotangent)


class LineScatter:
    def __init__(self, n, w, terms, bufs, ssem, rsem, chunks):
        self.n, self.w, self.terms, self.bufs = n, w, terms, bufs
        self.ssem, self.rsem, self.chunks = ssem, rsem, chunks
        self.rows = terms.shape[1] // chunks

    def span(self, i):
        return pl.ds(pl.multiple_of(i * self.rows, self.rows), self.rows)

    def term(self, d, i):
        return self.terms.at[d, self.span(i), :]

    def slot(self, way, slot, i):
        return self.bufs[way].at[slot, self.span(i), :]

    def put(self, way, here, d, i, src):
        slot = d - here - 1 if way == 0 else here - 1 - d
        k = (way * 3 + slot) * self.chunks + i
        to = here + 1 - 2 * way
        return send(src, self.slot(way, slot, i), self.ssem.at[k], self.rsem.at[k], self.n, to)

    def came(self, way, slot, i):
        k = (way * 3 + slot) * self.chunks + i
        ref = self.slot(way, slot, i)
        send(ref, ref, self.ssem.at[k], self.rsem.at[k], self.n, 1).wait_recv()

    def begin(self, i):
        for here, way in ((0, 0), (3, 1)):

            @pl.when(self.w == here)
            def _():
                for d in (3, 2, 1) if way == 0 else (0, 1, 2):
                    self.put(way, here, d, i, self.term(d, i)).start()

    def join(self, way, here, d, i):
        slot = d - here if way == 0 else here - d
        self.came(way, slot, i)
        mine, sum_ = self.term(d, i), self.slot(way, slot, i)
        sum_[...] = (mine[...].astype(F32) + sum_[...].astype(F32)).astype(BF)
        self.put(way, here, d, i, sum_).start()

    def pass_on(self, i):
        @pl.when(self.w == 1)
        def _():
            self.join(0, 1, 3, i)
            self.join(0, 1, 2, i)

        @pl.when(self.w == 2)
        def _():
            self.join(1, 2, 0, i)
            self.join(1, 2, 1, i)

    def pass_end(self, i):
        @pl.when(self.w == 1)
        def _():
            self.join(1, 1, 0, i)

        @pl.when(self.w == 2)
        def _():
            self.join(0, 2, 3, i)

    def finish(self, i, out):
        for here, ways in ((0, (1,)), (1, (0, 1)), (2, (0, 1)), (3, (0,))):

            @pl.when(self.w == here)
            def _():
                for way in ways:
                    self.came(way, 0, i)
                total = self.term(here, i)[...].astype(F32)
                for way in ways:
                    total = total + self.slot(way, 0, i)[...].astype(F32)
                out[self.span(i), :] = total.astype(out.dtype)

    def drain(self):
        sent = {
            0: ((0, 3), (0, 2), (0, 1)),
            1: ((0, 3), (0, 2), (1, 0)),
            2: ((1, 0), (1, 1), (0, 3)),
            3: ((1, 0), (1, 1), (1, 2)),
        }
        for here in range(4):

            @pl.when(self.w == here)
            def _():
                for i in range(self.chunks):
                    for way, d in sent[here]:
                        self.put(way, here, d, i, self.term(d, i)).wait_send()


def middle_kernel(
    mixed,
    cot,
    wg,
    wu,
    wd,
    live,
    back_out,
    partial_out,
    gate_go,
    gate_stay,
    up_go,
    up_stay,
    low_go,
    low_stay,
    high_go,
    high_stay,
    x_all,
    cot_v,
    wg_v,
    wu_v,
    wd_v,
    gate_f,
    up_f,
    back_f,
    hid,
    gb,
    ub,
    terms,
    from_left,
    from_right,
    part_buf,
    gate_k,
    up_k,
    down_k,
    in_sem,
    ag_s,
    ag_r,
    rs_s,
    rs_r,
    part_sem,
    sw_s,
    sw_r,
    out_sem,
    ready,
):
    n, w = lax.axis_index("narrow"), lax.axis_index("wide")
    y, x, core = n // 4, lax.rem(n // 2, 2), lax.rem(n, 2)
    mate = flip(n, 1)
    chunks = 4
    rows = mixed.shape[0] // chunks
    tokens, model = 4 * mixed.shape[0], mixed.shape[1]
    width = wg.shape[1]
    batch = 4 * rows
    loads = [
        pltpu.make_async_copy(src, dst, in_sem.at[k])
        for k, (src, dst) in enumerate(
            ((mixed, x_all.at[w]), (wg, wg_v), (wu, wu_v), (cot, cot_v), (wd, wd_v))
        )
    ]
    for cp in loads:
        cp.start()
    greet([mate], n, w, True)

    gather = LineGather(n, w, mixed, x_all, ag_s, ag_r, chunks)
    scatter = LineScatter(n, w, terms, (from_left, from_right), rs_s, rs_r, chunks)
    gather.start_chunk(0)
    gather.start_chunk(1)
    gather.near(0)
    gather.far(0)
    for cp in loads:
        cp.wait()

    def rows_of(ref, i):
        r = pl.ds(pl.multiple_of(i * rows, rows), rows)
        return ref[:, r, :].reshape(batch, ref.shape[2])

    def store(i):
        return pltpu.make_async_copy(
            part_buf.at[lax.rem(i, 2)],
            partial_out.at[:, pl.ds(pl.multiple_of(i * rows, rows), rows), :],
            part_sem.at[lax.rem(i, 2)],
        )

    @pl.loop(0, chunks)
    def _(i):
        r = pl.ds(pl.multiple_of(i * rows, rows), rows)
        gather.ready(i)
        xs = rows_of(x_all, i)
        gate_f[...] = jnp.dot(xs, wg_v[...], preferred_element_type=F32)
        up_f[...] = jnp.dot(xs, wu_v[...], preferred_element_type=F32)

        @pl.when(i < chunks - 1)
        def _():
            gather.near(i + 1)

        @pl.when(i < chunks - 2)
        def _():
            gather.start_chunk(i + 2)

        back_f[...] = contract_cols(rows_of(cot_v, i), wd_v[...])
        step = 16

        @pl.loop(0, batch // step)
        def _(t):
            s = pl.ds(pl.multiple_of(t * step, step), step)
            d = t // (rows // step)
            into = pl.ds(
                pl.multiple_of(i * rows + lax.rem(t, rows // step) * step, step), step
            )
            gate, up = gate_f[s, :], up_f[s, :] * live[...]
            sigma = jax.nn.sigmoid(gate)
            silu = gate * sigma
            hid[d, into, :] = (silu * up).astype(BF)
            back = back_f[s, :]
            gb[d, into, :] = (back * up * sigma * (1.0 + gate * (1.0 - sigma))).astype(BF)
            ub[d, into, :] = (back * silu * live[...]).astype(BF)

        @pl.when(i > 0)
        def _():
            scatter.pass_on(i - 1)

        @pl.when(i < chunks - 1)
        def _():
            gather.far(i + 1)

        terms[:, r, :] = (
            (contract_cols(rows_of(gb, i), wg_v[...]) + contract_cols(rows_of(ub, i), wu_v[...]))
            .astype(BF)
            .reshape(4, rows, model)
        )
        scatter.begin(i)

        @pl.when(i > 1)
        def _():
            store(i - 2).wait()

        part_buf[lax.rem(i, 2)] = (
            jnp.dot(rows_of(hid, i), wd_v[...], preferred_element_type=F32)
            .astype(BF)
            .reshape(4, rows, model)
        )
        store(i).start()

        @pl.when(i > 0)
        def _():
            scatter.pass_end(i - 1)

    pl.semaphore_signal(
        ready, inc=1, device_id=at(mate, w), device_id_type=pl.DeviceIdType.MESH
    )

    def row_grad(back, block):
        cols = pl.ds(pl.multiple_of(block * (model // 8), model // 8), model // 8)
        return contract_rows(
            x_all[:, :, cols].reshape(tokens, model // 8), back[...].reshape(tokens, width)
        )

    def col_grad(block):
        cols = pl.ds(pl.multiple_of(block * (model // 8), model // 8), model // 8)
        return contract_rows(
            hid[...].reshape(tokens, width), cot_v[:, :, cols].reshape(tokens, model // 8)
        )

    eighth, half = model // 8, model // 2

    def place(j, base):
        return pl.ds(pl.multiple_of(base + j * eighth, eighth), eighth)

    swaps = [
        send(buf.at[pl.ds(half, half), :], buf.at[pl.ds(0, half), :], sw_s.at[k], sw_r.at[k], mate, w)
        for k, buf in enumerate((wg_v, wu_v))
    ]
    swaps.append(
        send(
            wd_v.at[:, pl.ds(half, half)], wd_v.at[:, pl.ds(0, half)], sw_s.at[2], sw_r.at[2], mate, w
        )
    )

    @pl.loop(0, 4)
    def _(j):
        wg_v[place(j, half), :] = row_grad(gb, 2 * j + 1 - core).astype(BF)

    scatter.pass_on(chunks - 1)
    pl.semaphore_wait(ready, 1)
    swaps[0].start()

    @pl.loop(0, 4)
    def _(j):
        wu_v[place(j, half), :] = row_grad(ub, 2 * j + 1 - core).astype(BF)

    swaps[1].start()

    @pl.loop(0, 4)
    def _(j):
        wd_v[:, place(j, half)] = col_grad(2 * j + 1 - core).astype(BF)

    swaps[2].start()
    swaps[0].wait_recv()

    @pl.loop(0, 4)
    def _(j):
        gate_k[j // 2, lax.rem(j, 2)] = (
            row_grad(gb, 2 * j + core) + wg_v[place(j, 0), :].astype(F32)
        ).astype(BF)

    cut = width // 2
    pieces = (
        (gate_k.at[:, 1 - x], gate_go),
        (gate_k.at[:, x], gate_stay),
        (up_k.at[1 - y], up_go),
        (up_k.at[y], up_stay),
        (down_k.at[:, 1 - x, pl.ds(0, cut), :], low_go),
        (down_k.at[:, x, pl.ds(0, cut), :], low_stay),
        (down_k.at[1 - y, :, pl.ds(cut, cut), :], high_go),
        (down_k.at[y, :, pl.ds(cut, cut), :], high_stay),
    )
    puts = [
        pltpu.make_async_copy(src, dst, out_sem.at[k]) for k, (src, dst) in enumerate(pieces)
    ]
    for k in (0, 1):
        puts[k].start()
    scatter.pass_end(chunks - 1)
    swaps[1].wait_recv()

    @pl.loop(0, 4)
    def _(j):
        up_k[j // 2, lax.rem(j, 2)] = (
            row_grad(ub, 2 * j + core) + wu_v[place(j, 0), :].astype(F32)
        ).astype(BF)

    for k in (2, 3):
        puts[k].start()
    swaps[2].wait_recv()

    @pl.loop(0, 4)
    def _(j):
        down_k[j // 2, lax.rem(j, 2)] = (
            col_grad(2 * j + core) + wd_v[:, place(j, 0)].astype(F32)
        ).astype(BF)

    for k in (4, 5, 6, 7):
        puts[k].start()
    for i in range(chunks):
        scatter.finish(i, back_out)
    scatter.drain()
    gather.finish_sends()
    for k in range(3):
        swaps[k].wait_send()
    store(chunks - 2).wait()
    store(chunks - 1).wait()
    for cp in puts:
        cp.wait()


def feed_forward(mixed, cot, gate_weight, up_weight, down_weight, live):
    tokens_here, model = mixed.shape
    width = gate_weight.shape[1]
    rows, eighth, cut = tokens_here // 4, model // 8, width // 2
    hbm, vmem = pl.BlockSpec(memory_space=pl.ANY), pl.BlockSpec(memory_space=pltpu.VMEM)
    row_piece = jax.ShapeDtypeStruct((2, eighth, width), BF)
    col_piece = jax.ShapeDtypeStruct((2, cut, eighth), BF)
    dma = pltpu.SemaphoreType.DMA
    acc = pltpu.VMEM((4 * rows, width), F32)
    act = pltpu.VMEM((4, tokens_here, width), BF)
    tok = pltpu.VMEM((4, tokens_here, model), BF)
    three = pltpu.VMEM((3, tokens_here, model), BF)
    return pl.pallas_call(
        middle_kernel,
        name="feed_forward",
        out_shape=(
            jax.ShapeDtypeStruct(mixed.shape, F32),
            jax.ShapeDtypeStruct((4,) + mixed.shape, BF),
        )
        + (row_piece,) * 4
        + (col_piece,) * 4,
        in_specs=[hbm] * 5 + [vmem],
        out_specs=[vmem] + [hbm] * 9,
        scratch_shapes=[
            tok,
            tok,
            pltpu.VMEM(gate_weight.shape, BF),
            pltpu.VMEM(up_weight.shape, BF),
            pltpu.VMEM(down_weight.shape, BF),
            acc,
            acc,
            acc,
            act,
            act,
            act,
            tok,
            three,
            three,
            pltpu.VMEM((2, 4, rows, model), BF),
            pltpu.VMEM((2, 2, eighth, width), BF),
            pltpu.VMEM((2, 2, eighth, width), BF),
            pltpu.VMEM((2, 2, width, eighth), BF),
            dma((5,)),
            dma((32,)),
            dma((16,)),
            dma((24,)),
            dma((24,)),
            dma((2,)),
            dma((3,)),
            dma((3,)),
            dma((8,)),
            pltpu.SemaphoreType.REGULAR,
        ],
        compiler_params=pltpu.CompilerParams(
            collective_id=5, has_side_effects=True, vmem_limit_bytes=64 * 1024 * 1024 - 65536
        ),
    )(mixed, cot, gate_weight, up_weight, down_weight, live)


class Reduce:
    def __init__(self, me, part, cols, x_first, bufs, sems, k):
        self.n, self.w, self.y, self.x, self.core = me
        self.part, self.cols, self.x_first = part, pl.ds(*cols), x_first
        self.sum, self.pair, self.one, self.two = bufs
        self.sems, self.k = sems, k
        self.rows = part.shape[3]
        self.near = flip(self.n, 2) if x_first else flip(self.n, 4)
        self.next = flip(self.n, 4) if x_first else flip(self.n, 2)

    def load(self):
        return pltpu.make_async_copy(
            self.part.at[:, :, self.core, :, self.cols], self.sum, self.sems[0].at[self.k]
        )

    def swap(self):
        return send(
            self.part.at[:, :, 1 - self.core, :, self.cols],
            self.pair,
            self.sems[1].at[self.k],
            self.sems[2].at[self.k],
            flip(self.n, 1),
            self.w,
        )

    def block(self, first, second):
        return (second, first) if self.x_first else (first, second)

    def axes(self):
        return (self.x, self.y) if self.x_first else (self.y, self.x)

    def stage(self, s):
        a, b = self.axes()
        if s == 1:
            src = self.sum.at[:, 1 - a] if self.x_first else self.sum.at[1 - a]
            dst, peer = self.one, self.near
        else:
            src = self.sum.at[self.block(a, 1 - b)]
            dst, peer = self.two, self.next
        k = 2 * self.k + s - 1
        return send(src, dst, self.sems[3].at[k], self.sems[4].at[k], peer, self.w)

    def add(self, block, other):
        step = 64 if self.rows % 64 == 0 else 48

        @pl.loop(0, self.rows // step)
        def _(i):
            r = pl.ds(pl.multiple_of(i * step, step), step)
            self.sum[block[0], block[1], r, :] = (
                self.sum[block[0], block[1], r, :] + other[r, :]
            )

    def after_swap(self):
        a, b = self.axes()
        self.swap().wait_recv()
        self.load().wait()
        for first in (1 - a, a):
            for second in (1 - b, b):
                block = self.block(first, second)
                self.add(block, self.pair.at[block])
            if first is not a:
                self.stage(1).start()

    def after_one(self):
        a, b = self.axes()
        self.stage(1).wait()
        self.add(self.block(a, 1 - b), self.one.at[1 - b])
        self.stage(2).start()
        self.add(self.block(a, b), self.one.at[b])

    def after_two(self):
        a, b = self.axes()
        self.stage(2).wait()
        self.add(self.block(a, b), self.two)

    def result(self):
        return self.sum.at[self.y, self.x]


class Half:
    def __init__(self, me, kept, came, x_first, bufs, sems, k):
        self.n, self.w, self.y, self.x, self.core = me
        self.kept, self.came, self.x_first = kept, came, x_first
        self.sum, self.one, self.two = bufs
        self.sems, self.k = sems, k
        self.rows = kept.shape[1]
        self.next = flip(self.n, 4) if x_first else flip(self.n, 2)
        self.here = self.y if x_first else self.x

    def loads(self):
        return [
            pltpu.make_async_copy(self.kept, self.sum, self.sems[0].at[2 * self.k]),
            pltpu.make_async_copy(self.came, self.one, self.sems[0].at[2 * self.k + 1]),
        ]

    def stage(self):
        return send(
            self.sum.at[1 - self.here],
            self.two,
            self.sems[1].at[self.k],
            self.sems[2].at[self.k],
            self.next,
            self.w,
        )

    def add(self, block, other):
        @pl.loop(0, self.rows // 64)
        def _(i):
            r = pl.ds(pl.multiple_of(i * 64, 64), 64)
            self.sum[block, r, :] = self.sum[block, r, :] + other[r, :]

    def after_one(self):
        for cp in self.loads():
            cp.wait()
        self.add(1 - self.here, self.one.at[1 - self.here])
        self.stage().start()
        self.add(self.here, self.one.at[self.here])

    def after_two(self):
        self.stage().wait()
        self.add(self.here, self.two)

    def result(self):
        return self.sum.at[self.here]


class Spread:
    def __init__(self, item, region, sems, k):
        self.item, self.region, self.sems, self.k = item, region, sems, k
        n = item.n
        self.blocks = (n, flip(n, 2), flip(n, 4), flip(flip(n, 2), 4))

    def copy(self, kind, src, block, peer):
        k = 7 * self.k + kind
        return send(
            src, self.region(block), self.sems[0].at[k], self.sems[1].at[k], peer, self.item.w
        )

    def own(self, kind):
        n = self.item.n
        return self.copy(kind, self.item.result(), n, (flip(n, 2), flip(n, 4), flip(n, 1))[kind])

    def corner(self):
        n, b = self.item.n, self.blocks
        if self.item.x_first:
            return self.copy(3, self.region(b[2]), b[2], flip(n, 2))
        return self.copy(3, self.region(b[1]), b[1], flip(n, 4))

    def to_core(self, which):
        block = self.blocks[which]
        return self.copy(3 + which, self.region(block), block, flip(self.item.n, 1))

    def keep(self):
        return pltpu.make_async_copy(
            self.item.result(), self.region(self.item.n), self.sems[2].at[self.k]
        )

    def start(self):
        order = (1, 0, 2) if self.item.x_first else (0, 1, 2)
        for kind in order:
            self.own(kind).start()
        self.keep().start()

    def relay(self):
        first, second = (1, 0) if self.item.x_first else (0, 1)
        self.own(first).wait_recv()
        self.corner().start()
        self.to_core(1 + first).start()
        self.own(second).wait_recv()
        self.to_core(1 + second).start()

    def last(self):
        self.corner().wait_recv()
        self.to_core(3).start()

    def finish(self):
        for kind in range(2):
            self.own(kind).wait_send()
        self.own(2).wait()
        self.corner().wait_send()
        for which in range(1, 4):
            self.to_core(which).wait()
        self.keep().wait()


class Rows:
    def __init__(self, ref):
        self.ref = ref
        self.shape = (4, ref.shape[0] // 4, ref.shape[1])

    @property
    def at(self):
        return self

    def __getitem__(self, index):
        d, r, _ = index
        start = pl.multiple_of(d * self.shape[1] + r.start, r.size)
        return self.ref.at[pl.ds(start, r.size), :]


def last_kernel(items, *refs):
    refs = list(refs)

    def take(count):
        out = refs[:count]
        del refs[:count]
        return out

    parts = take(2)
    stays, comes = take(4), take(4)
    feed_terms, gain_parts = take(2)
    outs = take(4)
    gate_full, up_full, down_full = take(3)
    feed_out, gain_out = take(2)
    attn_bufs = [take(4) for _ in range(4)]
    ffn_bufs = [take(3) for _ in range(4)]
    line_bufs = [take(3) for _ in range(4)]
    feed_v, feed_left, feed_right = take(3)
    gain_in, gain_sum, gain_line = take(3)
    load_sem, swap_s, swap_r, st_s, st_r = take(5)
    half_sems = take(3)
    sp_sems = take(3)
    lr_s, lr_r, lg_s, lg_r, lg_l = take(5)
    fd_s, fd_r, fd_l = take(3)
    gn_s, gn_r, gz_s, gz_r = take(4)

    n, w = lax.axis_index("narrow"), lax.axis_index("wide")
    me = (n, w, n // 4, lax.rem(n // 2, 2), lax.rem(n, 2))
    attn = [
        Reduce(me, parts[p], cols, xf, attn_bufs[k], (load_sem, swap_s, swap_r, st_s, st_r), k)
        for k, (p, cols, xf) in enumerate(items)
    ]
    ffn = [
        Half(me, stays[k], comes[k], k % 2 == 0, ffn_bufs[k], half_sems, k) for k in range(4)
    ]
    cut, eighth = stays[2].shape[1], stays[2].shape[2]

    def down_region(k):
        return lambda block: down_full.at[
            pl.ds(k * cut, cut), pl.ds(pl.multiple_of(block * eighth, eighth), eighth)
        ]

    regions = (
        lambda block: gate_full.at[block],
        lambda block: up_full.at[block],
        down_region(0),
        down_region(1),
    )
    spread = [Spread(ffn[k], regions[k], sp_sems, k) for k in range(4)]
    for item in ffn:
        for cp in item.loads():
            cp.start()
    for item in attn:
        item.load().start()
    feed_load = pltpu.make_async_copy(feed_terms, feed_v, fd_l)
    feed_load.start()

    barrier = pltpu.get_barrier_semaphore()
    narrow_peers = [lax.rem(n + i, 8) for i in range(1, 8)]
    wide_peers = [lax.rem(w + i, 4) for i in range(1, 4)]
    for peer in narrow_peers:
        pl.semaphore_signal(
            barrier, inc=1, device_id=at(peer, w), device_id_type=pl.DeviceIdType.MESH
        )
    for peer in wide_peers:
        pl.semaphore_signal(
            barrier, inc=1, device_id=at(n, peer), device_id_type=pl.DeviceIdType.MESH
        )
    pl.semaphore_wait(barrier, 10)

    for item in attn:
        item.swap().start()
    feed_load.wait()
    feed = LineScatter(n, w, feed_v, (feed_left, feed_right), fd_s, fd_r, 4)
    for i in range(4):
        feed.begin(i)

    def gain_narrow(i):
        peer = narrow_peers[i]
        return send(gain_parts.at[peer], gain_in.at[i], gn_s.at[i], gn_r.at[i], peer, w)

    def gain_wide(i):
        return send(gain_sum, gain_line.at[i], gz_s.at[i], gz_r.at[i], n, wide_peers[i])

    for i in range(7):
        gain_narrow(i).start()

    for item in ffn:
        item.after_one()
    feed.pass_on(0)
    for item in attn:
        item.after_swap()
    feed.pass_on(1)
    feed.pass_end(0)
    for i in range(7):
        gain_narrow(i).wait()
    total = gain_parts[n]
    for i in range(7):
        total = total + gain_in[i]
    gain_sum[...] = total
    for i in range(3):
        gain_wide(i).start()
    feed.pass_on(2)
    feed.pass_end(1)
    for item in attn[:2]:
        item.after_one()
    feed.pass_on(3)
    feed.pass_end(2)
    for item in attn[2:]:
        item.after_one()
    feed.pass_end(3)
    for k in range(4):
        ffn[k].after_two()
        spread[k].start()

    scatters, gathers = [], []
    for k, item in enumerate(attn):
        left, right, own = line_bufs[k]
        scatters.append(
            LineScatter(n, w, Rows(item.result()), (left, right), lr_s.at[k], lr_r.at[k], 1)
        )
        gathers.append(LineGather(n, w, own, outs[k], lg_s.at[k], lg_r.at[k], 1))

    def keep(k):
        return pltpu.make_async_copy(line_bufs[k][2], outs[k].at[w], lg_l.at[k])

    def line_turn(k):
        scatters[k].finish(0, line_bufs[k][2])
        gathers[k].start()
        keep(k).start()

    for k in (0, 1):
        attn[k].after_two()
        scatters[k].begin(0)
    for i in range(4):
        feed.finish(i, feed_out)
    for k in (2, 3):
        attn[k].after_two()
        scatters[k].begin(0)
    for k in (0, 1, 2, 3):
        scatters[k].pass_on(0)
    for k in (0, 1, 2, 3):
        scatters[k].pass_end(0)
    for k in (0, 1, 2, 3):
        line_turn(k)
    for s in spread[:2]:
        s.relay()
    for k in (0, 1, 2, 3):
        gathers[k].near(0)
    for k in (0, 1, 2, 3):
        gathers[k].far(0)
    for s in spread[2:]:
        s.relay()
    for i in range(3):
        gain_wide(i).wait()
    gain_out[...] = (gain_sum[...] + gain_line[0]) + (gain_line[1] + gain_line[2])
    for s in spread:
        s.last()
    for s in spread:
        s.finish()
    for item in attn:
        item.swap().wait_send()
    for k in range(4):
        scatters[k].drain()
        gathers[k].finish()
        keep(k).wait()
    feed.drain()


def reduce_last(qkv_part, project_part, stays, comes, feed_terms, gain_parts):
    parts = [p.reshape(2, 2, 2, p.shape[0] // 8, p.shape[1]) for p in (qkv_part, project_part)]
    rows = parts[0].shape[3]
    items = []
    for p, xf in ((0, True), (0, False), (1, True), (1, False)):
        half = parts[p].shape[4] // 2
        items.append((p, (0 if xf else half, half), xf))
    scratch = []
    for _, (_, cols), _ in items:
        scratch += [
            pltpu.VMEM((2, 2, rows, cols), BF),
            pltpu.VMEM((2, 2, rows, cols), BF),
            pltpu.VMEM((2, rows, cols), BF),
            pltpu.VMEM((rows, cols), BF),
        ]
    for stay in stays:
        scratch += [
            pltpu.VMEM(stay.shape, BF),
            pltpu.VMEM(stay.shape, BF),
            pltpu.VMEM(stay.shape[1:], BF),
        ]
    outs = []
    for _, (_, cols), _ in items:
        scratch += [pltpu.VMEM((3, rows // 4, cols), BF)] * 2 + [pltpu.VMEM((rows // 4, cols), BF)]
        outs.append(jax.ShapeDtypeStruct((4, rows // 4, cols), BF))
    outs.append(jax.ShapeDtypeStruct((8,) + stays[0].shape[1:], BF))
    outs.append(jax.ShapeDtypeStruct((8,) + stays[1].shape[1:], BF))
    outs.append(jax.ShapeDtypeStruct((2 * stays[2].shape[1], 8 * stays[2].shape[2]), BF))
    outs.append(jax.ShapeDtypeStruct(feed_terms.shape[1:], F32))
    outs.append(jax.ShapeDtypeStruct(gain_parts.shape[1:], F32))
    scratch += [pltpu.VMEM(feed_terms.shape, BF)]
    scratch += [pltpu.VMEM((3,) + feed_terms.shape[1:], BF)] * 2
    scratch += [
        pltpu.VMEM((7,) + gain_parts.shape[1:], F32),
        pltpu.VMEM(gain_parts.shape[1:], F32),
        pltpu.VMEM((3,) + gain_parts.shape[1:], F32),
    ]
    dma = pltpu.SemaphoreType.DMA
    scratch += [dma((4,)), dma((4,)), dma((4,)), dma((8,)), dma((8,))]
    scratch += [dma((8,)), dma((4,)), dma((4,))]
    scratch += [dma((28,)), dma((28,)), dma((4,))]
    scratch += [dma((4, 6)), dma((4, 6)), dma((4, 8)), dma((4, 4)), dma((4,))]
    scratch += [dma((24,)), dma((24,)), dma]
    scratch += [dma((7,)), dma((7,)), dma((3,)), dma((3,))]
    hbm, vmem = pl.BlockSpec(memory_space=pl.ANY), pl.BlockSpec(memory_space=pltpu.VMEM)
    out = pl.pallas_call(
        functools.partial(last_kernel, items),
        name="reduce_last",
        out_shape=tuple(outs),
        in_specs=[hbm] * 11 + [vmem],
        out_specs=[hbm] * 7 + [vmem] * 2,
        scratch_shapes=scratch,
        compiler_params=pltpu.CompilerParams(
            collective_id=4, has_side_effects=True, vmem_limit_bytes=64 * 1024 * 1024 - 65536
        ),
    )(*parts, *stays, *comes, feed_terms, gain_parts)
    qkv = jnp.concatenate([out[0].reshape(rows, -1), out[1].reshape(rows, -1)], axis=1)
    project = jnp.concatenate([out[2].reshape(rows, -1), out[3].reshape(rows, -1)], axis=1)
    width = out[4].shape[2]
    ffn = [out[4].reshape(-1, width), out[5].reshape(-1, width), out[6]]
    return qkv, project, ffn, out[7], out[8]


def per_device(
    fast,
    block_input,
    cotangent,
    query_weight,
    key_weight,
    value_weight,
    project_weight,
    prenorm_gain,
    midnorm_gain,
    gate_weight,
    up_weight,
    down_weight,
    doc_lengths,
    tile_counts,
):
    tokens_here, model = block_input.shape
    if fast:
        gains = jnp.stack([prenorm_gain, midnorm_gain]).astype(F32).reshape(1, -1)
        qkv_full, project_full, gains_full, grad_rows = gather_first(
            query_weight, key_weight, value_weight, project_weight, gains, cotangent
        )
        gains_full = gains_full.reshape(8, 2, -1)
        first_gain = gains_full[:, 0].reshape(-1)
        second_gain = gains_full[:, 1].reshape(-1)
    else:
        qkv_full = jnp.concatenate(
            [
                lax.all_gather(query_weight, "narrow", axis=0, tiled=True),
                lax.all_gather(key_weight, "narrow", axis=0, tiled=True),
                lax.all_gather(value_weight, "narrow", axis=0, tiled=True),
            ],
            axis=1,
        )
        project_full = lax.all_gather(project_weight, "narrow", axis=1, tiled=True)
        first_gain = lax.all_gather(prenorm_gain, "narrow", axis=0, tiled=True).astype(F32)
        second_gain = lax.all_gather(midnorm_gain, "narrow", axis=0, tiled=True).astype(F32)
        grad_rows = lax.all_gather(cotangent, "wide", axis=0, tiled=True)
    group = HEADS // KV_HEADS
    scale = HEAD_DIM ** (-0.5)
    q_cols, k_cols = HEADS * HEAD_DIM, KV_HEADS * HEAD_DIM
    inputs_f = block_input.astype(jnp.float32)
    normed = rms_scale(inputs_f, first_gain).astype(jnp.bfloat16)
    qkv = jnp.dot(normed, qkv_full, preferred_element_type=jnp.float32).astype(jnp.bfloat16)
    query_rows = qkv[:, :q_cols].reshape(tokens_here, KV_HEADS, group, HEAD_DIM)
    key_rows = qkv[:, q_cols : q_cols + k_cols].reshape(tokens_here, KV_HEADS, HEAD_DIM)
    value_rows = qkv[:, q_cols + k_cols :].reshape(tokens_here, KV_HEADS, HEAD_DIM)
    ends = jnp.cumsum(doc_lengths[0])
    position = jnp.arange(tokens_here, dtype=jnp.int32)
    segment = jnp.sum((position[:, None] >= ends[None, :]).astype(jnp.int32), axis=1)
    allowed = (segment[:, None] == segment[None, :]) & (position[None, :] <= position[:, None])
    scores = (
        jnp.einsum("qcgd,kcd->cgqk", query_rows, key_rows, preferred_element_type=jnp.float32)
        * scale
    )
    masked = jnp.where(allowed, scores, -1e30)
    peak = jnp.max(masked, axis=-1, keepdims=True)
    expo = jnp.exp(masked - peak)
    total = jnp.sum(expo, axis=-1, keepdims=True)
    probs_low = (expo / total).astype(jnp.bfloat16)
    logsum = peak + jnp.log(total)
    attended = (
        jnp.einsum("cgqk,kcd->qcgd", probs_low, value_rows, preferred_element_type=jnp.float32)
        .astype(jnp.bfloat16)
        .reshape(tokens_here, HEADS * HEAD_DIM)
    )
    branch = jnp.dot(attended, project_full, preferred_element_type=jnp.float32)
    middle = inputs_f + branch
    mixed_in = rms_scale(middle, second_gain).astype(jnp.bfloat16)
    width = gate_weight.shape[1]
    wide_index = lax.axis_index("wide")
    my_count = jnp.sum(
        jnp.where(jnp.arange(tile_counts.shape[0], dtype=jnp.int32) == wide_index, tile_counts, 0)
    )
    live = (jnp.arange(width, dtype=jnp.int32) // TILE < my_count).astype(jnp.float32)
    if fast:
        mixed_back, feed_terms, *pieces = feed_forward(
            mixed_in, grad_rows, gate_weight, up_weight, down_weight, live.reshape(1, -1)
        )
        stays = pieces[1::2]
        comes = [
            lax.ppermute(piece, "narrow", [(i, i ^ bit) for i in range(8)])
            for piece, bit in zip(pieces[0::2], (2, 4, 2, 4))
        ]
    else:
        gathered = lax.all_gather(mixed_in, "wide", axis=0, tiled=True)
        gate_pre = jnp.dot(gathered, gate_weight, preferred_element_type=jnp.float32)
        up_pre = jnp.dot(gathered, up_weight, preferred_element_type=jnp.float32)
        hidden_back = contract_cols(grad_rows, down_weight)
        sigma = jax.nn.sigmoid(gate_pre)
        hidden = (gate_pre * sigma * up_pre * live).astype(BF)
        gate_back = (
            hidden_back * up_pre * live * sigma * (1.0 + gate_pre * (1.0 - sigma))
        ).astype(BF)
        up_back = (hidden_back * gate_pre * sigma * live).astype(BF)
        mixed_terms = (
            contract_cols(gate_back, gate_weight) + contract_cols(up_back, up_weight)
        ).astype(BF)
        mixed_back = lax.psum_scatter(
            mixed_terms, "wide", scatter_dimension=0, tiled=True
        ).astype(F32)
        partial_rows = jnp.dot(hidden, down_weight, preferred_element_type=jnp.float32)
        down_part = contract_rows(hidden, grad_rows)
        gate_part = contract_rows(gathered, gate_back)
        up_part = contract_rows(gathered, up_back)
    out_grad = cotangent.astype(jnp.float32)
    unused_second, second_backward = jax.vjp(rms_scale, middle, second_gain)
    middle_norm_back, second_gain_part = second_backward(mixed_back)
    middle_back = out_grad + middle_norm_back
    branch_back = middle_back.astype(jnp.bfloat16)
    project_part = contract_rows(branch_back, attended)
    attended_back = (
        contract_cols(branch_back, project_full)
        .astype(jnp.bfloat16)
        .reshape(tokens_here, KV_HEADS, group, HEAD_DIM)
    )
    scores_again = (
        jnp.einsum("qcgd,kcd->cgqk", query_rows, key_rows, preferred_element_type=jnp.float32)
        * scale
    )
    probs_again = jnp.where(allowed, jnp.exp(scores_again - logsum), 0.0)
    probs_again_low = probs_again.astype(jnp.bfloat16)
    value_back = (
        jnp.einsum(
            "cgqk,qcgd->kcd", probs_again_low, attended_back, preferred_element_type=jnp.float32
        )
        .astype(jnp.bfloat16)
        .reshape(tokens_here, KV_HEADS * HEAD_DIM)
    )
    probs_back = jnp.einsum(
        "qcgd,kcd->cgqk", attended_back, value_rows, preferred_element_type=jnp.float32
    )
    scores_back = (
        probs_again * (probs_back - jnp.sum(probs_again * probs_back, axis=-1, keepdims=True))
    ).astype(jnp.bfloat16)
    query_back = (
        (
            jnp.einsum("cgqk,kcd->qcgd", scores_back, key_rows, preferred_element_type=jnp.float32)
            * scale
        )
        .astype(jnp.bfloat16)
        .reshape(tokens_here, HEADS * HEAD_DIM)
    )
    key_back = (
        (
            jnp.einsum(
                "cgqk,qcgd->kcd", scores_back, query_rows, preferred_element_type=jnp.float32
            )
            * scale
        )
        .astype(jnp.bfloat16)
        .reshape(tokens_here, KV_HEADS * HEAD_DIM)
    )
    qkv_back = jnp.concatenate([query_back, key_back, value_back], axis=1)
    qkv_part = contract_rows(normed, qkv_back)
    normed_back = contract_cols(qkv_back, qkv_full)
    unused_first, first_backward = jax.vjp(rms_scale, inputs_f, first_gain)
    input_norm_back, first_gain_part = first_backward(normed_back)
    input_grad = (middle_back + input_norm_back).astype(jnp.bfloat16)

    if fast:
        gain_parts = jnp.stack(
            [first_gain_part.reshape(8, -1), second_gain_part.reshape(8, -1)], axis=1
        ).reshape(8, 1, -1)
        qkv_total, project_total, ffn_totals, feed, gain_total = reduce_last(
            qkv_part.astype(BF),
            project_part.astype(BF),
            stays,
            comes,
            feed_terms,
            gain_parts,
        )
        gain_total = gain_total.reshape(2, -1)
        first_total, second_total = gain_total[0], gain_total[1]
        qkv_total = qkv_total.astype(F32)
        project_total = project_total.T.astype(F32)
        gate_total, up_total, down_total = [t.astype(F32) for t in ffn_totals]
    else:

        def owned(part):
            share = lax.psum_scatter(part.astype(BF), "narrow", scatter_dimension=0, tiled=True)
            return lax.psum(share, "wide").astype(F32)

        qkv_total = owned(qkv_part)
        project_total = owned(project_part).T
        first_total = owned(first_gain_part)
        second_total = owned(second_gain_part)
        gate_total, up_total, down_total = (
            lax.psum(gate_part.astype(BF), "narrow").astype(F32),
            lax.psum(up_part.astype(BF), "narrow").astype(F32),
            lax.psum(down_part.astype(BF), "narrow").astype(F32),
        )
        feed = lax.psum_scatter(
            partial_rows.astype(BF), "wide", scatter_dimension=0, tiled=True
        ).astype(F32)
    block_output = (middle + feed).astype(BF)
    return (
        block_output,
        input_grad,
        qkv_total[:, :q_cols],
        qkv_total[:, q_cols : q_cols + k_cols],
        qkv_total[:, q_cols + k_cols :],
        project_total,
        first_total,
        second_total,
        gate_total,
        up_total,
        down_total,
    )


def solution(mesh):
    fast = mesh.shape["narrow"] == 8 and mesh.shape["wide"] == 4
    placed = (
        P(("narrow", "wide"), None),
        P(("narrow", "wide"), None),
        P("narrow", None),
        P("narrow", None),
        P("narrow", None),
        P(None, "narrow"),
        P("narrow"),
        P("narrow"),
        P(None, "wide"),
        P(None, "wide"),
        P("wide", None),
        P(("narrow", "wide"), None),
        P(),
    )
    return jax.shard_map(
        functools.partial(per_device, fast),
        mesh=mesh,
        in_specs=placed,
        out_specs=(
            P(("narrow", "wide"), None),
            P(("narrow", "wide"), None),
            P("narrow", None),
            P("narrow", None),
            P("narrow", None),
            P(None, "narrow"),
            P("narrow"),
            P("narrow"),
            P(None, "wide"),
            P(None, "wide"),
            P("wide", None),
        ),
        check_vma=False,
    )
```

```python
import functools

import jax
import jax.numpy as jnp
from jax import lax
from jax.experimental import pallas as pl
from jax.experimental.pallas import tpu as pltpu
from jax.sharding import PartitionSpec as P

HEADS = 24
KV_HEADS = 6
HEAD_DIM = 64
TILE = 128


EPSILON = 1e-06

BF = jnp.bfloat16
F32 = jnp.float32


def rms_scale(rows, gain):
    factor = lax.rsqrt(jnp.mean(rows * rows, axis=-1, keepdims=True) + EPSILON)
    return rows * factor * gain


def contract_rows(left, right):
    return lax.dot_general(
        left, right, (((0,), (0,)), ((), ())), preferred_element_type=jnp.float32
    )


def contract_cols(left, right):
    return lax.dot_general(
        left, right, (((1,), (1,)), ((), ())), preferred_element_type=jnp.float32
    )


def flip(n, bit):
    return n + bit - 2 * bit * lax.rem(n // bit, 2)


def at(n, w):
    return {"narrow": n, "wide": w}


def send(src, dst, ssem, rsem, n, w):
    return pltpu.make_async_remote_copy(
        src_ref=src,
        dst_ref=dst,
        send_sem=ssem,
        recv_sem=rsem,
        device_id=at(n, w),
        device_id_type=pl.DeviceIdType.MESH,
    )


def greet(narrow_peers, n, w, line):
    barrier = pltpu.get_barrier_semaphore()
    for peer in narrow_peers:
        pl.semaphore_signal(
            barrier, inc=1, device_id=at(peer, w), device_id_type=pl.DeviceIdType.MESH
        )
    if not line:
        pl.semaphore_wait(barrier, len(narrow_peers))
    if line:

        @pl.when(w > 0)
        def _():
            pl.semaphore_signal(
                barrier, inc=1, device_id=at(n, w - 1), device_id_type=pl.DeviceIdType.MESH
            )

        @pl.when(w < 3)
        def _():
            pl.semaphore_signal(
                barrier, inc=1, device_id=at(n, w + 1), device_id_type=pl.DeviceIdType.MESH
            )

        @pl.when((w == 0) | (w == 3))
        def _():
            pl.semaphore_wait(barrier, len(narrow_peers) + 1)

        @pl.when((w == 1) | (w == 2))
        def _():
            pl.semaphore_wait(barrier, len(narrow_peers) + 2)


class LineGather:
    def __init__(self, n, w, own, whole, ssem, rsem, chunks):
        self.n, self.w, self.own, self.whole = n, w, own, whole
        self.ssem, self.rsem, self.chunks = ssem, rsem, chunks
        self.rows = own.shape[0] // chunks

    def span(self, i):
        return pl.ds(pl.multiple_of(i * self.rows, self.rows), self.rows)

    def part(self, shard, i):
        return self.whole.at[shard, self.span(i), :]

    def put(self, way, here, shard, i):
        src = self.own.at[self.span(i), :] if shard is here else self.part(shard, i)
        to = here + 1 - 2 * way
        s = (way * 4 + shard) * self.chunks + i
        r = shard * self.chunks + i
        return send(src, self.part(shard, i), self.ssem.at[s], self.rsem.at[r], self.n, to)

    def came(self, shard, i):
        self.put(0, 0, shard, i).wait_recv()

    def start_chunk(self, i):
        @pl.when(self.w < 3)
        def _():
            self.put(0, self.w, self.w, i).start()

        @pl.when(self.w > 0)
        def _():
            self.put(1, self.w, self.w, i).start()

    def start(self):
        for i in range(self.chunks):
            self.start_chunk(i)

    def near(self, i):
        @pl.when(self.w == 1)
        def _():
            self.came(0, i)
            self.put(0, 1, 0, i).start()
            self.came(2, i)
            self.put(1, 1, 2, i).start()

        @pl.when(self.w == 2)
        def _():
            self.came(3, i)
            self.put(1, 2, 3, i).start()
            self.came(1, i)
            self.put(0, 2, 1, i).start()

    def far(self, i):
        @pl.when(self.w == 1)
        def _():
            self.came(3, i)
            self.put(1, 1, 3, i).start()

        @pl.when(self.w == 2)
        def _():
            self.came(0, i)
            self.put(0, 2, 0, i).start()

    def ready(self, i):
        @pl.when(self.w == 0)
        def _():
            for shard in (1, 2, 3):
                self.came(shard, i)

        @pl.when(self.w == 3)
        def _():
            for shard in (2, 1, 0):
                self.came(shard, i)

    def finish_sends(self):
        for here in range(4):

            @pl.when(self.w == here)
            def _():
                for i in range(self.chunks):
                    if here < 3:
                        for shard in range(here + 1):
                            self.put(0, here, shard, i).wait_send()
                    if here > 0:
                        for shard in range(here, 4):
                            self.put(1, here, shard, i).wait_send()

    def finish(self):
        for i in range(self.chunks):
            self.ready(i)
        self.finish_sends()


def first_kernel(
    q_ref,
    k_ref,
    v_ref,
    p_ref,
    g_ref,
    c_ref,
    qkv_full,
    p_full,
    g_full,
    c_full,
    q_buf,
    k_buf,
    v_buf,
    p_buf,
    g_buf,
    c_buf,
    in_sem,
    out_sem,
    ssem,
    rsem,
    gs_sem,
    gr_sem,
    zs_sem,
    zr_sem,
):
    n, w = lax.axis_index("narrow"), lax.axis_index("wide")
    x, y, c, d = flip(n, 2), flip(n, 4), flip(n, 1), flip(flip(n, 2), 4)
    others = [lax.rem(n + i, 8) for i in range(1, 8)]
    rows = q_ref.shape[0]
    half = rows // 2
    depth = p_ref.shape[0]
    qc, kc = q_ref.shape[1], k_ref.shape[1]
    cols = ((0, qc), (qc, kc), (qc + kc, kc))

    locals_in = []
    for i, (src, dst) in enumerate(
        ((q_ref, q_buf), (k_ref, k_buf), (v_ref, v_buf), (p_ref, p_buf), (g_ref, g_buf), (c_ref, c_buf))
    ):
        cp = pltpu.make_async_copy(src, dst, in_sem.at[i])
        cp.start()
        locals_in.append(cp)

    greet(others, n, w, True)

    def region(t, block, h):
        if t == 3:
            r = pl.ds(0, depth) if h == 2 else pl.ds(h * (depth // 2), depth // 2)
            return p_full.at[r, pl.ds(pl.multiple_of(block * rows, rows), rows)]
        r = pl.ds(block * rows, rows) if h == 2 else pl.ds(block * rows + h * half, half)
        return qkv_full.at[r, pl.ds(cols[t][0], cols[t][1])]

    def own(t, h):
        ref = (q_ref, k_ref, v_ref, p_ref)[t]
        if h == 2:
            return ref
        size = ref.shape[0] // 2
        return ref.at[pl.ds(h * size, size), :]

    def msg(t, kind, src, block, h, peer):
        k = t * 10 + kind
        return send(src, region(t, block, h), ssem.at[k], rsem.at[k], peer, w)

    def to_x(t, h):
        return msg(t, h, own(t, h), n, h, x)

    def to_y(t, h):
        return msg(t, 2 + h, own(t, h), n, h, y)

    def on_x(t):
        return msg(t, 4, region(t, y, 0), y, 0, x)

    def on_y(t):
        return msg(t, 5, region(t, x, 1), x, 1, y)

    def to_c(t, which):
        block = (n, x, y, d)[which]
        src = own(t, 2) if which == 0 else region(t, block, 2)
        return msg(t, 6 + which, src, block, 2, c)

    line = LineGather(n, w, c_ref, c_full, zs_sem, zr_sem, 4)
    for t in range(4):
        to_x(t, 1).start()
        to_y(t, 0).start()
        to_x(t, 0).start()
        to_y(t, 1).start()
        if t == 0:
            line.start()
    for t in range(4):
        to_c(t, 0).start()
    for i, peer in enumerate(others):
        send(g_ref, g_full.at[n], gs_sem.at[i], gr_sem.at[i], peer, w).start()

    outs = (
        (q_buf, region(0, n, 2)),
        (k_buf, region(1, n, 2)),
        (v_buf, region(2, n, 2)),
        (p_buf, region(3, n, 2)),
        (g_buf, g_full.at[n]),
        (c_buf, c_full.at[w]),
    )
    locals_out = []
    for i, (src, dst) in enumerate(outs):
        locals_in[i].wait()
        cp = pltpu.make_async_copy(src, dst, out_sem.at[i])
        cp.start()
        locals_out.append(cp)

    def relay(t):
        to_y(t, 0).wait_recv()
        on_x(t).start()
        to_x(t, 1).wait_recv()
        on_y(t).start()
        to_x(t, 0).wait_recv()
        to_c(t, 1).start()
        to_y(t, 1).wait_recv()
        to_c(t, 2).start()

    def corner(t):
        on_x(t).wait_recv()
        on_y(t).wait_recv()
        to_c(t, 3).start()

    for i in range(3):
        line.near(i)
    relay(0)
    line.near(3)
    relay(1)
    relay(2)
    for i in range(3):
        line.far(i)
    relay(3)
    line.far(3)
    for t in range(4):
        corner(t)
    for t in range(4):
        for h in range(2):
            to_x(t, h).wait_send()
            to_y(t, h).wait_send()
        on_x(t).wait_send()
        on_y(t).wait_send()
        for which in range(4):
            to_c(t, which).wait()
    for i, peer in enumerate(others):
        send(g_ref, g_full.at[n], gs_sem.at[i], gr_sem.at[i], peer, w).wait()
    line.finish()
    for cp in locals_out:
        cp.wait()


def gather_first(query, key, value, project, gains, cotangent):
    rows = query.shape[0]
    width = query.shape[1] + 2 * key.shape[1]
    spec = pl.BlockSpec(memory_space=pl.ANY)
    return pl.pallas_call(
        first_kernel,
        name="gather_first",
        out_shape=(
            jax.ShapeDtypeStruct((8 * rows, width), BF),
            jax.ShapeDtypeStruct((project.shape[0], 8 * rows), BF),
            jax.ShapeDtypeStruct((8,) + gains.shape, gains.dtype),
            jax.ShapeDtypeStruct((4,) + cotangent.shape, BF),
        ),
        in_specs=[spec] * 6,
        out_specs=[spec] * 4,
        scratch_shapes=[
            pltpu.VMEM(query.shape, BF),
            pltpu.VMEM(key.shape, BF),
            pltpu.VMEM(value.shape, BF),
            pltpu.VMEM(project.shape, BF),
            pltpu.VMEM(gains.shape, gains.dtype),
            pltpu.VMEM(cotangent.shape, BF),
            pltpu.SemaphoreType.DMA((6,)),
            pltpu.SemaphoreType.DMA((6,)),
            pltpu.SemaphoreType.DMA((40,)),
            pltpu.SemaphoreType.DMA((40,)),
            pltpu.SemaphoreType.DMA((7,)),
            pltpu.SemaphoreType.DMA((7,)),
            pltpu.SemaphoreType.DMA((32,)),
            pltpu.SemaphoreType.DMA((16,)),
        ],
        compiler_params=pltpu.CompilerParams(collective_id=1, has_side_effects=True),
    )(query, key, value, project, gains, cotangent)


class LineScatter:
    def __init__(self, n, w, terms, bufs, ssem, rsem, chunks):
        self.n, self.w, self.terms, self.bufs = n, w, terms, bufs
        self.ssem, self.rsem, self.chunks = ssem, rsem, chunks
        self.rows = terms.shape[1] // chunks

    def span(self, i):
        return pl.ds(pl.multiple_of(i * self.rows, self.rows), self.rows)

    def term(self, d, i):
        return self.terms.at[d, self.span(i), :]

    def slot(self, way, slot, i):
        return self.bufs[way].at[slot, self.span(i), :]

    def put(self, way, here, d, i, src):
        slot = d - here - 1 if way == 0 else here - 1 - d
        k = (way * 3 + slot) * self.chunks + i
        to = here + 1 - 2 * way
        return send(src, self.slot(way, slot, i), self.ssem.at[k], self.rsem.at[k], self.n, to)

    def came(self, way, slot, i):
        k = (way * 3 + slot) * self.chunks + i
        ref = self.slot(way, slot, i)
        send(ref, ref, self.ssem.at[k], self.rsem.at[k], self.n, 1).wait_recv()

    def begin(self, i):
        for here, way in ((0, 0), (3, 1)):

            @pl.when(self.w == here)
            def _():
                for d in (3, 2, 1) if way == 0 else (0, 1, 2):
                    self.put(way, here, d, i, self.term(d, i)).start()

    def join(self, way, here, d, i):
        slot = d - here if way == 0 else here - d
        self.came(way, slot, i)
        mine, sum_ = self.term(d, i), self.slot(way, slot, i)
        sum_[...] = (mine[...].astype(F32) + sum_[...].astype(F32)).astype(BF)
        self.put(way, here, d, i, sum_).start()

    def pass_on(self, i):
        @pl.when(self.w == 1)
        def _():
            self.join(0, 1, 3, i)
            self.join(0, 1, 2, i)

        @pl.when(self.w == 2)
        def _():
            self.join(1, 2, 0, i)
            self.join(1, 2, 1, i)

    def pass_end(self, i):
        @pl.when(self.w == 1)
        def _():
            self.join(1, 1, 0, i)

        @pl.when(self.w == 2)
        def _():
            self.join(0, 2, 3, i)

    def finish(self, i, out):
        for here, ways in ((0, (1,)), (1, (0, 1)), (2, (0, 1)), (3, (0,))):

            @pl.when(self.w == here)
            def _():
                for way in ways:
                    self.came(way, 0, i)
                total = self.term(here, i)[...].astype(F32)
                for way in ways:
                    total = total + self.slot(way, 0, i)[...].astype(F32)
                out[self.span(i), :] = total.astype(out.dtype)

    def drain(self):
        sent = {
            0: ((0, 3), (0, 2), (0, 1)),
            1: ((0, 3), (0, 2), (1, 0)),
            2: ((1, 0), (1, 1), (0, 3)),
            3: ((1, 0), (1, 1), (1, 2)),
        }
        for here in range(4):

            @pl.when(self.w == here)
            def _():
                for i in range(self.chunks):
                    for way, d in sent[here]:
                        self.put(way, here, d, i, self.term(d, i)).wait_send()


def middle_kernel(
    mixed,
    cot,
    wg,
    wu,
    wd,
    live,
    back_out,
    partial_out,
    gate_go,
    gate_stay,
    up_go,
    up_stay,
    low_go,
    low_stay,
    high_go,
    high_stay,
    x_all,
    cot_v,
    wg_v,
    wu_v,
    wd_v,
    gate_f,
    up_f,
    back_f,
    hid,
    gb,
    ub,
    terms,
    from_left,
    from_right,
    part_buf,
    gate_k,
    up_k,
    down_k,
    in_sem,
    ag_s,
    ag_r,
    rs_s,
    rs_r,
    part_sem,
    sw_s,
    sw_r,
    out_sem,
    ready,
):
    n, w = lax.axis_index("narrow"), lax.axis_index("wide")
    y, x, core = n // 4, lax.rem(n // 2, 2), lax.rem(n, 2)
    mate = flip(n, 1)
    chunks = 4
    rows = mixed.shape[0] // chunks
    tokens, model = 4 * mixed.shape[0], mixed.shape[1]
    width = wg.shape[1]
    batch = 4 * rows
    loads = [
        pltpu.make_async_copy(src, dst, in_sem.at[k])
        for k, (src, dst) in enumerate(
            ((mixed, x_all.at[w]), (wg, wg_v), (wu, wu_v), (cot, cot_v), (wd, wd_v))
        )
    ]
    for cp in loads:
        cp.start()
    greet([mate], n, w, True)

    gather = LineGather(n, w, mixed, x_all, ag_s, ag_r, chunks)
    scatter = LineScatter(n, w, terms, (from_left, from_right), rs_s, rs_r, chunks)
    gather.start_chunk(0)
    gather.start_chunk(1)
    gather.near(0)
    gather.far(0)
    for cp in loads:
        cp.wait()

    def rows_of(ref, i):
        r = pl.ds(pl.multiple_of(i * rows, rows), rows)
        return ref[:, r, :].reshape(batch, ref.shape[2])

    def store(i):
        return pltpu.make_async_copy(
            part_buf.at[lax.rem(i, 2)],
            partial_out.at[:, pl.ds(pl.multiple_of(i * rows, rows), rows), :],
            part_sem.at[lax.rem(i, 2)],
        )

    @pl.loop(0, chunks)
    def _(i):
        r = pl.ds(pl.multiple_of(i * rows, rows), rows)
        gather.ready(i)
        xs = rows_of(x_all, i)
        gate_f[...] = jnp.dot(xs, wg_v[...], preferred_element_type=F32)
        up_f[...] = jnp.dot(xs, wu_v[...], preferred_element_type=F32)

        @pl.when(i < chunks - 1)
        def _():
            gather.near(i + 1)

        @pl.when(i < chunks - 2)
        def _():
            gather.start_chunk(i + 2)

        back_f[...] = contract_cols(rows_of(cot_v, i), wd_v[...])
        step = 16

        @pl.loop(0, batch // step)
        def _(t):
            s = pl.ds(pl.multiple_of(t * step, step), step)
            d = t // (rows // step)
            into = pl.ds(
                pl.multiple_of(i * rows + lax.rem(t, rows // step) * step, step), step
            )
            gate, up = gate_f[s, :], up_f[s, :] * live[...]
            sigma = jax.nn.sigmoid(gate)
            silu = gate * sigma
            hid[d, into, :] = (silu * up).astype(BF)
            back = back_f[s, :]
            gb[d, into, :] = (back * up * sigma * (1.0 + gate * (1.0 - sigma))).astype(BF)
            ub[d, into, :] = (back * silu * live[...]).astype(BF)

        @pl.when(i > 0)
        def _():
            scatter.pass_on(i - 1)

        @pl.when(i < chunks - 1)
        def _():
            gather.far(i + 1)

        terms[:, r, :] = (
            (contract_cols(rows_of(gb, i), wg_v[...]) + contract_cols(rows_of(ub, i), wu_v[...]))
            .astype(BF)
            .reshape(4, rows, model)
        )
        scatter.begin(i)

        @pl.when(i > 1)
        def _():
            store(i - 2).wait()

        part_buf[lax.rem(i, 2)] = (
            jnp.dot(rows_of(hid, i), wd_v[...], preferred_element_type=F32)
            .astype(BF)
            .reshape(4, rows, model)
        )
        store(i).start()

        @pl.when(i > 0)
        def _():
            scatter.pass_end(i - 1)

    pl.semaphore_signal(
        ready, inc=1, device_id=at(mate, w), device_id_type=pl.DeviceIdType.MESH
    )

    def row_grad(back, block):
        cols = pl.ds(pl.multiple_of(block * (model // 8), model // 8), model // 8)
        return contract_rows(
            x_all[:, :, cols].reshape(tokens, model // 8), back[...].reshape(tokens, width)
        )

    def col_grad(block):
        cols = pl.ds(pl.multiple_of(block * (model // 8), model // 8), model // 8)
        return contract_rows(
            hid[...].reshape(tokens, width), cot_v[:, :, cols].reshape(tokens, model // 8)
        )

    eighth, half = model // 8, model // 2

    def place(j, base):
        return pl.ds(pl.multiple_of(base + j * eighth, eighth), eighth)

    swaps = [
        send(buf.at[pl.ds(half, half), :], buf.at[pl.ds(0, half), :], sw_s.at[k], sw_r.at[k], mate, w)
        for k, buf in enumerate((wg_v, wu_v))
    ]
    swaps.append(
        send(
            wd_v.at[:, pl.ds(half, half)], wd_v.at[:, pl.ds(0, half)], sw_s.at[2], sw_r.at[2], mate, w
        )
    )

    @pl.loop(0, 4)
    def _(j):
        wg_v[place(j, half), :] = row_grad(gb, 2 * j + 1 - core).astype(BF)

    scatter.pass_on(chunks - 1)
    pl.semaphore_wait(ready, 1)
    swaps[0].start()

    @pl.loop(0, 4)
    def _(j):
        wu_v[place(j, half), :] = row_grad(ub, 2 * j + 1 - core).astype(BF)

    swaps[1].start()

    @pl.loop(0, 4)
    def _(j):
        wd_v[:, place(j, half)] = col_grad(2 * j + 1 - core).astype(BF)

    swaps[2].start()
    swaps[0].wait_recv()

    @pl.loop(0, 4)
    def _(j):
        gate_k[j // 2, lax.rem(j, 2)] = (
            row_grad(gb, 2 * j + core) + wg_v[place(j, 0), :].astype(F32)
        ).astype(BF)

    cut = width // 2
    pieces = (
        (gate_k.at[:, 1 - x], gate_go),
        (gate_k.at[:, x], gate_stay),
        (up_k.at[1 - y], up_go),
        (up_k.at[y], up_stay),
        (down_k.at[:, 1 - x, pl.ds(0, cut), :], low_go),
        (down_k.at[:, x, pl.ds(0, cut), :], low_stay),
        (down_k.at[1 - y, :, pl.ds(cut, cut), :], high_go),
        (down_k.at[y, :, pl.ds(cut, cut), :], high_stay),
    )
    puts = [
        pltpu.make_async_copy(src, dst, out_sem.at[k]) for k, (src, dst) in enumerate(pieces)
    ]
    for k in (0, 1):
        puts[k].start()
    scatter.pass_end(chunks - 1)
    swaps[1].wait_recv()

    @pl.loop(0, 4)
    def _(j):
        up_k[j // 2, lax.rem(j, 2)] = (
            row_grad(ub, 2 * j + core) + wu_v[place(j, 0), :].astype(F32)
        ).astype(BF)

    for k in (2, 3):
        puts[k].start()
    swaps[2].wait_recv()

    @pl.loop(0, 4)
    def _(j):
        down_k[j // 2, lax.rem(j, 2)] = (
            col_grad(2 * j + core) + wd_v[:, place(j, 0)].astype(F32)
        ).astype(BF)

    for k in (4, 5, 6, 7):
        puts[k].start()
    for i in range(chunks):
        scatter.finish(i, back_out)
    scatter.drain()
    gather.finish_sends()
    for k in range(3):
        swaps[k].wait_send()
    store(chunks - 2).wait()
    store(chunks - 1).wait()
    for cp in puts:
        cp.wait()


def feed_forward(mixed, cot, gate_weight, up_weight, down_weight, live):
    tokens_here, model = mixed.shape
    width = gate_weight.shape[1]
    rows, eighth, cut = tokens_here // 4, model // 8, width // 2
    hbm, vmem = pl.BlockSpec(memory_space=pl.ANY), pl.BlockSpec(memory_space=pltpu.VMEM)
    row_piece = jax.ShapeDtypeStruct((2, eighth, width), BF)
    col_piece = jax.ShapeDtypeStruct((2, cut, eighth), BF)
    dma = pltpu.SemaphoreType.DMA
    acc = pltpu.VMEM((4 * rows, width), F32)
    act = pltpu.VMEM((4, tokens_here, width), BF)
    tok = pltpu.VMEM((4, tokens_here, model), BF)
    three = pltpu.VMEM((3, tokens_here, model), BF)
    return pl.pallas_call(
        middle_kernel,
        name="feed_forward",
        out_shape=(
            jax.ShapeDtypeStruct(mixed.shape, F32),
            jax.ShapeDtypeStruct((4,) + mixed.shape, BF),
        )
        + (row_piece,) * 4
        + (col_piece,) * 4,
        in_specs=[hbm] * 5 + [vmem],
        out_specs=[vmem] + [hbm] * 9,
        scratch_shapes=[
            tok,
            tok,
            pltpu.VMEM(gate_weight.shape, BF),
            pltpu.VMEM(up_weight.shape, BF),
            pltpu.VMEM(down_weight.shape, BF),
            acc,
            acc,
            acc,
            act,
            act,
            act,
            tok,
            three,
            three,
            pltpu.VMEM((2, 4, rows, model), BF),
            pltpu.VMEM((2, 2, eighth, width), BF),
            pltpu.VMEM((2, 2, eighth, width), BF),
            pltpu.VMEM((2, 2, width, eighth), BF),
            dma((5,)),
            dma((32,)),
            dma((16,)),
            dma((24,)),
            dma((24,)),
            dma((2,)),
            dma((3,)),
            dma((3,)),
            dma((8,)),
            pltpu.SemaphoreType.REGULAR,
        ],
        compiler_params=pltpu.CompilerParams(
            collective_id=5, has_side_effects=True, vmem_limit_bytes=64 * 1024 * 1024 - 65536
        ),
    )(mixed, cot, gate_weight, up_weight, down_weight, live)


class Reduce:
    def __init__(self, me, factors, cols, x_first, bufs, sems, k):
        self.n, self.w, self.y, self.x, self.core = me
        self.left, self.right = factors
        self.cols, self.x_first = pl.ds(*cols), x_first
        self.away, self.sum, self.pair, self.one, self.two = bufs
        self.sems, self.k = sems, k
        self.rows = self.sum.shape[2]
        self.near = flip(self.n, 2) if x_first else flip(self.n, 4)
        self.next = flip(self.n, 4) if x_first else flip(self.n, 2)

    def term(self, block):
        own = pl.ds(pl.multiple_of(block * self.rows, self.rows), self.rows)
        return contract_rows(self.left[:, own], self.right[:, self.cols])

    def swap(self):
        return send(
            self.away,
            self.pair,
            self.sems[0].at[self.k],
            self.sems[1].at[self.k],
            flip(self.n, 1),
            self.w,
        )

    def before_swap(self):
        @pl.loop(0, 4)
        def _(j):
            self.away[j // 2, lax.rem(j, 2)] = self.term(2 * j + 1 - self.core).astype(BF)

        self.swap().start()

    def block(self, first, second):
        return (second, first) if self.x_first else (first, second)

    def axes(self):
        return (self.x, self.y) if self.x_first else (self.y, self.x)

    def stage(self, s):
        a, b = self.axes()
        if s == 1:
            src = self.sum.at[:, 1 - a] if self.x_first else self.sum.at[1 - a]
            dst, peer = self.one, self.near
        else:
            src = self.sum.at[self.block(a, 1 - b)]
            dst, peer = self.two, self.next
        k = 2 * self.k + s - 1
        return send(src, dst, self.sems[2].at[k], self.sems[3].at[k], peer, self.w)

    def add(self, block, other):
        step = 64 if self.rows % 64 == 0 else 48

        @pl.loop(0, self.rows // step)
        def _(i):
            r = pl.ds(pl.multiple_of(i * step, step), step)
            self.sum[block[0], block[1], r, :] = (
                self.sum[block[0], block[1], r, :] + other[r, :]
            )

    def after_swap(self):
        a, _ = self.axes()
        self.swap().wait_recv()

        @pl.loop(0, 4)
        def _(j):
            first = lax.rem(1 - a + j // 2, 2)
            y, x = self.block(first, lax.rem(j, 2))
            total = self.term(4 * y + 2 * x + self.core) + self.pair[y, x].astype(F32)
            self.sum[y, x] = total.astype(BF)

        self.stage(1).start()

    def after_one(self):
        a, b = self.axes()
        self.stage(1).wait()
        self.add(self.block(a, 1 - b), self.one.at[1 - b])
        self.stage(2).start()
        self.add(self.block(a, b), self.one.at[b])

    def after_two(self):
        a, b = self.axes()
        self.stage(2).wait()
        self.add(self.block(a, b), self.two)

    def result(self):
        return self.sum.at[self.y, self.x]


class Half:
    def __init__(self, me, kept, came, x_first, bufs, sems, k):
        self.n, self.w, self.y, self.x, self.core = me
        self.kept, self.came, self.x_first = kept, came, x_first
        self.sum, self.one, self.two = bufs
        self.sems, self.k = sems, k
        self.rows = kept.shape[1]
        self.next = flip(self.n, 4) if x_first else flip(self.n, 2)
        self.here = self.y if x_first else self.x

    def loads(self):
        return [
            pltpu.make_async_copy(self.kept, self.sum, self.sems[0].at[2 * self.k]),
            pltpu.make_async_copy(self.came, self.one, self.sems[0].at[2 * self.k + 1]),
        ]

    def stage(self):
        return send(
            self.sum.at[1 - self.here],
            self.two,
            self.sems[1].at[self.k],
            self.sems[2].at[self.k],
            self.next,
            self.w,
        )

    def add(self, block, other):
        @pl.loop(0, self.rows // 64)
        def _(i):
            r = pl.ds(pl.multiple_of(i * 64, 64), 64)
            self.sum[block, r, :] = self.sum[block, r, :] + other[r, :]

    def after_one(self):
        for cp in self.loads():
            cp.wait()
        self.add(1 - self.here, self.one.at[1 - self.here])
        self.stage().start()
        self.add(self.here, self.one.at[self.here])

    def after_two(self):
        self.stage().wait()
        self.add(self.here, self.two)

    def result(self):
        return self.sum.at[self.here]


class Spread:
    def __init__(self, item, region, sems, k):
        self.item, self.region, self.sems, self.k = item, region, sems, k
        n = item.n
        self.blocks = (n, flip(n, 2), flip(n, 4), flip(flip(n, 2), 4))

    def copy(self, kind, src, block, peer):
        k = 7 * self.k + kind
        return send(
            src, self.region(block), self.sems[0].at[k], self.sems[1].at[k], peer, self.item.w
        )

    def own(self, kind):
        n = self.item.n
        return self.copy(kind, self.item.result(), n, (flip(n, 2), flip(n, 4), flip(n, 1))[kind])

    def corner(self):
        n, b = self.item.n, self.blocks
        if self.item.x_first:
            return self.copy(3, self.region(b[2]), b[2], flip(n, 2))
        return self.copy(3, self.region(b[1]), b[1], flip(n, 4))

    def to_core(self, which):
        block = self.blocks[which]
        return self.copy(3 + which, self.region(block), block, flip(self.item.n, 1))

    def keep(self):
        return pltpu.make_async_copy(
            self.item.result(), self.region(self.item.n), self.sems[2].at[self.k]
        )

    def start(self):
        order = (1, 0, 2) if self.item.x_first else (0, 1, 2)
        for kind in order:
            self.own(kind).start()
        self.keep().start()

    def relay(self):
        first, second = (1, 0) if self.item.x_first else (0, 1)
        self.own(first).wait_recv()
        self.corner().start()
        self.to_core(1 + first).start()
        self.own(second).wait_recv()
        self.to_core(1 + second).start()

    def last(self):
        self.corner().wait_recv()
        self.to_core(3).start()

    def finish(self):
        for kind in range(2):
            self.own(kind).wait_send()
        self.own(2).wait()
        self.corner().wait_send()
        for which in range(1, 4):
            self.to_core(which).wait()
        self.keep().wait()


class Rows:
    def __init__(self, ref):
        self.ref = ref
        self.shape = (4, ref.shape[0] // 4, ref.shape[1])

    @property
    def at(self):
        return self

    def __getitem__(self, index):
        d, r, _ = index
        start = pl.multiple_of(d * self.shape[1] + r.start, r.size)
        return self.ref.at[pl.ds(start, r.size), :]


def last_kernel(items, *refs):
    refs = list(refs)

    def take(count):
        out = refs[:count]
        del refs[:count]
        return out

    factors = take(4)
    stays, comes = take(4), take(4)
    feed_terms, gain_parts = take(2)
    outs = take(4)
    gate_full, up_full, down_full = take(3)
    feed_out, gain_out = take(2)
    attn_bufs = [take(5) for _ in range(4)]
    ffn_bufs = [take(3) for _ in range(4)]
    line_bufs = [take(3) for _ in range(4)]
    feed_v, feed_left, feed_right = take(3)
    gain_in, gain_sum, gain_line = take(3)
    factor_bufs = take(4)
    load_sem, swap_s, swap_r, st_s, st_r = take(5)
    half_sems = take(3)
    sp_sems = take(3)
    lr_s, lr_r, lg_s, lg_r, lg_l = take(5)
    fd_s, fd_r, fd_l = take(3)
    gn_s, gn_r, gz_s, gz_r = take(4)

    n, w = lax.axis_index("narrow"), lax.axis_index("wide")
    me = (n, w, n // 4, lax.rem(n // 2, 2), lax.rem(n, 2))
    attn = [
        Reduce(
            me,
            factor_bufs[2 * p : 2 * p + 2],
            cols,
            xf,
            attn_bufs[k],
            (swap_s, swap_r, st_s, st_r),
            k,
        )
        for k, (p, cols, xf) in enumerate(items)
    ]
    ffn = [
        Half(me, stays[k], comes[k], k % 2 == 0, ffn_bufs[k], half_sems, k) for k in range(4)
    ]
    cut, eighth = stays[2].shape[1], stays[2].shape[2]

    def down_region(k):
        return lambda block: down_full.at[
            pl.ds(k * cut, cut), pl.ds(pl.multiple_of(block * eighth, eighth), eighth)
        ]

    regions = (
        lambda block: gate_full.at[block],
        lambda block: up_full.at[block],
        down_region(0),
        down_region(1),
    )
    spread = [Spread(ffn[k], regions[k], sp_sems, k) for k in range(4)]
    for item in ffn:
        for cp in item.loads():
            cp.start()
    factor_loads = [
        pltpu.make_async_copy(src, dst, load_sem.at[k])
        for k, (src, dst) in enumerate(zip(factors, factor_bufs))
    ]
    for cp in factor_loads:
        cp.start()
    feed_load = pltpu.make_async_copy(feed_terms, feed_v, fd_l)
    feed_load.start()

    barrier = pltpu.get_barrier_semaphore()
    narrow_peers = [lax.rem(n + i, 8) for i in range(1, 8)]
    wide_peers = [lax.rem(w + i, 4) for i in range(1, 4)]
    for peer in narrow_peers:
        pl.semaphore_signal(
            barrier, inc=1, device_id=at(peer, w), device_id_type=pl.DeviceIdType.MESH
        )
    for peer in wide_peers:
        pl.semaphore_signal(
            barrier, inc=1, device_id=at(n, peer), device_id_type=pl.DeviceIdType.MESH
        )
    pl.semaphore_wait(barrier, 10)

    feed_load.wait()
    feed = LineScatter(n, w, feed_v, (feed_left, feed_right), fd_s, fd_r, 4)
    for i in range(4):
        feed.begin(i)

    def gain_narrow(i):
        peer = narrow_peers[i]
        return send(gain_parts.at[peer], gain_in.at[i], gn_s.at[i], gn_r.at[i], peer, w)

    def gain_wide(i):
        return send(gain_sum, gain_line.at[i], gz_s.at[i], gz_r.at[i], n, wide_peers[i])

    for i in range(7):
        gain_narrow(i).start()

    for item in ffn:
        item.after_one()
    for cp in factor_loads:
        cp.wait()
    for item in attn:
        item.before_swap()
    feed.pass_on(0)
    for item in attn:
        item.after_swap()
    feed.pass_on(1)
    feed.pass_end(0)
    for i in range(7):
        gain_narrow(i).wait()
    total = gain_parts[n]
    for i in range(7):
        total = total + gain_in[i]
    gain_sum[...] = total
    for i in range(3):
        gain_wide(i).start()
    feed.pass_on(2)
    feed.pass_end(1)
    for item in attn[:2]:
        item.after_one()
    feed.pass_on(3)
    feed.pass_end(2)
    for item in attn[2:]:
        item.after_one()
    feed.pass_end(3)
    for k in range(4):
        ffn[k].after_two()
        spread[k].start()

    scatters, gathers = [], []
    for k, item in enumerate(attn):
        left, right, own = line_bufs[k]
        scatters.append(
            LineScatter(n, w, Rows(item.result()), (left, right), lr_s.at[k], lr_r.at[k], 1)
        )
        gathers.append(LineGather(n, w, own, outs[k], lg_s.at[k], lg_r.at[k], 1))

    def keep(k):
        return pltpu.make_async_copy(line_bufs[k][2], outs[k].at[w], lg_l.at[k])

    def line_turn(k):
        scatters[k].finish(0, line_bufs[k][2])
        gathers[k].start()
        keep(k).start()

    for k in (0, 1):
        attn[k].after_two()
        scatters[k].begin(0)
    for i in range(4):
        feed.finish(i, feed_out)
    for k in (2, 3):
        attn[k].after_two()
        scatters[k].begin(0)
    for k in (0, 1, 2, 3):
        scatters[k].pass_on(0)
    for k in (0, 1, 2, 3):
        scatters[k].pass_end(0)
    for k in (0, 1, 2, 3):
        line_turn(k)
    for s in spread[:2]:
        s.relay()
    for k in (0, 1, 2, 3):
        gathers[k].near(0)
    for k in (0, 1, 2, 3):
        gathers[k].far(0)
    for s in spread[2:]:
        s.relay()
    for i in range(3):
        gain_wide(i).wait()
    gain_out[...] = (gain_sum[...] + gain_line[0]) + (gain_line[1] + gain_line[2])
    for s in spread:
        s.last()
    for s in spread:
        s.finish()
    for item in attn:
        item.swap().wait_send()
    for k in range(4):
        scatters[k].drain()
        gathers[k].finish()
        keep(k).wait()
    feed.drain()


def reduce_last(factors, stays, comes, feed_terms, gain_parts):
    rows = factors[0].shape[1] // 8
    items = []
    for p, xf in ((0, True), (0, False), (1, True), (1, False)):
        half = factors[2 * p + 1].shape[1] // 2
        items.append((p, (0 if xf else half, half), xf))
    scratch = []
    for _, (_, cols), _ in items:
        scratch += [
            pltpu.VMEM((2, 2, rows, cols), BF),
            pltpu.VMEM((2, 2, rows, cols), BF),
            pltpu.VMEM((2, 2, rows, cols), BF),
            pltpu.VMEM((2, rows, cols), BF),
            pltpu.VMEM((rows, cols), BF),
        ]
    for stay in stays:
        scratch += [
            pltpu.VMEM(stay.shape, BF),
            pltpu.VMEM(stay.shape, BF),
            pltpu.VMEM(stay.shape[1:], BF),
        ]
    outs = []
    for _, (_, cols), _ in items:
        scratch += [pltpu.VMEM((3, rows // 4, cols), BF)] * 2 + [pltpu.VMEM((rows // 4, cols), BF)]
        outs.append(jax.ShapeDtypeStruct((4, rows // 4, cols), BF))
    outs.append(jax.ShapeDtypeStruct((8,) + stays[0].shape[1:], BF))
    outs.append(jax.ShapeDtypeStruct((8,) + stays[1].shape[1:], BF))
    outs.append(jax.ShapeDtypeStruct((2 * stays[2].shape[1], 8 * stays[2].shape[2]), BF))
    outs.append(jax.ShapeDtypeStruct(feed_terms.shape[1:], F32))
    outs.append(jax.ShapeDtypeStruct(gain_parts.shape[1:], F32))
    scratch += [pltpu.VMEM(feed_terms.shape, BF)]
    scratch += [pltpu.VMEM((3,) + feed_terms.shape[1:], BF)] * 2
    scratch += [
        pltpu.VMEM((7,) + gain_parts.shape[1:], F32),
        pltpu.VMEM(gain_parts.shape[1:], F32),
        pltpu.VMEM((3,) + gain_parts.shape[1:], F32),
    ]
    scratch += [pltpu.VMEM(f.shape, BF) for f in factors]
    dma = pltpu.SemaphoreType.DMA
    scratch += [dma((4,)), dma((4,)), dma((4,)), dma((8,)), dma((8,))]
    scratch += [dma((8,)), dma((4,)), dma((4,))]
    scratch += [dma((28,)), dma((28,)), dma((4,))]
    scratch += [dma((4, 6)), dma((4, 6)), dma((4, 8)), dma((4, 4)), dma((4,))]
    scratch += [dma((24,)), dma((24,)), dma]
    scratch += [dma((7,)), dma((7,)), dma((3,)), dma((3,))]
    hbm, vmem = pl.BlockSpec(memory_space=pl.ANY), pl.BlockSpec(memory_space=pltpu.VMEM)
    out = pl.pallas_call(
        functools.partial(last_kernel, items),
        name="reduce_last",
        out_shape=tuple(outs),
        in_specs=[hbm] * 13 + [vmem],
        out_specs=[hbm] * 7 + [vmem] * 2,
        scratch_shapes=scratch,
        compiler_params=pltpu.CompilerParams(
            collective_id=4, has_side_effects=True, vmem_limit_bytes=64 * 1024 * 1024 - 65536
        ),
    )(*factors, *stays, *comes, feed_terms, gain_parts)
    qkv = jnp.concatenate([out[0].reshape(rows, -1), out[1].reshape(rows, -1)], axis=1)
    project = jnp.concatenate([out[2].reshape(rows, -1), out[3].reshape(rows, -1)], axis=1)
    width = out[4].shape[2]
    ffn = [out[4].reshape(-1, width), out[5].reshape(-1, width), out[6]]
    return qkv, project, ffn, out[7], out[8]


def per_device(
    fast,
    block_input,
    cotangent,
    query_weight,
    key_weight,
    value_weight,
    project_weight,
    prenorm_gain,
    midnorm_gain,
    gate_weight,
    up_weight,
    down_weight,
    doc_lengths,
    tile_counts,
):
    tokens_here, model = block_input.shape
    if fast:
        gains = jnp.stack([prenorm_gain, midnorm_gain]).astype(F32).reshape(1, -1)
        qkv_full, project_full, gains_full, grad_rows = gather_first(
            query_weight, key_weight, value_weight, project_weight, gains, cotangent
        )
        gains_full = gains_full.reshape(8, 2, -1)
        first_gain = gains_full[:, 0].reshape(-1)
        second_gain = gains_full[:, 1].reshape(-1)
    else:
        qkv_full = jnp.concatenate(
            [
                lax.all_gather(query_weight, "narrow", axis=0, tiled=True),
                lax.all_gather(key_weight, "narrow", axis=0, tiled=True),
                lax.all_gather(value_weight, "narrow", axis=0, tiled=True),
            ],
            axis=1,
        )
        project_full = lax.all_gather(project_weight, "narrow", axis=1, tiled=True)
        first_gain = lax.all_gather(prenorm_gain, "narrow", axis=0, tiled=True).astype(F32)
        second_gain = lax.all_gather(midnorm_gain, "narrow", axis=0, tiled=True).astype(F32)
        grad_rows = lax.all_gather(cotangent, "wide", axis=0, tiled=True)
    group = HEADS // KV_HEADS
    scale = HEAD_DIM ** (-0.5)
    q_cols, k_cols = HEADS * HEAD_DIM, KV_HEADS * HEAD_DIM
    inputs_f = block_input.astype(jnp.float32)
    normed = rms_scale(inputs_f, first_gain).astype(jnp.bfloat16)
    qkv = jnp.dot(normed, qkv_full, preferred_element_type=jnp.float32).astype(jnp.bfloat16)
    query_rows = qkv[:, :q_cols].reshape(tokens_here, KV_HEADS, group, HEAD_DIM)
    key_rows = qkv[:, q_cols : q_cols + k_cols].reshape(tokens_here, KV_HEADS, HEAD_DIM)
    value_rows = qkv[:, q_cols + k_cols :].reshape(tokens_here, KV_HEADS, HEAD_DIM)
    ends = jnp.cumsum(doc_lengths[0])
    position = jnp.arange(tokens_here, dtype=jnp.int32)
    segment = jnp.sum((position[:, None] >= ends[None, :]).astype(jnp.int32), axis=1)
    allowed = (segment[:, None] == segment[None, :]) & (position[None, :] <= position[:, None])
    scores = (
        jnp.einsum("qcgd,kcd->cgqk", query_rows, key_rows, preferred_element_type=jnp.float32)
        * scale
    )
    masked = jnp.where(allowed, scores, -1e30)
    peak = jnp.max(masked, axis=-1, keepdims=True)
    expo = jnp.exp(masked - peak)
    total = jnp.sum(expo, axis=-1, keepdims=True)
    probs_low = (expo / total).astype(jnp.bfloat16)
    logsum = peak + jnp.log(total)
    attended = (
        jnp.einsum("cgqk,kcd->qcgd", probs_low, value_rows, preferred_element_type=jnp.float32)
        .astype(jnp.bfloat16)
        .reshape(tokens_here, HEADS * HEAD_DIM)
    )
    branch = jnp.dot(attended, project_full, preferred_element_type=jnp.float32)
    middle = inputs_f + branch
    mixed_in = rms_scale(middle, second_gain).astype(jnp.bfloat16)
    width = gate_weight.shape[1]
    wide_index = lax.axis_index("wide")
    my_count = jnp.sum(
        jnp.where(jnp.arange(tile_counts.shape[0], dtype=jnp.int32) == wide_index, tile_counts, 0)
    )
    live = (jnp.arange(width, dtype=jnp.int32) // TILE < my_count).astype(jnp.float32)
    if fast:
        mixed_back, feed_terms, *pieces = feed_forward(
            mixed_in, grad_rows, gate_weight, up_weight, down_weight, live.reshape(1, -1)
        )
        stays = pieces[1::2]
        comes = [
            lax.ppermute(piece, "narrow", [(i, i ^ bit) for i in range(8)])
            for piece, bit in zip(pieces[0::2], (2, 4, 2, 4))
        ]
    else:
        gathered = lax.all_gather(mixed_in, "wide", axis=0, tiled=True)
        gate_pre = jnp.dot(gathered, gate_weight, preferred_element_type=jnp.float32)
        up_pre = jnp.dot(gathered, up_weight, preferred_element_type=jnp.float32)
        hidden_back = contract_cols(grad_rows, down_weight)
        sigma = jax.nn.sigmoid(gate_pre)
        hidden = (gate_pre * sigma * up_pre * live).astype(BF)
        gate_back = (
            hidden_back * up_pre * live * sigma * (1.0 + gate_pre * (1.0 - sigma))
        ).astype(BF)
        up_back = (hidden_back * gate_pre * sigma * live).astype(BF)
        mixed_terms = (
            contract_cols(gate_back, gate_weight) + contract_cols(up_back, up_weight)
        ).astype(BF)
        mixed_back = lax.psum_scatter(
            mixed_terms, "wide", scatter_dimension=0, tiled=True
        ).astype(F32)
        partial_rows = jnp.dot(hidden, down_weight, preferred_element_type=jnp.float32)
        down_part = contract_rows(hidden, grad_rows)
        gate_part = contract_rows(gathered, gate_back)
        up_part = contract_rows(gathered, up_back)
    out_grad = cotangent.astype(jnp.float32)
    unused_second, second_backward = jax.vjp(rms_scale, middle, second_gain)
    middle_norm_back, second_gain_part = second_backward(mixed_back)
    middle_back = out_grad + middle_norm_back
    branch_back = middle_back.astype(jnp.bfloat16)
    attended_back = (
        contract_cols(branch_back, project_full)
        .astype(jnp.bfloat16)
        .reshape(tokens_here, KV_HEADS, group, HEAD_DIM)
    )
    scores_again = (
        jnp.einsum("qcgd,kcd->cgqk", query_rows, key_rows, preferred_element_type=jnp.float32)
        * scale
    )
    probs_again = jnp.where(allowed, jnp.exp(scores_again - logsum), 0.0)
    probs_again_low = probs_again.astype(jnp.bfloat16)
    value_back = (
        jnp.einsum(
            "cgqk,qcgd->kcd", probs_again_low, attended_back, preferred_element_type=jnp.float32
        )
        .astype(jnp.bfloat16)
        .reshape(tokens_here, KV_HEADS * HEAD_DIM)
    )
    probs_back = jnp.einsum(
        "qcgd,kcd->cgqk", attended_back, value_rows, preferred_element_type=jnp.float32
    )
    scores_back = (
        probs_again * (probs_back - jnp.sum(probs_again * probs_back, axis=-1, keepdims=True))
    ).astype(jnp.bfloat16)
    query_back = (
        (
            jnp.einsum("cgqk,kcd->qcgd", scores_back, key_rows, preferred_element_type=jnp.float32)
            * scale
        )
        .astype(jnp.bfloat16)
        .reshape(tokens_here, HEADS * HEAD_DIM)
    )
    key_back = (
        (
            jnp.einsum(
                "cgqk,qcgd->kcd", scores_back, query_rows, preferred_element_type=jnp.float32
            )
            * scale
        )
        .astype(jnp.bfloat16)
        .reshape(tokens_here, KV_HEADS * HEAD_DIM)
    )
    qkv_back = jnp.concatenate([query_back, key_back, value_back], axis=1)
    normed_back = contract_cols(qkv_back, qkv_full)
    unused_first, first_backward = jax.vjp(rms_scale, inputs_f, first_gain)
    input_norm_back, first_gain_part = first_backward(normed_back)
    input_grad = (middle_back + input_norm_back).astype(jnp.bfloat16)

    if fast:
        gain_parts = jnp.stack(
            [first_gain_part.reshape(8, -1), second_gain_part.reshape(8, -1)], axis=1
        ).reshape(8, 1, -1)
        qkv_total, project_total, ffn_totals, feed, gain_total = reduce_last(
            (normed, qkv_back, branch_back, attended),
            stays,
            comes,
            feed_terms,
            gain_parts,
        )
        gain_total = gain_total.reshape(2, -1)
        first_total, second_total = gain_total[0], gain_total[1]
        qkv_total = qkv_total.astype(F32)
        project_total = project_total.T.astype(F32)
        gate_total, up_total, down_total = [t.astype(F32) for t in ffn_totals]
    else:

        def owned(part):
            share = lax.psum_scatter(part.astype(BF), "narrow", scatter_dimension=0, tiled=True)
            return lax.psum(share, "wide").astype(F32)

        qkv_total = owned(contract_rows(normed, qkv_back))
        project_total = owned(contract_rows(branch_back, attended)).T
        first_total = owned(first_gain_part)
        second_total = owned(second_gain_part)
        gate_total, up_total, down_total = (
            lax.psum(gate_part.astype(BF), "narrow").astype(F32),
            lax.psum(up_part.astype(BF), "narrow").astype(F32),
            lax.psum(down_part.astype(BF), "narrow").astype(F32),
        )
        feed = lax.psum_scatter(
            partial_rows.astype(BF), "wide", scatter_dimension=0, tiled=True
        ).astype(F32)
    block_output = (middle + feed).astype(BF)
    return (
        block_output,
        input_grad,
        qkv_total[:, :q_cols],
        qkv_total[:, q_cols : q_cols + k_cols],
        qkv_total[:, q_cols + k_cols :],
        project_total,
        first_total,
        second_total,
        gate_total,
        up_total,
        down_total,
    )


def solution(mesh):
    fast = mesh.shape["narrow"] == 8 and mesh.shape["wide"] == 4
    placed = (
        P(("narrow", "wide"), None),
        P(("narrow", "wide"), None),
        P("narrow", None),
        P("narrow", None),
        P("narrow", None),
        P(None, "narrow"),
        P("narrow"),
        P("narrow"),
        P(None, "wide"),
        P(None, "wide"),
        P("wide", None),
        P(("narrow", "wide"), None),
        P(),
    )
    return jax.shard_map(
        functools.partial(per_device, fast),
        mesh=mesh,
        in_specs=placed,
        out_specs=(
            P(("narrow", "wide"), None),
            P(("narrow", "wide"), None),
            P("narrow", None),
            P("narrow", None),
            P("narrow", None),
            P(None, "narrow"),
            P("narrow"),
            P("narrow"),
            P(None, "wide"),
            P(None, "wide"),
            P("wide", None),
        ),
        check_vma=False,
    )
```

```python
import functools

import jax
import jax.numpy as jnp
from jax import lax
from jax.experimental import pallas as pl
from jax.experimental.pallas import tpu as pltpu
from jax.sharding import PartitionSpec as P

HEADS = 24
KV_HEADS = 6
HEAD_DIM = 64
TILE = 128


EPSILON = 1e-06

BF = jnp.bfloat16
F32 = jnp.float32


def rms_scale(rows, gain):
    factor = lax.rsqrt(jnp.mean(rows * rows, axis=-1, keepdims=True) + EPSILON)
    return rows * factor * gain


def contract_rows(left, right):
    return lax.dot_general(
        left, right, (((0,), (0,)), ((), ())), preferred_element_type=jnp.float32
    )


def contract_cols(left, right):
    return lax.dot_general(
        left, right, (((1,), (1,)), ((), ())), preferred_element_type=jnp.float32
    )


def flip(n, bit):
    return n + bit - 2 * bit * lax.rem(n // bit, 2)


def at(n, w):
    return {"narrow": n, "wide": w}


def send(src, dst, ssem, rsem, n, w):
    return pltpu.make_async_remote_copy(
        src_ref=src,
        dst_ref=dst,
        send_sem=ssem,
        recv_sem=rsem,
        device_id=at(n, w),
        device_id_type=pl.DeviceIdType.MESH,
    )


def greet(narrow_peers, n, w, line):
    barrier = pltpu.get_barrier_semaphore()
    for peer in narrow_peers:
        pl.semaphore_signal(
            barrier, inc=1, device_id=at(peer, w), device_id_type=pl.DeviceIdType.MESH
        )
    if not line:
        pl.semaphore_wait(barrier, len(narrow_peers))
    if line:

        @pl.when(w > 0)
        def _():
            pl.semaphore_signal(
                barrier, inc=1, device_id=at(n, w - 1), device_id_type=pl.DeviceIdType.MESH
            )

        @pl.when(w < 3)
        def _():
            pl.semaphore_signal(
                barrier, inc=1, device_id=at(n, w + 1), device_id_type=pl.DeviceIdType.MESH
            )

        @pl.when((w == 0) | (w == 3))
        def _():
            pl.semaphore_wait(barrier, len(narrow_peers) + 1)

        @pl.when((w == 1) | (w == 2))
        def _():
            pl.semaphore_wait(barrier, len(narrow_peers) + 2)


class LineGather:
    def __init__(self, n, w, own, whole, ssem, rsem, chunks):
        self.n, self.w, self.own, self.whole = n, w, own, whole
        self.ssem, self.rsem, self.chunks = ssem, rsem, chunks
        self.rows = own.shape[0] // chunks

    def span(self, i):
        return pl.ds(pl.multiple_of(i * self.rows, self.rows), self.rows)

    def part(self, shard, i):
        return self.whole.at[shard, self.span(i), :]

    def put(self, way, here, shard, i):
        src = self.own.at[self.span(i), :] if shard is here else self.part(shard, i)
        to = here + 1 - 2 * way
        s = (way * 4 + shard) * self.chunks + i
        r = shard * self.chunks + i
        return send(src, self.part(shard, i), self.ssem.at[s], self.rsem.at[r], self.n, to)

    def came(self, shard, i):
        self.put(0, 0, shard, i).wait_recv()

    def start_chunk(self, i):
        @pl.when(self.w < 3)
        def _():
            self.put(0, self.w, self.w, i).start()

        @pl.when(self.w > 0)
        def _():
            self.put(1, self.w, self.w, i).start()

    def start(self):
        for i in range(self.chunks):
            self.start_chunk(i)

    def near(self, i):
        @pl.when(self.w == 1)
        def _():
            self.came(0, i)
            self.put(0, 1, 0, i).start()
            self.came(2, i)
            self.put(1, 1, 2, i).start()

        @pl.when(self.w == 2)
        def _():
            self.came(3, i)
            self.put(1, 2, 3, i).start()
            self.came(1, i)
            self.put(0, 2, 1, i).start()

    def far(self, i):
        @pl.when(self.w == 1)
        def _():
            self.came(3, i)
            self.put(1, 1, 3, i).start()

        @pl.when(self.w == 2)
        def _():
            self.came(0, i)
            self.put(0, 2, 0, i).start()

    def ready(self, i):
        @pl.when(self.w == 0)
        def _():
            for shard in (1, 2, 3):
                self.came(shard, i)

        @pl.when(self.w == 3)
        def _():
            for shard in (2, 1, 0):
                self.came(shard, i)

    def finish_sends(self):
        for here in range(4):

            @pl.when(self.w == here)
            def _():
                for i in range(self.chunks):
                    if here < 3:
                        for shard in range(here + 1):
                            self.put(0, here, shard, i).wait_send()
                    if here > 0:
                        for shard in range(here, 4):
                            self.put(1, here, shard, i).wait_send()

    def finish(self):
        for i in range(self.chunks):
            self.ready(i)
        self.finish_sends()


def first_kernel(
    x_ref,
    q_ref,
    k_ref,
    v_ref,
    p_ref,
    g_ref,
    c_ref,
    bias_ref,
    qkv_out,
    p_full,
    c_full,
    normed_out,
    rows_out,
    att_out,
    g_full,
    log_out,
    qkv_full,
    p_buf,
    c_buf,
    x_buf,
    gain_row,
    normed,
    qkv,
    att,
    in_sem,
    out_sem,
    ssem,
    rsem,
    gs_sem,
    gr_sem,
    zs_sem,
    zr_sem,
):
    n, w = lax.axis_index("narrow"), lax.axis_index("wide")
    x, y, c, d = flip(n, 2), flip(n, 4), flip(n, 1), flip(flip(n, 2), 4)
    others = [lax.rem(n + i, 8) for i in range(1, 8)]
    rows = q_ref.shape[0]
    half = rows // 2
    depth = p_ref.shape[0]
    qc, kc = q_ref.shape[1], k_ref.shape[1]
    cols = ((0, qc), (qc, kc), (qc + kc, kc))

    def region(t, block, h):
        if t == 3:
            r = pl.ds(0, depth) if h == 2 else pl.ds(h * (depth // 2), depth // 2)
            return p_full.at[r, pl.ds(pl.multiple_of(block * rows, rows), rows)]
        start = pl.multiple_of(block * rows, rows)
        r = pl.ds(start, rows) if h == 2 else pl.ds(start + h * half, half)
        return qkv_full.at[r, pl.ds(cols[t][0], cols[t][1])]

    locals_in = []
    for i, (src, dst) in enumerate(
        (
            (g_ref, g_full.at[n]),
            (x_ref, x_buf),
            (p_ref, p_buf),
            (c_ref, c_buf),
            (q_ref, region(0, n, 2)),
            (k_ref, region(1, n, 2)),
            (v_ref, region(2, n, 2)),
        )
    ):
        cp = pltpu.make_async_copy(src, dst, in_sem.at[i])
        cp.start()
        locals_in.append(cp)

    greet(others, n, w, True)

    def own(t, h):
        ref = (q_ref, k_ref, v_ref, p_ref)[t]
        if h == 2:
            return ref
        size = ref.shape[0] // 2
        return ref.at[pl.ds(h * size, size), :]

    def msg(t, kind, src, block, h, peer):
        k = t * 10 + kind
        return send(src, region(t, block, h), ssem.at[k], rsem.at[k], peer, w)

    def to_x(t, h):
        return msg(t, h, own(t, h), n, h, x)

    def to_y(t, h):
        return msg(t, 2 + h, own(t, h), n, h, y)

    def on_x(t):
        return msg(t, 4, region(t, y, 0), y, 0, x)

    def on_y(t):
        return msg(t, 5, region(t, x, 1), x, 1, y)

    def to_c(t, which):
        block = (n, x, y, d)[which]
        src = own(t, 2) if which == 0 else region(t, block, 2)
        return msg(t, 6 + which, src, block, 2, c)

    def start_own(t):
        to_x(t, 1).start()
        to_y(t, 0).start()
        to_x(t, 0).start()
        to_y(t, 1).start()

    def gain(i):
        return send(g_ref, g_full.at[n], gs_sem.at[i], gr_sem.at[i], others[i], w)

    line = LineGather(n, w, c_ref, c_full, zs_sem, zr_sem, 4)
    for i in range(7):
        gain(i).start()
    start_own(0)
    line.start()
    for t in (1, 2):
        start_own(t)
    for t in range(3):
        to_c(t, 0).start()

    locals_out = []

    def put(src, dst):
        cp = pltpu.make_async_copy(src, dst, out_sem.at[len(locals_out)])
        cp.start()
        locals_out.append(cp)

    for i in range(7):
        gain(i).wait()
    for cp in locals_in:
        cp.wait()
    put(p_buf, region(3, n, 2))
    put(c_buf, c_full.at[w])
    for k in range(8):
        gain_row[:, pl.ds(k * rows, rows)] = g_full[k, :, :rows]
    strip = 16

    @pl.loop(0, x_buf.shape[0] // strip)
    def _(i):
        s = pl.ds(pl.multiple_of(i * strip, strip), strip)
        normed[s, :] = rms_scale(x_buf[s, :].astype(F32), gain_row[...]).astype(BF)

    put(normed, normed_out)

    def relay(t):
        to_y(t, 0).wait_recv()
        on_x(t).start()
        to_x(t, 1).wait_recv()
        on_y(t).start()
        to_x(t, 0).wait_recv()
        to_c(t, 1).start()
        to_y(t, 1).wait_recv()
        to_c(t, 2).start()

    def corner(t):
        on_x(t).wait_recv()
        on_y(t).wait_recv()
        to_c(t, 3).start()

    line.near(0)
    relay(0)
    line.near(1)
    relay(1)
    line.near(2)
    relay(2)
    start_own(3)
    to_c(3, 0).start()
    line.near(3)
    line.far(0)
    line.far(1)
    for t in range(3):
        corner(t)
    line.far(2)
    for t in range(3):
        for which in range(4):
            to_c(t, which).wait_recv()
    put(qkv_full, qkv_out)
    tile = 256

    @pl.loop(0, qkv.shape[1] // tile)
    def _(i):
        s = pl.ds(pl.multiple_of(i * tile, tile), tile)
        qkv[:, s] = jnp.dot(normed[...], qkv_full[:, s], preferred_element_type=F32).astype(BF)

    put(qkv, rows_out)
    line.far(3)

    log_out[...] = jnp.zeros(log_out.shape, F32)
    pair = 2 * HEAD_DIM
    group = HEADS // KV_HEADS

    @pl.loop(0, KV_HEADS // 2)
    def _(i):
        keys = qkv[:, pl.ds(pl.multiple_of(qc + i * pair, pair), pair)]
        values = qkv[:, pl.ds(pl.multiple_of(qc + kc + i * pair, pair), pair)]
        lane = lax.broadcasted_iota(jnp.int32, log_out.shape, 1)
        for b in range(group):
            at_cols = pl.ds(pl.multiple_of((i * group + b) * pair, pair), pair)
            queries = qkv[:, at_cols]
            side = (2 * b) // group
            key = keys[:, side * HEAD_DIM : (side + 1) * HEAD_DIM]
            value = values[:, side * HEAD_DIM : (side + 1) * HEAD_DIM]
            heads = []
            for e in range(2):
                query = queries[:, e * HEAD_DIM : (e + 1) * HEAD_DIM]
                masked = contract_cols(query, key) * (HEAD_DIM**-0.5) + bias_ref[...]
                peak = jnp.max(masked, axis=-1, keepdims=True)
                expo = jnp.exp(masked - peak)
                total = jnp.sum(expo, axis=-1, keepdims=True)
                probs = (expo * (1.0 / total)).astype(BF)
                heads.append(jnp.dot(probs, value, preferred_element_type=F32))
                log_out[...] = jnp.where(
                    lane == 2 * (i * group + b) + e, peak + jnp.log(total), log_out[...]
                )
            att[:, at_cols] = jnp.concatenate(heads, axis=1).astype(BF)

    put(att, att_out)
    relay(3)
    corner(3)
    for t in range(4):
        for h in range(2):
            to_x(t, h).wait_send()
            to_y(t, h).wait_send()
        on_x(t).wait_send()
        on_y(t).wait_send()
        for which in range(4):
            if t == 3:
                to_c(t, which).wait_recv()
            to_c(t, which).wait_send()
    line.finish()
    for cp in locals_out:
        cp.wait()


def gather_first(rows_in, query, key, value, project, gains, cotangent, bias):
    rows = query.shape[0]
    width = query.shape[1] + 2 * key.shape[1]
    tokens_here, model = rows_in.shape
    hbm, vmem = pl.BlockSpec(memory_space=pl.ANY), pl.BlockSpec(memory_space=pltpu.VMEM)
    return pl.pallas_call(
        first_kernel,
        name="gather_first",
        out_shape=(
            jax.ShapeDtypeStruct((8 * rows, width), BF),
            jax.ShapeDtypeStruct((project.shape[0], 8 * rows), BF),
            jax.ShapeDtypeStruct((4,) + cotangent.shape, BF),
            jax.ShapeDtypeStruct((tokens_here, model), BF),
            jax.ShapeDtypeStruct((tokens_here, width), BF),
            jax.ShapeDtypeStruct((tokens_here, query.shape[1]), BF),
            jax.ShapeDtypeStruct((8,) + gains.shape, gains.dtype),
            jax.ShapeDtypeStruct((tokens_here, 128), F32),
        ),
        in_specs=[hbm] * 7 + [vmem],
        out_specs=[hbm] * 6 + [vmem] * 2,
        scratch_shapes=[
            pltpu.VMEM((8 * rows, width), BF),
            pltpu.VMEM(project.shape, BF),
            pltpu.VMEM(cotangent.shape, BF),
            pltpu.VMEM((tokens_here, model), BF),
            pltpu.VMEM((1, model), F32),
            pltpu.VMEM((tokens_here, model), BF),
            pltpu.VMEM((tokens_here, width), BF),
            pltpu.VMEM((tokens_here, query.shape[1]), BF),
            pltpu.SemaphoreType.DMA((7,)),
            pltpu.SemaphoreType.DMA((6,)),
            pltpu.SemaphoreType.DMA((40,)),
            pltpu.SemaphoreType.DMA((40,)),
            pltpu.SemaphoreType.DMA((7,)),
            pltpu.SemaphoreType.DMA((7,)),
            pltpu.SemaphoreType.DMA((32,)),
            pltpu.SemaphoreType.DMA((16,)),
        ],
        compiler_params=pltpu.CompilerParams(collective_id=1, has_side_effects=True),
    )(rows_in, query, key, value, project, gains, cotangent, bias)


class LineScatter:
    def __init__(self, n, w, terms, bufs, ssem, rsem, chunks):
        self.n, self.w, self.terms, self.bufs = n, w, terms, bufs
        self.ssem, self.rsem, self.chunks = ssem, rsem, chunks
        self.rows = terms.shape[1] // chunks

    def span(self, i):
        return pl.ds(pl.multiple_of(i * self.rows, self.rows), self.rows)

    def term(self, d, i):
        return self.terms.at[d, self.span(i), :]

    def slot(self, way, slot, i):
        return self.bufs[way].at[slot, self.span(i), :]

    def put(self, way, here, d, i, src):
        slot = d - here - 1 if way == 0 else here - 1 - d
        k = (way * 3 + slot) * self.chunks + i
        to = here + 1 - 2 * way
        return send(src, self.slot(way, slot, i), self.ssem.at[k], self.rsem.at[k], self.n, to)

    def came(self, way, slot, i):
        k = (way * 3 + slot) * self.chunks + i
        ref = self.slot(way, slot, i)
        send(ref, ref, self.ssem.at[k], self.rsem.at[k], self.n, 1).wait_recv()

    def begin(self, i):
        for here, way in ((0, 0), (3, 1)):

            @pl.when(self.w == here)
            def _():
                for d in (3, 2, 1) if way == 0 else (0, 1, 2):
                    self.put(way, here, d, i, self.term(d, i)).start()

    def join(self, way, here, d, i):
        slot = d - here if way == 0 else here - d
        self.came(way, slot, i)
        mine, sum_ = self.term(d, i), self.slot(way, slot, i)
        sum_[...] = (mine[...].astype(F32) + sum_[...].astype(F32)).astype(BF)
        self.put(way, here, d, i, sum_).start()

    def pass_on(self, i):
        @pl.when(self.w == 1)
        def _():
            self.join(0, 1, 3, i)
            self.join(0, 1, 2, i)

        @pl.when(self.w == 2)
        def _():
            self.join(1, 2, 0, i)
            self.join(1, 2, 1, i)

    def pass_end(self, i):
        @pl.when(self.w == 1)
        def _():
            self.join(1, 1, 0, i)

        @pl.when(self.w == 2)
        def _():
            self.join(0, 2, 3, i)

    def finish(self, i, out):
        for here, ways in ((0, (1,)), (1, (0, 1)), (2, (0, 1)), (3, (0,))):

            @pl.when(self.w == here)
            def _():
                for way in ways:
                    self.came(way, 0, i)
                total = self.term(here, i)[...].astype(F32)
                for way in ways:
                    total = total + self.slot(way, 0, i)[...].astype(F32)
                out[self.span(i), :] = total.astype(out.dtype)

    def drain(self):
        sent = {
            0: ((0, 3), (0, 2), (0, 1)),
            1: ((0, 3), (0, 2), (1, 0)),
            2: ((1, 0), (1, 1), (0, 3)),
            3: ((1, 0), (1, 1), (1, 2)),
        }
        for here in range(4):

            @pl.when(self.w == here)
            def _():
                for i in range(self.chunks):
                    for way, d in sent[here]:
                        self.put(way, here, d, i, self.term(d, i)).wait_send()


def middle_kernel(
    mixed,
    cot,
    wg,
    wu,
    wd,
    live,
    back_out,
    partial_out,
    gate_go,
    gate_stay,
    up_go,
    up_stay,
    low_go,
    low_stay,
    high_go,
    high_stay,
    x_all,
    cot_v,
    wg_v,
    wu_v,
    wd_v,
    gate_f,
    up_f,
    back_f,
    hid,
    gb,
    ub,
    terms,
    from_left,
    from_right,
    part_buf,
    gate_k,
    up_k,
    down_k,
    in_sem,
    ag_s,
    ag_r,
    rs_s,
    rs_r,
    part_sem,
    sw_s,
    sw_r,
    out_sem,
    ready,
):
    n, w = lax.axis_index("narrow"), lax.axis_index("wide")
    y, x, core = n // 4, lax.rem(n // 2, 2), lax.rem(n, 2)
    mate = flip(n, 1)
    chunks = 4
    rows = mixed.shape[0] // chunks
    tokens, model = 4 * mixed.shape[0], mixed.shape[1]
    width = wg.shape[1]
    batch = 4 * rows
    loads = [
        pltpu.make_async_copy(src, dst, in_sem.at[k])
        for k, (src, dst) in enumerate(
            ((mixed, x_all.at[w]), (wg, wg_v), (wu, wu_v), (cot, cot_v), (wd, wd_v))
        )
    ]
    for cp in loads:
        cp.start()
    greet([mate], n, w, True)

    gather = LineGather(n, w, mixed, x_all, ag_s, ag_r, chunks)
    scatter = LineScatter(n, w, terms, (from_left, from_right), rs_s, rs_r, chunks)
    gather.start_chunk(0)
    gather.start_chunk(1)
    gather.near(0)
    gather.far(0)
    for cp in loads:
        cp.wait()

    def rows_of(ref, i):
        r = pl.ds(pl.multiple_of(i * rows, rows), rows)
        return ref[:, r, :].reshape(batch, ref.shape[2])

    def store(i):
        return pltpu.make_async_copy(
            part_buf.at[lax.rem(i, 2)],
            partial_out.at[:, pl.ds(pl.multiple_of(i * rows, rows), rows), :],
            part_sem.at[lax.rem(i, 2)],
        )

    @pl.loop(0, chunks)
    def _(i):
        r = pl.ds(pl.multiple_of(i * rows, rows), rows)
        gather.ready(i)
        xs = rows_of(x_all, i)
        gate_f[...] = jnp.dot(xs, wg_v[...], preferred_element_type=F32)
        up_f[...] = jnp.dot(xs, wu_v[...], preferred_element_type=F32)

        @pl.when(i < chunks - 1)
        def _():
            gather.near(i + 1)

        @pl.when(i < chunks - 2)
        def _():
            gather.start_chunk(i + 2)

        back_f[...] = contract_cols(rows_of(cot_v, i), wd_v[...])
        step = 16

        @pl.loop(0, batch // step)
        def _(t):
            s = pl.ds(pl.multiple_of(t * step, step), step)
            d = t // (rows // step)
            into = pl.ds(
                pl.multiple_of(i * rows + lax.rem(t, rows // step) * step, step), step
            )
            gate, up = gate_f[s, :], up_f[s, :] * live[...]
            sigma = jax.nn.sigmoid(gate)
            silu = gate * sigma
            hid[d, into, :] = (silu * up).astype(BF)
            back = back_f[s, :]
            gb[d, into, :] = (back * up * sigma * (1.0 + gate * (1.0 - sigma))).astype(BF)
            ub[d, into, :] = (back * silu * live[...]).astype(BF)

        @pl.when(i > 0)
        def _():
            scatter.pass_on(i - 1)

        @pl.when(i < chunks - 1)
        def _():
            gather.far(i + 1)

        terms[:, r, :] = (
            (contract_cols(rows_of(gb, i), wg_v[...]) + contract_cols(rows_of(ub, i), wu_v[...]))
            .astype(BF)
            .reshape(4, rows, model)
        )
        scatter.begin(i)

        @pl.when(i > 1)
        def _():
            store(i - 2).wait()

        part_buf[lax.rem(i, 2)] = (
            jnp.dot(rows_of(hid, i), wd_v[...], preferred_element_type=F32)
            .astype(BF)
            .reshape(4, rows, model)
        )
        store(i).start()

        @pl.when(i > 0)
        def _():
            scatter.pass_end(i - 1)

    pl.semaphore_signal(
        ready, inc=1, device_id=at(mate, w), device_id_type=pl.DeviceIdType.MESH
    )

    def row_grad(back, block):
        cols = pl.ds(pl.multiple_of(block * (model // 8), model // 8), model // 8)
        return contract_rows(
            x_all[:, :, cols].reshape(tokens, model // 8), back[...].reshape(tokens, width)
        )

    def col_grad(block):
        cols = pl.ds(pl.multiple_of(block * (model // 8), model // 8), model // 8)
        return contract_rows(
            hid[...].reshape(tokens, width), cot_v[:, :, cols].reshape(tokens, model // 8)
        )

    eighth, half = model // 8, model // 2

    def place(j, base):
        return pl.ds(pl.multiple_of(base + j * eighth, eighth), eighth)

    swaps = [
        send(buf.at[pl.ds(half, half), :], buf.at[pl.ds(0, half), :], sw_s.at[k], sw_r.at[k], mate, w)
        for k, buf in enumerate((wg_v, wu_v))
    ]
    swaps.append(
        send(
            wd_v.at[:, pl.ds(half, half)], wd_v.at[:, pl.ds(0, half)], sw_s.at[2], sw_r.at[2], mate, w
        )
    )

    @pl.loop(0, 4)
    def _(j):
        wg_v[place(j, half), :] = row_grad(gb, 2 * j + 1 - core).astype(BF)

    scatter.pass_on(chunks - 1)
    pl.semaphore_wait(ready, 1)
    swaps[0].start()

    @pl.loop(0, 4)
    def _(j):
        wu_v[place(j, half), :] = row_grad(ub, 2 * j + 1 - core).astype(BF)

    swaps[1].start()

    @pl.loop(0, 4)
    def _(j):
        wd_v[:, place(j, half)] = col_grad(2 * j + 1 - core).astype(BF)

    swaps[2].start()
    swaps[0].wait_recv()

    @pl.loop(0, 4)
    def _(j):
        gate_k[j // 2, lax.rem(j, 2)] = (
            row_grad(gb, 2 * j + core) + wg_v[place(j, 0), :].astype(F32)
        ).astype(BF)

    cut = width // 2
    pieces = (
        (gate_k.at[:, 1 - x], gate_go),
        (gate_k.at[:, x], gate_stay),
        (up_k.at[1 - y], up_go),
        (up_k.at[y], up_stay),
        (down_k.at[:, 1 - x, pl.ds(0, cut), :], low_go),
        (down_k.at[:, x, pl.ds(0, cut), :], low_stay),
        (down_k.at[1 - y, :, pl.ds(cut, cut), :], high_go),
        (down_k.at[y, :, pl.ds(cut, cut), :], high_stay),
    )
    puts = [
        pltpu.make_async_copy(src, dst, out_sem.at[k]) for k, (src, dst) in enumerate(pieces)
    ]
    for k in (0, 1):
        puts[k].start()
    scatter.pass_end(chunks - 1)
    swaps[1].wait_recv()

    @pl.loop(0, 4)
    def _(j):
        up_k[j // 2, lax.rem(j, 2)] = (
            row_grad(ub, 2 * j + core) + wu_v[place(j, 0), :].astype(F32)
        ).astype(BF)

    for k in (2, 3):
        puts[k].start()
    swaps[2].wait_recv()

    @pl.loop(0, 4)
    def _(j):
        down_k[j // 2, lax.rem(j, 2)] = (
            col_grad(2 * j + core) + wd_v[:, place(j, 0)].astype(F32)
        ).astype(BF)

    for k in (4, 5, 6, 7):
        puts[k].start()
    for i in range(chunks):
        scatter.finish(i, back_out)
    scatter.drain()
    gather.finish_sends()
    for k in range(3):
        swaps[k].wait_send()
    store(chunks - 2).wait()
    store(chunks - 1).wait()
    for cp in puts:
        cp.wait()


def feed_forward(mixed, cot, gate_weight, up_weight, down_weight, live):
    tokens_here, model = mixed.shape
    width = gate_weight.shape[1]
    rows, eighth, cut = tokens_here // 4, model // 8, width // 2
    hbm, vmem = pl.BlockSpec(memory_space=pl.ANY), pl.BlockSpec(memory_space=pltpu.VMEM)
    row_piece = jax.ShapeDtypeStruct((2, eighth, width), BF)
    col_piece = jax.ShapeDtypeStruct((2, cut, eighth), BF)
    dma = pltpu.SemaphoreType.DMA
    acc = pltpu.VMEM((4 * rows, width), F32)
    act = pltpu.VMEM((4, tokens_here, width), BF)
    tok = pltpu.VMEM((4, tokens_here, model), BF)
    three = pltpu.VMEM((3, tokens_here, model), BF)
    return pl.pallas_call(
        middle_kernel,
        name="feed_forward",
        out_shape=(
            jax.ShapeDtypeStruct(mixed.shape, F32),
            jax.ShapeDtypeStruct((4,) + mixed.shape, BF),
        )
        + (row_piece,) * 4
        + (col_piece,) * 4,
        in_specs=[hbm] * 5 + [vmem],
        out_specs=[vmem] + [hbm] * 9,
        scratch_shapes=[
            tok,
            tok,
            pltpu.VMEM(gate_weight.shape, BF),
            pltpu.VMEM(up_weight.shape, BF),
            pltpu.VMEM(down_weight.shape, BF),
            acc,
            acc,
            acc,
            act,
            act,
            act,
            tok,
            three,
            three,
            pltpu.VMEM((2, 4, rows, model), BF),
            pltpu.VMEM((2, 2, eighth, width), BF),
            pltpu.VMEM((2, 2, eighth, width), BF),
            pltpu.VMEM((2, 2, width, eighth), BF),
            dma((5,)),
            dma((32,)),
            dma((16,)),
            dma((24,)),
            dma((24,)),
            dma((2,)),
            dma((3,)),
            dma((3,)),
            dma((8,)),
            pltpu.SemaphoreType.REGULAR,
        ],
        compiler_params=pltpu.CompilerParams(
            collective_id=5, has_side_effects=True, vmem_limit_bytes=64 * 1024 * 1024 - 65536
        ),
    )(mixed, cot, gate_weight, up_weight, down_weight, live)


class Reduce:
    def __init__(self, me, factors, cols, x_first, bufs, sems, k):
        self.n, self.w, self.y, self.x, self.core = me
        self.left, self.right = factors
        self.cols, self.x_first = pl.ds(*cols), x_first
        self.away, self.sum, self.pair, self.one, self.two = bufs
        self.sems, self.k = sems, k
        self.rows = self.sum.shape[2]
        self.near = flip(self.n, 2) if x_first else flip(self.n, 4)
        self.next = flip(self.n, 4) if x_first else flip(self.n, 2)

    def term(self, block):
        own = pl.ds(pl.multiple_of(block * self.rows, self.rows), self.rows)
        return contract_rows(self.left[:, own], self.right[:, self.cols])

    def swap(self):
        return send(
            self.away,
            self.pair,
            self.sems[0].at[self.k],
            self.sems[1].at[self.k],
            flip(self.n, 1),
            self.w,
        )

    def before_swap(self):
        @pl.loop(0, 4)
        def _(j):
            self.away[j // 2, lax.rem(j, 2)] = self.term(2 * j + 1 - self.core).astype(BF)

        self.swap().start()

    def block(self, first, second):
        return (second, first) if self.x_first else (first, second)

    def axes(self):
        return (self.x, self.y) if self.x_first else (self.y, self.x)

    def stage(self, s):
        a, b = self.axes()
        if s == 1:
            src = self.sum.at[:, 1 - a] if self.x_first else self.sum.at[1 - a]
            dst, peer = self.one, self.near
        else:
            src = self.sum.at[self.block(a, 1 - b)]
            dst, peer = self.two, self.next
        k = 2 * self.k + s - 1
        return send(src, dst, self.sems[2].at[k], self.sems[3].at[k], peer, self.w)

    def add(self, block, other):
        step = 64 if self.rows % 64 == 0 else 48

        @pl.loop(0, self.rows // step)
        def _(i):
            r = pl.ds(pl.multiple_of(i * step, step), step)
            self.sum[block[0], block[1], r, :] = (
                self.sum[block[0], block[1], r, :] + other[r, :]
            )

    def after_swap(self):
        a, _ = self.axes()
        self.swap().wait_recv()

        @pl.loop(0, 4)
        def _(j):
            first = lax.rem(1 - a + j // 2, 2)
            y, x = self.block(first, lax.rem(j, 2))
            total = self.term(4 * y + 2 * x + self.core) + self.pair[y, x].astype(F32)
            self.sum[y, x] = total.astype(BF)

        self.stage(1).start()

    def after_one(self):
        a, b = self.axes()
        self.stage(1).wait()
        self.add(self.block(a, 1 - b), self.one.at[1 - b])
        self.stage(2).start()
        self.add(self.block(a, b), self.one.at[b])

    def after_two(self):
        a, b = self.axes()
        self.stage(2).wait()
        self.add(self.block(a, b), self.two)

    def result(self):
        return self.sum.at[self.y, self.x]


class Half:
    def __init__(self, me, kept, came, x_first, bufs, sems, k):
        self.n, self.w, self.y, self.x, self.core = me
        self.kept, self.came, self.x_first = kept, came, x_first
        self.sum, self.one, self.two = bufs
        self.sems, self.k = sems, k
        self.rows = kept.shape[1]
        self.next = flip(self.n, 4) if x_first else flip(self.n, 2)
        self.here = self.y if x_first else self.x

    def loads(self):
        return [
            pltpu.make_async_copy(self.kept, self.sum, self.sems[0].at[2 * self.k]),
            pltpu.make_async_copy(self.came, self.one, self.sems[0].at[2 * self.k + 1]),
        ]

    def stage(self):
        return send(
            self.sum.at[1 - self.here],
            self.two,
            self.sems[1].at[self.k],
            self.sems[2].at[self.k],
            self.next,
            self.w,
        )

    def add(self, block, other):
        @pl.loop(0, self.rows // 64)
        def _(i):
            r = pl.ds(pl.multiple_of(i * 64, 64), 64)
            self.sum[block, r, :] = self.sum[block, r, :] + other[r, :]

    def after_one(self):
        for cp in self.loads():
            cp.wait()
        self.add(1 - self.here, self.one.at[1 - self.here])
        self.stage().start()
        self.add(self.here, self.one.at[self.here])

    def after_two(self):
        self.stage().wait()
        self.add(self.here, self.two)

    def result(self):
        return self.sum.at[self.here]


class Spread:
    def __init__(self, item, region, sems, k):
        self.item, self.region, self.sems, self.k = item, region, sems, k
        n = item.n
        self.blocks = (n, flip(n, 2), flip(n, 4), flip(flip(n, 2), 4))

    def copy(self, kind, src, block, peer):
        k = 7 * self.k + kind
        return send(
            src, self.region(block), self.sems[0].at[k], self.sems[1].at[k], peer, self.item.w
        )

    def own(self, kind):
        n = self.item.n
        return self.copy(kind, self.item.result(), n, (flip(n, 2), flip(n, 4), flip(n, 1))[kind])

    def corner(self):
        n, b = self.item.n, self.blocks
        if self.item.x_first:
            return self.copy(3, self.region(b[2]), b[2], flip(n, 2))
        return self.copy(3, self.region(b[1]), b[1], flip(n, 4))

    def to_core(self, which):
        block = self.blocks[which]
        return self.copy(3 + which, self.region(block), block, flip(self.item.n, 1))

    def keep(self):
        return pltpu.make_async_copy(
            self.item.result(), self.region(self.item.n), self.sems[2].at[self.k]
        )

    def start(self):
        order = (1, 0, 2) if self.item.x_first else (0, 1, 2)
        for kind in order:
            self.own(kind).start()
        self.keep().start()

    def relay(self):
        first, second = (1, 0) if self.item.x_first else (0, 1)
        self.own(first).wait_recv()
        self.corner().start()
        self.to_core(1 + first).start()
        self.own(second).wait_recv()
        self.to_core(1 + second).start()

    def last(self):
        self.corner().wait_recv()
        self.to_core(3).start()

    def finish(self):
        for kind in range(2):
            self.own(kind).wait_send()
        self.own(2).wait()
        self.corner().wait_send()
        for which in range(1, 4):
            self.to_core(which).wait()
        self.keep().wait()


class Rows:
    def __init__(self, ref):
        self.ref = ref
        self.shape = (4, ref.shape[0] // 4, ref.shape[1])

    @property
    def at(self):
        return self

    def __getitem__(self, index):
        d, r, _ = index
        start = pl.multiple_of(d * self.shape[1] + r.start, r.size)
        return self.ref.at[pl.ds(start, r.size), :]


def last_kernel(items, *refs):
    refs = list(refs)

    def take(count):
        out = refs[:count]
        del refs[:count]
        return out

    factors = take(4)
    stays, comes = take(4), take(4)
    feed_terms, gain_parts = take(2)
    outs = take(4)
    gate_full, up_full, down_full = take(3)
    feed_out, gain_out = take(2)
    attn_bufs = [take(5) for _ in range(4)]
    ffn_bufs = [take(3) for _ in range(4)]
    line_bufs = [take(3) for _ in range(4)]
    feed_v, feed_left, feed_right = take(3)
    gain_in, gain_sum, gain_line = take(3)
    factor_bufs = take(4)
    load_sem, swap_s, swap_r, st_s, st_r = take(5)
    half_sems = take(3)
    sp_sems = take(3)
    lr_s, lr_r, lg_s, lg_r, lg_l = take(5)
    fd_s, fd_r, fd_l = take(3)
    gn_s, gn_r, gz_s, gz_r = take(4)

    n, w = lax.axis_index("narrow"), lax.axis_index("wide")
    me = (n, w, n // 4, lax.rem(n // 2, 2), lax.rem(n, 2))
    attn = [
        Reduce(
            me,
            factor_bufs[2 * p : 2 * p + 2],
            cols,
            xf,
            attn_bufs[k],
            (swap_s, swap_r, st_s, st_r),
            k,
        )
        for k, (p, cols, xf) in enumerate(items)
    ]
    ffn = [
        Half(me, stays[k], comes[k], k % 2 == 0, ffn_bufs[k], half_sems, k) for k in range(4)
    ]
    cut, eighth = stays[2].shape[1], stays[2].shape[2]

    def down_region(k):
        return lambda block: down_full.at[
            pl.ds(k * cut, cut), pl.ds(pl.multiple_of(block * eighth, eighth), eighth)
        ]

    regions = (
        lambda block: gate_full.at[block],
        lambda block: up_full.at[block],
        down_region(0),
        down_region(1),
    )
    spread = [Spread(ffn[k], regions[k], sp_sems, k) for k in range(4)]
    for item in ffn:
        for cp in item.loads():
            cp.start()
    factor_loads = [
        pltpu.make_async_copy(src, dst, load_sem.at[k])
        for k, (src, dst) in enumerate(zip(factors, factor_bufs))
    ]
    for cp in factor_loads:
        cp.start()
    feed_load = pltpu.make_async_copy(feed_terms, feed_v, fd_l)
    feed_load.start()

    barrier = pltpu.get_barrier_semaphore()
    narrow_peers = [lax.rem(n + i, 8) for i in range(1, 8)]
    wide_peers = [lax.rem(w + i, 4) for i in range(1, 4)]
    for peer in narrow_peers:
        pl.semaphore_signal(
            barrier, inc=1, device_id=at(peer, w), device_id_type=pl.DeviceIdType.MESH
        )
    for peer in wide_peers:
        pl.semaphore_signal(
            barrier, inc=1, device_id=at(n, peer), device_id_type=pl.DeviceIdType.MESH
        )
    pl.semaphore_wait(barrier, 10)

    feed_load.wait()
    feed = LineScatter(n, w, feed_v, (feed_left, feed_right), fd_s, fd_r, 4)
    for i in range(4):
        feed.begin(i)

    def gain_narrow(i):
        peer = narrow_peers[i]
        return send(gain_parts.at[peer], gain_in.at[i], gn_s.at[i], gn_r.at[i], peer, w)

    def gain_wide(i):
        return send(gain_sum, gain_line.at[i], gz_s.at[i], gz_r.at[i], n, wide_peers[i])

    for i in range(7):
        gain_narrow(i).start()

    for item in ffn:
        item.after_one()
    for cp in factor_loads:
        cp.wait()
    for item in attn:
        item.before_swap()
    feed.pass_on(0)
    for item in attn:
        item.after_swap()
    feed.pass_on(1)
    feed.pass_end(0)
    for i in range(7):
        gain_narrow(i).wait()
    total = gain_parts[n]
    for i in range(7):
        total = total + gain_in[i]
    gain_sum[...] = total
    for i in range(3):
        gain_wide(i).start()
    feed.pass_on(2)
    feed.pass_end(1)
    for item in attn[:2]:
        item.after_one()
    feed.pass_on(3)
    feed.pass_end(2)
    for item in attn[2:]:
        item.after_one()
    feed.pass_end(3)
    for k in range(4):
        ffn[k].after_two()
        spread[k].start()

    scatters, gathers = [], []
    for k, item in enumerate(attn):
        left, right, own = line_bufs[k]
        scatters.append(
            LineScatter(n, w, Rows(item.result()), (left, right), lr_s.at[k], lr_r.at[k], 1)
        )
        gathers.append(LineGather(n, w, own, outs[k], lg_s.at[k], lg_r.at[k], 1))

    def keep(k):
        return pltpu.make_async_copy(line_bufs[k][2], outs[k].at[w], lg_l.at[k])

    def line_turn(k):
        scatters[k].finish(0, line_bufs[k][2])
        gathers[k].start()
        keep(k).start()

    for k in (0, 1):
        attn[k].after_two()
        scatters[k].begin(0)
    for i in range(4):
        feed.finish(i, feed_out)
    for k in (2, 3):
        attn[k].after_two()
        scatters[k].begin(0)
    for k in (0, 1, 2, 3):
        scatters[k].pass_on(0)
    for k in (0, 1, 2, 3):
        scatters[k].pass_end(0)
    for k in (0, 1, 2, 3):
        line_turn(k)
    for s in spread[:2]:
        s.relay()
    for k in (0, 1, 2, 3):
        gathers[k].near(0)
    for k in (0, 1, 2, 3):
        gathers[k].far(0)
    for s in spread[2:]:
        s.relay()
    for i in range(3):
        gain_wide(i).wait()
    gain_out[...] = (gain_sum[...] + gain_line[0]) + (gain_line[1] + gain_line[2])
    for s in spread:
        s.last()
    for s in spread:
        s.finish()
    for item in attn:
        item.swap().wait_send()
    for k in range(4):
        scatters[k].drain()
        gathers[k].finish()
        keep(k).wait()
    feed.drain()


def reduce_last(factors, stays, comes, feed_terms, gain_parts):
    rows = factors[0].shape[1] // 8
    items = []
    for p, xf in ((0, True), (0, False), (1, True), (1, False)):
        half = factors[2 * p + 1].shape[1] // 2
        items.append((p, (0 if xf else half, half), xf))
    scratch = []
    for _, (_, cols), _ in items:
        scratch += [
            pltpu.VMEM((2, 2, rows, cols), BF),
            pltpu.VMEM((2, 2, rows, cols), BF),
            pltpu.VMEM((2, 2, rows, cols), BF),
            pltpu.VMEM((2, rows, cols), BF),
            pltpu.VMEM((rows, cols), BF),
        ]
    for stay in stays:
        scratch += [
            pltpu.VMEM(stay.shape, BF),
            pltpu.VMEM(stay.shape, BF),
            pltpu.VMEM(stay.shape[1:], BF),
        ]
    outs = []
    for _, (_, cols), _ in items:
        scratch += [pltpu.VMEM((3, rows // 4, cols), BF)] * 2 + [pltpu.VMEM((rows // 4, cols), BF)]
        outs.append(jax.ShapeDtypeStruct((4, rows // 4, cols), BF))
    outs.append(jax.ShapeDtypeStruct((8,) + stays[0].shape[1:], BF))
    outs.append(jax.ShapeDtypeStruct((8,) + stays[1].shape[1:], BF))
    outs.append(jax.ShapeDtypeStruct((2 * stays[2].shape[1], 8 * stays[2].shape[2]), BF))
    outs.append(jax.ShapeDtypeStruct(feed_terms.shape[1:], F32))
    outs.append(jax.ShapeDtypeStruct(gain_parts.shape[1:], F32))
    scratch += [pltpu.VMEM(feed_terms.shape, BF)]
    scratch += [pltpu.VMEM((3,) + feed_terms.shape[1:], BF)] * 2
    scratch += [
        pltpu.VMEM((7,) + gain_parts.shape[1:], F32),
        pltpu.VMEM(gain_parts.shape[1:], F32),
        pltpu.VMEM((3,) + gain_parts.shape[1:], F32),
    ]
    scratch += [pltpu.VMEM(f.shape, BF) for f in factors]
    dma = pltpu.SemaphoreType.DMA
    scratch += [dma((4,)), dma((4,)), dma((4,)), dma((8,)), dma((8,))]
    scratch += [dma((8,)), dma((4,)), dma((4,))]
    scratch += [dma((28,)), dma((28,)), dma((4,))]
    scratch += [dma((4, 6)), dma((4, 6)), dma((4, 8)), dma((4, 4)), dma((4,))]
    scratch += [dma((24,)), dma((24,)), dma]
    scratch += [dma((7,)), dma((7,)), dma((3,)), dma((3,))]
    hbm, vmem = pl.BlockSpec(memory_space=pl.ANY), pl.BlockSpec(memory_space=pltpu.VMEM)
    out = pl.pallas_call(
        functools.partial(last_kernel, items),
        name="reduce_last",
        out_shape=tuple(outs),
        in_specs=[hbm] * 13 + [vmem],
        out_specs=[hbm] * 7 + [vmem] * 2,
        scratch_shapes=scratch,
        compiler_params=pltpu.CompilerParams(
            collective_id=4, has_side_effects=True, vmem_limit_bytes=64 * 1024 * 1024 - 65536
        ),
    )(*factors, *stays, *comes, feed_terms, gain_parts)
    qkv = jnp.concatenate([out[0].reshape(rows, -1), out[1].reshape(rows, -1)], axis=1)
    project = jnp.concatenate([out[2].reshape(rows, -1), out[3].reshape(rows, -1)], axis=1)
    width = out[4].shape[2]
    ffn = [out[4].reshape(-1, width), out[5].reshape(-1, width), out[6]]
    return qkv, project, ffn, out[7], out[8]


def per_device(
    fast,
    block_input,
    cotangent,
    query_weight,
    key_weight,
    value_weight,
    project_weight,
    prenorm_gain,
    midnorm_gain,
    gate_weight,
    up_weight,
    down_weight,
    doc_lengths,
    tile_counts,
):
    tokens_here, model = block_input.shape
    group = HEADS // KV_HEADS
    scale = HEAD_DIM ** (-0.5)
    q_cols, k_cols = HEADS * HEAD_DIM, KV_HEADS * HEAD_DIM
    inputs_f = block_input.astype(jnp.float32)
    ends = jnp.cumsum(doc_lengths[0])
    position = jnp.arange(tokens_here, dtype=jnp.int32)
    segment = jnp.sum((position[:, None] >= ends[None, :]).astype(jnp.int32), axis=1)
    allowed = (segment[:, None] == segment[None, :]) & (position[None, :] <= position[:, None])
    if fast:
        gains = jnp.stack([prenorm_gain, midnorm_gain]).astype(F32).reshape(1, -1)
        bias = jnp.where(allowed, 0.0, -1e30).astype(F32)
        qkv_full, project_full, grad_rows, normed, qkv, attended, gains_full, logs = gather_first(
            block_input,
            query_weight,
            key_weight,
            value_weight,
            project_weight,
            gains,
            cotangent,
            bias,
        )
        gains_full = gains_full.reshape(8, 2, -1)
        first_gain = gains_full[:, 0].reshape(-1)
        second_gain = gains_full[:, 1].reshape(-1)
        logsum = logs[:, :HEADS].T.reshape(KV_HEADS, group, tokens_here, 1)
    else:
        qkv_full = jnp.concatenate(
            [
                lax.all_gather(query_weight, "narrow", axis=0, tiled=True),
                lax.all_gather(key_weight, "narrow", axis=0, tiled=True),
                lax.all_gather(value_weight, "narrow", axis=0, tiled=True),
            ],
            axis=1,
        )
        project_full = lax.all_gather(project_weight, "narrow", axis=1, tiled=True)
        first_gain = lax.all_gather(prenorm_gain, "narrow", axis=0, tiled=True).astype(F32)
        second_gain = lax.all_gather(midnorm_gain, "narrow", axis=0, tiled=True).astype(F32)
        grad_rows = lax.all_gather(cotangent, "wide", axis=0, tiled=True)
        normed = rms_scale(inputs_f, first_gain).astype(jnp.bfloat16)
        qkv = jnp.dot(normed, qkv_full, preferred_element_type=jnp.float32).astype(jnp.bfloat16)
    query_rows = qkv[:, :q_cols].reshape(tokens_here, KV_HEADS, group, HEAD_DIM)
    key_rows = qkv[:, q_cols : q_cols + k_cols].reshape(tokens_here, KV_HEADS, HEAD_DIM)
    value_rows = qkv[:, q_cols + k_cols :].reshape(tokens_here, KV_HEADS, HEAD_DIM)
    if not fast:
        scores = (
            jnp.einsum("qcgd,kcd->cgqk", query_rows, key_rows, preferred_element_type=jnp.float32)
            * scale
        )
        masked = jnp.where(allowed, scores, -1e30)
        peak = jnp.max(masked, axis=-1, keepdims=True)
        expo = jnp.exp(masked - peak)
        total = jnp.sum(expo, axis=-1, keepdims=True)
        probs_low = (expo / total).astype(jnp.bfloat16)
        logsum = peak + jnp.log(total)
        attended = (
            jnp.einsum("cgqk,kcd->qcgd", probs_low, value_rows, preferred_element_type=jnp.float32)
            .astype(jnp.bfloat16)
            .reshape(tokens_here, HEADS * HEAD_DIM)
        )
    branch = jnp.dot(attended, project_full, preferred_element_type=jnp.float32)
    middle = inputs_f + branch
    mixed_in = rms_scale(middle, second_gain).astype(jnp.bfloat16)
    width = gate_weight.shape[1]
    wide_index = lax.axis_index("wide")
    my_count = jnp.sum(
        jnp.where(jnp.arange(tile_counts.shape[0], dtype=jnp.int32) == wide_index, tile_counts, 0)
    )
    live = (jnp.arange(width, dtype=jnp.int32) // TILE < my_count).astype(jnp.float32)
    if fast:
        mixed_back, feed_terms, *pieces = feed_forward(
            mixed_in, grad_rows, gate_weight, up_weight, down_weight, live.reshape(1, -1)
        )
        stays = pieces[1::2]
        comes = [
            lax.ppermute(piece, "narrow", [(i, i ^ bit) for i in range(8)])
            for piece, bit in zip(pieces[0::2], (2, 4, 2, 4))
        ]
    else:
        gathered = lax.all_gather(mixed_in, "wide", axis=0, tiled=True)
        gate_pre = jnp.dot(gathered, gate_weight, preferred_element_type=jnp.float32)
        up_pre = jnp.dot(gathered, up_weight, preferred_element_type=jnp.float32)
        hidden_back = contract_cols(grad_rows, down_weight)
        sigma = jax.nn.sigmoid(gate_pre)
        hidden = (gate_pre * sigma * up_pre * live).astype(BF)
        gate_back = (
            hidden_back * up_pre * live * sigma * (1.0 + gate_pre * (1.0 - sigma))
        ).astype(BF)
        up_back = (hidden_back * gate_pre * sigma * live).astype(BF)
        mixed_terms = (
            contract_cols(gate_back, gate_weight) + contract_cols(up_back, up_weight)
        ).astype(BF)
        mixed_back = lax.psum_scatter(
            mixed_terms, "wide", scatter_dimension=0, tiled=True
        ).astype(F32)
        partial_rows = jnp.dot(hidden, down_weight, preferred_element_type=jnp.float32)
        down_part = contract_rows(hidden, grad_rows)
        gate_part = contract_rows(gathered, gate_back)
        up_part = contract_rows(gathered, up_back)
    out_grad = cotangent.astype(jnp.float32)
    unused_second, second_backward = jax.vjp(rms_scale, middle, second_gain)
    middle_norm_back, second_gain_part = second_backward(mixed_back)
    middle_back = out_grad + middle_norm_back
    branch_back = middle_back.astype(jnp.bfloat16)
    attended_back = (
        contract_cols(branch_back, project_full)
        .astype(jnp.bfloat16)
        .reshape(tokens_here, KV_HEADS, group, HEAD_DIM)
    )
    scores_again = (
        jnp.einsum("qcgd,kcd->cgqk", query_rows, key_rows, preferred_element_type=jnp.float32)
        * scale
    )
    probs_again = jnp.where(allowed, jnp.exp(scores_again - logsum), 0.0)
    probs_again_low = probs_again.astype(jnp.bfloat16)
    value_back = (
        jnp.einsum(
            "cgqk,qcgd->kcd", probs_again_low, attended_back, preferred_element_type=jnp.float32
        )
        .astype(jnp.bfloat16)
        .reshape(tokens_here, KV_HEADS * HEAD_DIM)
    )
    probs_back = jnp.einsum(
        "qcgd,kcd->cgqk", attended_back, value_rows, preferred_element_type=jnp.float32
    )
    scores_back = (
        probs_again * (probs_back - jnp.sum(probs_again * probs_back, axis=-1, keepdims=True))
    ).astype(jnp.bfloat16)
    query_back = (
        (
            jnp.einsum("cgqk,kcd->qcgd", scores_back, key_rows, preferred_element_type=jnp.float32)
            * scale
        )
        .astype(jnp.bfloat16)
        .reshape(tokens_here, HEADS * HEAD_DIM)
    )
    key_back = (
        (
            jnp.einsum(
                "cgqk,qcgd->kcd", scores_back, query_rows, preferred_element_type=jnp.float32
            )
            * scale
        )
        .astype(jnp.bfloat16)
        .reshape(tokens_here, KV_HEADS * HEAD_DIM)
    )
    qkv_back = jnp.concatenate([query_back, key_back, value_back], axis=1)
    normed_back = contract_cols(qkv_back, qkv_full)
    unused_first, first_backward = jax.vjp(rms_scale, inputs_f, first_gain)
    input_norm_back, first_gain_part = first_backward(normed_back)
    input_grad = (middle_back + input_norm_back).astype(jnp.bfloat16)

    if fast:
        gain_parts = jnp.stack(
            [first_gain_part.reshape(8, -1), second_gain_part.reshape(8, -1)], axis=1
        ).reshape(8, 1, -1)
        input_grad, qkv_back = lax.optimization_barrier((input_grad, qkv_back))
        qkv_total, project_total, ffn_totals, feed, gain_total = reduce_last(
            (normed, qkv_back, branch_back, attended),
            stays,
            comes,
            feed_terms,
            gain_parts,
        )
        gain_total = gain_total.reshape(2, -1)
        first_total, second_total = gain_total[0], gain_total[1]
        qkv_total = qkv_total.astype(F32)
        project_total = project_total.T.astype(F32)
        gate_total, up_total, down_total = [t.astype(F32) for t in ffn_totals]
    else:

        def owned(part):
            share = lax.psum_scatter(part.astype(BF), "narrow", scatter_dimension=0, tiled=True)
            return lax.psum(share, "wide").astype(F32)

        qkv_total = owned(contract_rows(normed, qkv_back))
        project_total = owned(contract_rows(branch_back, attended)).T
        first_total = owned(first_gain_part)
        second_total = owned(second_gain_part)
        gate_total, up_total, down_total = (
            lax.psum(gate_part.astype(BF), "narrow").astype(F32),
            lax.psum(up_part.astype(BF), "narrow").astype(F32),
            lax.psum(down_part.astype(BF), "narrow").astype(F32),
        )
        feed = lax.psum_scatter(
            partial_rows.astype(BF), "wide", scatter_dimension=0, tiled=True
        ).astype(F32)
    block_output = (middle + feed).astype(BF)
    return (
        block_output,
        input_grad,
        qkv_total[:, :q_cols],
        qkv_total[:, q_cols : q_cols + k_cols],
        qkv_total[:, q_cols + k_cols :],
        project_total,
        first_total,
        second_total,
        gate_total,
        up_total,
        down_total,
    )


def solution(mesh):
    fast = mesh.shape["narrow"] == 8 and mesh.shape["wide"] == 4
    placed = (
        P(("narrow", "wide"), None),
        P(("narrow", "wide"), None),
        P("narrow", None),
        P("narrow", None),
        P("narrow", None),
        P(None, "narrow"),
        P("narrow"),
        P("narrow"),
        P(None, "wide"),
        P(None, "wide"),
        P("wide", None),
        P(("narrow", "wide"), None),
        P(),
    )
    return jax.shard_map(
        functools.partial(per_device, fast),
        mesh=mesh,
        in_specs=placed,
        out_specs=(
            P(("narrow", "wide"), None),
            P(("narrow", "wide"), None),
            P("narrow", None),
            P("narrow", None),
            P("narrow", None),
            P(None, "narrow"),
            P("narrow"),
            P("narrow"),
            P(None, "wide"),
            P(None, "wide"),
            P("wide", None),
        ),
        check_vma=False,
    )
```

```python
import functools

import jax
import jax.numpy as jnp
from jax import lax
from jax.experimental import pallas as pl
from jax.experimental.pallas import tpu as pltpu
from jax.sharding import PartitionSpec as P

HEADS = 24
KV_HEADS = 6
HEAD_DIM = 64
TILE = 128


EPSILON = 1e-06

BF = jnp.bfloat16
F32 = jnp.float32


def rms_scale(rows, gain):
    factor = lax.rsqrt(jnp.mean(rows * rows, axis=-1, keepdims=True) + EPSILON)
    return rows * factor * gain


def contract_rows(left, right):
    return lax.dot_general(
        left, right, (((0,), (0,)), ((), ())), preferred_element_type=jnp.float32
    )


def contract_cols(left, right):
    return lax.dot_general(
        left, right, (((1,), (1,)), ((), ())), preferred_element_type=jnp.float32
    )


def flip(n, bit):
    return n + bit - 2 * bit * lax.rem(n // bit, 2)


def at(n, w):
    return {"narrow": n, "wide": w}


def send(src, dst, ssem, rsem, n, w):
    return pltpu.make_async_remote_copy(
        src_ref=src,
        dst_ref=dst,
        send_sem=ssem,
        recv_sem=rsem,
        device_id=at(n, w),
        device_id_type=pl.DeviceIdType.MESH,
    )


def greet(narrow_peers, n, w, line):
    barrier = pltpu.get_barrier_semaphore()
    for peer in narrow_peers:
        pl.semaphore_signal(
            barrier, inc=1, device_id=at(peer, w), device_id_type=pl.DeviceIdType.MESH
        )
    if not line:
        pl.semaphore_wait(barrier, len(narrow_peers))
    if line:

        @pl.when(w > 0)
        def _():
            pl.semaphore_signal(
                barrier, inc=1, device_id=at(n, w - 1), device_id_type=pl.DeviceIdType.MESH
            )

        @pl.when(w < 3)
        def _():
            pl.semaphore_signal(
                barrier, inc=1, device_id=at(n, w + 1), device_id_type=pl.DeviceIdType.MESH
            )

        @pl.when((w == 0) | (w == 3))
        def _():
            pl.semaphore_wait(barrier, len(narrow_peers) + 1)

        @pl.when((w == 1) | (w == 2))
        def _():
            pl.semaphore_wait(barrier, len(narrow_peers) + 2)


class LineGather:
    def __init__(self, n, w, own, whole, ssem, rsem, chunks):
        self.n, self.w, self.own, self.whole = n, w, own, whole
        self.ssem, self.rsem, self.chunks = ssem, rsem, chunks
        self.rows = own.shape[0] // chunks

    def span(self, i):
        return pl.ds(pl.multiple_of(i * self.rows, self.rows), self.rows)

    def part(self, shard, i):
        return self.whole.at[shard, self.span(i), :]

    def put(self, way, here, shard, i):
        src = self.own.at[self.span(i), :] if shard is here else self.part(shard, i)
        to = here + 1 - 2 * way
        s = (way * 4 + shard) * self.chunks + i
        r = shard * self.chunks + i
        return send(src, self.part(shard, i), self.ssem.at[s], self.rsem.at[r], self.n, to)

    def came(self, shard, i):
        self.put(0, 0, shard, i).wait_recv()

    def start_chunk(self, i):
        @pl.when(self.w < 3)
        def _():
            self.put(0, self.w, self.w, i).start()

        @pl.when(self.w > 0)
        def _():
            self.put(1, self.w, self.w, i).start()

    def start(self):
        for i in range(self.chunks):
            self.start_chunk(i)

    def near(self, i):
        @pl.when(self.w == 1)
        def _():
            self.came(0, i)
            self.put(0, 1, 0, i).start()
            self.came(2, i)
            self.put(1, 1, 2, i).start()

        @pl.when(self.w == 2)
        def _():
            self.came(3, i)
            self.put(1, 2, 3, i).start()
            self.came(1, i)
            self.put(0, 2, 1, i).start()

    def far(self, i):
        @pl.when(self.w == 1)
        def _():
            self.came(3, i)
            self.put(1, 1, 3, i).start()

        @pl.when(self.w == 2)
        def _():
            self.came(0, i)
            self.put(0, 2, 0, i).start()

    def ready(self, i):
        @pl.when(self.w == 0)
        def _():
            for shard in (1, 2, 3):
                self.came(shard, i)

        @pl.when(self.w == 3)
        def _():
            for shard in (2, 1, 0):
                self.came(shard, i)

    def finish_sends(self):
        for here in range(4):

            @pl.when(self.w == here)
            def _():
                for i in range(self.chunks):
                    if here < 3:
                        for shard in range(here + 1):
                            self.put(0, here, shard, i).wait_send()
                    if here > 0:
                        for shard in range(here, 4):
                            self.put(1, here, shard, i).wait_send()

    def finish(self):
        for i in range(self.chunks):
            self.ready(i)
        self.finish_sends()


def first_kernel(
    x_ref,
    q_ref,
    k_ref,
    v_ref,
    p_ref,
    g_ref,
    c_ref,
    bias_ref,
    qkv_out,
    p_full,
    c_full,
    normed_out,
    rows_out,
    att_out,
    g_full,
    log_out,
    qkv_full,
    p_buf,
    c_buf,
    x_buf,
    gain_row,
    normed,
    qkv,
    att,
    in_sem,
    out_sem,
    ssem,
    rsem,
    gs_sem,
    gr_sem,
    zs_sem,
    zr_sem,
):
    n, w = lax.axis_index("narrow"), lax.axis_index("wide")
    x, y, c, d = flip(n, 2), flip(n, 4), flip(n, 1), flip(flip(n, 2), 4)
    others = [lax.rem(n + i, 8) for i in range(1, 8)]
    rows = q_ref.shape[0]
    half = rows // 2
    depth = p_ref.shape[0]
    qc, kc = q_ref.shape[1], k_ref.shape[1]
    cols = ((0, qc), (qc, kc), (qc + kc, kc))

    def region(t, block, h):
        if t == 3:
            r = pl.ds(0, depth) if h == 2 else pl.ds(h * (depth // 2), depth // 2)
            return p_full.at[r, pl.ds(pl.multiple_of(block * rows, rows), rows)]
        start = pl.multiple_of(block * rows, rows)
        r = pl.ds(start, rows) if h == 2 else pl.ds(start + h * half, half)
        return qkv_full.at[r, pl.ds(cols[t][0], cols[t][1])]

    locals_in = []
    for i, (src, dst) in enumerate(
        (
            (g_ref, g_full.at[n]),
            (x_ref, x_buf),
            (p_ref, p_buf),
            (c_ref, c_buf),
            (q_ref, region(0, n, 2)),
            (k_ref, region(1, n, 2)),
            (v_ref, region(2, n, 2)),
        )
    ):
        cp = pltpu.make_async_copy(src, dst, in_sem.at[i])
        cp.start()
        locals_in.append(cp)

    greet(others, n, w, True)

    def own(t, h):
        ref = (q_ref, k_ref, v_ref, p_ref)[t]
        if h == 2:
            return ref
        size = ref.shape[0] // 2
        return ref.at[pl.ds(h * size, size), :]

    def msg(t, kind, src, block, h, peer):
        k = t * 10 + kind
        return send(src, region(t, block, h), ssem.at[k], rsem.at[k], peer, w)

    def to_x(t, h):
        return msg(t, h, own(t, h), n, h, x)

    def to_y(t, h):
        return msg(t, 2 + h, own(t, h), n, h, y)

    def on_x(t):
        return msg(t, 4, region(t, y, 0), y, 0, x)

    def on_y(t):
        return msg(t, 5, region(t, x, 1), x, 1, y)

    def to_c(t, which):
        block = (n, x, y, d)[which]
        src = own(t, 2) if which == 0 else region(t, block, 2)
        return msg(t, 6 + which, src, block, 2, c)

    def start_own(t):
        to_x(t, 1).start()
        to_y(t, 0).start()
        to_x(t, 0).start()
        to_y(t, 1).start()

    def gain(i):
        return send(g_ref, g_full.at[n], gs_sem.at[i], gr_sem.at[i], others[i], w)

    line = LineGather(n, w, c_ref, c_full, zs_sem, zr_sem, 4)
    for i in range(7):
        gain(i).start()
    start_own(0)
    line.start()
    for t in (1, 2):
        start_own(t)
    for t in range(3):
        to_c(t, 0).start()

    locals_out = []

    def put(src, dst):
        cp = pltpu.make_async_copy(src, dst, out_sem.at[len(locals_out)])
        cp.start()
        locals_out.append(cp)

    for i in range(7):
        gain(i).wait()
    for cp in locals_in:
        cp.wait()
    put(p_buf, region(3, n, 2))
    put(c_buf, c_full.at[w])
    for k in range(8):
        gain_row[:, pl.ds(k * rows, rows)] = g_full[k, :, :rows]
    strip = 16

    @pl.loop(0, x_buf.shape[0] // strip)
    def _(i):
        s = pl.ds(pl.multiple_of(i * strip, strip), strip)
        normed[s, :] = rms_scale(x_buf[s, :].astype(F32), gain_row[...]).astype(BF)

    put(normed, normed_out)

    def relay(t):
        to_y(t, 0).wait_recv()
        on_x(t).start()
        to_x(t, 1).wait_recv()
        on_y(t).start()
        to_x(t, 0).wait_recv()
        to_c(t, 1).start()
        to_y(t, 1).wait_recv()
        to_c(t, 2).start()

    def corner(t):
        on_x(t).wait_recv()
        on_y(t).wait_recv()
        to_c(t, 3).start()

    line.near(0)
    relay(0)
    line.near(1)
    relay(1)
    line.near(2)
    relay(2)
    start_own(3)
    to_c(3, 0).start()
    line.near(3)
    line.far(0)
    line.far(1)
    for t in range(3):
        corner(t)
    line.far(2)
    for t in range(3):
        for which in range(4):
            to_c(t, which).wait_recv()
    put(qkv_full, qkv_out)
    tile = 256

    @pl.loop(0, qkv.shape[1] // tile)
    def _(i):
        s = pl.ds(pl.multiple_of(i * tile, tile), tile)
        qkv[:, s] = jnp.dot(normed[...], qkv_full[:, s], preferred_element_type=F32).astype(BF)

    put(qkv, rows_out)
    line.far(3)

    log_out[...] = jnp.zeros(log_out.shape, F32)
    pair = 2 * HEAD_DIM
    group = HEADS // KV_HEADS

    @pl.loop(0, KV_HEADS // 2)
    def _(i):
        keys = qkv[:, pl.ds(pl.multiple_of(qc + i * pair, pair), pair)]
        values = qkv[:, pl.ds(pl.multiple_of(qc + kc + i * pair, pair), pair)]
        lane = lax.broadcasted_iota(jnp.int32, log_out.shape, 1)
        for b in range(group):
            at_cols = pl.ds(pl.multiple_of((i * group + b) * pair, pair), pair)
            queries = qkv[:, at_cols]
            side = (2 * b) // group
            key = keys[:, side * HEAD_DIM : (side + 1) * HEAD_DIM]
            value = values[:, side * HEAD_DIM : (side + 1) * HEAD_DIM]
            heads = []
            for e in range(2):
                query = queries[:, e * HEAD_DIM : (e + 1) * HEAD_DIM]
                masked = contract_cols(query, key) * (HEAD_DIM**-0.5) + bias_ref[...]
                peak = jnp.max(masked, axis=-1, keepdims=True)
                expo = jnp.exp(masked - peak)
                total = jnp.sum(expo, axis=-1, keepdims=True)
                probs = (expo * (1.0 / total)).astype(BF)
                heads.append(jnp.dot(probs, value, preferred_element_type=F32))
                log_out[...] = jnp.where(
                    lane == 2 * (i * group + b) + e, peak + jnp.log(total), log_out[...]
                )
            att[:, at_cols] = jnp.concatenate(heads, axis=1).astype(BF)

    put(att, att_out)
    relay(3)
    corner(3)
    for t in range(4):
        for h in range(2):
            to_x(t, h).wait_send()
            to_y(t, h).wait_send()
        on_x(t).wait_send()
        on_y(t).wait_send()
        for which in range(4):
            if t == 3:
                to_c(t, which).wait_recv()
            to_c(t, which).wait_send()
    line.finish()
    for cp in locals_out:
        cp.wait()


def gather_first(rows_in, query, key, value, project, gains, cotangent, bias):
    rows = query.shape[0]
    width = query.shape[1] + 2 * key.shape[1]
    tokens_here, model = rows_in.shape
    hbm, vmem = pl.BlockSpec(memory_space=pl.ANY), pl.BlockSpec(memory_space=pltpu.VMEM)
    return pl.pallas_call(
        first_kernel,
        name="gather_first",
        out_shape=(
            jax.ShapeDtypeStruct((8 * rows, width), BF),
            jax.ShapeDtypeStruct((project.shape[0], 8 * rows), BF),
            jax.ShapeDtypeStruct((4,) + cotangent.shape, BF),
            jax.ShapeDtypeStruct((tokens_here, model), BF),
            jax.ShapeDtypeStruct((tokens_here, width), BF),
            jax.ShapeDtypeStruct((tokens_here, query.shape[1]), BF),
            jax.ShapeDtypeStruct((8,) + gains.shape, gains.dtype),
            jax.ShapeDtypeStruct((tokens_here, 128), F32),
        ),
        in_specs=[hbm] * 7 + [vmem],
        out_specs=[hbm] * 6 + [vmem] * 2,
        scratch_shapes=[
            pltpu.VMEM((8 * rows, width), BF),
            pltpu.VMEM(project.shape, BF),
            pltpu.VMEM(cotangent.shape, BF),
            pltpu.VMEM((tokens_here, model), BF),
            pltpu.VMEM((1, model), F32),
            pltpu.VMEM((tokens_here, model), BF),
            pltpu.VMEM((tokens_here, width), BF),
            pltpu.VMEM((tokens_here, query.shape[1]), BF),
            pltpu.SemaphoreType.DMA((7,)),
            pltpu.SemaphoreType.DMA((6,)),
            pltpu.SemaphoreType.DMA((40,)),
            pltpu.SemaphoreType.DMA((40,)),
            pltpu.SemaphoreType.DMA((7,)),
            pltpu.SemaphoreType.DMA((7,)),
            pltpu.SemaphoreType.DMA((32,)),
            pltpu.SemaphoreType.DMA((16,)),
        ],
        compiler_params=pltpu.CompilerParams(collective_id=1, has_side_effects=True),
    )(rows_in, query, key, value, project, gains, cotangent, bias)


def attention_back_kernel(qkv, back, logs, bias, out):
    q_cols, k_cols = HEADS * HEAD_DIM, KV_HEADS * HEAD_DIM
    pair = 2 * HEAD_DIM
    group = HEADS // KV_HEADS
    scale = HEAD_DIM**-0.5

    @pl.loop(0, KV_HEADS // 2)
    def _(i):
        key_at = pl.ds(pl.multiple_of(q_cols + i * pair, pair), pair)
        value_at = pl.ds(pl.multiple_of(q_cols + k_cols + i * pair, pair), pair)
        keys, values = qkv[:, key_at], qkv[:, value_at]
        lane = lax.broadcasted_iota(jnp.int32, logs.shape, 1)
        key_backs, value_backs = [], []
        for side in range(2):
            key = keys[:, side * HEAD_DIM : (side + 1) * HEAD_DIM]
            value = values[:, side * HEAD_DIM : (side + 1) * HEAD_DIM]
            key_back = jnp.zeros(key.shape, F32)
            value_back = jnp.zeros(key.shape, F32)
            for b in range(side * group // 2, (side + 1) * group // 2):
                at_cols = pl.ds(pl.multiple_of((i * group + b) * pair, pair), pair)
                queries, backs = qkv[:, at_cols], back[:, at_cols]
                heads = []
                for e in range(2):
                    query = queries[:, e * HEAD_DIM : (e + 1) * HEAD_DIM]
                    given = backs[:, e * HEAD_DIM : (e + 1) * HEAD_DIM]
                    logsum = jnp.sum(
                        jnp.where(lane == 2 * (i * group + b) + e, logs[...], 0.0),
                        axis=-1,
                        keepdims=True,
                    )
                    probs = jnp.exp(contract_cols(query, key) * scale + bias[...] - logsum)
                    value_back = value_back + contract_rows(probs.astype(BF), given)
                    probs_back = contract_cols(given, value)
                    inner = jnp.sum(probs * probs_back, axis=-1, keepdims=True)
                    scores_back = (probs * (probs_back - inner)).astype(BF)
                    heads.append(jnp.dot(scores_back, key, preferred_element_type=F32) * scale)
                    key_back = key_back + contract_rows(scores_back, query)
                out[:, at_cols] = jnp.concatenate(heads, axis=1).astype(BF)
            key_backs.append(key_back * scale)
            value_backs.append(value_back)
        out[:, key_at] = jnp.concatenate(key_backs, axis=1).astype(BF)
        out[:, value_at] = jnp.concatenate(value_backs, axis=1).astype(BF)


def attention_back(qkv, back, logs, bias):
    vmem = pl.BlockSpec(memory_space=pltpu.VMEM)
    heads = HEADS * qkv.shape[0] * qkv.shape[0]
    return pl.pallas_call(
        attention_back_kernel,
        name="attention_back",
        out_shape=jax.ShapeDtypeStruct(qkv.shape, BF),
        in_specs=[vmem] * 4,
        out_specs=vmem,
        cost_estimate=pl.CostEstimate(
            flops=10 * heads * HEAD_DIM, bytes_accessed=8 * qkv.size, transcendentals=heads
        ),
    )(qkv, back, logs, bias)


class LineScatter:
    def __init__(self, n, w, terms, bufs, ssem, rsem, chunks):
        self.n, self.w, self.terms, self.bufs = n, w, terms, bufs
        self.ssem, self.rsem, self.chunks = ssem, rsem, chunks
        self.rows = terms.shape[1] // chunks

    def span(self, i):
        return pl.ds(pl.multiple_of(i * self.rows, self.rows), self.rows)

    def term(self, d, i):
        return self.terms.at[d, self.span(i), :]

    def slot(self, way, slot, i):
        return self.bufs[way].at[slot, self.span(i), :]

    def put(self, way, here, d, i, src):
        slot = d - here - 1 if way == 0 else here - 1 - d
        k = (way * 3 + slot) * self.chunks + i
        to = here + 1 - 2 * way
        return send(src, self.slot(way, slot, i), self.ssem.at[k], self.rsem.at[k], self.n, to)

    def came(self, way, slot, i):
        k = (way * 3 + slot) * self.chunks + i
        ref = self.slot(way, slot, i)
        send(ref, ref, self.ssem.at[k], self.rsem.at[k], self.n, 1).wait_recv()

    def begin(self, i):
        for here, way in ((0, 0), (3, 1)):

            @pl.when(self.w == here)
            def _():
                for d in (3, 2, 1) if way == 0 else (0, 1, 2):
                    self.put(way, here, d, i, self.term(d, i)).start()

    def join(self, way, here, d, i):
        slot = d - here if way == 0 else here - d
        self.came(way, slot, i)
        mine, sum_ = self.term(d, i), self.slot(way, slot, i)
        sum_[...] = (mine[...].astype(F32) + sum_[...].astype(F32)).astype(BF)
        self.put(way, here, d, i, sum_).start()

    def pass_on(self, i):
        @pl.when(self.w == 1)
        def _():
            self.join(0, 1, 3, i)
            self.join(0, 1, 2, i)

        @pl.when(self.w == 2)
        def _():
            self.join(1, 2, 0, i)
            self.join(1, 2, 1, i)

    def pass_end(self, i):
        @pl.when(self.w == 1)
        def _():
            self.join(1, 1, 0, i)

        @pl.when(self.w == 2)
        def _():
            self.join(0, 2, 3, i)

    def finish(self, i, out):
        for here, ways in ((0, (1,)), (1, (0, 1)), (2, (0, 1)), (3, (0,))):

            @pl.when(self.w == here)
            def _():
                for way in ways:
                    self.came(way, 0, i)
                total = self.term(here, i)[...].astype(F32)
                for way in ways:
                    total = total + self.slot(way, 0, i)[...].astype(F32)
                out[self.span(i), :] = total.astype(out.dtype)

    def drain(self):
        sent = {
            0: ((0, 3), (0, 2), (0, 1)),
            1: ((0, 3), (0, 2), (1, 0)),
            2: ((1, 0), (1, 1), (0, 3)),
            3: ((1, 0), (1, 1), (1, 2)),
        }
        for here in range(4):

            @pl.when(self.w == here)
            def _():
                for i in range(self.chunks):
                    for way, d in sent[here]:
                        self.put(way, here, d, i, self.term(d, i)).wait_send()


def middle_kernel(
    mixed,
    cot,
    wg,
    wu,
    wd,
    live,
    back_out,
    partial_out,
    gate_go,
    gate_stay,
    up_go,
    up_stay,
    low_go,
    low_stay,
    high_go,
    high_stay,
    x_all,
    cot_v,
    wg_v,
    wu_v,
    wd_v,
    gate_f,
    up_f,
    back_f,
    hid,
    gb,
    ub,
    terms,
    from_left,
    from_right,
    part_buf,
    gate_k,
    up_k,
    down_k,
    in_sem,
    ag_s,
    ag_r,
    rs_s,
    rs_r,
    part_sem,
    sw_s,
    sw_r,
    out_sem,
    ready,
):
    n, w = lax.axis_index("narrow"), lax.axis_index("wide")
    y, x, core = n // 4, lax.rem(n // 2, 2), lax.rem(n, 2)
    mate = flip(n, 1)
    chunks = 4
    rows = mixed.shape[0] // chunks
    tokens, model = 4 * mixed.shape[0], mixed.shape[1]
    width = wg.shape[1]
    batch = 4 * rows
    loads = [
        pltpu.make_async_copy(src, dst, in_sem.at[k])
        for k, (src, dst) in enumerate(
            ((mixed, x_all.at[w]), (wg, wg_v), (wu, wu_v), (cot, cot_v), (wd, wd_v))
        )
    ]
    for cp in loads:
        cp.start()
    greet([mate], n, w, True)

    gather = LineGather(n, w, mixed, x_all, ag_s, ag_r, chunks)
    scatter = LineScatter(n, w, terms, (from_left, from_right), rs_s, rs_r, chunks)
    gather.start_chunk(0)
    gather.start_chunk(1)
    gather.near(0)
    gather.far(0)
    for cp in loads:
        cp.wait()

    def rows_of(ref, i):
        r = pl.ds(pl.multiple_of(i * rows, rows), rows)
        return ref[:, r, :].reshape(batch, ref.shape[2])

    def store(i):
        return pltpu.make_async_copy(
            part_buf.at[lax.rem(i, 2)],
            partial_out.at[:, pl.ds(pl.multiple_of(i * rows, rows), rows), :],
            part_sem.at[lax.rem(i, 2)],
        )

    @pl.loop(0, chunks)
    def _(i):
        r = pl.ds(pl.multiple_of(i * rows, rows), rows)
        gather.ready(i)
        xs = rows_of(x_all, i)
        gate_f[...] = jnp.dot(xs, wg_v[...], preferred_element_type=F32)
        up_f[...] = jnp.dot(xs, wu_v[...], preferred_element_type=F32)

        @pl.when(i < chunks - 1)
        def _():
            gather.near(i + 1)

        @pl.when(i < chunks - 2)
        def _():
            gather.start_chunk(i + 2)

        back_f[...] = contract_cols(rows_of(cot_v, i), wd_v[...])
        step = 16

        @pl.loop(0, batch // step)
        def _(t):
            s = pl.ds(pl.multiple_of(t * step, step), step)
            d = t // (rows // step)
            into = pl.ds(
                pl.multiple_of(i * rows + lax.rem(t, rows // step) * step, step), step
            )
            gate, up = gate_f[s, :], up_f[s, :] * live[...]
            sigma = jax.nn.sigmoid(gate)
            silu = gate * sigma
            hid[d, into, :] = (silu * up).astype(BF)
            back = back_f[s, :]
            gb[d, into, :] = (back * up * sigma * (1.0 + gate * (1.0 - sigma))).astype(BF)
            ub[d, into, :] = (back * silu * live[...]).astype(BF)

        @pl.when(i > 0)
        def _():
            scatter.pass_on(i - 1)

        @pl.when(i < chunks - 1)
        def _():
            gather.far(i + 1)

        terms[:, r, :] = (
            (contract_cols(rows_of(gb, i), wg_v[...]) + contract_cols(rows_of(ub, i), wu_v[...]))
            .astype(BF)
            .reshape(4, rows, model)
        )
        scatter.begin(i)

        @pl.when(i > 1)
        def _():
            store(i - 2).wait()

        part_buf[lax.rem(i, 2)] = (
            jnp.dot(rows_of(hid, i), wd_v[...], preferred_element_type=F32)
            .astype(BF)
            .reshape(4, rows, model)
        )
        store(i).start()

        @pl.when(i > 0)
        def _():
            scatter.pass_end(i - 1)

    pl.semaphore_signal(
        ready, inc=1, device_id=at(mate, w), device_id_type=pl.DeviceIdType.MESH
    )

    def row_grad(back, block):
        cols = pl.ds(pl.multiple_of(block * (model // 8), model // 8), model // 8)
        return contract_rows(
            x_all[:, :, cols].reshape(tokens, model // 8), back[...].reshape(tokens, width)
        )

    def col_grad(block):
        cols = pl.ds(pl.multiple_of(block * (model // 8), model // 8), model // 8)
        return contract_rows(
            hid[...].reshape(tokens, width), cot_v[:, :, cols].reshape(tokens, model // 8)
        )

    eighth, half = model // 8, model // 2

    def place(j, base):
        return pl.ds(pl.multiple_of(base + j * eighth, eighth), eighth)

    swaps = [
        send(buf.at[pl.ds(half, half), :], buf.at[pl.ds(0, half), :], sw_s.at[k], sw_r.at[k], mate, w)
        for k, buf in enumerate((wg_v, wu_v))
    ]
    swaps.append(
        send(
            wd_v.at[:, pl.ds(half, half)], wd_v.at[:, pl.ds(0, half)], sw_s.at[2], sw_r.at[2], mate, w
        )
    )

    @pl.loop(0, 4)
    def _(j):
        wg_v[place(j, half), :] = row_grad(gb, 2 * j + 1 - core).astype(BF)

    scatter.pass_on(chunks - 1)
    pl.semaphore_wait(ready, 1)
    swaps[0].start()

    @pl.loop(0, 4)
    def _(j):
        wu_v[place(j, half), :] = row_grad(ub, 2 * j + 1 - core).astype(BF)

    swaps[1].start()

    @pl.loop(0, 4)
    def _(j):
        wd_v[:, place(j, half)] = col_grad(2 * j + 1 - core).astype(BF)

    swaps[2].start()
    swaps[0].wait_recv()

    @pl.loop(0, 4)
    def _(j):
        gate_k[j // 2, lax.rem(j, 2)] = (
            row_grad(gb, 2 * j + core) + wg_v[place(j, 0), :].astype(F32)
        ).astype(BF)

    cut = width // 2
    pieces = (
        (gate_k.at[:, 1 - x], gate_go),
        (gate_k.at[:, x], gate_stay),
        (up_k.at[1 - y], up_go),
        (up_k.at[y], up_stay),
        (down_k.at[:, 1 - x, pl.ds(0, cut), :], low_go),
        (down_k.at[:, x, pl.ds(0, cut), :], low_stay),
        (down_k.at[1 - y, :, pl.ds(cut, cut), :], high_go),
        (down_k.at[y, :, pl.ds(cut, cut), :], high_stay),
    )
    puts = [
        pltpu.make_async_copy(src, dst, out_sem.at[k]) for k, (src, dst) in enumerate(pieces)
    ]
    for k in (0, 1):
        puts[k].start()
    scatter.pass_end(chunks - 1)
    swaps[1].wait_recv()

    @pl.loop(0, 4)
    def _(j):
        up_k[j // 2, lax.rem(j, 2)] = (
            row_grad(ub, 2 * j + core) + wu_v[place(j, 0), :].astype(F32)
        ).astype(BF)

    for k in (2, 3):
        puts[k].start()
    swaps[2].wait_recv()

    @pl.loop(0, 4)
    def _(j):
        down_k[j // 2, lax.rem(j, 2)] = (
            col_grad(2 * j + core) + wd_v[:, place(j, 0)].astype(F32)
        ).astype(BF)

    for k in (4, 5, 6, 7):
        puts[k].start()
    for i in range(chunks):
        scatter.finish(i, back_out)
    scatter.drain()
    gather.finish_sends()
    for k in range(3):
        swaps[k].wait_send()
    store(chunks - 2).wait()
    store(chunks - 1).wait()
    for cp in puts:
        cp.wait()


def feed_forward(mixed, cot, gate_weight, up_weight, down_weight, live):
    tokens_here, model = mixed.shape
    width = gate_weight.shape[1]
    rows, eighth, cut = tokens_here // 4, model // 8, width // 2
    hbm, vmem = pl.BlockSpec(memory_space=pl.ANY), pl.BlockSpec(memory_space=pltpu.VMEM)
    row_piece = jax.ShapeDtypeStruct((2, eighth, width), BF)
    col_piece = jax.ShapeDtypeStruct((2, cut, eighth), BF)
    dma = pltpu.SemaphoreType.DMA
    acc = pltpu.VMEM((4 * rows, width), F32)
    act = pltpu.VMEM((4, tokens_here, width), BF)
    tok = pltpu.VMEM((4, tokens_here, model), BF)
    three = pltpu.VMEM((3, tokens_here, model), BF)
    return pl.pallas_call(
        middle_kernel,
        name="feed_forward",
        out_shape=(
            jax.ShapeDtypeStruct(mixed.shape, F32),
            jax.ShapeDtypeStruct((4,) + mixed.shape, BF),
        )
        + (row_piece,) * 4
        + (col_piece,) * 4,
        in_specs=[hbm] * 5 + [vmem],
        out_specs=[vmem] + [hbm] * 9,
        scratch_shapes=[
            tok,
            tok,
            pltpu.VMEM(gate_weight.shape, BF),
            pltpu.VMEM(up_weight.shape, BF),
            pltpu.VMEM(down_weight.shape, BF),
            acc,
            acc,
            acc,
            act,
            act,
            act,
            tok,
            three,
            three,
            pltpu.VMEM((2, 4, rows, model), BF),
            pltpu.VMEM((2, 2, eighth, width), BF),
            pltpu.VMEM((2, 2, eighth, width), BF),
            pltpu.VMEM((2, 2, width, eighth), BF),
            dma((5,)),
            dma((32,)),
            dma((16,)),
            dma((24,)),
            dma((24,)),
            dma((2,)),
            dma((3,)),
            dma((3,)),
            dma((8,)),
            pltpu.SemaphoreType.REGULAR,
        ],
        compiler_params=pltpu.CompilerParams(
            collective_id=5, has_side_effects=True, vmem_limit_bytes=64 * 1024 * 1024 - 65536
        ),
    )(mixed, cot, gate_weight, up_weight, down_weight, live)


class Reduce:
    def __init__(self, me, factors, cols, x_first, bufs, sems, k):
        self.n, self.w, self.y, self.x, self.core = me
        self.left, self.right = factors
        self.cols, self.x_first = pl.ds(*cols), x_first
        self.away, self.sum, self.pair, self.one, self.two = bufs
        self.sems, self.k = sems, k
        self.rows = self.sum.shape[2]
        self.near = flip(self.n, 2) if x_first else flip(self.n, 4)
        self.next = flip(self.n, 4) if x_first else flip(self.n, 2)

    def term(self, block):
        own = pl.ds(pl.multiple_of(block * self.rows, self.rows), self.rows)
        return contract_rows(self.left[:, own], self.right[:, self.cols])

    def swap(self):
        return send(
            self.away,
            self.pair,
            self.sems[0].at[self.k],
            self.sems[1].at[self.k],
            flip(self.n, 1),
            self.w,
        )

    def before_swap(self):
        @pl.loop(0, 4)
        def _(j):
            self.away[j // 2, lax.rem(j, 2)] = self.term(2 * j + 1 - self.core).astype(BF)

        self.swap().start()

    def block(self, first, second):
        return (second, first) if self.x_first else (first, second)

    def axes(self):
        return (self.x, self.y) if self.x_first else (self.y, self.x)

    def stage(self, s):
        a, b = self.axes()
        if s == 1:
            src = self.sum.at[:, 1 - a] if self.x_first else self.sum.at[1 - a]
            dst, peer = self.one, self.near
        else:
            src = self.sum.at[self.block(a, 1 - b)]
            dst, peer = self.two, self.next
        k = 2 * self.k + s - 1
        return send(src, dst, self.sems[2].at[k], self.sems[3].at[k], peer, self.w)

    def add(self, block, other):
        step = 64 if self.rows % 64 == 0 else 48

        @pl.loop(0, self.rows // step)
        def _(i):
            r = pl.ds(pl.multiple_of(i * step, step), step)
            self.sum[block[0], block[1], r, :] = (
                self.sum[block[0], block[1], r, :] + other[r, :]
            )

    def after_swap(self):
        a, _ = self.axes()
        self.swap().wait_recv()

        @pl.loop(0, 4)
        def _(j):
            first = lax.rem(1 - a + j // 2, 2)
            y, x = self.block(first, lax.rem(j, 2))
            total = self.term(4 * y + 2 * x + self.core) + self.pair[y, x].astype(F32)
            self.sum[y, x] = total.astype(BF)

        self.stage(1).start()

    def after_one(self):
        a, b = self.axes()
        self.stage(1).wait()
        self.add(self.block(a, 1 - b), self.one.at[1 - b])
        self.stage(2).start()
        self.add(self.block(a, b), self.one.at[b])

    def after_two(self):
        a, b = self.axes()
        self.stage(2).wait()
        self.add(self.block(a, b), self.two)

    def result(self):
        return self.sum.at[self.y, self.x]


class Half:
    def __init__(self, me, kept, came, x_first, bufs, sems, k):
        self.n, self.w, self.y, self.x, self.core = me
        self.kept, self.came, self.x_first = kept, came, x_first
        self.sum, self.one, self.two = bufs
        self.sems, self.k = sems, k
        self.rows = kept.shape[1]
        self.next = flip(self.n, 4) if x_first else flip(self.n, 2)
        self.here = self.y if x_first else self.x

    def loads(self):
        return [
            pltpu.make_async_copy(self.kept, self.sum, self.sems[0].at[2 * self.k]),
            pltpu.make_async_copy(self.came, self.one, self.sems[0].at[2 * self.k + 1]),
        ]

    def stage(self):
        return send(
            self.sum.at[1 - self.here],
            self.two,
            self.sems[1].at[self.k],
            self.sems[2].at[self.k],
            self.next,
            self.w,
        )

    def add(self, block, other):
        @pl.loop(0, self.rows // 64)
        def _(i):
            r = pl.ds(pl.multiple_of(i * 64, 64), 64)
            self.sum[block, r, :] = self.sum[block, r, :] + other[r, :]

    def after_one(self):
        for cp in self.loads():
            cp.wait()
        self.add(1 - self.here, self.one.at[1 - self.here])
        self.stage().start()
        self.add(self.here, self.one.at[self.here])

    def after_two(self):
        self.stage().wait()
        self.add(self.here, self.two)

    def result(self):
        return self.sum.at[self.here]


class Spread:
    def __init__(self, item, region, sems, k):
        self.item, self.region, self.sems, self.k = item, region, sems, k
        n = item.n
        self.blocks = (n, flip(n, 2), flip(n, 4), flip(flip(n, 2), 4))

    def copy(self, kind, src, block, peer):
        k = 7 * self.k + kind
        return send(
            src, self.region(block), self.sems[0].at[k], self.sems[1].at[k], peer, self.item.w
        )

    def own(self, kind):
        n = self.item.n
        return self.copy(kind, self.item.result(), n, (flip(n, 2), flip(n, 4), flip(n, 1))[kind])

    def corner(self):
        n, b = self.item.n, self.blocks
        if self.item.x_first:
            return self.copy(3, self.region(b[2]), b[2], flip(n, 2))
        return self.copy(3, self.region(b[1]), b[1], flip(n, 4))

    def to_core(self, which):
        block = self.blocks[which]
        return self.copy(3 + which, self.region(block), block, flip(self.item.n, 1))

    def keep(self):
        return pltpu.make_async_copy(
            self.item.result(), self.region(self.item.n), self.sems[2].at[self.k]
        )

    def start(self):
        order = (1, 0, 2) if self.item.x_first else (0, 1, 2)
        for kind in order:
            self.own(kind).start()
        self.keep().start()

    def relay(self):
        first, second = (1, 0) if self.item.x_first else (0, 1)
        self.own(first).wait_recv()
        self.corner().start()
        self.to_core(1 + first).start()
        self.own(second).wait_recv()
        self.to_core(1 + second).start()

    def last(self):
        self.corner().wait_recv()
        self.to_core(3).start()

    def finish(self):
        for kind in range(2):
            self.own(kind).wait_send()
        self.own(2).wait()
        self.corner().wait_send()
        for which in range(1, 4):
            self.to_core(which).wait()
        self.keep().wait()


class Rows:
    def __init__(self, ref):
        self.ref = ref
        self.shape = (4, ref.shape[0] // 4, ref.shape[1])

    @property
    def at(self):
        return self

    def __getitem__(self, index):
        d, r, _ = index
        start = pl.multiple_of(d * self.shape[1] + r.start, r.size)
        return self.ref.at[pl.ds(start, r.size), :]


def last_kernel(items, *refs):
    refs = list(refs)

    def take(count):
        out = refs[:count]
        del refs[:count]
        return out

    factors = take(4)
    stays, comes = take(4), take(4)
    feed_terms, gain_parts = take(2)
    outs = take(4)
    gate_full, up_full, down_full = take(3)
    feed_out, gain_out = take(2)
    attn_bufs = [take(5) for _ in range(4)]
    ffn_bufs = [take(3) for _ in range(4)]
    line_bufs = [take(3) for _ in range(4)]
    feed_v, feed_left, feed_right = take(3)
    gain_in, gain_sum, gain_line = take(3)
    factor_bufs = take(4)
    load_sem, swap_s, swap_r, st_s, st_r = take(5)
    half_sems = take(3)
    sp_sems = take(3)
    lr_s, lr_r, lg_s, lg_r, lg_l = take(5)
    fd_s, fd_r, fd_l = take(3)
    gn_s, gn_r, gz_s, gz_r = take(4)

    n, w = lax.axis_index("narrow"), lax.axis_index("wide")
    me = (n, w, n // 4, lax.rem(n // 2, 2), lax.rem(n, 2))
    attn = [
        Reduce(
            me,
            factor_bufs[2 * p : 2 * p + 2],
            cols,
            xf,
            attn_bufs[k],
            (swap_s, swap_r, st_s, st_r),
            k,
        )
        for k, (p, cols, xf) in enumerate(items)
    ]
    ffn = [
        Half(me, stays[k], comes[k], k % 2 == 0, ffn_bufs[k], half_sems, k) for k in range(4)
    ]
    cut, eighth = stays[2].shape[1], stays[2].shape[2]

    def down_region(k):
        return lambda block: down_full.at[
            pl.ds(k * cut, cut), pl.ds(pl.multiple_of(block * eighth, eighth), eighth)
        ]

    regions = (
        lambda block: gate_full.at[block],
        lambda block: up_full.at[block],
        down_region(0),
        down_region(1),
    )
    spread = [Spread(ffn[k], regions[k], sp_sems, k) for k in range(4)]
    for item in ffn:
        for cp in item.loads():
            cp.start()
    factor_loads = [
        pltpu.make_async_copy(src, dst, load_sem.at[k])
        for k, (src, dst) in enumerate(zip(factors, factor_bufs))
    ]
    for cp in factor_loads:
        cp.start()
    feed_load = pltpu.make_async_copy(feed_terms, feed_v, fd_l)
    feed_load.start()

    barrier = pltpu.get_barrier_semaphore()
    narrow_peers = [lax.rem(n + i, 8) for i in range(1, 8)]
    wide_peers = [lax.rem(w + i, 4) for i in range(1, 4)]
    for peer in narrow_peers:
        pl.semaphore_signal(
            barrier, inc=1, device_id=at(peer, w), device_id_type=pl.DeviceIdType.MESH
        )
    for peer in wide_peers:
        pl.semaphore_signal(
            barrier, inc=1, device_id=at(n, peer), device_id_type=pl.DeviceIdType.MESH
        )
    pl.semaphore_wait(barrier, 10)

    feed_load.wait()
    feed = LineScatter(n, w, feed_v, (feed_left, feed_right), fd_s, fd_r, 4)
    for i in range(4):
        feed.begin(i)

    def gain_narrow(i):
        peer = narrow_peers[i]
        return send(gain_parts.at[peer], gain_in.at[i], gn_s.at[i], gn_r.at[i], peer, w)

    def gain_wide(i):
        return send(gain_sum, gain_line.at[i], gz_s.at[i], gz_r.at[i], n, wide_peers[i])

    for i in range(7):
        gain_narrow(i).start()

    for item in ffn:
        item.after_one()
    for cp in factor_loads:
        cp.wait()
    for item in attn:
        item.before_swap()
    feed.pass_on(0)
    for item in attn:
        item.after_swap()
    feed.pass_on(1)
    feed.pass_end(0)
    for i in range(7):
        gain_narrow(i).wait()
    total = gain_parts[n]
    for i in range(7):
        total = total + gain_in[i]
    gain_sum[...] = total
    for i in range(3):
        gain_wide(i).start()
    feed.pass_on(2)
    feed.pass_end(1)
    for item in attn[:2]:
        item.after_one()
    feed.pass_on(3)
    feed.pass_end(2)
    for item in attn[2:]:
        item.after_one()
    feed.pass_end(3)
    for k in range(4):
        ffn[k].after_two()
        spread[k].start()

    scatters, gathers = [], []
    for k, item in enumerate(attn):
        left, right, own = line_bufs[k]
        scatters.append(
            LineScatter(n, w, Rows(item.result()), (left, right), lr_s.at[k], lr_r.at[k], 1)
        )
        gathers.append(LineGather(n, w, own, outs[k], lg_s.at[k], lg_r.at[k], 1))

    def keep(k):
        return pltpu.make_async_copy(line_bufs[k][2], outs[k].at[w], lg_l.at[k])

    def line_turn(k):
        scatters[k].finish(0, line_bufs[k][2])
        gathers[k].start()
        keep(k).start()

    for k in (0, 1):
        attn[k].after_two()
        scatters[k].begin(0)
    for i in range(4):
        feed.finish(i, feed_out)
    for k in (2, 3):
        attn[k].after_two()
        scatters[k].begin(0)
    for k in (0, 1, 2, 3):
        scatters[k].pass_on(0)
    for k in (0, 1, 2, 3):
        scatters[k].pass_end(0)
    for k in (0, 1, 2, 3):
        line_turn(k)
    for s in spread[:2]:
        s.relay()
    for k in (0, 1, 2, 3):
        gathers[k].near(0)
    for k in (0, 1, 2, 3):
        gathers[k].far(0)
    for s in spread[2:]:
        s.relay()
    for i in range(3):
        gain_wide(i).wait()
    gain_out[...] = (gain_sum[...] + gain_line[0]) + (gain_line[1] + gain_line[2])
    for s in spread:
        s.last()
    for s in spread:
        s.finish()
    for item in attn:
        item.swap().wait_send()
    for k in range(4):
        scatters[k].drain()
        gathers[k].finish()
        keep(k).wait()
    feed.drain()


def reduce_last(factors, stays, comes, feed_terms, gain_parts):
    rows = factors[0].shape[1] // 8
    items = []
    for p, xf in ((0, True), (0, False), (1, True), (1, False)):
        half = factors[2 * p + 1].shape[1] // 2
        items.append((p, (0 if xf else half, half), xf))
    scratch = []
    for _, (_, cols), _ in items:
        scratch += [
            pltpu.VMEM((2, 2, rows, cols), BF),
            pltpu.VMEM((2, 2, rows, cols), BF),
            pltpu.VMEM((2, 2, rows, cols), BF),
            pltpu.VMEM((2, rows, cols), BF),
            pltpu.VMEM((rows, cols), BF),
        ]
    for stay in stays:
        scratch += [
            pltpu.VMEM(stay.shape, BF),
            pltpu.VMEM(stay.shape, BF),
            pltpu.VMEM(stay.shape[1:], BF),
        ]
    outs = []
    for _, (_, cols), _ in items:
        scratch += [pltpu.VMEM((3, rows // 4, cols), BF)] * 2 + [pltpu.VMEM((rows // 4, cols), BF)]
        outs.append(jax.ShapeDtypeStruct((4, rows // 4, cols), BF))
    outs.append(jax.ShapeDtypeStruct((8,) + stays[0].shape[1:], BF))
    outs.append(jax.ShapeDtypeStruct((8,) + stays[1].shape[1:], BF))
    outs.append(jax.ShapeDtypeStruct((2 * stays[2].shape[1], 8 * stays[2].shape[2]), BF))
    outs.append(jax.ShapeDtypeStruct(feed_terms.shape[1:], F32))
    outs.append(jax.ShapeDtypeStruct(gain_parts.shape[1:], F32))
    scratch += [pltpu.VMEM(feed_terms.shape, BF)]
    scratch += [pltpu.VMEM((3,) + feed_terms.shape[1:], BF)] * 2
    scratch += [
        pltpu.VMEM((7,) + gain_parts.shape[1:], F32),
        pltpu.VMEM(gain_parts.shape[1:], F32),
        pltpu.VMEM((3,) + gain_parts.shape[1:], F32),
    ]
    scratch += [pltpu.VMEM(f.shape, BF) for f in factors]
    dma = pltpu.SemaphoreType.DMA
    scratch += [dma((4,)), dma((4,)), dma((4,)), dma((8,)), dma((8,))]
    scratch += [dma((8,)), dma((4,)), dma((4,))]
    scratch += [dma((28,)), dma((28,)), dma((4,))]
    scratch += [dma((4, 6)), dma((4, 6)), dma((4, 8)), dma((4, 4)), dma((4,))]
    scratch += [dma((24,)), dma((24,)), dma]
    scratch += [dma((7,)), dma((7,)), dma((3,)), dma((3,))]
    hbm, vmem = pl.BlockSpec(memory_space=pl.ANY), pl.BlockSpec(memory_space=pltpu.VMEM)
    out = pl.pallas_call(
        functools.partial(last_kernel, items),
        name="reduce_last",
        out_shape=tuple(outs),
        in_specs=[hbm] * 13 + [vmem],
        out_specs=[hbm] * 7 + [vmem] * 2,
        scratch_shapes=scratch,
        compiler_params=pltpu.CompilerParams(
            collective_id=4, has_side_effects=True, vmem_limit_bytes=64 * 1024 * 1024 - 65536
        ),
    )(*factors, *stays, *comes, feed_terms, gain_parts)
    qkv = jnp.concatenate([out[0].reshape(rows, -1), out[1].reshape(rows, -1)], axis=1)
    project = jnp.concatenate([out[2].reshape(rows, -1), out[3].reshape(rows, -1)], axis=1)
    width = out[4].shape[2]
    ffn = [out[4].reshape(-1, width), out[5].reshape(-1, width), out[6]]
    return qkv, project, ffn, out[7], out[8]


def per_device(
    fast,
    block_input,
    cotangent,
    query_weight,
    key_weight,
    value_weight,
    project_weight,
    prenorm_gain,
    midnorm_gain,
    gate_weight,
    up_weight,
    down_weight,
    doc_lengths,
    tile_counts,
):
    tokens_here, model = block_input.shape
    group = HEADS // KV_HEADS
    scale = HEAD_DIM ** (-0.5)
    q_cols, k_cols = HEADS * HEAD_DIM, KV_HEADS * HEAD_DIM
    inputs_f = block_input.astype(jnp.float32)
    ends = jnp.cumsum(doc_lengths[0])
    position = jnp.arange(tokens_here, dtype=jnp.int32)
    segment = jnp.sum((position[:, None] >= ends[None, :]).astype(jnp.int32), axis=1)
    allowed = (segment[:, None] == segment[None, :]) & (position[None, :] <= position[:, None])
    if fast:
        gains = jnp.stack([prenorm_gain, midnorm_gain]).astype(F32).reshape(1, -1)
        bias = jnp.where(allowed, 0.0, -1e30).astype(F32)
        qkv_full, project_full, grad_rows, normed, qkv, attended, gains_full, logs = gather_first(
            block_input,
            query_weight,
            key_weight,
            value_weight,
            project_weight,
            gains,
            cotangent,
            bias,
        )
        gains_full = gains_full.reshape(8, 2, -1)
        first_gain = gains_full[:, 0].reshape(-1)
        second_gain = gains_full[:, 1].reshape(-1)
    else:
        qkv_full = jnp.concatenate(
            [
                lax.all_gather(query_weight, "narrow", axis=0, tiled=True),
                lax.all_gather(key_weight, "narrow", axis=0, tiled=True),
                lax.all_gather(value_weight, "narrow", axis=0, tiled=True),
            ],
            axis=1,
        )
        project_full = lax.all_gather(project_weight, "narrow", axis=1, tiled=True)
        first_gain = lax.all_gather(prenorm_gain, "narrow", axis=0, tiled=True).astype(F32)
        second_gain = lax.all_gather(midnorm_gain, "narrow", axis=0, tiled=True).astype(F32)
        grad_rows = lax.all_gather(cotangent, "wide", axis=0, tiled=True)
        normed = rms_scale(inputs_f, first_gain).astype(jnp.bfloat16)
        qkv = jnp.dot(normed, qkv_full, preferred_element_type=jnp.float32).astype(jnp.bfloat16)
    if not fast:
        query_rows = qkv[:, :q_cols].reshape(tokens_here, KV_HEADS, group, HEAD_DIM)
        key_rows = qkv[:, q_cols : q_cols + k_cols].reshape(tokens_here, KV_HEADS, HEAD_DIM)
        value_rows = qkv[:, q_cols + k_cols :].reshape(tokens_here, KV_HEADS, HEAD_DIM)
        scores = (
            jnp.einsum("qcgd,kcd->cgqk", query_rows, key_rows, preferred_element_type=jnp.float32)
            * scale
        )
        masked = jnp.where(allowed, scores, -1e30)
        peak = jnp.max(masked, axis=-1, keepdims=True)
        expo = jnp.exp(masked - peak)
        total = jnp.sum(expo, axis=-1, keepdims=True)
        probs_low = (expo / total).astype(jnp.bfloat16)
        logsum = peak + jnp.log(total)
        attended = (
            jnp.einsum("cgqk,kcd->qcgd", probs_low, value_rows, preferred_element_type=jnp.float32)
            .astype(jnp.bfloat16)
            .reshape(tokens_here, HEADS * HEAD_DIM)
        )
    branch = jnp.dot(attended, project_full, preferred_element_type=jnp.float32)
    middle = inputs_f + branch
    mixed_in = rms_scale(middle, second_gain).astype(jnp.bfloat16)
    width = gate_weight.shape[1]
    wide_index = lax.axis_index("wide")
    my_count = jnp.sum(
        jnp.where(jnp.arange(tile_counts.shape[0], dtype=jnp.int32) == wide_index, tile_counts, 0)
    )
    live = (jnp.arange(width, dtype=jnp.int32) // TILE < my_count).astype(jnp.float32)
    if fast:
        mixed_back, feed_terms, *pieces = feed_forward(
            mixed_in, grad_rows, gate_weight, up_weight, down_weight, live.reshape(1, -1)
        )
        stays = pieces[1::2]
        comes = [
            lax.ppermute(piece, "narrow", [(i, i ^ bit) for i in range(8)])
            for piece, bit in zip(pieces[0::2], (2, 4, 2, 4))
        ]
    else:
        gathered = lax.all_gather(mixed_in, "wide", axis=0, tiled=True)
        gate_pre = jnp.dot(gathered, gate_weight, preferred_element_type=jnp.float32)
        up_pre = jnp.dot(gathered, up_weight, preferred_element_type=jnp.float32)
        hidden_back = contract_cols(grad_rows, down_weight)
        sigma = jax.nn.sigmoid(gate_pre)
        hidden = (gate_pre * sigma * up_pre * live).astype(BF)
        gate_back = (
            hidden_back * up_pre * live * sigma * (1.0 + gate_pre * (1.0 - sigma))
        ).astype(BF)
        up_back = (hidden_back * gate_pre * sigma * live).astype(BF)
        mixed_terms = (
            contract_cols(gate_back, gate_weight) + contract_cols(up_back, up_weight)
        ).astype(BF)
        mixed_back = lax.psum_scatter(
            mixed_terms, "wide", scatter_dimension=0, tiled=True
        ).astype(F32)
        partial_rows = jnp.dot(hidden, down_weight, preferred_element_type=jnp.float32)
        down_part = contract_rows(hidden, grad_rows)
        gate_part = contract_rows(gathered, gate_back)
        up_part = contract_rows(gathered, up_back)
    out_grad = cotangent.astype(jnp.float32)
    unused_second, second_backward = jax.vjp(rms_scale, middle, second_gain)
    middle_norm_back, second_gain_part = second_backward(mixed_back)
    middle_back = out_grad + middle_norm_back
    branch_back = middle_back.astype(jnp.bfloat16)
    attended_back = contract_cols(branch_back, project_full).astype(jnp.bfloat16)
    if fast:
        qkv_back = attention_back(qkv, attended_back, logs, bias)
    else:
        attended_back = attended_back.reshape(tokens_here, KV_HEADS, group, HEAD_DIM)
        scores_again = (
            jnp.einsum("qcgd,kcd->cgqk", query_rows, key_rows, preferred_element_type=jnp.float32)
            * scale
        )
        probs_again = jnp.where(allowed, jnp.exp(scores_again - logsum), 0.0)
        probs_again_low = probs_again.astype(jnp.bfloat16)
        value_back = (
            jnp.einsum(
                "cgqk,qcgd->kcd", probs_again_low, attended_back, preferred_element_type=jnp.float32
            )
            .astype(jnp.bfloat16)
            .reshape(tokens_here, KV_HEADS * HEAD_DIM)
        )
        probs_back = jnp.einsum(
            "qcgd,kcd->cgqk", attended_back, value_rows, preferred_element_type=jnp.float32
        )
        scores_back = (
            probs_again * (probs_back - jnp.sum(probs_again * probs_back, axis=-1, keepdims=True))
        ).astype(jnp.bfloat16)
        query_back = (
            (
                jnp.einsum("cgqk,kcd->qcgd", scores_back, key_rows, preferred_element_type=jnp.float32)
                * scale
            )
            .astype(jnp.bfloat16)
            .reshape(tokens_here, HEADS * HEAD_DIM)
        )
        key_back = (
            (
                jnp.einsum(
                    "cgqk,qcgd->kcd", scores_back, query_rows, preferred_element_type=jnp.float32
                )
                * scale
            )
            .astype(jnp.bfloat16)
            .reshape(tokens_here, KV_HEADS * HEAD_DIM)
        )
        qkv_back = jnp.concatenate([query_back, key_back, value_back], axis=1)
    normed_back = contract_cols(qkv_back, qkv_full)
    unused_first, first_backward = jax.vjp(rms_scale, inputs_f, first_gain)
    input_norm_back, first_gain_part = first_backward(normed_back)
    input_grad = (middle_back + input_norm_back).astype(jnp.bfloat16)

    if fast:
        gain_parts = jnp.stack(
            [first_gain_part.reshape(8, -1), second_gain_part.reshape(8, -1)], axis=1
        ).reshape(8, 1, -1)
        input_grad, qkv_back = lax.optimization_barrier((input_grad, qkv_back))
        qkv_total, project_total, ffn_totals, feed, gain_total = reduce_last(
            (normed, qkv_back, branch_back, attended),
            stays,
            comes,
            feed_terms,
            gain_parts,
        )
        gain_total = gain_total.reshape(2, -1)
        first_total, second_total = gain_total[0], gain_total[1]
        qkv_total = qkv_total.astype(F32)
        project_total = project_total.T.astype(F32)
        gate_total, up_total, down_total = [t.astype(F32) for t in ffn_totals]
    else:

        def owned(part):
            share = lax.psum_scatter(part.astype(BF), "narrow", scatter_dimension=0, tiled=True)
            return lax.psum(share, "wide").astype(F32)

        qkv_total = owned(contract_rows(normed, qkv_back))
        project_total = owned(contract_rows(branch_back, attended)).T
        first_total = owned(first_gain_part)
        second_total = owned(second_gain_part)
        gate_total, up_total, down_total = (
            lax.psum(gate_part.astype(BF), "narrow").astype(F32),
            lax.psum(up_part.astype(BF), "narrow").astype(F32),
            lax.psum(down_part.astype(BF), "narrow").astype(F32),
        )
        feed = lax.psum_scatter(
            partial_rows.astype(BF), "wide", scatter_dimension=0, tiled=True
        ).astype(F32)
    block_output = (middle + feed).astype(BF)
    return (
        block_output,
        input_grad,
        qkv_total[:, :q_cols],
        qkv_total[:, q_cols : q_cols + k_cols],
        qkv_total[:, q_cols + k_cols :],
        project_total,
        first_total,
        second_total,
        gate_total,
        up_total,
        down_total,
    )


def solution(mesh):
    fast = mesh.shape["narrow"] == 8 and mesh.shape["wide"] == 4
    placed = (
        P(("narrow", "wide"), None),
        P(("narrow", "wide"), None),
        P("narrow", None),
        P("narrow", None),
        P("narrow", None),
        P(None, "narrow"),
        P("narrow"),
        P("narrow"),
        P(None, "wide"),
        P(None, "wide"),
        P("wide", None),
        P(("narrow", "wide"), None),
        P(),
    )
    return jax.shard_map(
        functools.partial(per_device, fast),
        mesh=mesh,
        in_specs=placed,
        out_specs=(
            P(("narrow", "wide"), None),
            P(("narrow", "wide"), None),
            P("narrow", None),
            P("narrow", None),
            P("narrow", None),
            P(None, "narrow"),
            P("narrow"),
            P("narrow"),
            P(None, "wide"),
            P(None, "wide"),
            P("wide", None),
        ),
        check_vma=False,
    )
```

```python
import functools

import jax
import jax.numpy as jnp
from jax import lax
from jax.experimental import pallas as pl
from jax.experimental.pallas import tpu as pltpu
from jax.sharding import PartitionSpec as P

HEADS = 24
KV_HEADS = 6
HEAD_DIM = 64
TILE = 128


EPSILON = 1e-06

BF = jnp.bfloat16
F32 = jnp.float32


def rms_scale(rows, gain):
    factor = lax.rsqrt(jnp.mean(rows * rows, axis=-1, keepdims=True) + EPSILON)
    return rows * factor * gain


def contract_rows(left, right):
    return lax.dot_general(
        left, right, (((0,), (0,)), ((), ())), preferred_element_type=jnp.float32
    )


def contract_cols(left, right):
    return lax.dot_general(
        left, right, (((1,), (1,)), ((), ())), preferred_element_type=jnp.float32
    )


def flip(n, bit):
    return n + bit - 2 * bit * lax.rem(n // bit, 2)


def at(n, w):
    return {"narrow": n, "wide": w}


def send(src, dst, ssem, rsem, n, w):
    return pltpu.make_async_remote_copy(
        src_ref=src,
        dst_ref=dst,
        send_sem=ssem,
        recv_sem=rsem,
        device_id=at(n, w),
        device_id_type=pl.DeviceIdType.MESH,
    )


def greet(narrow_peers, n, w, line):
    barrier = pltpu.get_barrier_semaphore()
    for peer in narrow_peers:
        pl.semaphore_signal(
            barrier, inc=1, device_id=at(peer, w), device_id_type=pl.DeviceIdType.MESH
        )
    if not line:
        pl.semaphore_wait(barrier, len(narrow_peers))
    if line:

        @pl.when(w > 0)
        def _():
            pl.semaphore_signal(
                barrier, inc=1, device_id=at(n, w - 1), device_id_type=pl.DeviceIdType.MESH
            )

        @pl.when(w < 3)
        def _():
            pl.semaphore_signal(
                barrier, inc=1, device_id=at(n, w + 1), device_id_type=pl.DeviceIdType.MESH
            )

        @pl.when((w == 0) | (w == 3))
        def _():
            pl.semaphore_wait(barrier, len(narrow_peers) + 1)

        @pl.when((w == 1) | (w == 2))
        def _():
            pl.semaphore_wait(barrier, len(narrow_peers) + 2)


class LineGather:
    def __init__(self, n, w, own, whole, ssem, rsem, chunks):
        self.n, self.w, self.own, self.whole = n, w, own, whole
        self.ssem, self.rsem, self.chunks = ssem, rsem, chunks
        self.rows = own.shape[0] // chunks

    def span(self, i):
        return pl.ds(pl.multiple_of(i * self.rows, self.rows), self.rows)

    def part(self, shard, i):
        return self.whole.at[shard, self.span(i), :]

    def put(self, way, here, shard, i):
        src = self.own.at[self.span(i), :] if shard is here else self.part(shard, i)
        to = here + 1 - 2 * way
        s = (way * 4 + shard) * self.chunks + i
        r = shard * self.chunks + i
        return send(src, self.part(shard, i), self.ssem.at[s], self.rsem.at[r], self.n, to)

    def came(self, shard, i):
        self.put(0, 0, shard, i).wait_recv()

    def start_chunk(self, i):
        @pl.when(self.w < 3)
        def _():
            self.put(0, self.w, self.w, i).start()

        @pl.when(self.w > 0)
        def _():
            self.put(1, self.w, self.w, i).start()

    def start(self):
        for i in range(self.chunks):
            self.start_chunk(i)

    def near(self, i):
        @pl.when(self.w == 1)
        def _():
            self.came(0, i)
            self.put(0, 1, 0, i).start()
            self.came(2, i)
            self.put(1, 1, 2, i).start()

        @pl.when(self.w == 2)
        def _():
            self.came(3, i)
            self.put(1, 2, 3, i).start()
            self.came(1, i)
            self.put(0, 2, 1, i).start()

    def far(self, i):
        @pl.when(self.w == 1)
        def _():
            self.came(3, i)
            self.put(1, 1, 3, i).start()

        @pl.when(self.w == 2)
        def _():
            self.came(0, i)
            self.put(0, 2, 0, i).start()

    def ready(self, i):
        @pl.when(self.w == 0)
        def _():
            for shard in (1, 2, 3):
                self.came(shard, i)

        @pl.when(self.w == 3)
        def _():
            for shard in (2, 1, 0):
                self.came(shard, i)

    def finish_sends(self):
        for here in range(4):

            @pl.when(self.w == here)
            def _():
                for i in range(self.chunks):
                    if here < 3:
                        for shard in range(here + 1):
                            self.put(0, here, shard, i).wait_send()
                    if here > 0:
                        for shard in range(here, 4):
                            self.put(1, here, shard, i).wait_send()

    def finish(self):
        for i in range(self.chunks):
            self.ready(i)
        self.finish_sends()


def first_kernel(
    x_ref,
    q_ref,
    k_ref,
    v_ref,
    p_ref,
    g_ref,
    c_ref,
    bias_ref,
    qkv_out,
    p_full,
    c_full,
    normed_out,
    rows_out,
    att_out,
    g_full,
    log_out,
    qkv_full,
    p_buf,
    c_buf,
    x_buf,
    gain_row,
    normed,
    qkv,
    att,
    in_sem,
    out_sem,
    ssem,
    rsem,
    gs_sem,
    gr_sem,
    zs_sem,
    zr_sem,
):
    n, w = lax.axis_index("narrow"), lax.axis_index("wide")
    x, y, c, d = flip(n, 2), flip(n, 4), flip(n, 1), flip(flip(n, 2), 4)
    others = [lax.rem(n + i, 8) for i in range(1, 8)]
    rows = q_ref.shape[0]
    half = rows // 2
    depth = p_ref.shape[0]
    qc, kc = q_ref.shape[1], k_ref.shape[1]
    cols = ((0, qc), (qc, kc), (qc + kc, kc))

    def region(t, block, h):
        if t == 3:
            r = pl.ds(0, depth) if h == 2 else pl.ds(h * (depth // 2), depth // 2)
            return p_full.at[r, pl.ds(pl.multiple_of(block * rows, rows), rows)]
        start = pl.multiple_of(block * rows, rows)
        r = pl.ds(start, rows) if h == 2 else pl.ds(start + h * half, half)
        return qkv_full.at[r, pl.ds(cols[t][0], cols[t][1])]

    locals_in = []
    for i, (src, dst) in enumerate(
        (
            (g_ref, g_full.at[n]),
            (x_ref, x_buf),
            (p_ref, p_buf),
            (c_ref, c_buf),
            (q_ref, region(0, n, 2)),
            (k_ref, region(1, n, 2)),
            (v_ref, region(2, n, 2)),
        )
    ):
        cp = pltpu.make_async_copy(src, dst, in_sem.at[i])
        cp.start()
        locals_in.append(cp)

    greet(others, n, w, True)

    def own(t, h):
        ref = (q_ref, k_ref, v_ref, p_ref)[t]
        if h == 2:
            return ref
        size = ref.shape[0] // 2
        return ref.at[pl.ds(h * size, size), :]

    def msg(t, kind, src, block, h, peer):
        k = t * 10 + kind
        return send(src, region(t, block, h), ssem.at[k], rsem.at[k], peer, w)

    def to_x(t, h):
        return msg(t, h, own(t, h), n, h, x)

    def to_y(t, h):
        return msg(t, 2 + h, own(t, h), n, h, y)

    def on_x(t):
        return msg(t, 4, region(t, y, 0), y, 0, x)

    def on_y(t):
        return msg(t, 5, region(t, x, 1), x, 1, y)

    def to_c(t, which):
        block = (n, x, y, d)[which]
        src = own(t, 2) if which == 0 else region(t, block, 2)
        return msg(t, 6 + which, src, block, 2, c)

    def start_own(t):
        to_x(t, 1).start()
        to_y(t, 0).start()
        to_x(t, 0).start()
        to_y(t, 1).start()

    def gain(i):
        return send(g_ref, g_full.at[n], gs_sem.at[i], gr_sem.at[i], others[i], w)

    line = LineGather(n, w, c_ref, c_full, zs_sem, zr_sem, 4)
    for i in range(7):
        gain(i).start()
    start_own(0)
    line.start()
    for t in (1, 2):
        start_own(t)
    for t in range(3):
        to_c(t, 0).start()

    locals_out = []

    def put(src, dst):
        cp = pltpu.make_async_copy(src, dst, out_sem.at[len(locals_out)])
        cp.start()
        locals_out.append(cp)

    for i in range(7):
        gain(i).wait()
    for cp in locals_in:
        cp.wait()
    put(p_buf, region(3, n, 2))
    put(c_buf, c_full.at[w])
    for k in range(8):
        gain_row[:, pl.ds(k * rows, rows)] = g_full[k, :, :rows]
    strip = 16

    @pl.loop(0, x_buf.shape[0] // strip)
    def _(i):
        s = pl.ds(pl.multiple_of(i * strip, strip), strip)
        normed[s, :] = rms_scale(x_buf[s, :].astype(F32), gain_row[...]).astype(BF)

    put(normed, normed_out)

    def relay(t):
        to_y(t, 0).wait_recv()
        on_x(t).start()
        to_x(t, 1).wait_recv()
        on_y(t).start()
        to_x(t, 0).wait_recv()
        to_c(t, 1).start()
        to_y(t, 1).wait_recv()
        to_c(t, 2).start()

    def corner(t):
        on_x(t).wait_recv()
        on_y(t).wait_recv()
        to_c(t, 3).start()

    line.near(0)
    relay(0)
    line.near(1)
    relay(1)
    line.near(2)
    relay(2)
    start_own(3)
    to_c(3, 0).start()
    line.near(3)
    line.far(0)
    line.far(1)
    for t in range(3):
        corner(t)
    line.far(2)
    for t in range(3):
        for which in range(4):
            to_c(t, which).wait_recv()
    put(qkv_full, qkv_out)
    tile = 256

    @pl.loop(0, qkv.shape[1] // tile)
    def _(i):
        s = pl.ds(pl.multiple_of(i * tile, tile), tile)
        qkv[:, s] = jnp.dot(normed[...], qkv_full[:, s], preferred_element_type=F32).astype(BF)

    put(qkv, rows_out)
    line.far(3)

    log_out[...] = jnp.zeros(log_out.shape, F32)
    pair = 2 * HEAD_DIM
    group = HEADS // KV_HEADS

    @pl.loop(0, KV_HEADS // 2)
    def _(i):
        keys = qkv[:, pl.ds(pl.multiple_of(qc + i * pair, pair), pair)]
        values = qkv[:, pl.ds(pl.multiple_of(qc + kc + i * pair, pair), pair)]
        lane = lax.broadcasted_iota(jnp.int32, log_out.shape, 1)
        for b in range(group):
            at_cols = pl.ds(pl.multiple_of((i * group + b) * pair, pair), pair)
            queries = qkv[:, at_cols]
            side = (2 * b) // group
            key = keys[:, side * HEAD_DIM : (side + 1) * HEAD_DIM]
            value = values[:, side * HEAD_DIM : (side + 1) * HEAD_DIM]
            heads = []
            for e in range(2):
                query = queries[:, e * HEAD_DIM : (e + 1) * HEAD_DIM]
                masked = contract_cols(query, key) * (HEAD_DIM**-0.5) + bias_ref[...]
                peak = jnp.max(masked, axis=-1, keepdims=True)
                expo = jnp.exp(masked - peak)
                total = jnp.sum(expo, axis=-1, keepdims=True)
                probs = (expo * (1.0 / total)).astype(BF)
                heads.append(jnp.dot(probs, value, preferred_element_type=F32))
                log_out[...] = jnp.where(
                    lane == 2 * (i * group + b) + e, peak + jnp.log(total), log_out[...]
                )
            att[:, at_cols] = jnp.concatenate(heads, axis=1).astype(BF)

    put(att, att_out)
    relay(3)
    corner(3)
    for t in range(4):
        for h in range(2):
            to_x(t, h).wait_send()
            to_y(t, h).wait_send()
        on_x(t).wait_send()
        on_y(t).wait_send()
        for which in range(4):
            if t == 3:
                to_c(t, which).wait_recv()
            to_c(t, which).wait_send()
    line.finish()
    for cp in locals_out:
        cp.wait()


def gather_first(rows_in, query, key, value, project, gains, cotangent, bias):
    rows = query.shape[0]
    width = query.shape[1] + 2 * key.shape[1]
    tokens_here, model = rows_in.shape
    hbm, vmem = pl.BlockSpec(memory_space=pl.ANY), pl.BlockSpec(memory_space=pltpu.VMEM)
    return pl.pallas_call(
        first_kernel,
        name="gather_first",
        out_shape=(
            jax.ShapeDtypeStruct((8 * rows, width), BF),
            jax.ShapeDtypeStruct((project.shape[0], 8 * rows), BF),
            jax.ShapeDtypeStruct((4,) + cotangent.shape, BF),
            jax.ShapeDtypeStruct((tokens_here, model), BF),
            jax.ShapeDtypeStruct((tokens_here, width), BF),
            jax.ShapeDtypeStruct((tokens_here, query.shape[1]), BF),
            jax.ShapeDtypeStruct((8,) + gains.shape, gains.dtype),
            jax.ShapeDtypeStruct((tokens_here, 128), F32),
        ),
        in_specs=[hbm] * 7 + [vmem],
        out_specs=[hbm] * 6 + [vmem] * 2,
        scratch_shapes=[
            pltpu.VMEM((8 * rows, width), BF),
            pltpu.VMEM(project.shape, BF),
            pltpu.VMEM(cotangent.shape, BF),
            pltpu.VMEM((tokens_here, model), BF),
            pltpu.VMEM((1, model), F32),
            pltpu.VMEM((tokens_here, model), BF),
            pltpu.VMEM((tokens_here, width), BF),
            pltpu.VMEM((tokens_here, query.shape[1]), BF),
            pltpu.SemaphoreType.DMA((7,)),
            pltpu.SemaphoreType.DMA((6,)),
            pltpu.SemaphoreType.DMA((40,)),
            pltpu.SemaphoreType.DMA((40,)),
            pltpu.SemaphoreType.DMA((7,)),
            pltpu.SemaphoreType.DMA((7,)),
            pltpu.SemaphoreType.DMA((32,)),
            pltpu.SemaphoreType.DMA((16,)),
        ],
        compiler_params=pltpu.CompilerParams(collective_id=1, has_side_effects=True),
    )(rows_in, query, key, value, project, gains, cotangent, bias)


def attention_back_kernel(qkv, back, logs, bias, out):
    q_cols, k_cols = HEADS * HEAD_DIM, KV_HEADS * HEAD_DIM
    pair = 2 * HEAD_DIM
    group = HEADS // KV_HEADS
    scale = HEAD_DIM**-0.5

    @pl.loop(0, KV_HEADS // 2)
    def _(i):
        key_at = pl.ds(pl.multiple_of(q_cols + i * pair, pair), pair)
        value_at = pl.ds(pl.multiple_of(q_cols + k_cols + i * pair, pair), pair)
        keys, values = qkv[:, key_at], qkv[:, value_at]
        lane = lax.broadcasted_iota(jnp.int32, logs.shape, 1)
        key_backs, value_backs = [], []
        for side in range(2):
            key = keys[:, side * HEAD_DIM : (side + 1) * HEAD_DIM]
            value = values[:, side * HEAD_DIM : (side + 1) * HEAD_DIM]
            key_back = jnp.zeros(key.shape, F32)
            value_back = jnp.zeros(key.shape, F32)
            for b in range(side * group // 2, (side + 1) * group // 2):
                at_cols = pl.ds(pl.multiple_of((i * group + b) * pair, pair), pair)
                queries, backs = qkv[:, at_cols], back[:, at_cols]
                heads = []
                for e in range(2):
                    query = queries[:, e * HEAD_DIM : (e + 1) * HEAD_DIM]
                    given = backs[:, e * HEAD_DIM : (e + 1) * HEAD_DIM]
                    logsum = jnp.sum(
                        jnp.where(lane == 2 * (i * group + b) + e, logs[...], 0.0),
                        axis=-1,
                        keepdims=True,
                    )
                    probs = jnp.exp(contract_cols(query, key) * scale + bias[...] - logsum)
                    value_back = value_back + contract_rows(probs.astype(BF), given)
                    probs_back = contract_cols(given, value)
                    inner = jnp.sum(probs * probs_back, axis=-1, keepdims=True)
                    scores_back = (probs * (probs_back - inner)).astype(BF)
                    heads.append(jnp.dot(scores_back, key, preferred_element_type=F32) * scale)
                    key_back = key_back + contract_rows(scores_back, query)
                out[:, at_cols] = jnp.concatenate(heads, axis=1).astype(BF)
            key_backs.append(key_back * scale)
            value_backs.append(value_back)
        out[:, key_at] = jnp.concatenate(key_backs, axis=1).astype(BF)
        out[:, value_at] = jnp.concatenate(value_backs, axis=1).astype(BF)


def attention_back(qkv, back, logs, bias):
    vmem = pl.BlockSpec(memory_space=pltpu.VMEM)
    heads = HEADS * qkv.shape[0] * qkv.shape[0]
    return pl.pallas_call(
        attention_back_kernel,
        name="attention_back",
        out_shape=jax.ShapeDtypeStruct(qkv.shape, BF),
        in_specs=[vmem] * 4,
        out_specs=vmem,
        cost_estimate=pl.CostEstimate(
            flops=10 * heads * HEAD_DIM, bytes_accessed=8 * qkv.size, transcendentals=heads
        ),
    )(qkv, back, logs, bias)


class LineScatter:
    def __init__(self, n, w, terms, bufs, ssem, rsem, chunks):
        self.n, self.w, self.terms, self.bufs = n, w, terms, bufs
        self.ssem, self.rsem, self.chunks = ssem, rsem, chunks
        self.rows = terms.shape[1] // chunks

    def span(self, i):
        return pl.ds(pl.multiple_of(i * self.rows, self.rows), self.rows)

    def term(self, d, i):
        return self.terms.at[d, self.span(i), :]

    def slot(self, way, slot, i):
        return self.bufs[way].at[slot, self.span(i), :]

    def put(self, way, here, d, i, src):
        slot = d - here - 1 if way == 0 else here - 1 - d
        k = (way * 3 + slot) * self.chunks + i
        to = here + 1 - 2 * way
        return send(src, self.slot(way, slot, i), self.ssem.at[k], self.rsem.at[k], self.n, to)

    def came(self, way, slot, i):
        k = (way * 3 + slot) * self.chunks + i
        ref = self.slot(way, slot, i)
        send(ref, ref, self.ssem.at[k], self.rsem.at[k], self.n, 1).wait_recv()

    def begin(self, i):
        for here, way in ((0, 0), (3, 1)):

            @pl.when(self.w == here)
            def _():
                for d in (3, 2, 1) if way == 0 else (0, 1, 2):
                    self.put(way, here, d, i, self.term(d, i)).start()

    def join(self, way, here, d, i):
        slot = d - here if way == 0 else here - d
        self.came(way, slot, i)
        mine, sum_ = self.term(d, i), self.slot(way, slot, i)
        sum_[...] = (mine[...].astype(F32) + sum_[...].astype(F32)).astype(BF)
        self.put(way, here, d, i, sum_).start()

    def pass_on(self, i):
        @pl.when(self.w == 1)
        def _():
            self.join(0, 1, 3, i)
            self.join(0, 1, 2, i)

        @pl.when(self.w == 2)
        def _():
            self.join(1, 2, 0, i)
            self.join(1, 2, 1, i)

    def pass_end(self, i):
        @pl.when(self.w == 1)
        def _():
            self.join(1, 1, 0, i)

        @pl.when(self.w == 2)
        def _():
            self.join(0, 2, 3, i)

    def finish(self, i, out):
        for here, ways in ((0, (1,)), (1, (0, 1)), (2, (0, 1)), (3, (0,))):

            @pl.when(self.w == here)
            def _():
                for way in ways:
                    self.came(way, 0, i)
                total = self.term(here, i)[...].astype(F32)
                for way in ways:
                    total = total + self.slot(way, 0, i)[...].astype(F32)
                out[self.span(i), :] = total.astype(out.dtype)

    def drain(self):
        sent = {
            0: ((0, 3), (0, 2), (0, 1)),
            1: ((0, 3), (0, 2), (1, 0)),
            2: ((1, 0), (1, 1), (0, 3)),
            3: ((1, 0), (1, 1), (1, 2)),
        }
        for here in range(4):

            @pl.when(self.w == here)
            def _():
                for i in range(self.chunks):
                    for way, d in sent[here]:
                        self.put(way, here, d, i, self.term(d, i)).wait_send()


def middle_kernel(
    mixed,
    cot,
    wg,
    wu,
    wd,
    live,
    back_out,
    partial_out,
    gate_go,
    gate_stay,
    up_go,
    up_stay,
    low_go,
    low_stay,
    high_go,
    high_stay,
    x_all,
    cot_v,
    wg_v,
    wu_v,
    wd_v,
    gate_f,
    up_f,
    back_f,
    hid,
    gb,
    ub,
    terms,
    from_left,
    from_right,
    part_buf,
    gate_k,
    up_k,
    down_k,
    in_sem,
    ag_s,
    ag_r,
    rs_s,
    rs_r,
    part_sem,
    sw_s,
    sw_r,
    out_sem,
    st_s,
    st_r,
    ready,
    ready_x,
    ready_y,
):
    n, w = lax.axis_index("narrow"), lax.axis_index("wide")
    y, x, core = n // 4, lax.rem(n // 2, 2), lax.rem(n, 2)
    mate, peer_x, peer_y = flip(n, 1), flip(n, 2), flip(n, 4)
    chunks = 4
    rows = mixed.shape[0] // chunks
    tokens, model = 4 * mixed.shape[0], mixed.shape[1]
    width = wg.shape[1]
    batch, block = 4 * rows, 512
    loads = [
        pltpu.make_async_copy(src, dst, in_sem.at[k])
        for k, (src, dst) in enumerate(
            ((mixed, x_all.at[w]), (wg, wg_v), (wu, wu_v), (cot, cot_v), (wd, wd_v))
        )
    ]
    for cp in loads:
        cp.start()
    greet([mate, peer_x, peer_y], n, w, True)

    gather = LineGather(n, w, mixed, x_all, ag_s, ag_r, chunks)
    scatter = LineScatter(n, w, terms, (from_left, from_right), rs_s, rs_r, chunks)
    gather.start_chunk(0)
    gather.start_chunk(1)
    gather.near(0)
    gather.far(0)
    for cp in loads:
        cp.wait()

    def rows_of(ref, i):
        r = pl.ds(pl.multiple_of(i * rows, rows), rows)
        return ref[:, r, :].reshape(batch, ref.shape[2])

    def store(i):
        return pltpu.make_async_copy(
            part_buf.at[lax.rem(i, 2)],
            partial_out.at[:, pl.ds(pl.multiple_of(i * rows, rows), rows), :],
            part_sem.at[lax.rem(i, 2)],
        )

    @pl.loop(0, chunks)
    def _(i):
        r = pl.ds(pl.multiple_of(i * rows, rows), rows)
        gather.ready(i)
        xs = rows_of(x_all, i)
        gate_f[...] = jnp.dot(xs, wg_v[...], preferred_element_type=F32)
        up_f[...] = jnp.dot(xs, wu_v[...], preferred_element_type=F32)

        @pl.when(i < chunks - 1)
        def _():
            gather.near(i + 1)

        @pl.when(i < chunks - 2)
        def _():
            gather.start_chunk(i + 2)

        back_f[...] = contract_cols(rows_of(cot_v, i), wd_v[...])
        step = 16

        @pl.loop(0, batch // step)
        def _(t):
            s = pl.ds(pl.multiple_of(t * step, step), step)
            d = t // (rows // step)
            into = pl.ds(
                pl.multiple_of(i * rows + lax.rem(t, rows // step) * step, step), step
            )
            gate, up = gate_f[s, :], up_f[s, :] * live[...]
            sigma = jax.nn.sigmoid(gate)
            silu = gate * sigma
            hid[d, into, :] = (silu * up).astype(BF)
            back = back_f[s, :]
            gb[d, into, :] = (back * up * sigma * (1.0 + gate * (1.0 - sigma))).astype(BF)
            ub[d, into, :] = (back * silu * live[...]).astype(BF)

        @pl.when(i > 0)
        def _():
            scatter.pass_on(i - 1)

        @pl.when(i < chunks - 1)
        def _():
            gather.far(i + 1)

        @pl.loop(0, model // block)
        def _(j):
            b = pl.ds(pl.multiple_of(j * block, block), block)
            terms[:, r, b] = (
                (
                    contract_cols(rows_of(gb, i), wg_v[b, :])
                    + contract_cols(rows_of(ub, i), wu_v[b, :])
                )
                .astype(BF)
                .reshape(4, rows, block)
            )

        scatter.begin(i)

        @pl.when(i > 1)
        def _():
            store(i - 2).wait()

        @pl.loop(0, model // block)
        def _(j):
            b = pl.ds(pl.multiple_of(j * block, block), block)
            part_buf[lax.rem(i, 2), :, :, b] = (
                jnp.dot(rows_of(hid, i), wd_v[:, b], preferred_element_type=F32)
                .astype(BF)
                .reshape(4, rows, block)
            )

        store(i).start()

        @pl.when(i > 0)
        def _():
            scatter.pass_end(i - 1)

    pl.semaphore_signal(
        ready, inc=1, device_id=at(mate, w), device_id_type=pl.DeviceIdType.MESH
    )

    def row_grad(back, block):
        cols = pl.ds(pl.multiple_of(block * (model // 8), model // 8), model // 8)
        return contract_rows(
            x_all[:, :, cols].reshape(tokens, model // 8), back[...].reshape(tokens, width)
        )

    def col_grad(block):
        cols = pl.ds(pl.multiple_of(block * (model // 8), model // 8), model // 8)
        return contract_rows(
            hid[...].reshape(tokens, width), cot_v[:, :, cols].reshape(tokens, model // 8)
        )

    eighth, half = model // 8, model // 2

    def place(j, base):
        return pl.ds(pl.multiple_of(base + j * eighth, eighth), eighth)

    swaps = [
        send(buf.at[pl.ds(half, half), :], buf.at[pl.ds(0, half), :], sw_s.at[k], sw_r.at[k], mate, w)
        for k, buf in enumerate((wg_v, wu_v))
    ]
    swaps.append(
        send(
            wd_v.at[:, pl.ds(half, half)], wd_v.at[:, pl.ds(0, half)], sw_s.at[2], sw_r.at[2], mate, w
        )
    )

    @pl.loop(0, 4)
    def _(j):
        wg_v[place(j, half), :] = row_grad(gb, 2 * j + 1 - core).astype(BF)

    pl.semaphore_wait(ready, 1)
    swaps[0].start()

    @pl.loop(0, 4)
    def _(j):
        wu_v[place(j, half), :] = row_grad(ub, 2 * j + 1 - core).astype(BF)

    swaps[1].start()
    scatter.pass_on(chunks - 1)

    @pl.loop(0, 4)
    def _(j):
        wd_v[:, place(j, half)] = col_grad(2 * j + 1 - core).astype(BF)

    swaps[2].start()
    swaps[0].wait_recv()

    @pl.loop(0, 4)
    def _(j):
        gate_k[j // 2, lax.rem(j, 2)] = (
            row_grad(gb, 2 * j + core) + wg_v[place(j, 0), :].astype(F32)
        ).astype(BF)

    def gate_send(b, k):
        src, dst = gate_k.at[b, 1 - x], wg_v.at[place(b, 0), :]
        return send(src, dst, st_s.at[k], st_r.at[k], peer_x, w)

    def up_send(b, k):
        src, dst = up_k.at[1 - y, b], wu_v.at[place(b, 0), :]
        return send(src, dst, st_s.at[2 + k], st_r.at[2 + k], peer_y, w)

    pl.semaphore_signal(
        ready_x, inc=1, device_id=at(peer_x, w), device_id_type=pl.DeviceIdType.MESH
    )
    swaps[0].wait_send()
    pl.semaphore_wait(ready_x, 1)
    gate_send(1 - y, 0).start()
    gate_send(y, 1).start()
    swaps[1].wait_recv()

    @pl.loop(0, 4)
    def _(j):
        up_k[j // 2, lax.rem(j, 2)] = (
            row_grad(ub, 2 * j + core) + wu_v[place(j, 0), :].astype(F32)
        ).astype(BF)

    pl.semaphore_signal(
        ready_y, inc=1, device_id=at(peer_y, w), device_id_type=pl.DeviceIdType.MESH
    )
    swaps[1].wait_send()
    pl.semaphore_wait(ready_y, 1)
    up_send(1 - x, 0).start()
    up_send(x, 1).start()
    swaps[2].wait_recv()

    @pl.loop(0, 4)
    def _(j):
        down_k[j // 2, lax.rem(j, 2)] = (
            col_grad(2 * j + core) + wd_v[:, place(j, 0)].astype(F32)
        ).astype(BF)

    cut = width // 2
    pieces = (
        (gate_k.at[1 - y, x], gate_go),
        (gate_k.at[y, x], gate_stay),
        (up_k.at[y, 1 - x], up_go),
        (up_k.at[y, x], up_stay),
        (down_k.at[:, 1 - x, pl.ds(0, cut), :], low_go),
        (down_k.at[:, x, pl.ds(0, cut), :], low_stay),
        (down_k.at[1 - y, :, pl.ds(cut, cut), :], high_go),
        (down_k.at[y, :, pl.ds(cut, cut), :], high_stay),
    )
    puts = [
        pltpu.make_async_copy(src, dst, out_sem.at[k]) for k, (src, dst) in enumerate(pieces)
    ]
    for k in (4, 5, 6, 7):
        puts[k].start()
    scatter.pass_end(chunks - 1)
    for i in range(chunks):
        scatter.finish(i, back_out)
    step = 64

    def join(sums, b0, b1, came, b):
        @pl.loop(0, eighth // step)
        def _(t):
            s = pl.ds(pl.multiple_of(t * step, step), step)
            o = pl.ds(pl.multiple_of(b * eighth + t * step, step), step)
            sums[b0, b1, s, :] = sums[b0, b1, s, :] + came[o, :]

    for k, b in enumerate((1 - y, y)):
        gate_send(b, k).wait_recv()
        join(gate_k, b, x, wg_v, b)
        puts[k].start()
    for k, b in enumerate((1 - x, x)):
        up_send(b, k).wait_recv()
        join(up_k, y, b, wu_v, b)
        puts[2 + k].start()
    scatter.drain()
    gather.finish_sends()
    swaps[2].wait_send()
    for k in range(2):
        gate_send(0, k).wait_send()
        up_send(0, k).wait_send()
    store(chunks - 2).wait()
    store(chunks - 1).wait()
    for cp in puts:
        cp.wait()


def feed_forward(mixed, cot, gate_weight, up_weight, down_weight, live):
    tokens_here, model = mixed.shape
    width = gate_weight.shape[1]
    rows, eighth, cut = tokens_here // 4, model // 8, width // 2
    hbm, vmem = pl.BlockSpec(memory_space=pl.ANY), pl.BlockSpec(memory_space=pltpu.VMEM)
    row_piece = jax.ShapeDtypeStruct((eighth, width), BF)
    col_piece = jax.ShapeDtypeStruct((2, cut, eighth), BF)
    dma = pltpu.SemaphoreType.DMA
    acc = pltpu.VMEM((4 * rows, width), F32)
    act = pltpu.VMEM((4, tokens_here, width), BF)
    tok = pltpu.VMEM((4, tokens_here, model), BF)
    three = pltpu.VMEM((3, tokens_here, model), BF)
    return pl.pallas_call(
        middle_kernel,
        name="feed_forward",
        out_shape=(
            jax.ShapeDtypeStruct(mixed.shape, F32),
            jax.ShapeDtypeStruct((4,) + mixed.shape, BF),
        )
        + (row_piece,) * 4
        + (col_piece,) * 4,
        in_specs=[hbm] * 5 + [vmem],
        out_specs=[vmem] + [hbm] * 9,
        scratch_shapes=[
            tok,
            tok,
            pltpu.VMEM(gate_weight.shape, BF),
            pltpu.VMEM(up_weight.shape, BF),
            pltpu.VMEM(down_weight.shape, BF),
            acc,
            acc,
            acc,
            act,
            act,
            act,
            tok,
            three,
            three,
            pltpu.VMEM((2, 4, rows, model), BF),
            pltpu.VMEM((2, 2, eighth, width), BF),
            pltpu.VMEM((2, 2, eighth, width), BF),
            pltpu.VMEM((2, 2, width, eighth), BF),
            dma((5,)),
            dma((32,)),
            dma((16,)),
            dma((24,)),
            dma((24,)),
            dma((2,)),
            dma((3,)),
            dma((3,)),
            dma((8,)),
            dma((4,)),
            dma((4,)),
            pltpu.SemaphoreType.REGULAR,
            pltpu.SemaphoreType.REGULAR,
            pltpu.SemaphoreType.REGULAR,
        ],
        compiler_params=pltpu.CompilerParams(
            collective_id=5, has_side_effects=True, vmem_limit_bytes=64 * 1024 * 1024 - 65536
        ),
    )(mixed, cot, gate_weight, up_weight, down_weight, live)


class Reduce:
    def __init__(self, me, factors, cols, x_first, bufs, sems, k):
        self.n, self.w, self.y, self.x, self.core = me
        self.left, self.right = factors
        self.cols, self.x_first = pl.ds(*cols), x_first
        self.away, self.sum, self.pair, self.one, self.two = bufs
        self.sems, self.k = sems, k
        self.rows = self.sum.shape[2]
        self.near = flip(self.n, 2) if x_first else flip(self.n, 4)
        self.next = flip(self.n, 4) if x_first else flip(self.n, 2)

    def term(self, block):
        own = pl.ds(pl.multiple_of(block * self.rows, self.rows), self.rows)
        return contract_rows(self.left[:, own], self.right[:, self.cols])

    def swap(self):
        return send(
            self.away,
            self.pair,
            self.sems[0].at[self.k],
            self.sems[1].at[self.k],
            flip(self.n, 1),
            self.w,
        )

    def before_swap(self):
        @pl.loop(0, 4)
        def _(j):
            self.away[j // 2, lax.rem(j, 2)] = self.term(2 * j + 1 - self.core).astype(BF)

        self.swap().start()

    def block(self, first, second):
        return (second, first) if self.x_first else (first, second)

    def axes(self):
        return (self.x, self.y) if self.x_first else (self.y, self.x)

    def stage(self, s):
        a, b = self.axes()
        if s == 1:
            src = self.sum.at[:, 1 - a] if self.x_first else self.sum.at[1 - a]
            dst, peer = self.one, self.near
        else:
            src = self.sum.at[self.block(a, 1 - b)]
            dst, peer = self.two, self.next
        k = 2 * self.k + s - 1
        return send(src, dst, self.sems[2].at[k], self.sems[3].at[k], peer, self.w)

    def add(self, block, other):
        step = 64 if self.rows % 64 == 0 else 48

        @pl.loop(0, self.rows // step)
        def _(i):
            r = pl.ds(pl.multiple_of(i * step, step), step)
            self.sum[block[0], block[1], r, :] = (
                self.sum[block[0], block[1], r, :] + other[r, :]
            )

    def after_swap(self):
        a, _ = self.axes()
        self.swap().wait_recv()

        @pl.loop(0, 4)
        def _(j):
            first = lax.rem(1 - a + j // 2, 2)
            y, x = self.block(first, lax.rem(j, 2))
            total = self.term(4 * y + 2 * x + self.core) + self.pair[y, x].astype(F32)
            self.sum[y, x] = total.astype(BF)

        self.stage(1).start()

    def after_one(self):
        a, b = self.axes()
        self.stage(1).wait()
        self.add(self.block(a, 1 - b), self.one.at[1 - b])
        self.stage(2).start()
        self.add(self.block(a, b), self.one.at[b])

    def after_two(self):
        a, b = self.axes()
        self.stage(2).wait()
        self.add(self.block(a, b), self.two)

    def result(self):
        return self.sum.at[self.y, self.x]


class Half:
    def __init__(self, me, kept, came, x_first, bufs, sems, k):
        self.n, self.w, self.y, self.x, self.core = me
        self.kept, self.came, self.x_first = kept, came, x_first
        self.sum, self.one, self.two = bufs
        self.sems, self.k = sems, k
        self.rows = kept.shape[1]
        self.next = flip(self.n, 4) if x_first else flip(self.n, 2)
        self.here = self.y if x_first else self.x

    def loads(self):
        return [
            pltpu.make_async_copy(self.kept, self.sum, self.sems[0].at[2 * self.k]),
            pltpu.make_async_copy(self.came, self.one, self.sems[0].at[2 * self.k + 1]),
        ]

    def stage(self):
        return send(
            self.sum.at[1 - self.here],
            self.two,
            self.sems[1].at[self.k],
            self.sems[2].at[self.k],
            self.next,
            self.w,
        )

    def add(self, block, other):
        @pl.loop(0, self.rows // 64)
        def _(i):
            r = pl.ds(pl.multiple_of(i * 64, 64), 64)
            self.sum[block, r, :] = self.sum[block, r, :] + other[r, :]

    def after_one(self):
        for cp in self.loads():
            cp.wait()
        self.add(1 - self.here, self.one.at[1 - self.here])
        self.stage().start()
        self.add(self.here, self.one.at[self.here])

    def after_two(self):
        self.stage().wait()
        self.add(self.here, self.two)

    def result(self):
        return self.sum.at[self.here]


class Whole:
    def __init__(self, me, kept, came, x_first, bufs, sems, k):
        self.n, self.w = me[:2]
        self.kept, self.came, self.x_first = kept, came, x_first
        self.sum, self.one = bufs
        self.sems, self.k = sems, k

    def loads(self):
        return [
            pltpu.make_async_copy(self.kept, self.sum, self.sems[0].at[2 * self.k]),
            pltpu.make_async_copy(self.came, self.one, self.sems[0].at[2 * self.k + 1]),
        ]

    def join(self):
        for cp in self.loads():
            cp.wait()

        @pl.loop(0, self.sum.shape[0] // 64)
        def _(i):
            r = pl.ds(pl.multiple_of(i * 64, 64), 64)
            self.sum[r, :] = self.sum[r, :] + self.one[r, :]

    def result(self):
        return self.sum


class Spread:
    def __init__(self, item, region, sems, k):
        self.item, self.region, self.sems, self.k = item, region, sems, k
        n = item.n
        self.blocks = (n, flip(n, 2), flip(n, 4), flip(flip(n, 2), 4))

    def copy(self, kind, src, block, peer):
        k = 7 * self.k + kind
        return send(
            src, self.region(block), self.sems[0].at[k], self.sems[1].at[k], peer, self.item.w
        )

    def own(self, kind):
        n = self.item.n
        return self.copy(kind, self.item.result(), n, (flip(n, 2), flip(n, 4), flip(n, 1))[kind])

    def corner(self):
        n, b = self.item.n, self.blocks
        if self.item.x_first:
            return self.copy(3, self.region(b[2]), b[2], flip(n, 2))
        return self.copy(3, self.region(b[1]), b[1], flip(n, 4))

    def to_core(self, which):
        block = self.blocks[which]
        return self.copy(3 + which, self.region(block), block, flip(self.item.n, 1))

    def keep(self):
        return pltpu.make_async_copy(
            self.item.result(), self.region(self.item.n), self.sems[2].at[self.k]
        )

    def start(self):
        order = (1, 0, 2) if self.item.x_first else (0, 1, 2)
        for kind in order:
            self.own(kind).start()
        self.keep().start()

    def relay(self):
        first, second = (1, 0) if self.item.x_first else (0, 1)
        self.own(first).wait_recv()
        self.corner().start()
        self.to_core(1 + first).start()
        self.own(second).wait_recv()
        self.to_core(1 + second).start()

    def last(self):
        self.corner().wait_recv()
        self.to_core(3).start()

    def finish(self):
        for kind in range(2):
            self.own(kind).wait_send()
        self.own(2).wait()
        self.corner().wait_send()
        for which in range(1, 4):
            self.to_core(which).wait()
        self.keep().wait()


class Rows:
    def __init__(self, ref):
        self.ref = ref
        self.shape = (4, ref.shape[0] // 4, ref.shape[1])

    @property
    def at(self):
        return self

    def __getitem__(self, index):
        d, r, _ = index
        start = pl.multiple_of(d * self.shape[1] + r.start, r.size)
        return self.ref.at[pl.ds(start, r.size), :]


def last_kernel(items, *refs):
    refs = list(refs)

    def take(count):
        out = refs[:count]
        del refs[:count]
        return out

    factors = take(4)
    stays, comes = take(4), take(4)
    feed_terms, gain_parts = take(2)
    outs = take(4)
    gate_full, up_full, down_full = take(3)
    feed_out, gain_out = take(2)
    attn_bufs = [take(5) for _ in range(4)]
    ffn_bufs = [take(count) for count in (2, 2, 3, 3)]
    line_bufs = [take(3) for _ in range(4)]
    feed_v, feed_left, feed_right = take(3)
    gain_in, gain_sum, gain_line = take(3)
    factor_bufs = take(4)
    load_sem, swap_s, swap_r, st_s, st_r = take(5)
    half_sems = take(3)
    sp_sems = take(3)
    lr_s, lr_r, lg_s, lg_r, lg_l = take(5)
    fd_s, fd_r, fd_l = take(3)
    gn_s, gn_r, gz_s, gz_r = take(4)

    n, w = lax.axis_index("narrow"), lax.axis_index("wide")
    me = (n, w, n // 4, lax.rem(n // 2, 2), lax.rem(n, 2))
    attn = [
        Reduce(
            me,
            factor_bufs[2 * p : 2 * p + 2],
            cols,
            xf,
            attn_bufs[k],
            (swap_s, swap_r, st_s, st_r),
            k,
        )
        for k, (p, cols, xf) in enumerate(items)
    ]
    ffn = [
        (Whole, Half)[k // 2](me, stays[k], comes[k], k % 2 == 0, ffn_bufs[k], half_sems, k)
        for k in range(4)
    ]
    cut, eighth = stays[2].shape[1], stays[2].shape[2]

    def down_region(k):
        return lambda block: down_full.at[
            pl.ds(k * cut, cut), pl.ds(pl.multiple_of(block * eighth, eighth), eighth)
        ]

    regions = (
        lambda block: gate_full.at[block],
        lambda block: up_full.at[block],
        down_region(0),
        down_region(1),
    )
    spread = [Spread(ffn[k], regions[k], sp_sems, k) for k in range(4)]
    for item in ffn:
        for cp in item.loads():
            cp.start()
    factor_loads = [
        pltpu.make_async_copy(src, dst, load_sem.at[k])
        for k, (src, dst) in enumerate(zip(factors, factor_bufs))
    ]
    for cp in factor_loads:
        cp.start()
    feed_load = pltpu.make_async_copy(feed_terms, feed_v, fd_l)
    feed_load.start()

    barrier = pltpu.get_barrier_semaphore()
    narrow_peers = [lax.rem(n + i, 8) for i in range(1, 8)]
    wide_peers = [lax.rem(w + i, 4) for i in range(1, 4)]
    for peer in narrow_peers:
        pl.semaphore_signal(
            barrier, inc=1, device_id=at(peer, w), device_id_type=pl.DeviceIdType.MESH
        )
    for peer in wide_peers:
        pl.semaphore_signal(
            barrier, inc=1, device_id=at(n, peer), device_id_type=pl.DeviceIdType.MESH
        )
    pl.semaphore_wait(barrier, 10)

    feed_load.wait()
    feed = LineScatter(n, w, feed_v, (feed_left, feed_right), fd_s, fd_r, 4)
    for i in range(4):
        feed.begin(i)

    def gain_narrow(i):
        peer = narrow_peers[i]
        return send(gain_parts.at[peer], gain_in.at[i], gn_s.at[i], gn_r.at[i], peer, w)

    def gain_wide(i):
        return send(gain_sum, gain_line.at[i], gz_s.at[i], gz_r.at[i], n, wide_peers[i])

    for i in range(7):
        gain_narrow(i).start()

    for item in ffn[2:]:
        item.after_one()
    ffn[0].join()
    spread[0].start()
    for cp in factor_loads:
        cp.wait()
    for item in attn:
        item.before_swap()
    feed.pass_on(0)
    for item in attn:
        item.after_swap()
    feed.pass_on(1)
    feed.pass_end(0)
    for i in range(7):
        gain_narrow(i).wait()
    total = gain_parts[n]
    for i in range(7):
        total = total + gain_in[i]
    gain_sum[...] = total
    for i in range(3):
        gain_wide(i).start()
    feed.pass_on(2)
    feed.pass_end(1)
    for item in attn[:2]:
        item.after_one()
    feed.pass_on(3)
    feed.pass_end(2)
    for item in attn[2:]:
        item.after_one()
    feed.pass_end(3)
    spread[0].relay()
    ffn[1].join()
    spread[1].start()
    for k in (2, 3):
        ffn[k].after_two()
        spread[k].start()

    scatters, gathers = [], []
    for k, item in enumerate(attn):
        left, right, own = line_bufs[k]
        scatters.append(
            LineScatter(n, w, Rows(item.result()), (left, right), lr_s.at[k], lr_r.at[k], 1)
        )
        gathers.append(LineGather(n, w, own, outs[k], lg_s.at[k], lg_r.at[k], 1))

    def keep(k):
        return pltpu.make_async_copy(line_bufs[k][2], outs[k].at[w], lg_l.at[k])

    def line_turn(k):
        scatters[k].finish(0, line_bufs[k][2])
        gathers[k].start()
        keep(k).start()

    for k in (0, 1):
        attn[k].after_two()
        scatters[k].begin(0)
    for i in range(4):
        feed.finish(i, feed_out)
    for k in (2, 3):
        attn[k].after_two()
        scatters[k].begin(0)
    for k in (0, 1, 2, 3):
        scatters[k].pass_on(0)
    for k in (0, 1, 2, 3):
        scatters[k].pass_end(0)
    for k in (0, 1, 2, 3):
        line_turn(k)
    spread[1].relay()
    for k in (0, 1, 2, 3):
        gathers[k].near(0)
    for k in (0, 1, 2, 3):
        gathers[k].far(0)
    for s in spread[2:]:
        s.relay()
    for i in range(3):
        gain_wide(i).wait()
    gain_out[...] = (gain_sum[...] + gain_line[0]) + (gain_line[1] + gain_line[2])
    for s in spread:
        s.last()
    for s in spread:
        s.finish()
    for item in attn:
        item.swap().wait_send()
    for k in range(4):
        scatters[k].drain()
        gathers[k].finish()
        keep(k).wait()
    feed.drain()


def reduce_last(factors, stays, comes, feed_terms, gain_parts):
    rows = factors[0].shape[1] // 8
    items = []
    for p, xf in ((0, True), (0, False), (1, True), (1, False)):
        half = factors[2 * p + 1].shape[1] // 2
        items.append((p, (0 if xf else half, half), xf))
    scratch = []
    for _, (_, cols), _ in items:
        scratch += [
            pltpu.VMEM((2, 2, rows, cols), BF),
            pltpu.VMEM((2, 2, rows, cols), BF),
            pltpu.VMEM((2, 2, rows, cols), BF),
            pltpu.VMEM((2, rows, cols), BF),
            pltpu.VMEM((rows, cols), BF),
        ]
    for k, stay in enumerate(stays):
        scratch += [pltpu.VMEM(stay.shape, BF), pltpu.VMEM(stay.shape, BF)]
        if k > 1:
            scratch += [pltpu.VMEM(stay.shape[1:], BF)]
    outs = []
    for _, (_, cols), _ in items:
        scratch += [pltpu.VMEM((3, rows // 4, cols), BF)] * 2 + [pltpu.VMEM((rows // 4, cols), BF)]
        outs.append(jax.ShapeDtypeStruct((4, rows // 4, cols), BF))
    outs.append(jax.ShapeDtypeStruct((8,) + stays[0].shape, BF))
    outs.append(jax.ShapeDtypeStruct((8,) + stays[1].shape, BF))
    outs.append(jax.ShapeDtypeStruct((2 * stays[2].shape[1], 8 * stays[2].shape[2]), BF))
    outs.append(jax.ShapeDtypeStruct(feed_terms.shape[1:], F32))
    outs.append(jax.ShapeDtypeStruct(gain_parts.shape[1:], F32))
    scratch += [pltpu.VMEM(feed_terms.shape, BF)]
    scratch += [pltpu.VMEM((3,) + feed_terms.shape[1:], BF)] * 2
    scratch += [
        pltpu.VMEM((7,) + gain_parts.shape[1:], F32),
        pltpu.VMEM(gain_parts.shape[1:], F32),
        pltpu.VMEM((3,) + gain_parts.shape[1:], F32),
    ]
    scratch += [pltpu.VMEM(f.shape, BF) for f in factors]
    dma = pltpu.SemaphoreType.DMA
    scratch += [dma((4,)), dma((4,)), dma((4,)), dma((8,)), dma((8,))]
    scratch += [dma((8,)), dma((4,)), dma((4,))]
    scratch += [dma((28,)), dma((28,)), dma((4,))]
    scratch += [dma((4, 6)), dma((4, 6)), dma((4, 8)), dma((4, 4)), dma((4,))]
    scratch += [dma((24,)), dma((24,)), dma]
    scratch += [dma((7,)), dma((7,)), dma((3,)), dma((3,))]
    hbm, vmem = pl.BlockSpec(memory_space=pl.ANY), pl.BlockSpec(memory_space=pltpu.VMEM)
    out = pl.pallas_call(
        functools.partial(last_kernel, items),
        name="reduce_last",
        out_shape=tuple(outs),
        in_specs=[hbm] * 13 + [vmem],
        out_specs=[hbm] * 7 + [vmem] * 2,
        scratch_shapes=scratch,
        compiler_params=pltpu.CompilerParams(
            collective_id=4, has_side_effects=True, vmem_limit_bytes=64 * 1024 * 1024 - 65536
        ),
    )(*factors, *stays, *comes, feed_terms, gain_parts)
    qkv = jnp.concatenate([out[0].reshape(rows, -1), out[1].reshape(rows, -1)], axis=1)
    project = jnp.concatenate([out[2].reshape(rows, -1), out[3].reshape(rows, -1)], axis=1)
    width = out[4].shape[2]
    ffn = [out[4].reshape(-1, width), out[5].reshape(-1, width), out[6]]
    return qkv, project, ffn, out[7], out[8]


def per_device(
    fast,
    block_input,
    cotangent,
    query_weight,
    key_weight,
    value_weight,
    project_weight,
    prenorm_gain,
    midnorm_gain,
    gate_weight,
    up_weight,
    down_weight,
    doc_lengths,
    tile_counts,
):
    tokens_here, model = block_input.shape
    group = HEADS // KV_HEADS
    scale = HEAD_DIM ** (-0.5)
    q_cols, k_cols = HEADS * HEAD_DIM, KV_HEADS * HEAD_DIM
    inputs_f = block_input.astype(jnp.float32)
    ends = jnp.cumsum(doc_lengths[0])
    position = jnp.arange(tokens_here, dtype=jnp.int32)
    segment = jnp.sum((position[:, None] >= ends[None, :]).astype(jnp.int32), axis=1)
    allowed = (segment[:, None] == segment[None, :]) & (position[None, :] <= position[:, None])
    if fast:
        gains = jnp.stack([prenorm_gain, midnorm_gain]).astype(F32).reshape(1, -1)
        bias = jnp.where(allowed, 0.0, -1e30).astype(F32)
        qkv_full, project_full, grad_rows, normed, qkv, attended, gains_full, logs = gather_first(
            block_input,
            query_weight,
            key_weight,
            value_weight,
            project_weight,
            gains,
            cotangent,
            bias,
        )
        gains_full = gains_full.reshape(8, 2, -1)
        first_gain = gains_full[:, 0].reshape(-1)
        second_gain = gains_full[:, 1].reshape(-1)
    else:
        qkv_full = jnp.concatenate(
            [
                lax.all_gather(query_weight, "narrow", axis=0, tiled=True),
                lax.all_gather(key_weight, "narrow", axis=0, tiled=True),
                lax.all_gather(value_weight, "narrow", axis=0, tiled=True),
            ],
            axis=1,
        )
        project_full = lax.all_gather(project_weight, "narrow", axis=1, tiled=True)
        first_gain = lax.all_gather(prenorm_gain, "narrow", axis=0, tiled=True).astype(F32)
        second_gain = lax.all_gather(midnorm_gain, "narrow", axis=0, tiled=True).astype(F32)
        grad_rows = lax.all_gather(cotangent, "wide", axis=0, tiled=True)
        normed = rms_scale(inputs_f, first_gain).astype(jnp.bfloat16)
        qkv = jnp.dot(normed, qkv_full, preferred_element_type=jnp.float32).astype(jnp.bfloat16)
    if not fast:
        query_rows = qkv[:, :q_cols].reshape(tokens_here, KV_HEADS, group, HEAD_DIM)
        key_rows = qkv[:, q_cols : q_cols + k_cols].reshape(tokens_here, KV_HEADS, HEAD_DIM)
        value_rows = qkv[:, q_cols + k_cols :].reshape(tokens_here, KV_HEADS, HEAD_DIM)
        scores = (
            jnp.einsum("qcgd,kcd->cgqk", query_rows, key_rows, preferred_element_type=jnp.float32)
            * scale
        )
        masked = jnp.where(allowed, scores, -1e30)
        peak = jnp.max(masked, axis=-1, keepdims=True)
        expo = jnp.exp(masked - peak)
        total = jnp.sum(expo, axis=-1, keepdims=True)
        probs_low = (expo / total).astype(jnp.bfloat16)
        logsum = peak + jnp.log(total)
        attended = (
            jnp.einsum("cgqk,kcd->qcgd", probs_low, value_rows, preferred_element_type=jnp.float32)
            .astype(jnp.bfloat16)
            .reshape(tokens_here, HEADS * HEAD_DIM)
        )
    branch = jnp.dot(attended, project_full, preferred_element_type=jnp.float32)
    middle = inputs_f + branch
    mixed_in = rms_scale(middle, second_gain).astype(jnp.bfloat16)
    width = gate_weight.shape[1]
    wide_index = lax.axis_index("wide")
    my_count = jnp.sum(
        jnp.where(jnp.arange(tile_counts.shape[0], dtype=jnp.int32) == wide_index, tile_counts, 0)
    )
    live = (jnp.arange(width, dtype=jnp.int32) // TILE < my_count).astype(jnp.float32)
    if fast:
        mixed_back, feed_terms, *pieces = feed_forward(
            mixed_in, grad_rows, gate_weight, up_weight, down_weight, live.reshape(1, -1)
        )
        stays = pieces[1::2]
        comes = [
            lax.ppermute(piece, "narrow", [(i, i ^ bit) for i in range(8)])
            for piece, bit in zip(pieces[0::2], (4, 2, 2, 4))
        ]
    else:
        gathered = lax.all_gather(mixed_in, "wide", axis=0, tiled=True)
        gate_pre = jnp.dot(gathered, gate_weight, preferred_element_type=jnp.float32)
        up_pre = jnp.dot(gathered, up_weight, preferred_element_type=jnp.float32)
        hidden_back = contract_cols(grad_rows, down_weight)
        sigma = jax.nn.sigmoid(gate_pre)
        hidden = (gate_pre * sigma * up_pre * live).astype(BF)
        gate_back = (
            hidden_back * up_pre * live * sigma * (1.0 + gate_pre * (1.0 - sigma))
        ).astype(BF)
        up_back = (hidden_back * gate_pre * sigma * live).astype(BF)
        mixed_terms = (
            contract_cols(gate_back, gate_weight) + contract_cols(up_back, up_weight)
        ).astype(BF)
        mixed_back = lax.psum_scatter(
            mixed_terms, "wide", scatter_dimension=0, tiled=True
        ).astype(F32)
        partial_rows = jnp.dot(hidden, down_weight, preferred_element_type=jnp.float32)
        down_part = contract_rows(hidden, grad_rows)
        gate_part = contract_rows(gathered, gate_back)
        up_part = contract_rows(gathered, up_back)
    out_grad = cotangent.astype(jnp.float32)
    unused_second, second_backward = jax.vjp(rms_scale, middle, second_gain)
    middle_norm_back, second_gain_part = second_backward(mixed_back)
    middle_back = out_grad + middle_norm_back
    branch_back = middle_back.astype(jnp.bfloat16)
    attended_back = contract_cols(branch_back, project_full).astype(jnp.bfloat16)
    if fast:
        qkv_back = attention_back(qkv, attended_back, logs, bias)
    else:
        attended_back = attended_back.reshape(tokens_here, KV_HEADS, group, HEAD_DIM)
        scores_again = (
            jnp.einsum("qcgd,kcd->cgqk", query_rows, key_rows, preferred_element_type=jnp.float32)
            * scale
        )
        probs_again = jnp.where(allowed, jnp.exp(scores_again - logsum), 0.0)
        probs_again_low = probs_again.astype(jnp.bfloat16)
        value_back = (
            jnp.einsum(
                "cgqk,qcgd->kcd", probs_again_low, attended_back, preferred_element_type=jnp.float32
            )
            .astype(jnp.bfloat16)
            .reshape(tokens_here, KV_HEADS * HEAD_DIM)
        )
        probs_back = jnp.einsum(
            "qcgd,kcd->cgqk", attended_back, value_rows, preferred_element_type=jnp.float32
        )
        scores_back = (
            probs_again * (probs_back - jnp.sum(probs_again * probs_back, axis=-1, keepdims=True))
        ).astype(jnp.bfloat16)
        query_back = (
            (
                jnp.einsum("cgqk,kcd->qcgd", scores_back, key_rows, preferred_element_type=jnp.float32)
                * scale
            )
            .astype(jnp.bfloat16)
            .reshape(tokens_here, HEADS * HEAD_DIM)
        )
        key_back = (
            (
                jnp.einsum(
                    "cgqk,qcgd->kcd", scores_back, query_rows, preferred_element_type=jnp.float32
                )
                * scale
            )
            .astype(jnp.bfloat16)
            .reshape(tokens_here, KV_HEADS * HEAD_DIM)
        )
        qkv_back = jnp.concatenate([query_back, key_back, value_back], axis=1)
    normed_back = contract_cols(qkv_back, qkv_full)
    unused_first, first_backward = jax.vjp(rms_scale, inputs_f, first_gain)
    input_norm_back, first_gain_part = first_backward(normed_back)
    input_grad = (middle_back + input_norm_back).astype(jnp.bfloat16)

    if fast:
        gain_parts = jnp.stack(
            [first_gain_part.reshape(8, -1), second_gain_part.reshape(8, -1)], axis=1
        ).reshape(8, 1, -1)
        input_grad, qkv_back = lax.optimization_barrier((input_grad, qkv_back))
        qkv_total, project_total, ffn_totals, feed, gain_total = reduce_last(
            (normed, qkv_back, branch_back, attended),
            stays,
            comes,
            feed_terms,
            gain_parts,
        )
        gain_total = gain_total.reshape(2, -1)
        first_total, second_total = gain_total[0], gain_total[1]
        qkv_total = qkv_total.astype(F32)
        project_total = project_total.T.astype(F32)
        gate_total, up_total, down_total = [t.astype(F32) for t in ffn_totals]
    else:

        def owned(part):
            share = lax.psum_scatter(part.astype(BF), "narrow", scatter_dimension=0, tiled=True)
            return lax.psum(share, "wide").astype(F32)

        qkv_total = owned(contract_rows(normed, qkv_back))
        project_total = owned(contract_rows(branch_back, attended)).T
        first_total = owned(first_gain_part)
        second_total = owned(second_gain_part)
        gate_total, up_total, down_total = (
            lax.psum(gate_part.astype(BF), "narrow").astype(F32),
            lax.psum(up_part.astype(BF), "narrow").astype(F32),
            lax.psum(down_part.astype(BF), "narrow").astype(F32),
        )
        feed = lax.psum_scatter(
            partial_rows.astype(BF), "wide", scatter_dimension=0, tiled=True
        ).astype(F32)
    block_output = (middle + feed).astype(BF)
    return (
        block_output,
        input_grad,
        qkv_total[:, :q_cols],
        qkv_total[:, q_cols : q_cols + k_cols],
        qkv_total[:, q_cols + k_cols :],
        project_total,
        first_total,
        second_total,
        gate_total,
        up_total,
        down_total,
    )


def solution(mesh):
    fast = mesh.shape["narrow"] == 8 and mesh.shape["wide"] == 4
    placed = (
        P(("narrow", "wide"), None),
        P(("narrow", "wide"), None),
        P("narrow", None),
        P("narrow", None),
        P("narrow", None),
        P(None, "narrow"),
        P("narrow"),
        P("narrow"),
        P(None, "wide"),
        P(None, "wide"),
        P("wide", None),
        P(("narrow", "wide"), None),
        P(),
    )
    return jax.shard_map(
        functools.partial(per_device, fast),
        mesh=mesh,
        in_specs=placed,
        out_specs=(
            P(("narrow", "wide"), None),
            P(("narrow", "wide"), None),
            P("narrow", None),
            P("narrow", None),
            P("narrow", None),
            P(None, "narrow"),
            P("narrow"),
            P("narrow"),
            P(None, "wide"),
            P(None, "wide"),
            P("wide", None),
        ),
        check_vma=False,
    )
```

```python
import functools

import jax
import jax.numpy as jnp
from jax import lax
from jax.experimental import pallas as pl
from jax.experimental.pallas import tpu as pltpu
from jax.sharding import PartitionSpec as P

HEADS = 24
KV_HEADS = 6
HEAD_DIM = 64
TILE = 128


EPSILON = 1e-06

BF = jnp.bfloat16
F32 = jnp.float32


def rms_scale(rows, gain):
    factor = lax.rsqrt(jnp.mean(rows * rows, axis=-1, keepdims=True) + EPSILON)
    return rows * factor * gain


def contract_rows(left, right):
    return lax.dot_general(
        left, right, (((0,), (0,)), ((), ())), preferred_element_type=jnp.float32
    )


def contract_cols(left, right):
    return lax.dot_general(
        left, right, (((1,), (1,)), ((), ())), preferred_element_type=jnp.float32
    )


def flip(n, bit):
    return n + bit - 2 * bit * lax.rem(n // bit, 2)


def at(n, w):
    return {"narrow": n, "wide": w}


def send(src, dst, ssem, rsem, n, w):
    return pltpu.make_async_remote_copy(
        src_ref=src,
        dst_ref=dst,
        send_sem=ssem,
        recv_sem=rsem,
        device_id=at(n, w),
        device_id_type=pl.DeviceIdType.MESH,
    )


def greet(narrow_peers, n, w, line):
    barrier = pltpu.get_barrier_semaphore()
    for peer in narrow_peers:
        pl.semaphore_signal(
            barrier, inc=1, device_id=at(peer, w), device_id_type=pl.DeviceIdType.MESH
        )
    if not line:
        pl.semaphore_wait(barrier, len(narrow_peers))
    if line:

        @pl.when(w > 0)
        def _():
            pl.semaphore_signal(
                barrier, inc=1, device_id=at(n, w - 1), device_id_type=pl.DeviceIdType.MESH
            )

        @pl.when(w < 3)
        def _():
            pl.semaphore_signal(
                barrier, inc=1, device_id=at(n, w + 1), device_id_type=pl.DeviceIdType.MESH
            )

        @pl.when((w == 0) | (w == 3))
        def _():
            pl.semaphore_wait(barrier, len(narrow_peers) + 1)

        @pl.when((w == 1) | (w == 2))
        def _():
            pl.semaphore_wait(barrier, len(narrow_peers) + 2)


class LineGather:
    def __init__(self, n, w, own, whole, ssem, rsem, chunks):
        self.n, self.w, self.own, self.whole = n, w, own, whole
        self.ssem, self.rsem, self.chunks = ssem, rsem, chunks
        self.rows = own.shape[0] // chunks

    def span(self, i):
        return pl.ds(pl.multiple_of(i * self.rows, self.rows), self.rows)

    def part(self, shard, i):
        return self.whole.at[shard, self.span(i), :]

    def put(self, way, here, shard, i):
        src = self.own.at[self.span(i), :] if shard is here else self.part(shard, i)
        to = here + 1 - 2 * way
        s = (way * 4 + shard) * self.chunks + i
        r = shard * self.chunks + i
        return send(src, self.part(shard, i), self.ssem.at[s], self.rsem.at[r], self.n, to)

    def came(self, shard, i):
        self.put(0, 0, shard, i).wait_recv()

    def start_chunk(self, i):
        @pl.when(self.w < 3)
        def _():
            self.put(0, self.w, self.w, i).start()

        @pl.when(self.w > 0)
        def _():
            self.put(1, self.w, self.w, i).start()

    def start(self):
        for i in range(self.chunks):
            self.start_chunk(i)

    def near(self, i):
        @pl.when(self.w == 1)
        def _():
            self.came(0, i)
            self.put(0, 1, 0, i).start()
            self.came(2, i)
            self.put(1, 1, 2, i).start()

        @pl.when(self.w == 2)
        def _():
            self.came(3, i)
            self.put(1, 2, 3, i).start()
            self.came(1, i)
            self.put(0, 2, 1, i).start()

    def far(self, i):
        @pl.when(self.w == 1)
        def _():
            self.came(3, i)
            self.put(1, 1, 3, i).start()

        @pl.when(self.w == 2)
        def _():
            self.came(0, i)
            self.put(0, 2, 0, i).start()

    def ready(self, i):
        @pl.when(self.w == 0)
        def _():
            for shard in (1, 2, 3):
                self.came(shard, i)

        @pl.when(self.w == 3)
        def _():
            for shard in (2, 1, 0):
                self.came(shard, i)

    def finish_sends(self):
        for here in range(4):

            @pl.when(self.w == here)
            def _():
                for i in range(self.chunks):
                    if here < 3:
                        for shard in range(here + 1):
                            self.put(0, here, shard, i).wait_send()
                    if here > 0:
                        for shard in range(here, 4):
                            self.put(1, here, shard, i).wait_send()

    def finish(self):
        for i in range(self.chunks):
            self.ready(i)
        self.finish_sends()


def first_kernel(
    x_ref,
    q_ref,
    k_ref,
    v_ref,
    p_ref,
    g_ref,
    c_ref,
    bias_ref,
    qkv_out,
    p_full,
    c_full,
    normed_out,
    rows_out,
    att_out,
    g_full,
    log_out,
    qkv_full,
    p_buf,
    c_buf,
    x_buf,
    gain_row,
    normed,
    qkv,
    att,
    in_sem,
    out_sem,
    ssem,
    rsem,
    gs_sem,
    gr_sem,
    zs_sem,
    zr_sem,
):
    n, w = lax.axis_index("narrow"), lax.axis_index("wide")
    x, y, c, d = flip(n, 2), flip(n, 4), flip(n, 1), flip(flip(n, 2), 4)
    others = [lax.rem(n + i, 8) for i in range(1, 8)]
    rows = q_ref.shape[0]
    half = rows // 2
    depth = p_ref.shape[0]
    qc, kc = q_ref.shape[1], k_ref.shape[1]
    cols = ((0, qc), (qc, kc), (qc + kc, kc))

    def region(t, block, h):
        if t == 3:
            r = pl.ds(0, depth) if h == 2 else pl.ds(h * (depth // 2), depth // 2)
            return p_full.at[r, pl.ds(pl.multiple_of(block * rows, rows), rows)]
        start = pl.multiple_of(block * rows, rows)
        r = pl.ds(start, rows) if h == 2 else pl.ds(start + h * half, half)
        return qkv_full.at[r, pl.ds(cols[t][0], cols[t][1])]

    locals_in = []
    for i, (src, dst) in enumerate(
        (
            (g_ref, g_full.at[n]),
            (x_ref, x_buf),
            (p_ref, p_buf),
            (c_ref, c_buf),
            (q_ref, region(0, n, 2)),
            (k_ref, region(1, n, 2)),
            (v_ref, region(2, n, 2)),
        )
    ):
        cp = pltpu.make_async_copy(src, dst, in_sem.at[i])
        cp.start()
        locals_in.append(cp)

    greet(others, n, w, True)

    def own(t, h):
        ref = (q_ref, k_ref, v_ref, p_ref)[t]
        if h == 2:
            return ref
        size = ref.shape[0] // 2
        return ref.at[pl.ds(h * size, size), :]

    def msg(t, kind, src, block, h, peer):
        k = t * 10 + kind
        return send(src, region(t, block, h), ssem.at[k], rsem.at[k], peer, w)

    def to_x(t, h):
        return msg(t, h, own(t, h), n, h, x)

    def to_y(t, h):
        return msg(t, 2 + h, own(t, h), n, h, y)

    def on_x(t):
        return msg(t, 4, region(t, y, 0), y, 0, x)

    def on_y(t):
        return msg(t, 5, region(t, x, 1), x, 1, y)

    def to_c(t, which):
        block = (n, x, y, d)[which]
        src = own(t, 2) if which == 0 else region(t, block, 2)
        return msg(t, 6 + which, src, block, 2, c)

    def start_own(t):
        to_x(t, 1).start()
        to_y(t, 0).start()
        to_x(t, 0).start()
        to_y(t, 1).start()

    def gain(i):
        return send(g_ref, g_full.at[n], gs_sem.at[i], gr_sem.at[i], others[i], w)

    line = LineGather(n, w, c_ref, c_full, zs_sem, zr_sem, 4)
    for i in range(7):
        gain(i).start()
    start_own(0)
    line.start()
    for t in (1, 2):
        start_own(t)
    for t in range(3):
        to_c(t, 0).start()

    locals_out = []

    def put(src, dst):
        cp = pltpu.make_async_copy(src, dst, out_sem.at[len(locals_out)])
        cp.start()
        locals_out.append(cp)

    for i in range(7):
        gain(i).wait()
    for cp in locals_in:
        cp.wait()
    put(p_buf, region(3, n, 2))
    put(c_buf, c_full.at[w])
    for k in range(8):
        gain_row[:, pl.ds(k * rows, rows)] = g_full[k, :, :rows]
    strip = 16

    @pl.loop(0, x_buf.shape[0] // strip)
    def _(i):
        s = pl.ds(pl.multiple_of(i * strip, strip), strip)
        normed[s, :] = rms_scale(x_buf[s, :].astype(F32), gain_row[...]).astype(BF)

    put(normed, normed_out)

    def relay(t):
        to_y(t, 0).wait_recv()
        on_x(t).start()
        to_x(t, 1).wait_recv()
        on_y(t).start()
        to_x(t, 0).wait_recv()
        to_c(t, 1).start()
        to_y(t, 1).wait_recv()
        to_c(t, 2).start()

    def corner(t):
        on_x(t).wait_recv()
        on_y(t).wait_recv()
        to_c(t, 3).start()

    line.near(0)
    relay(0)
    line.near(1)
    relay(1)
    line.near(2)
    relay(2)
    start_own(3)
    to_c(3, 0).start()
    line.near(3)
    line.far(0)
    line.far(1)
    for t in range(3):
        corner(t)
    line.far(2)
    for t in range(3):
        for which in range(4):
            to_c(t, which).wait_recv()
    put(qkv_full, qkv_out)
    tile = 256

    @pl.loop(0, qkv.shape[1] // tile)
    def _(i):
        s = pl.ds(pl.multiple_of(i * tile, tile), tile)
        qkv[:, s] = jnp.dot(normed[...], qkv_full[:, s], preferred_element_type=F32).astype(BF)

    put(qkv, rows_out)
    line.far(3)

    log_out[...] = jnp.zeros(log_out.shape, F32)
    pair = 2 * HEAD_DIM
    group = HEADS // KV_HEADS

    @pl.loop(0, KV_HEADS // 2)
    def _(i):
        keys = qkv[:, pl.ds(pl.multiple_of(qc + i * pair, pair), pair)]
        values = qkv[:, pl.ds(pl.multiple_of(qc + kc + i * pair, pair), pair)]
        lane = lax.broadcasted_iota(jnp.int32, log_out.shape, 1)
        for b in range(group):
            at_cols = pl.ds(pl.multiple_of((i * group + b) * pair, pair), pair)
            queries = qkv[:, at_cols]
            side = (2 * b) // group
            key = keys[:, side * HEAD_DIM : (side + 1) * HEAD_DIM]
            value = values[:, side * HEAD_DIM : (side + 1) * HEAD_DIM]
            heads = []
            for e in range(2):
                query = queries[:, e * HEAD_DIM : (e + 1) * HEAD_DIM]
                masked = contract_cols(query, key) * (HEAD_DIM**-0.5) + bias_ref[...]
                peak = jnp.max(masked, axis=-1, keepdims=True)
                expo = jnp.exp(masked - peak)
                total = jnp.sum(expo, axis=-1, keepdims=True)
                probs = (expo * (1.0 / total)).astype(BF)
                heads.append(jnp.dot(probs, value, preferred_element_type=F32))
                log_out[...] = jnp.where(
                    lane == 2 * (i * group + b) + e, peak + jnp.log(total), log_out[...]
                )
            att[:, at_cols] = jnp.concatenate(heads, axis=1).astype(BF)

    put(att, att_out)
    relay(3)
    corner(3)
    for t in range(4):
        for h in range(2):
            to_x(t, h).wait_send()
            to_y(t, h).wait_send()
        on_x(t).wait_send()
        on_y(t).wait_send()
        for which in range(4):
            if t == 3:
                to_c(t, which).wait_recv()
            to_c(t, which).wait_send()
    line.finish()
    for cp in locals_out:
        cp.wait()


def gather_first(rows_in, query, key, value, project, gains, cotangent, bias):
    rows = query.shape[0]
    width = query.shape[1] + 2 * key.shape[1]
    tokens_here, model = rows_in.shape
    hbm, vmem = pl.BlockSpec(memory_space=pl.ANY), pl.BlockSpec(memory_space=pltpu.VMEM)
    return pl.pallas_call(
        first_kernel,
        name="gather_first",
        out_shape=(
            jax.ShapeDtypeStruct((8 * rows, width), BF),
            jax.ShapeDtypeStruct((project.shape[0], 8 * rows), BF),
            jax.ShapeDtypeStruct((4,) + cotangent.shape, BF),
            jax.ShapeDtypeStruct((tokens_here, model), BF),
            jax.ShapeDtypeStruct((tokens_here, width), BF),
            jax.ShapeDtypeStruct((tokens_here, query.shape[1]), BF),
            jax.ShapeDtypeStruct((8,) + gains.shape, gains.dtype),
            jax.ShapeDtypeStruct((tokens_here, 128), F32),
        ),
        in_specs=[hbm] * 7 + [vmem],
        out_specs=[hbm] * 6 + [vmem] * 2,
        scratch_shapes=[
            pltpu.VMEM((8 * rows, width), BF),
            pltpu.VMEM(project.shape, BF),
            pltpu.VMEM(cotangent.shape, BF),
            pltpu.VMEM((tokens_here, model), BF),
            pltpu.VMEM((1, model), F32),
            pltpu.VMEM((tokens_here, model), BF),
            pltpu.VMEM((tokens_here, width), BF),
            pltpu.VMEM((tokens_here, query.shape[1]), BF),
            pltpu.SemaphoreType.DMA((7,)),
            pltpu.SemaphoreType.DMA((6,)),
            pltpu.SemaphoreType.DMA((40,)),
            pltpu.SemaphoreType.DMA((40,)),
            pltpu.SemaphoreType.DMA((7,)),
            pltpu.SemaphoreType.DMA((7,)),
            pltpu.SemaphoreType.DMA((32,)),
            pltpu.SemaphoreType.DMA((16,)),
        ],
        compiler_params=pltpu.CompilerParams(collective_id=1, has_side_effects=True),
    )(rows_in, query, key, value, project, gains, cotangent, bias)


def attention_back_kernel(qkv, back, logs, bias, out):
    q_cols, k_cols = HEADS * HEAD_DIM, KV_HEADS * HEAD_DIM
    pair = 2 * HEAD_DIM
    group = HEADS // KV_HEADS
    scale = HEAD_DIM**-0.5

    @pl.loop(0, KV_HEADS // 2)
    def _(i):
        key_at = pl.ds(pl.multiple_of(q_cols + i * pair, pair), pair)
        value_at = pl.ds(pl.multiple_of(q_cols + k_cols + i * pair, pair), pair)
        keys, values = qkv[:, key_at], qkv[:, value_at]
        lane = lax.broadcasted_iota(jnp.int32, logs.shape, 1)
        key_backs, value_backs = [], []
        for side in range(2):
            key = keys[:, side * HEAD_DIM : (side + 1) * HEAD_DIM]
            value = values[:, side * HEAD_DIM : (side + 1) * HEAD_DIM]
            key_back = jnp.zeros(key.shape, F32)
            value_back = jnp.zeros(key.shape, F32)
            for b in range(side * group // 2, (side + 1) * group // 2):
                at_cols = pl.ds(pl.multiple_of((i * group + b) * pair, pair), pair)
                queries, backs = qkv[:, at_cols], back[:, at_cols]
                heads = []
                for e in range(2):
                    query = queries[:, e * HEAD_DIM : (e + 1) * HEAD_DIM]
                    given = backs[:, e * HEAD_DIM : (e + 1) * HEAD_DIM]
                    logsum = jnp.sum(
                        jnp.where(lane == 2 * (i * group + b) + e, logs[...], 0.0),
                        axis=-1,
                        keepdims=True,
                    )
                    probs = jnp.exp(contract_cols(query, key) * scale + bias[...] - logsum)
                    value_back = value_back + contract_rows(probs.astype(BF), given)
                    probs_back = contract_cols(given, value)
                    inner = jnp.sum(probs * probs_back, axis=-1, keepdims=True)
                    scores_back = (probs * (probs_back - inner)).astype(BF)
                    heads.append(jnp.dot(scores_back, key, preferred_element_type=F32) * scale)
                    key_back = key_back + contract_rows(scores_back, query)
                out[:, at_cols] = jnp.concatenate(heads, axis=1).astype(BF)
            key_backs.append(key_back * scale)
            value_backs.append(value_back)
        out[:, key_at] = jnp.concatenate(key_backs, axis=1).astype(BF)
        out[:, value_at] = jnp.concatenate(value_backs, axis=1).astype(BF)


def attention_back(qkv, back, logs, bias):
    vmem = pl.BlockSpec(memory_space=pltpu.VMEM)
    heads = HEADS * qkv.shape[0] * qkv.shape[0]
    return pl.pallas_call(
        attention_back_kernel,
        name="attention_back",
        out_shape=jax.ShapeDtypeStruct(qkv.shape, BF),
        in_specs=[vmem] * 4,
        out_specs=vmem,
        cost_estimate=pl.CostEstimate(
            flops=10 * heads * HEAD_DIM, bytes_accessed=8 * qkv.size, transcendentals=heads
        ),
    )(qkv, back, logs, bias)


class LineScatter:
    def __init__(self, n, w, terms, bufs, ssem, rsem, chunks):
        self.n, self.w, self.terms, self.bufs = n, w, terms, bufs
        self.ssem, self.rsem, self.chunks = ssem, rsem, chunks
        self.rows = terms.shape[1] // chunks

    def span(self, i):
        return pl.ds(pl.multiple_of(i * self.rows, self.rows), self.rows)

    def term(self, d, i):
        return self.terms.at[d, self.span(i), :]

    def slot(self, way, slot, i):
        return self.bufs[way].at[slot, self.span(i), :]

    def put(self, way, here, d, i, src):
        slot = d - here - 1 if way == 0 else here - 1 - d
        k = (way * 3 + slot) * self.chunks + i
        to = here + 1 - 2 * way
        return send(src, self.slot(way, slot, i), self.ssem.at[k], self.rsem.at[k], self.n, to)

    def came(self, way, slot, i):
        k = (way * 3 + slot) * self.chunks + i
        ref = self.slot(way, slot, i)
        send(ref, ref, self.ssem.at[k], self.rsem.at[k], self.n, 1).wait_recv()

    def begin(self, i):
        for here, way in ((0, 0), (3, 1)):

            @pl.when(self.w == here)
            def _():
                for d in (3, 2, 1) if way == 0 else (0, 1, 2):
                    self.put(way, here, d, i, self.term(d, i)).start()

    def join(self, way, here, d, i):
        slot = d - here if way == 0 else here - d
        self.came(way, slot, i)
        mine, sum_ = self.term(d, i), self.slot(way, slot, i)
        sum_[...] = (mine[...].astype(F32) + sum_[...].astype(F32)).astype(BF)
        self.put(way, here, d, i, sum_).start()

    def pass_on(self, i):
        @pl.when(self.w == 1)
        def _():
            self.join(0, 1, 3, i)
            self.join(0, 1, 2, i)

        @pl.when(self.w == 2)
        def _():
            self.join(1, 2, 0, i)
            self.join(1, 2, 1, i)

    def pass_end(self, i):
        @pl.when(self.w == 1)
        def _():
            self.join(1, 1, 0, i)

        @pl.when(self.w == 2)
        def _():
            self.join(0, 2, 3, i)

    def finish(self, i, out):
        for here, ways in ((0, (1,)), (1, (0, 1)), (2, (0, 1)), (3, (0,))):

            @pl.when(self.w == here)
            def _():
                for way in ways:
                    self.came(way, 0, i)
                total = self.term(here, i)[...].astype(F32)
                for way in ways:
                    total = total + self.slot(way, 0, i)[...].astype(F32)
                out[self.span(i), :] = total.astype(out.dtype)

    def drain(self):
        sent = {
            0: ((0, 3), (0, 2), (0, 1)),
            1: ((0, 3), (0, 2), (1, 0)),
            2: ((1, 0), (1, 1), (0, 3)),
            3: ((1, 0), (1, 1), (1, 2)),
        }
        for here in range(4):

            @pl.when(self.w == here)
            def _():
                for i in range(self.chunks):
                    for way, d in sent[here]:
                        self.put(way, here, d, i, self.term(d, i)).wait_send()


def middle_kernel(
    mixed,
    cot,
    wg,
    wu,
    wd,
    live,
    back_out,
    partial_out,
    gate_go,
    gate_stay,
    up_go,
    up_stay,
    low_go,
    low_stay,
    high_go,
    high_stay,
    x_all,
    cot_v,
    wg_v,
    wu_v,
    wd_v,
    gate_f,
    up_f,
    back_f,
    hid,
    gb,
    ub,
    terms,
    from_left,
    from_right,
    part_buf,
    gate_k,
    up_k,
    down_k,
    in_sem,
    ag_s,
    ag_r,
    rs_s,
    rs_r,
    part_sem,
    sw_s,
    sw_r,
    out_sem,
    ready,
):
    n, w = lax.axis_index("narrow"), lax.axis_index("wide")
    y, x, core = n // 4, lax.rem(n // 2, 2), lax.rem(n, 2)
    mate = flip(n, 1)
    chunks = 4
    rows = mixed.shape[0] // chunks
    tokens, model = 4 * mixed.shape[0], mixed.shape[1]
    width = wg.shape[1]
    batch, block = 4 * rows, 512
    loads = [
        pltpu.make_async_copy(src, dst, in_sem.at[k])
        for k, (src, dst) in enumerate(
            ((mixed, x_all.at[w]), (wg, wg_v), (wu, wu_v), (cot, cot_v), (wd, wd_v))
        )
    ]
    for cp in loads:
        cp.start()
    greet([mate], n, w, True)

    gather = LineGather(n, w, mixed, x_all, ag_s, ag_r, chunks)
    scatter = LineScatter(n, w, terms, (from_left, from_right), rs_s, rs_r, chunks)
    gather.start_chunk(0)
    gather.start_chunk(1)
    gather.near(0)
    gather.far(0)
    for cp in loads:
        cp.wait()

    def rows_of(ref, i):
        r = pl.ds(pl.multiple_of(i * rows, rows), rows)
        return ref[:, r, :].reshape(batch, ref.shape[2])

    def store(i):
        return pltpu.make_async_copy(
            part_buf.at[lax.rem(i, 2)],
            partial_out.at[:, pl.ds(pl.multiple_of(i * rows, rows), rows), :],
            part_sem.at[lax.rem(i, 2)],
        )

    @pl.loop(0, chunks)
    def _(i):
        r = pl.ds(pl.multiple_of(i * rows, rows), rows)
        gather.ready(i)
        xs = rows_of(x_all, i)
        gate_f[...] = jnp.dot(xs, wg_v[...], preferred_element_type=F32)
        up_f[...] = jnp.dot(xs, wu_v[...], preferred_element_type=F32)

        @pl.when(i < chunks - 1)
        def _():
            gather.near(i + 1)

        @pl.when(i < chunks - 2)
        def _():
            gather.start_chunk(i + 2)

        back_f[...] = contract_cols(rows_of(cot_v, i), wd_v[...])
        step = 16

        @pl.loop(0, batch // step)
        def _(t):
            s = pl.ds(pl.multiple_of(t * step, step), step)
            d = t // (rows // step)
            into = pl.ds(
                pl.multiple_of(i * rows + lax.rem(t, rows // step) * step, step), step
            )
            gate, up = gate_f[s, :], up_f[s, :] * live[...]
            sigma = jax.nn.sigmoid(gate)
            silu = gate * sigma
            hid[d, into, :] = (silu * up).astype(BF)
            back = back_f[s, :]
            gb[d, into, :] = (back * up * sigma * (1.0 + gate * (1.0 - sigma))).astype(BF)
            ub[d, into, :] = (back * silu * live[...]).astype(BF)

        @pl.when(i > 0)
        def _():
            scatter.pass_on(i - 1)

        @pl.when(i < chunks - 1)
        def _():
            gather.far(i + 1)

        @pl.loop(0, model // block)
        def _(j):
            b = pl.ds(pl.multiple_of(j * block, block), block)
            terms[:, r, b] = (
                (
                    contract_cols(rows_of(gb, i), wg_v[b, :])
                    + contract_cols(rows_of(ub, i), wu_v[b, :])
                )
                .astype(BF)
                .reshape(4, rows, block)
            )

        scatter.begin(i)

        @pl.when(i > 1)
        def _():
            store(i - 2).wait()

        @pl.loop(0, model // block)
        def _(j):
            b = pl.ds(pl.multiple_of(j * block, block), block)
            part_buf[lax.rem(i, 2), :, :, b] = (
                jnp.dot(rows_of(hid, i), wd_v[:, b], preferred_element_type=F32)
                .astype(BF)
                .reshape(4, rows, block)
            )

        store(i).start()

        @pl.when(i > 0)
        def _():
            scatter.pass_end(i - 1)

    pl.semaphore_signal(
        ready, inc=1, device_id=at(mate, w), device_id_type=pl.DeviceIdType.MESH
    )

    def row_grad(back, block):
        cols = pl.ds(pl.multiple_of(block * (model // 8), model // 8), model // 8)
        return contract_rows(
            x_all[:, :, cols].reshape(tokens, model // 8), back[...].reshape(tokens, width)
        )

    def col_grad(block):
        cols = pl.ds(pl.multiple_of(block * (model // 8), model // 8), model // 8)
        return contract_rows(
            hid[...].reshape(tokens, width), cot_v[:, :, cols].reshape(tokens, model // 8)
        )

    eighth, half = model // 8, model // 2

    def place(j, base):
        return pl.ds(pl.multiple_of(base + j * eighth, eighth), eighth)

    swaps = [
        send(buf.at[pl.ds(half, half), :], buf.at[pl.ds(0, half), :], sw_s.at[k], sw_r.at[k], mate, w)
        for k, buf in enumerate((wg_v, wu_v))
    ]
    swaps.append(
        send(
            wd_v.at[:, pl.ds(half, half)], wd_v.at[:, pl.ds(0, half)], sw_s.at[2], sw_r.at[2], mate, w
        )
    )

    @pl.loop(0, 4)
    def _(j):
        wg_v[place(j, half), :] = row_grad(gb, 2 * j + 1 - core).astype(BF)

    scatter.pass_on(chunks - 1)
    pl.semaphore_wait(ready, 1)
    swaps[0].start()

    @pl.loop(0, 4)
    def _(j):
        wu_v[place(j, half), :] = row_grad(ub, 2 * j + 1 - core).astype(BF)

    swaps[1].start()

    @pl.loop(0, 4)
    def _(j):
        wd_v[:, place(j, half)] = col_grad(2 * j + 1 - core).astype(BF)

    swaps[2].start()
    swaps[0].wait_recv()

    @pl.loop(0, 4)
    def _(j):
        gate_k[j // 2, lax.rem(j, 2)] = (
            row_grad(gb, 2 * j + core) + wg_v[place(j, 0), :].astype(F32)
        ).astype(BF)

    cut = width // 2
    pieces = (
        (gate_k.at[:, 1 - x], gate_go),
        (gate_k.at[:, x], gate_stay),
        (up_k.at[1 - y], up_go),
        (up_k.at[y], up_stay),
        (down_k.at[:, 1 - x, pl.ds(0, cut), :], low_go),
        (down_k.at[:, x, pl.ds(0, cut), :], low_stay),
        (down_k.at[1 - y, :, pl.ds(cut, cut), :], high_go),
        (down_k.at[y, :, pl.ds(cut, cut), :], high_stay),
    )
    puts = [
        pltpu.make_async_copy(src, dst, out_sem.at[k]) for k, (src, dst) in enumerate(pieces)
    ]
    for k in (0, 1):
        puts[k].start()
    scatter.pass_end(chunks - 1)
    swaps[1].wait_recv()

    @pl.loop(0, 4)
    def _(j):
        up_k[j // 2, lax.rem(j, 2)] = (
            row_grad(ub, 2 * j + core) + wu_v[place(j, 0), :].astype(F32)
        ).astype(BF)

    for k in (2, 3):
        puts[k].start()
    swaps[2].wait_recv()

    @pl.loop(0, 4)
    def _(j):
        down_k[j // 2, lax.rem(j, 2)] = (
            col_grad(2 * j + core) + wd_v[:, place(j, 0)].astype(F32)
        ).astype(BF)

    for k in (4, 5, 6, 7):
        puts[k].start()
    for i in range(chunks):
        scatter.finish(i, back_out)
    scatter.drain()
    gather.finish_sends()
    for k in range(3):
        swaps[k].wait_send()
    store(chunks - 2).wait()
    store(chunks - 1).wait()
    for cp in puts:
        cp.wait()


def feed_forward(mixed, cot, gate_weight, up_weight, down_weight, live):
    tokens_here, model = mixed.shape
    width = gate_weight.shape[1]
    rows, eighth, cut = tokens_here // 4, model // 8, width // 2
    hbm, vmem = pl.BlockSpec(memory_space=pl.ANY), pl.BlockSpec(memory_space=pltpu.VMEM)
    row_piece = jax.ShapeDtypeStruct((2, eighth, width), BF)
    col_piece = jax.ShapeDtypeStruct((2, cut, eighth), BF)
    dma = pltpu.SemaphoreType.DMA
    acc = pltpu.VMEM((4 * rows, width), F32)
    act = pltpu.VMEM((4, tokens_here, width), BF)
    tok = pltpu.VMEM((4, tokens_here, model), BF)
    three = pltpu.VMEM((3, tokens_here, model), BF)
    return pl.pallas_call(
        middle_kernel,
        name="feed_forward",
        out_shape=(
            jax.ShapeDtypeStruct(mixed.shape, F32),
            jax.ShapeDtypeStruct((4,) + mixed.shape, BF),
        )
        + (row_piece,) * 4
        + (col_piece,) * 4,
        in_specs=[hbm] * 5 + [vmem],
        out_specs=[vmem] + [hbm] * 9,
        scratch_shapes=[
            tok,
            tok,
            pltpu.VMEM(gate_weight.shape, BF),
            pltpu.VMEM(up_weight.shape, BF),
            pltpu.VMEM(down_weight.shape, BF),
            acc,
            acc,
            acc,
            act,
            act,
            act,
            tok,
            three,
            three,
            pltpu.VMEM((2, 4, rows, model), BF),
            pltpu.VMEM((2, 2, eighth, width), BF),
            pltpu.VMEM((2, 2, eighth, width), BF),
            pltpu.VMEM((2, 2, width, eighth), BF),
            dma((5,)),
            dma((32,)),
            dma((16,)),
            dma((24,)),
            dma((24,)),
            dma((2,)),
            dma((3,)),
            dma((3,)),
            dma((8,)),
            pltpu.SemaphoreType.REGULAR,
        ],
        compiler_params=pltpu.CompilerParams(
            collective_id=5, has_side_effects=True, vmem_limit_bytes=64 * 1024 * 1024 - 65536
        ),
    )(mixed, cot, gate_weight, up_weight, down_weight, live)


class Reduce:
    def __init__(self, me, factors, cols, x_first, bufs, sems, k):
        self.n, self.w, self.y, self.x, self.core = me
        self.left, self.right = factors
        self.cols, self.x_first = pl.ds(*cols), x_first
        self.away, self.sum, self.pair, self.one, self.two = bufs
        self.sems, self.k = sems, k
        self.rows = self.sum.shape[2]
        self.near = flip(self.n, 2) if x_first else flip(self.n, 4)
        self.next = flip(self.n, 4) if x_first else flip(self.n, 2)

    def term(self, block):
        own = pl.ds(pl.multiple_of(block * self.rows, self.rows), self.rows)
        return contract_rows(self.left[:, own], self.right[:, self.cols])

    def swap(self):
        return send(
            self.away,
            self.pair,
            self.sems[0].at[self.k],
            self.sems[1].at[self.k],
            flip(self.n, 1),
            self.w,
        )

    def before_swap(self):
        @pl.loop(0, 4)
        def _(j):
            self.away[j // 2, lax.rem(j, 2)] = self.term(2 * j + 1 - self.core).astype(BF)

        self.swap().start()

    def block(self, first, second):
        return (second, first) if self.x_first else (first, second)

    def axes(self):
        return (self.x, self.y) if self.x_first else (self.y, self.x)

    def stage(self, s):
        a, b = self.axes()
        if s == 1:
            src = self.sum.at[:, 1 - a] if self.x_first else self.sum.at[1 - a]
            dst, peer = self.one, self.near
        else:
            src = self.sum.at[self.block(a, 1 - b)]
            dst, peer = self.two, self.next
        k = 2 * self.k + s - 1
        return send(src, dst, self.sems[2].at[k], self.sems[3].at[k], peer, self.w)

    def add(self, block, other):
        step = 64 if self.rows % 64 == 0 else 48

        @pl.loop(0, self.rows // step)
        def _(i):
            r = pl.ds(pl.multiple_of(i * step, step), step)
            self.sum[block[0], block[1], r, :] = (
                self.sum[block[0], block[1], r, :] + other[r, :]
            )

    def after_swap(self):
        a, _ = self.axes()
        self.swap().wait_recv()

        @pl.loop(0, 4)
        def _(j):
            first = lax.rem(1 - a + j // 2, 2)
            y, x = self.block(first, lax.rem(j, 2))
            total = self.term(4 * y + 2 * x + self.core) + self.pair[y, x].astype(F32)
            self.sum[y, x] = total.astype(BF)

        self.stage(1).start()

    def after_one(self):
        a, b = self.axes()
        self.stage(1).wait()
        self.add(self.block(a, 1 - b), self.one.at[1 - b])
        self.stage(2).start()
        self.add(self.block(a, b), self.one.at[b])

    def after_two(self):
        a, b = self.axes()
        self.stage(2).wait()
        self.add(self.block(a, b), self.two)

    def result(self):
        return self.sum.at[self.y, self.x]


class Half:
    def __init__(self, me, kept, came, x_first, bufs, sems, k):
        self.n, self.w, self.y, self.x, self.core = me
        self.kept, self.came, self.x_first = kept, came, x_first
        self.sum, self.one, self.two = bufs
        self.sems, self.k = sems, k
        self.rows = kept.shape[1]
        self.next = flip(self.n, 4) if x_first else flip(self.n, 2)
        self.here = self.y if x_first else self.x

    def loads(self):
        return [
            pltpu.make_async_copy(self.kept, self.sum, self.sems[0].at[2 * self.k]),
            pltpu.make_async_copy(self.came, self.one, self.sems[0].at[2 * self.k + 1]),
        ]

    def stage(self):
        return send(
            self.sum.at[1 - self.here],
            self.two,
            self.sems[1].at[self.k],
            self.sems[2].at[self.k],
            self.next,
            self.w,
        )

    def add(self, block, other):
        @pl.loop(0, self.rows // 64)
        def _(i):
            r = pl.ds(pl.multiple_of(i * 64, 64), 64)
            self.sum[block, r, :] = self.sum[block, r, :] + other[r, :]

    def after_one(self):
        for cp in self.loads():
            cp.wait()
        self.add(1 - self.here, self.one.at[1 - self.here])
        self.stage().start()
        self.add(self.here, self.one.at[self.here])

    def after_two(self):
        self.stage().wait()
        self.add(self.here, self.two)

    def result(self):
        return self.sum.at[self.here]


class Spread:
    def __init__(self, item, region, sems, k):
        self.item, self.region, self.sems, self.k = item, region, sems, k
        n = item.n
        self.blocks = (n, flip(n, 2), flip(n, 4), flip(flip(n, 2), 4))

    def copy(self, kind, src, block, peer):
        k = 7 * self.k + kind
        return send(
            src, self.region(block), self.sems[0].at[k], self.sems[1].at[k], peer, self.item.w
        )

    def own(self, kind):
        n = self.item.n
        return self.copy(kind, self.item.result(), n, (flip(n, 2), flip(n, 4), flip(n, 1))[kind])

    def corner(self):
        n, b = self.item.n, self.blocks
        if self.item.x_first:
            return self.copy(3, self.region(b[2]), b[2], flip(n, 2))
        return self.copy(3, self.region(b[1]), b[1], flip(n, 4))

    def to_core(self, which):
        block = self.blocks[which]
        return self.copy(3 + which, self.region(block), block, flip(self.item.n, 1))

    def keep(self):
        return pltpu.make_async_copy(
            self.item.result(), self.region(self.item.n), self.sems[2].at[self.k]
        )

    def start(self):
        order = (1, 0, 2) if self.item.x_first else (0, 1, 2)
        for kind in order:
            self.own(kind).start()
        self.keep().start()

    def relay(self):
        first, second = (1, 0) if self.item.x_first else (0, 1)
        self.own(first).wait_recv()
        self.corner().start()
        self.to_core(1 + first).start()
        self.own(second).wait_recv()
        self.to_core(1 + second).start()

    def last(self):
        self.corner().wait_recv()
        self.to_core(3).start()

    def finish(self):
        for kind in range(2):
            self.own(kind).wait_send()
        self.own(2).wait()
        self.corner().wait_send()
        for which in range(1, 4):
            self.to_core(which).wait()
        self.keep().wait()


class Rows:
    def __init__(self, ref):
        self.ref = ref
        self.shape = (4, ref.shape[0] // 4, ref.shape[1])

    @property
    def at(self):
        return self

    def __getitem__(self, index):
        d, r, _ = index
        start = pl.multiple_of(d * self.shape[1] + r.start, r.size)
        return self.ref.at[pl.ds(start, r.size), :]


def last_kernel(items, *refs):
    refs = list(refs)

    def take(count):
        out = refs[:count]
        del refs[:count]
        return out

    factors = take(4)
    stays, comes = take(4), take(4)
    feed_terms, gain_parts = take(2)
    outs = take(4)
    gate_full, up_full, down_full = take(3)
    feed_out, gain_out = take(2)
    attn_bufs = [take(5) for _ in range(4)]
    ffn_bufs = [take(3) for _ in range(4)]
    line_bufs = [take(3) for _ in range(4)]
    feed_v, feed_left, feed_right = take(3)
    gain_in, gain_sum, gain_line = take(3)
    factor_bufs = take(4)
    load_sem, swap_s, swap_r, st_s, st_r = take(5)
    half_sems = take(3)
    sp_sems = take(3)
    lr_s, lr_r, lg_s, lg_r, lg_l = take(5)
    fd_s, fd_r, fd_l = take(3)
    gn_s, gn_r, gz_s, gz_r = take(4)

    n, w = lax.axis_index("narrow"), lax.axis_index("wide")
    me = (n, w, n // 4, lax.rem(n // 2, 2), lax.rem(n, 2))
    attn = [
        Reduce(
            me,
            factor_bufs[2 * p : 2 * p + 2],
            cols,
            xf,
            attn_bufs[k],
            (swap_s, swap_r, st_s, st_r),
            k,
        )
        for k, (p, cols, xf) in enumerate(items)
    ]
    ffn = [
        Half(me, stays[k], comes[k], k % 2 == 0, ffn_bufs[k], half_sems, k) for k in range(4)
    ]
    cut, eighth = stays[2].shape[1], stays[2].shape[2]

    def down_region(k):
        return lambda block: down_full.at[
            pl.ds(k * cut, cut), pl.ds(pl.multiple_of(block * eighth, eighth), eighth)
        ]

    regions = (
        lambda block: gate_full.at[block],
        lambda block: up_full.at[block],
        down_region(0),
        down_region(1),
    )
    spread = [Spread(ffn[k], regions[k], sp_sems, k) for k in range(4)]
    for item in ffn:
        for cp in item.loads():
            cp.start()
    factor_loads = [
        pltpu.make_async_copy(src, dst, load_sem.at[k])
        for k, (src, dst) in enumerate(zip(factors, factor_bufs))
    ]
    for cp in factor_loads:
        cp.start()
    feed_load = pltpu.make_async_copy(feed_terms, feed_v, fd_l)
    feed_load.start()

    barrier = pltpu.get_barrier_semaphore()
    narrow_peers = [lax.rem(n + i, 8) for i in range(1, 8)]
    wide_peers = [lax.rem(w + i, 4) for i in range(1, 4)]
    for peer in narrow_peers:
        pl.semaphore_signal(
            barrier, inc=1, device_id=at(peer, w), device_id_type=pl.DeviceIdType.MESH
        )
    for peer in wide_peers:
        pl.semaphore_signal(
            barrier, inc=1, device_id=at(n, peer), device_id_type=pl.DeviceIdType.MESH
        )
    pl.semaphore_wait(barrier, 10)

    feed_load.wait()
    feed = LineScatter(n, w, feed_v, (feed_left, feed_right), fd_s, fd_r, 4)
    for i in range(4):
        feed.begin(i)

    def gain_narrow(i):
        peer = narrow_peers[i]
        return send(gain_parts.at[peer], gain_in.at[i], gn_s.at[i], gn_r.at[i], peer, w)

    def gain_wide(i):
        return send(gain_sum, gain_line.at[i], gz_s.at[i], gz_r.at[i], n, wide_peers[i])

    for i in range(7):
        gain_narrow(i).start()

    for item in ffn:
        item.after_one()
    for cp in factor_loads:
        cp.wait()
    for item in attn:
        item.before_swap()
    feed.pass_on(0)
    for item in attn:
        item.after_swap()
    feed.pass_on(1)
    feed.pass_end(0)
    for i in range(7):
        gain_narrow(i).wait()
    total = gain_parts[n]
    for i in range(7):
        total = total + gain_in[i]
    gain_sum[...] = total
    for i in range(3):
        gain_wide(i).start()
    feed.pass_on(2)
    feed.pass_end(1)
    for item in attn[:2]:
        item.after_one()
    feed.pass_on(3)
    feed.pass_end(2)
    for item in attn[2:]:
        item.after_one()
    feed.pass_end(3)
    for k in range(4):
        ffn[k].after_two()
        spread[k].start()

    scatters, gathers = [], []
    for k, item in enumerate(attn):
        left, right, own = line_bufs[k]
        scatters.append(
            LineScatter(n, w, Rows(item.result()), (left, right), lr_s.at[k], lr_r.at[k], 1)
        )
        gathers.append(LineGather(n, w, own, outs[k], lg_s.at[k], lg_r.at[k], 1))

    def keep(k):
        return pltpu.make_async_copy(line_bufs[k][2], outs[k].at[w], lg_l.at[k])

    def line_turn(k):
        scatters[k].finish(0, line_bufs[k][2])
        gathers[k].start()
        keep(k).start()

    for k in range(4):
        attn[k].after_two()
        scatters[k].begin(0)
    for k in (0, 1):
        scatters[k].pass_on(0)
    for k in (0, 1):
        scatters[k].pass_end(0)
    for k in (0, 1):
        line_turn(k)
    for k in (2, 3):
        scatters[k].pass_on(0)
    for k in (0, 1):
        gathers[k].near(0)
    for k in (2, 3):
        scatters[k].pass_end(0)
    for k in (0, 1):
        spread[k].relay()
    for k in (0, 1):
        gathers[k].far(0)
    for k in (2, 3):
        line_turn(k)
    for i in range(4):
        feed.finish(i, feed_out)
    for s in spread[2:]:
        s.relay()
    for k in (2, 3):
        gathers[k].near(0)
    for k in (2, 3):
        gathers[k].far(0)
    for i in range(3):
        gain_wide(i).wait()
    gain_out[...] = (gain_sum[...] + gain_line[0]) + (gain_line[1] + gain_line[2])
    for s in spread:
        s.last()
    for s in spread:
        s.finish()
    for item in attn:
        item.swap().wait_send()
    for k in range(4):
        scatters[k].drain()
        gathers[k].finish()
        keep(k).wait()
    feed.drain()


def reduce_last(factors, stays, comes, feed_terms, gain_parts):
    rows = factors[0].shape[1] // 8
    items = []
    for p, xf in ((0, True), (0, False), (1, True), (1, False)):
        half = factors[2 * p + 1].shape[1] // 2
        items.append((p, (0 if xf else half, half), xf))
    scratch = []
    for _, (_, cols), _ in items:
        scratch += [
            pltpu.VMEM((2, 2, rows, cols), BF),
            pltpu.VMEM((2, 2, rows, cols), BF),
            pltpu.VMEM((2, 2, rows, cols), BF),
            pltpu.VMEM((2, rows, cols), BF),
            pltpu.VMEM((rows, cols), BF),
        ]
    for stay in stays:
        scratch += [
            pltpu.VMEM(stay.shape, BF),
            pltpu.VMEM(stay.shape, BF),
            pltpu.VMEM(stay.shape[1:], BF),
        ]
    outs = []
    for _, (_, cols), _ in items:
        scratch += [pltpu.VMEM((3, rows // 4, cols), BF)] * 2 + [pltpu.VMEM((rows // 4, cols), BF)]
        outs.append(jax.ShapeDtypeStruct((4, rows // 4, cols), BF))
    outs.append(jax.ShapeDtypeStruct((8,) + stays[0].shape[1:], BF))
    outs.append(jax.ShapeDtypeStruct((8,) + stays[1].shape[1:], BF))
    outs.append(jax.ShapeDtypeStruct((2 * stays[2].shape[1], 8 * stays[2].shape[2]), BF))
    outs.append(jax.ShapeDtypeStruct(feed_terms.shape[1:], F32))
    outs.append(jax.ShapeDtypeStruct(gain_parts.shape[1:], F32))
    scratch += [pltpu.VMEM(feed_terms.shape, BF)]
    scratch += [pltpu.VMEM((3,) + feed_terms.shape[1:], BF)] * 2
    scratch += [
        pltpu.VMEM((7,) + gain_parts.shape[1:], F32),
        pltpu.VMEM(gain_parts.shape[1:], F32),
        pltpu.VMEM((3,) + gain_parts.shape[1:], F32),
    ]
    scratch += [pltpu.VMEM(f.shape, BF) for f in factors]
    dma = pltpu.SemaphoreType.DMA
    scratch += [dma((4,)), dma((4,)), dma((4,)), dma((8,)), dma((8,))]
    scratch += [dma((8,)), dma((4,)), dma((4,))]
    scratch += [dma((28,)), dma((28,)), dma((4,))]
    scratch += [dma((4, 6)), dma((4, 6)), dma((4, 8)), dma((4, 4)), dma((4,))]
    scratch += [dma((24,)), dma((24,)), dma]
    scratch += [dma((7,)), dma((7,)), dma((3,)), dma((3,))]
    hbm, vmem = pl.BlockSpec(memory_space=pl.ANY), pl.BlockSpec(memory_space=pltpu.VMEM)
    out = pl.pallas_call(
        functools.partial(last_kernel, items),
        name="reduce_last",
        out_shape=tuple(outs),
        in_specs=[hbm] * 13 + [vmem],
        out_specs=[hbm] * 7 + [vmem] * 2,
        scratch_shapes=scratch,
        compiler_params=pltpu.CompilerParams(
            collective_id=4, has_side_effects=True, vmem_limit_bytes=64 * 1024 * 1024 - 65536
        ),
    )(*factors, *stays, *comes, feed_terms, gain_parts)
    qkv = jnp.concatenate([out[0].reshape(rows, -1), out[1].reshape(rows, -1)], axis=1)
    project = jnp.concatenate([out[2].reshape(rows, -1), out[3].reshape(rows, -1)], axis=1)
    width = out[4].shape[2]
    ffn = [out[4].reshape(-1, width), out[5].reshape(-1, width), out[6]]
    return qkv, project, ffn, out[7], out[8]


def per_device(
    fast,
    block_input,
    cotangent,
    query_weight,
    key_weight,
    value_weight,
    project_weight,
    prenorm_gain,
    midnorm_gain,
    gate_weight,
    up_weight,
    down_weight,
    doc_lengths,
    tile_counts,
):
    tokens_here, model = block_input.shape
    group = HEADS // KV_HEADS
    scale = HEAD_DIM ** (-0.5)
    q_cols, k_cols = HEADS * HEAD_DIM, KV_HEADS * HEAD_DIM
    inputs_f = block_input.astype(jnp.float32)
    ends = jnp.cumsum(doc_lengths[0])
    position = jnp.arange(tokens_here, dtype=jnp.int32)
    segment = jnp.sum((position[:, None] >= ends[None, :]).astype(jnp.int32), axis=1)
    allowed = (segment[:, None] == segment[None, :]) & (position[None, :] <= position[:, None])
    if fast:
        gains = jnp.stack([prenorm_gain, midnorm_gain]).astype(F32).reshape(1, -1)
        bias = jnp.where(allowed, 0.0, -1e30).astype(F32)
        qkv_full, project_full, grad_rows, normed, qkv, attended, gains_full, logs = gather_first(
            block_input,
            query_weight,
            key_weight,
            value_weight,
            project_weight,
            gains,
            cotangent,
            bias,
        )
        gains_full = gains_full.reshape(8, 2, -1)
        first_gain = gains_full[:, 0].reshape(-1)
        second_gain = gains_full[:, 1].reshape(-1)
    else:
        qkv_full = jnp.concatenate(
            [
                lax.all_gather(query_weight, "narrow", axis=0, tiled=True),
                lax.all_gather(key_weight, "narrow", axis=0, tiled=True),
                lax.all_gather(value_weight, "narrow", axis=0, tiled=True),
            ],
            axis=1,
        )
        project_full = lax.all_gather(project_weight, "narrow", axis=1, tiled=True)
        first_gain = lax.all_gather(prenorm_gain, "narrow", axis=0, tiled=True).astype(F32)
        second_gain = lax.all_gather(midnorm_gain, "narrow", axis=0, tiled=True).astype(F32)
        grad_rows = lax.all_gather(cotangent, "wide", axis=0, tiled=True)
        normed = rms_scale(inputs_f, first_gain).astype(jnp.bfloat16)
        qkv = jnp.dot(normed, qkv_full, preferred_element_type=jnp.float32).astype(jnp.bfloat16)
    if not fast:
        query_rows = qkv[:, :q_cols].reshape(tokens_here, KV_HEADS, group, HEAD_DIM)
        key_rows = qkv[:, q_cols : q_cols + k_cols].reshape(tokens_here, KV_HEADS, HEAD_DIM)
        value_rows = qkv[:, q_cols + k_cols :].reshape(tokens_here, KV_HEADS, HEAD_DIM)
        scores = (
            jnp.einsum("qcgd,kcd->cgqk", query_rows, key_rows, preferred_element_type=jnp.float32)
            * scale
        )
        masked = jnp.where(allowed, scores, -1e30)
        peak = jnp.max(masked, axis=-1, keepdims=True)
        expo = jnp.exp(masked - peak)
        total = jnp.sum(expo, axis=-1, keepdims=True)
        probs_low = (expo / total).astype(jnp.bfloat16)
        logsum = peak + jnp.log(total)
        attended = (
            jnp.einsum("cgqk,kcd->qcgd", probs_low, value_rows, preferred_element_type=jnp.float32)
            .astype(jnp.bfloat16)
            .reshape(tokens_here, HEADS * HEAD_DIM)
        )
    branch = jnp.dot(attended, project_full, preferred_element_type=jnp.float32)
    middle = inputs_f + branch
    mixed_in = rms_scale(middle, second_gain).astype(jnp.bfloat16)
    width = gate_weight.shape[1]
    wide_index = lax.axis_index("wide")
    my_count = jnp.sum(
        jnp.where(jnp.arange(tile_counts.shape[0], dtype=jnp.int32) == wide_index, tile_counts, 0)
    )
    live = (jnp.arange(width, dtype=jnp.int32) // TILE < my_count).astype(jnp.float32)
    if fast:
        mixed_back, feed_terms, *pieces = feed_forward(
            mixed_in, grad_rows, gate_weight, up_weight, down_weight, live.reshape(1, -1)
        )
        stays = pieces[1::2]
        comes = [
            lax.ppermute(piece, "narrow", [(i, i ^ bit) for i in range(8)])
            for piece, bit in zip(pieces[0::2], (2, 4, 2, 4))
        ]
    else:
        gathered = lax.all_gather(mixed_in, "wide", axis=0, tiled=True)
        gate_pre = jnp.dot(gathered, gate_weight, preferred_element_type=jnp.float32)
        up_pre = jnp.dot(gathered, up_weight, preferred_element_type=jnp.float32)
        hidden_back = contract_cols(grad_rows, down_weight)
        sigma = jax.nn.sigmoid(gate_pre)
        hidden = (gate_pre * sigma * up_pre * live).astype(BF)
        gate_back = (
            hidden_back * up_pre * live * sigma * (1.0 + gate_pre * (1.0 - sigma))
        ).astype(BF)
        up_back = (hidden_back * gate_pre * sigma * live).astype(BF)
        mixed_terms = (
            contract_cols(gate_back, gate_weight) + contract_cols(up_back, up_weight)
        ).astype(BF)
        mixed_back = lax.psum_scatter(
            mixed_terms, "wide", scatter_dimension=0, tiled=True
        ).astype(F32)
        partial_rows = jnp.dot(hidden, down_weight, preferred_element_type=jnp.float32)
        down_part = contract_rows(hidden, grad_rows)
        gate_part = contract_rows(gathered, gate_back)
        up_part = contract_rows(gathered, up_back)
    out_grad = cotangent.astype(jnp.float32)
    unused_second, second_backward = jax.vjp(rms_scale, middle, second_gain)
    middle_norm_back, second_gain_part = second_backward(mixed_back)
    middle_back = out_grad + middle_norm_back
    branch_back = middle_back.astype(jnp.bfloat16)
    attended_back = contract_cols(branch_back, project_full).astype(jnp.bfloat16)
    if fast:
        qkv_back = attention_back(qkv, attended_back, logs, bias)
    else:
        attended_back = attended_back.reshape(tokens_here, KV_HEADS, group, HEAD_DIM)
        scores_again = (
            jnp.einsum("qcgd,kcd->cgqk", query_rows, key_rows, preferred_element_type=jnp.float32)
            * scale
        )
        probs_again = jnp.where(allowed, jnp.exp(scores_again - logsum), 0.0)
        probs_again_low = probs_again.astype(jnp.bfloat16)
        value_back = (
            jnp.einsum(
                "cgqk,qcgd->kcd", probs_again_low, attended_back, preferred_element_type=jnp.float32
            )
            .astype(jnp.bfloat16)
            .reshape(tokens_here, KV_HEADS * HEAD_DIM)
        )
        probs_back = jnp.einsum(
            "qcgd,kcd->cgqk", attended_back, value_rows, preferred_element_type=jnp.float32
        )
        scores_back = (
            probs_again * (probs_back - jnp.sum(probs_again * probs_back, axis=-1, keepdims=True))
        ).astype(jnp.bfloat16)
        query_back = (
            (
                jnp.einsum("cgqk,kcd->qcgd", scores_back, key_rows, preferred_element_type=jnp.float32)
                * scale
            )
            .astype(jnp.bfloat16)
            .reshape(tokens_here, HEADS * HEAD_DIM)
        )
        key_back = (
            (
                jnp.einsum(
                    "cgqk,qcgd->kcd", scores_back, query_rows, preferred_element_type=jnp.float32
                )
                * scale
            )
            .astype(jnp.bfloat16)
            .reshape(tokens_here, KV_HEADS * HEAD_DIM)
        )
        qkv_back = jnp.concatenate([query_back, key_back, value_back], axis=1)
    normed_back = contract_cols(qkv_back, qkv_full)
    unused_first, first_backward = jax.vjp(rms_scale, inputs_f, first_gain)
    input_norm_back, first_gain_part = first_backward(normed_back)
    input_grad = (middle_back + input_norm_back).astype(jnp.bfloat16)

    if fast:
        gain_parts = jnp.stack(
            [first_gain_part.reshape(8, -1), second_gain_part.reshape(8, -1)], axis=1
        ).reshape(8, 1, -1)
        input_grad, qkv_back = lax.optimization_barrier((input_grad, qkv_back))
        qkv_total, project_total, ffn_totals, feed, gain_total = reduce_last(
            (normed, qkv_back, branch_back, attended),
            stays,
            comes,
            feed_terms,
            gain_parts,
        )
        gain_total = gain_total.reshape(2, -1)
        first_total, second_total = gain_total[0], gain_total[1]
        qkv_total = qkv_total.astype(F32)
        project_total = project_total.T.astype(F32)
        gate_total, up_total, down_total = [t.astype(F32) for t in ffn_totals]
    else:

        def owned(part):
            share = lax.psum_scatter(part.astype(BF), "narrow", scatter_dimension=0, tiled=True)
            return lax.psum(share, "wide").astype(F32)

        qkv_total = owned(contract_rows(normed, qkv_back))
        project_total = owned(contract_rows(branch_back, attended)).T
        first_total = owned(first_gain_part)
        second_total = owned(second_gain_part)
        gate_total, up_total, down_total = (
            lax.psum(gate_part.astype(BF), "narrow").astype(F32),
            lax.psum(up_part.astype(BF), "narrow").astype(F32),
            lax.psum(down_part.astype(BF), "narrow").astype(F32),
        )
        feed = lax.psum_scatter(
            partial_rows.astype(BF), "wide", scatter_dimension=0, tiled=True
        ).astype(F32)
    block_output = (middle + feed).astype(BF)
    return (
        block_output,
        input_grad,
        qkv_total[:, :q_cols],
        qkv_total[:, q_cols : q_cols + k_cols],
        qkv_total[:, q_cols + k_cols :],
        project_total,
        first_total,
        second_total,
        gate_total,
        up_total,
        down_total,
    )


def solution(mesh):
    fast = mesh.shape["narrow"] == 8 and mesh.shape["wide"] == 4
    placed = (
        P(("narrow", "wide"), None),
        P(("narrow", "wide"), None),
        P("narrow", None),
        P("narrow", None),
        P("narrow", None),
        P(None, "narrow"),
        P("narrow"),
        P("narrow"),
        P(None, "wide"),
        P(None, "wide"),
        P("wide", None),
        P(("narrow", "wide"), None),
        P(),
    )
    return jax.shard_map(
        functools.partial(per_device, fast),
        mesh=mesh,
        in_specs=placed,
        out_specs=(
            P(("narrow", "wide"), None),
            P(("narrow", "wide"), None),
            P("narrow", None),
            P("narrow", None),
            P("narrow", None),
            P(None, "narrow"),
            P("narrow"),
            P("narrow"),
            P(None, "wide"),
            P(None, "wide"),
            P("wide", None),
        ),
        check_vma=False,
    )
```

```python
import functools

import jax
import jax.numpy as jnp
from jax import lax
from jax.experimental import pallas as pl
from jax.experimental.pallas import tpu as pltpu
from jax.sharding import PartitionSpec as P

HEADS = 24
KV_HEADS = 6
HEAD_DIM = 64
TILE = 128


EPSILON = 1e-06

BF = jnp.bfloat16
F32 = jnp.float32


def rms_scale(rows, gain):
    factor = lax.rsqrt(jnp.mean(rows * rows, axis=-1, keepdims=True) + EPSILON)
    return rows * factor * gain


def contract_rows(left, right):
    return lax.dot_general(
        left, right, (((0,), (0,)), ((), ())), preferred_element_type=jnp.float32
    )


def contract_cols(left, right):
    return lax.dot_general(
        left, right, (((1,), (1,)), ((), ())), preferred_element_type=jnp.float32
    )


def flip(n, bit):
    return n + bit - 2 * bit * lax.rem(n // bit, 2)


def at(n, w):
    return {"narrow": n, "wide": w}


def send(src, dst, ssem, rsem, n, w):
    return pltpu.make_async_remote_copy(
        src_ref=src,
        dst_ref=dst,
        send_sem=ssem,
        recv_sem=rsem,
        device_id=at(n, w),
        device_id_type=pl.DeviceIdType.MESH,
    )


def greet(narrow_peers, n, w, line):
    barrier = pltpu.get_barrier_semaphore()
    for peer in narrow_peers:
        pl.semaphore_signal(
            barrier, inc=1, device_id=at(peer, w), device_id_type=pl.DeviceIdType.MESH
        )
    if not line:
        pl.semaphore_wait(barrier, len(narrow_peers))
    if line:

        @pl.when(w > 0)
        def _():
            pl.semaphore_signal(
                barrier, inc=1, device_id=at(n, w - 1), device_id_type=pl.DeviceIdType.MESH
            )

        @pl.when(w < 3)
        def _():
            pl.semaphore_signal(
                barrier, inc=1, device_id=at(n, w + 1), device_id_type=pl.DeviceIdType.MESH
            )

        @pl.when((w == 0) | (w == 3))
        def _():
            pl.semaphore_wait(barrier, len(narrow_peers) + 1)

        @pl.when((w == 1) | (w == 2))
        def _():
            pl.semaphore_wait(barrier, len(narrow_peers) + 2)


class LineGather:
    def __init__(self, n, w, own, whole, ssem, rsem, chunks):
        self.n, self.w, self.own, self.whole = n, w, own, whole
        self.ssem, self.rsem, self.chunks = ssem, rsem, chunks
        self.rows = own.shape[0] // chunks

    def span(self, i):
        return pl.ds(pl.multiple_of(i * self.rows, self.rows), self.rows)

    def part(self, shard, i):
        return self.whole.at[shard, self.span(i), :]

    def put(self, way, here, shard, i):
        src = self.own.at[self.span(i), :] if shard is here else self.part(shard, i)
        to = here + 1 - 2 * way
        s = (way * 4 + shard) * self.chunks + i
        r = shard * self.chunks + i
        return send(src, self.part(shard, i), self.ssem.at[s], self.rsem.at[r], self.n, to)

    def came(self, shard, i):
        self.put(0, 0, shard, i).wait_recv()

    def start_chunk(self, i):
        @pl.when(self.w < 3)
        def _():
            self.put(0, self.w, self.w, i).start()

        @pl.when(self.w > 0)
        def _():
            self.put(1, self.w, self.w, i).start()

    def start(self):
        for i in range(self.chunks):
            self.start_chunk(i)

    def near(self, i):
        @pl.when(self.w == 1)
        def _():
            self.came(0, i)
            self.put(0, 1, 0, i).start()
            self.came(2, i)
            self.put(1, 1, 2, i).start()

        @pl.when(self.w == 2)
        def _():
            self.came(3, i)
            self.put(1, 2, 3, i).start()
            self.came(1, i)
            self.put(0, 2, 1, i).start()

    def far(self, i):
        @pl.when(self.w == 1)
        def _():
            self.came(3, i)
            self.put(1, 1, 3, i).start()

        @pl.when(self.w == 2)
        def _():
            self.came(0, i)
            self.put(0, 2, 0, i).start()

    def ready(self, i):
        @pl.when(self.w == 0)
        def _():
            for shard in (1, 2, 3):
                self.came(shard, i)

        @pl.when(self.w == 3)
        def _():
            for shard in (2, 1, 0):
                self.came(shard, i)

    def finish_sends(self):
        for here in range(4):

            @pl.when(self.w == here)
            def _():
                for i in range(self.chunks):
                    if here < 3:
                        for shard in range(here + 1):
                            self.put(0, here, shard, i).wait_send()
                    if here > 0:
                        for shard in range(here, 4):
                            self.put(1, here, shard, i).wait_send()

    def finish(self):
        for i in range(self.chunks):
            self.ready(i)
        self.finish_sends()


def first_kernel(
    x_ref,
    q_ref,
    k_ref,
    v_ref,
    p_ref,
    g_ref,
    c_ref,
    docs_ref,
    qkv_out,
    p_full,
    c_full,
    normed_out,
    rows_out,
    att_out,
    gain_row,
    gain_late,
    bias_ref,
    log_out,
    g_full,
    qkv_full,
    p_buf,
    c_buf,
    x_buf,
    normed,
    qkv,
    att,
    in_sem,
    out_sem,
    ssem,
    rsem,
    gs_sem,
    gr_sem,
    zs_sem,
    zr_sem,
):
    n, w = lax.axis_index("narrow"), lax.axis_index("wide")
    x, y, c, d = flip(n, 2), flip(n, 4), flip(n, 1), flip(flip(n, 2), 4)
    others = [lax.rem(n + i, 8) for i in range(1, 8)]
    rows = q_ref.shape[0]
    half = rows // 2
    depth = p_ref.shape[0]
    qc, kc = q_ref.shape[1], k_ref.shape[1]
    cols = ((0, qc), (qc, kc), (qc + kc, kc))

    def region(t, block, h):
        if t == 3:
            r = pl.ds(0, depth) if h == 2 else pl.ds(h * (depth // 2), depth // 2)
            return p_full.at[r, pl.ds(pl.multiple_of(block * rows, rows), rows)]
        start = pl.multiple_of(block * rows, rows)
        r = pl.ds(start, rows) if h == 2 else pl.ds(start + h * half, half)
        return qkv_full.at[r, pl.ds(cols[t][0], cols[t][1])]

    locals_in = []
    for i, (src, dst) in enumerate(
        (
            (g_ref, g_full.at[n]),
            (x_ref, x_buf),
            (p_ref, p_buf),
            (c_ref, c_buf),
            (q_ref, region(0, n, 2)),
            (k_ref, region(1, n, 2)),
            (v_ref, region(2, n, 2)),
        )
    ):
        cp = pltpu.make_async_copy(src, dst, in_sem.at[i])
        cp.start()
        locals_in.append(cp)

    greet(others, n, w, True)

    def own(t, h):
        ref = (q_ref, k_ref, v_ref, p_ref)[t]
        if h == 2:
            return ref
        size = ref.shape[0] // 2
        return ref.at[pl.ds(h * size, size), :]

    def msg(t, kind, src, block, h, peer):
        k = t * 10 + kind
        return send(src, region(t, block, h), ssem.at[k], rsem.at[k], peer, w)

    def to_x(t, h):
        return msg(t, h, own(t, h), n, h, x)

    def to_y(t, h):
        return msg(t, 2 + h, own(t, h), n, h, y)

    def on_x(t):
        return msg(t, 4, region(t, y, 0), y, 0, x)

    def on_y(t):
        return msg(t, 5, region(t, x, 1), x, 1, y)

    def to_c(t, which):
        block = (n, x, y, d)[which]
        src = own(t, 2) if which == 0 else region(t, block, 2)
        return msg(t, 6 + which, src, block, 2, c)

    def start_own(t):
        to_x(t, 1).start()
        to_y(t, 0).start()
        to_x(t, 0).start()
        to_y(t, 1).start()

    def gain(i):
        return send(g_ref, g_full.at[n], gs_sem.at[i], gr_sem.at[i], others[i], w)

    line = LineGather(n, w, c_ref, c_full, zs_sem, zr_sem, 4)
    for i in range(7):
        gain(i).start()
    start_own(0)
    line.start()
    for t in (1, 2):
        start_own(t)
    for t in range(3):
        to_c(t, 0).start()

    locals_out = []

    def put(src, dst):
        cp = pltpu.make_async_copy(src, dst, out_sem.at[len(locals_out)])
        cp.start()
        locals_out.append(cp)

    for i in range(7):
        gain(i).wait()
    for cp in locals_in:
        cp.wait()
    put(p_buf, region(3, n, 2))
    put(c_buf, c_full.at[w])
    for k in range(8):
        gain_row[:, pl.ds(k * rows, rows)] = g_full[k, :, :rows]
        gain_late[:, pl.ds(k * rows, rows)] = g_full[k, :, rows:]
    strip = 16

    @pl.loop(0, x_buf.shape[0] // strip)
    def _(i):
        s = pl.ds(pl.multiple_of(i * strip, strip), strip)
        normed[s, :] = rms_scale(x_buf[s, :].astype(F32), gain_row[...]).astype(BF)

    put(normed, normed_out)

    docs = docs_ref[...]
    late = lax.broadcasted_iota(jnp.int32, bias_ref.shape, 0)
    early = lax.broadcasted_iota(jnp.int32, bias_ref.shape, 1)
    end = docs[:, :1]
    late_doc = jnp.where(late >= end, 1, 0)
    early_doc = jnp.where(early >= end, 1, 0)
    for k in range(1, docs.shape[1]):
        end = end + docs[:, k : k + 1]
        late_doc = late_doc + jnp.where(late >= end, 1, 0)
        early_doc = early_doc + jnp.where(early >= end, 1, 0)
    allowed = (late_doc == early_doc) & (early <= late)
    bias_ref[...] = jnp.where(allowed, 0.0, -1e30)

    def relay(t):
        to_y(t, 0).wait_recv()
        on_x(t).start()
        to_x(t, 1).wait_recv()
        on_y(t).start()
        to_x(t, 0).wait_recv()
        to_c(t, 1).start()
        to_y(t, 1).wait_recv()
        to_c(t, 2).start()

    def corner(t):
        on_x(t).wait_recv()
        on_y(t).wait_recv()
        to_c(t, 3).start()

    line.near(0)
    relay(0)
    line.near(1)
    relay(1)
    line.near(2)
    relay(2)
    start_own(3)
    to_c(3, 0).start()
    line.near(3)
    line.far(0)
    line.far(1)
    for t in range(3):
        corner(t)
    line.far(2)
    for t in range(3):
        for which in range(4):
            to_c(t, which).wait_recv()
    put(qkv_full, qkv_out)
    tile = 256

    @pl.loop(0, qkv.shape[1] // tile)
    def _(i):
        s = pl.ds(pl.multiple_of(i * tile, tile), tile)
        qkv[:, s] = jnp.dot(normed[...], qkv_full[:, s], preferred_element_type=F32).astype(BF)

    put(qkv, rows_out)
    line.far(3)

    log_out[...] = jnp.zeros(log_out.shape, F32)
    pair = 2 * HEAD_DIM
    group = HEADS // KV_HEADS

    @pl.loop(0, KV_HEADS // 2)
    def _(i):
        keys = qkv[:, pl.ds(pl.multiple_of(qc + i * pair, pair), pair)]
        values = qkv[:, pl.ds(pl.multiple_of(qc + kc + i * pair, pair), pair)]
        lane = lax.broadcasted_iota(jnp.int32, log_out.shape, 1)
        for b in range(group):
            at_cols = pl.ds(pl.multiple_of((i * group + b) * pair, pair), pair)
            queries = qkv[:, at_cols]
            side = (2 * b) // group
            key = keys[:, side * HEAD_DIM : (side + 1) * HEAD_DIM]
            value = values[:, side * HEAD_DIM : (side + 1) * HEAD_DIM]
            heads = []
            for e in range(2):
                query = queries[:, e * HEAD_DIM : (e + 1) * HEAD_DIM]
                masked = contract_cols(query, key) * (HEAD_DIM**-0.5) + bias_ref[...]
                peak = jnp.max(masked, axis=-1, keepdims=True)
                expo = jnp.exp(masked - peak)
                total = jnp.sum(expo, axis=-1, keepdims=True)
                probs = (expo * (1.0 / total)).astype(BF)
                heads.append(jnp.dot(probs, value, preferred_element_type=F32))
                log_out[...] = jnp.where(
                    lane == 2 * (i * group + b) + e, peak + jnp.log(total), log_out[...]
                )
            att[:, at_cols] = jnp.concatenate(heads, axis=1).astype(BF)

    put(att, att_out)
    relay(3)
    corner(3)
    for t in range(4):
        for h in range(2):
            to_x(t, h).wait_send()
            to_y(t, h).wait_send()
        on_x(t).wait_send()
        on_y(t).wait_send()
        for which in range(4):
            if t == 3:
                to_c(t, which).wait_recv()
            to_c(t, which).wait_send()
    line.finish()
    for cp in locals_out:
        cp.wait()


def gather_first(rows_in, query, key, value, project, gains, cotangent, docs):
    rows = query.shape[0]
    width = query.shape[1] + 2 * key.shape[1]
    tokens_here, model = rows_in.shape
    hbm, vmem = pl.BlockSpec(memory_space=pl.ANY), pl.BlockSpec(memory_space=pltpu.VMEM)
    return pl.pallas_call(
        first_kernel,
        name="gather_first",
        out_shape=(
            jax.ShapeDtypeStruct((8 * rows, width), BF),
            jax.ShapeDtypeStruct((project.shape[0], 8 * rows), BF),
            jax.ShapeDtypeStruct((4,) + cotangent.shape, BF),
            jax.ShapeDtypeStruct((tokens_here, model), BF),
            jax.ShapeDtypeStruct((tokens_here, width), BF),
            jax.ShapeDtypeStruct((tokens_here, query.shape[1]), BF),
            jax.ShapeDtypeStruct((1, model), F32),
            jax.ShapeDtypeStruct((1, model), F32),
            jax.ShapeDtypeStruct((tokens_here, tokens_here), F32),
            jax.ShapeDtypeStruct((tokens_here, 128), F32),
        ),
        in_specs=[hbm] * 7 + [vmem],
        out_specs=[hbm] * 6 + [vmem] * 4,
        scratch_shapes=[
            pltpu.VMEM((8,) + gains.shape, gains.dtype),
            pltpu.VMEM((8 * rows, width), BF),
            pltpu.VMEM(project.shape, BF),
            pltpu.VMEM(cotangent.shape, BF),
            pltpu.VMEM((tokens_here, model), BF),
            pltpu.VMEM((tokens_here, model), BF),
            pltpu.VMEM((tokens_here, width), BF),
            pltpu.VMEM((tokens_here, query.shape[1]), BF),
            pltpu.SemaphoreType.DMA((7,)),
            pltpu.SemaphoreType.DMA((6,)),
            pltpu.SemaphoreType.DMA((40,)),
            pltpu.SemaphoreType.DMA((40,)),
            pltpu.SemaphoreType.DMA((7,)),
            pltpu.SemaphoreType.DMA((7,)),
            pltpu.SemaphoreType.DMA((32,)),
            pltpu.SemaphoreType.DMA((16,)),
        ],
        compiler_params=pltpu.CompilerParams(collective_id=1, has_side_effects=True),
    )(rows_in, query, key, value, project, gains, cotangent, docs)


def attention_back_kernel(qkv, back, logs, bias, out):
    q_cols, k_cols = HEADS * HEAD_DIM, KV_HEADS * HEAD_DIM
    pair = 2 * HEAD_DIM
    group = HEADS // KV_HEADS
    scale = HEAD_DIM**-0.5

    @pl.loop(0, KV_HEADS // 2)
    def _(i):
        key_at = pl.ds(pl.multiple_of(q_cols + i * pair, pair), pair)
        value_at = pl.ds(pl.multiple_of(q_cols + k_cols + i * pair, pair), pair)
        keys, values = qkv[:, key_at], qkv[:, value_at]
        lane = lax.broadcasted_iota(jnp.int32, logs.shape, 1)
        key_backs, value_backs = [], []
        for side in range(2):
            key = keys[:, side * HEAD_DIM : (side + 1) * HEAD_DIM]
            value = values[:, side * HEAD_DIM : (side + 1) * HEAD_DIM]
            key_back = jnp.zeros(key.shape, F32)
            value_back = jnp.zeros(key.shape, F32)
            for b in range(side * group // 2, (side + 1) * group // 2):
                at_cols = pl.ds(pl.multiple_of((i * group + b) * pair, pair), pair)
                queries, backs = qkv[:, at_cols], back[:, at_cols]
                heads = []
                for e in range(2):
                    query = queries[:, e * HEAD_DIM : (e + 1) * HEAD_DIM]
                    given = backs[:, e * HEAD_DIM : (e + 1) * HEAD_DIM]
                    logsum = jnp.sum(
                        jnp.where(lane == 2 * (i * group + b) + e, logs[...], 0.0),
                        axis=-1,
                        keepdims=True,
                    )
                    probs = jnp.exp(contract_cols(query, key) * scale + bias[...] - logsum)
                    value_back = value_back + contract_rows(probs.astype(BF), given)
                    probs_back = contract_cols(given, value)
                    inner = jnp.sum(probs * probs_back, axis=-1, keepdims=True)
                    scores_back = (probs * (probs_back - inner)).astype(BF)
                    heads.append(jnp.dot(scores_back, key, preferred_element_type=F32) * scale)
                    key_back = key_back + contract_rows(scores_back, query)
                out[:, at_cols] = jnp.concatenate(heads, axis=1).astype(BF)
            key_backs.append(key_back * scale)
            value_backs.append(value_back)
        out[:, key_at] = jnp.concatenate(key_backs, axis=1).astype(BF)
        out[:, value_at] = jnp.concatenate(value_backs, axis=1).astype(BF)


def attention_back(qkv, back, logs, bias):
    vmem = pl.BlockSpec(memory_space=pltpu.VMEM)
    heads = HEADS * qkv.shape[0] * qkv.shape[0]
    return pl.pallas_call(
        attention_back_kernel,
        name="attention_back",
        out_shape=jax.ShapeDtypeStruct(qkv.shape, BF),
        in_specs=[vmem] * 4,
        out_specs=vmem,
        cost_estimate=pl.CostEstimate(
            flops=10 * heads * HEAD_DIM, bytes_accessed=8 * qkv.size, transcendentals=heads
        ),
    )(qkv, back, logs, bias)


class LineScatter:
    def __init__(self, n, w, terms, bufs, ssem, rsem, chunks):
        self.n, self.w, self.terms, self.bufs = n, w, terms, bufs
        self.ssem, self.rsem, self.chunks = ssem, rsem, chunks
        self.rows = terms.shape[1] // chunks

    def span(self, i):
        return pl.ds(pl.multiple_of(i * self.rows, self.rows), self.rows)

    def term(self, d, i):
        return self.terms.at[d, self.span(i), :]

    def slot(self, way, slot, i):
        return self.bufs[way].at[slot, self.span(i), :]

    def put(self, way, here, d, i, src):
        slot = d - here - 1 if way == 0 else here - 1 - d
        k = (way * 3 + slot) * self.chunks + i
        to = here + 1 - 2 * way
        return send(src, self.slot(way, slot, i), self.ssem.at[k], self.rsem.at[k], self.n, to)

    def came(self, way, slot, i):
        k = (way * 3 + slot) * self.chunks + i
        ref = self.slot(way, slot, i)
        send(ref, ref, self.ssem.at[k], self.rsem.at[k], self.n, 1).wait_recv()

    def begin(self, i):
        for here, way in ((0, 0), (3, 1)):

            @pl.when(self.w == here)
            def _():
                for d in (3, 2, 1) if way == 0 else (0, 1, 2):
                    self.put(way, here, d, i, self.term(d, i)).start()

    def join(self, way, here, d, i):
        slot = d - here if way == 0 else here - d
        self.came(way, slot, i)
        mine, sum_ = self.term(d, i), self.slot(way, slot, i)
        sum_[...] = (mine[...].astype(F32) + sum_[...].astype(F32)).astype(BF)
        self.put(way, here, d, i, sum_).start()

    def pass_on(self, i):
        @pl.when(self.w == 1)
        def _():
            self.join(0, 1, 3, i)
            self.join(0, 1, 2, i)

        @pl.when(self.w == 2)
        def _():
            self.join(1, 2, 0, i)
            self.join(1, 2, 1, i)

    def pass_end(self, i):
        @pl.when(self.w == 1)
        def _():
            self.join(1, 1, 0, i)

        @pl.when(self.w == 2)
        def _():
            self.join(0, 2, 3, i)

    def finish(self, i, out):
        for here, ways in ((0, (1,)), (1, (0, 1)), (2, (0, 1)), (3, (0,))):

            @pl.when(self.w == here)
            def _():
                for way in ways:
                    self.came(way, 0, i)
                total = self.term(here, i)[...].astype(F32)
                for way in ways:
                    total = total + self.slot(way, 0, i)[...].astype(F32)
                out[self.span(i), :] = total.astype(out.dtype)

    def drain(self):
        sent = {
            0: ((0, 3), (0, 2), (0, 1)),
            1: ((0, 3), (0, 2), (1, 0)),
            2: ((1, 0), (1, 1), (0, 3)),
            3: ((1, 0), (1, 1), (1, 2)),
        }
        for here in range(4):

            @pl.when(self.w == here)
            def _():
                for i in range(self.chunks):
                    for way, d in sent[here]:
                        self.put(way, here, d, i, self.term(d, i)).wait_send()


def middle_kernel(
    mixed,
    cot,
    wg,
    wu,
    wd,
    counts,
    back_out,
    partial_out,
    gate_go,
    gate_stay,
    up_go,
    up_stay,
    low_go,
    low_stay,
    high_go,
    high_stay,
    x_all,
    cot_v,
    wg_v,
    wu_v,
    wd_v,
    gate_f,
    up_f,
    back_f,
    hid,
    gb,
    ub,
    terms,
    from_left,
    from_right,
    part_buf,
    gate_k,
    up_k,
    down_k,
    in_sem,
    ag_s,
    ag_r,
    rs_s,
    rs_r,
    part_sem,
    sw_s,
    sw_r,
    out_sem,
    ready,
    live,
):
    n, w = lax.axis_index("narrow"), lax.axis_index("wide")
    y, x, core = n // 4, lax.rem(n // 2, 2), lax.rem(n, 2)
    mate = flip(n, 1)
    chunks = 4
    rows = mixed.shape[0] // chunks
    tokens, model = 4 * mixed.shape[0], mixed.shape[1]
    width = wg.shape[1]
    batch = 4 * rows
    loads = [
        pltpu.make_async_copy(src, dst, in_sem.at[k])
        for k, (src, dst) in enumerate(
            ((mixed, x_all.at[w]), (wg, wg_v), (wu, wu_v), (cot, cot_v), (wd, wd_v))
        )
    ]
    for cp in loads:
        cp.start()
    greet([mate], n, w, True)

    gather = LineGather(n, w, mixed, x_all, ag_s, ag_r, chunks)
    scatter = LineScatter(n, w, terms, (from_left, from_right), rs_s, rs_r, chunks)
    gather.start_chunk(0)
    gather.start_chunk(1)
    here = lax.broadcasted_iota(jnp.int32, counts.shape, 1) == w
    count = jnp.sum(jnp.where(here, counts[...].astype(F32), 0.0), axis=-1, keepdims=True)
    slot = lax.broadcasted_iota(jnp.int32, live.shape, 1) // TILE
    live[...] = jnp.where(slot.astype(F32) < count, 1.0, 0.0)
    gather.near(0)
    gather.far(0)
    for cp in loads:
        cp.wait()

    def rows_of(ref, i):
        r = pl.ds(pl.multiple_of(i * rows, rows), rows)
        return ref[:, r, :].reshape(batch, ref.shape[2])

    def store(i):
        return pltpu.make_async_copy(
            part_buf.at[lax.rem(i, 2)],
            partial_out.at[:, pl.ds(pl.multiple_of(i * rows, rows), rows), :],
            part_sem.at[lax.rem(i, 2)],
        )

    @pl.loop(0, chunks)
    def _(i):
        r = pl.ds(pl.multiple_of(i * rows, rows), rows)
        gather.ready(i)
        xs = rows_of(x_all, i)
        gate_f[...] = jnp.dot(xs, wg_v[...], preferred_element_type=F32)
        up_f[...] = jnp.dot(xs, wu_v[...], preferred_element_type=F32)

        @pl.when(i < chunks - 1)
        def _():
            gather.near(i + 1)

        @pl.when(i < chunks - 2)
        def _():
            gather.start_chunk(i + 2)

        back_f[...] = contract_cols(rows_of(cot_v, i), wd_v[...])
        step = 16

        @pl.loop(0, batch // step)
        def _(t):
            s = pl.ds(pl.multiple_of(t * step, step), step)
            d = t // (rows // step)
            into = pl.ds(
                pl.multiple_of(i * rows + lax.rem(t, rows // step) * step, step), step
            )
            gate, up = gate_f[s, :], up_f[s, :] * live[...]
            sigma = jax.nn.sigmoid(gate)
            silu = gate * sigma
            hid[d, into, :] = (silu * up).astype(BF)
            back = back_f[s, :]
            gb[d, into, :] = (back * up * sigma * (1.0 + gate * (1.0 - sigma))).astype(BF)
            ub[d, into, :] = (back * silu * live[...]).astype(BF)

        @pl.when(i > 0)
        def _():
            scatter.pass_on(i - 1)

        @pl.when(i < chunks - 1)
        def _():
            gather.far(i + 1)

        terms[:, r, :] = (
            (contract_cols(rows_of(gb, i), wg_v[...]) + contract_cols(rows_of(ub, i), wu_v[...]))
            .astype(BF)
            .reshape(4, rows, model)
        )
        scatter.begin(i)

        @pl.when(i > 1)
        def _():
            store(i - 2).wait()

        part_buf[lax.rem(i, 2)] = (
            jnp.dot(rows_of(hid, i), wd_v[...], preferred_element_type=F32)
            .astype(BF)
            .reshape(4, rows, model)
        )
        store(i).start()

        @pl.when(i > 0)
        def _():
            scatter.pass_end(i - 1)

    pl.semaphore_signal(
        ready, inc=1, device_id=at(mate, w), device_id_type=pl.DeviceIdType.MESH
    )

    def row_grad(back, block):
        cols = pl.ds(pl.multiple_of(block * (model // 8), model // 8), model // 8)
        return contract_rows(
            x_all[:, :, cols].reshape(tokens, model // 8), back[...].reshape(tokens, width)
        )

    def col_grad(block):
        cols = pl.ds(pl.multiple_of(block * (model // 8), model // 8), model // 8)
        return contract_rows(
            hid[...].reshape(tokens, width), cot_v[:, :, cols].reshape(tokens, model // 8)
        )

    eighth, half = model // 8, model // 2

    def place(j, base):
        return pl.ds(pl.multiple_of(base + j * eighth, eighth), eighth)

    swaps = [
        send(buf.at[pl.ds(half, half), :], buf.at[pl.ds(0, half), :], sw_s.at[k], sw_r.at[k], mate, w)
        for k, buf in enumerate((wg_v, wu_v))
    ]
    swaps.append(
        send(
            wd_v.at[:, pl.ds(half, half)], wd_v.at[:, pl.ds(0, half)], sw_s.at[2], sw_r.at[2], mate, w
        )
    )

    @pl.loop(0, 4)
    def _(j):
        wg_v[place(j, half), :] = row_grad(gb, 2 * j + 1 - core).astype(BF)

    scatter.pass_on(chunks - 1)
    pl.semaphore_wait(ready, 1)
    swaps[0].start()

    @pl.loop(0, 4)
    def _(j):
        wu_v[place(j, half), :] = row_grad(ub, 2 * j + 1 - core).astype(BF)

    swaps[1].start()

    @pl.loop(0, 4)
    def _(j):
        wd_v[:, place(j, half)] = col_grad(2 * j + 1 - core).astype(BF)

    swaps[2].start()
    swaps[0].wait_recv()

    @pl.loop(0, 4)
    def _(j):
        gate_k[j // 2, lax.rem(j, 2)] = (
            row_grad(gb, 2 * j + core) + wg_v[place(j, 0), :].astype(F32)
        ).astype(BF)

    cut = width // 2
    pieces = (
        (gate_k.at[:, 1 - x], gate_go),
        (gate_k.at[:, x], gate_stay),
        (up_k.at[1 - y], up_go),
        (up_k.at[y], up_stay),
        (down_k.at[:, 1 - x, pl.ds(0, cut), :], low_go),
        (down_k.at[:, x, pl.ds(0, cut), :], low_stay),
        (down_k.at[1 - y, :, pl.ds(cut, cut), :], high_go),
        (down_k.at[y, :, pl.ds(cut, cut), :], high_stay),
    )
    puts = [
        pltpu.make_async_copy(src, dst, out_sem.at[k]) for k, (src, dst) in enumerate(pieces)
    ]
    for k in (0, 1):
        puts[k].start()
    scatter.pass_end(chunks - 1)
    swaps[1].wait_recv()

    @pl.loop(0, 4)
    def _(j):
        up_k[j // 2, lax.rem(j, 2)] = (
            row_grad(ub, 2 * j + core) + wu_v[place(j, 0), :].astype(F32)
        ).astype(BF)

    for k in (2, 3):
        puts[k].start()
    swaps[2].wait_recv()

    @pl.loop(0, 4)
    def _(j):
        down_k[j // 2, lax.rem(j, 2)] = (
            col_grad(2 * j + core) + wd_v[:, place(j, 0)].astype(F32)
        ).astype(BF)

    for k in (4, 5, 6, 7):
        puts[k].start()
    for i in range(chunks):
        scatter.finish(i, back_out)
    scatter.drain()
    gather.finish_sends()
    for k in range(3):
        swaps[k].wait_send()
    store(chunks - 2).wait()
    store(chunks - 1).wait()
    for cp in puts:
        cp.wait()


def feed_forward(mixed, cot, gate_weight, up_weight, down_weight, counts):
    tokens_here, model = mixed.shape
    width = gate_weight.shape[1]
    rows, eighth, cut = tokens_here // 4, model // 8, width // 2
    hbm, vmem = pl.BlockSpec(memory_space=pl.ANY), pl.BlockSpec(memory_space=pltpu.VMEM)
    row_piece = jax.ShapeDtypeStruct((2, eighth, width), BF)
    col_piece = jax.ShapeDtypeStruct((2, cut, eighth), BF)
    dma = pltpu.SemaphoreType.DMA
    acc = pltpu.VMEM((4 * rows, width), F32)
    act = pltpu.VMEM((4, tokens_here, width), BF)
    tok = pltpu.VMEM((4, tokens_here, model), BF)
    three = pltpu.VMEM((3, tokens_here, model), BF)
    return pl.pallas_call(
        middle_kernel,
        name="feed_forward",
        out_shape=(
            jax.ShapeDtypeStruct(mixed.shape, F32),
            jax.ShapeDtypeStruct((4,) + mixed.shape, BF),
        )
        + (row_piece,) * 4
        + (col_piece,) * 4,
        in_specs=[hbm] * 5 + [vmem],
        out_specs=[vmem] + [hbm] * 9,
        scratch_shapes=[
            tok,
            tok,
            pltpu.VMEM(gate_weight.shape, BF),
            pltpu.VMEM(up_weight.shape, BF),
            pltpu.VMEM(down_weight.shape, BF),
            acc,
            acc,
            acc,
            act,
            act,
            act,
            tok,
            three,
            three,
            pltpu.VMEM((2, 4, rows, model), BF),
            pltpu.VMEM((2, 2, eighth, width), BF),
            pltpu.VMEM((2, 2, eighth, width), BF),
            pltpu.VMEM((2, 2, width, eighth), BF),
            dma((5,)),
            dma((32,)),
            dma((16,)),
            dma((24,)),
            dma((24,)),
            dma((2,)),
            dma((3,)),
            dma((3,)),
            dma((8,)),
            pltpu.SemaphoreType.REGULAR,
            pltpu.VMEM((1, width), F32),
        ],
        compiler_params=pltpu.CompilerParams(
            collective_id=5, has_side_effects=True, vmem_limit_bytes=64 * 1024 * 1024 - 65536
        ),
    )(mixed, cot, gate_weight, up_weight, down_weight, counts)


class Reduce:
    def __init__(self, me, factors, cols, x_first, bufs, sems, k):
        self.n, self.w, self.y, self.x, self.core = me
        self.left, self.right = factors
        self.cols, self.x_first = pl.ds(*cols), x_first
        self.away, self.sum, self.pair, self.one, self.two = bufs
        self.sems, self.k = sems, k
        self.rows = self.sum.shape[2]
        self.near = flip(self.n, 2) if x_first else flip(self.n, 4)
        self.next = flip(self.n, 4) if x_first else flip(self.n, 2)

    def term(self, block):
        own = pl.ds(pl.multiple_of(block * self.rows, self.rows), self.rows)
        return contract_rows(self.left[:, own], self.right[:, self.cols])

    def swap(self):
        return send(
            self.away,
            self.pair,
            self.sems[0].at[self.k],
            self.sems[1].at[self.k],
            flip(self.n, 1),
            self.w,
        )

    def before_swap(self):
        @pl.loop(0, 4)
        def _(j):
            self.away[j // 2, lax.rem(j, 2)] = self.term(2 * j + 1 - self.core).astype(BF)

        self.swap().start()

    def block(self, first, second):
        return (second, first) if self.x_first else (first, second)

    def axes(self):
        return (self.x, self.y) if self.x_first else (self.y, self.x)

    def stage(self, s):
        a, b = self.axes()
        if s == 1:
            src = self.sum.at[:, 1 - a] if self.x_first else self.sum.at[1 - a]
            dst, peer = self.one, self.near
        else:
            src = self.sum.at[self.block(a, 1 - b)]
            dst, peer = self.two, self.next
        k = 2 * self.k + s - 1
        return send(src, dst, self.sems[2].at[k], self.sems[3].at[k], peer, self.w)

    def add(self, block, other):
        step = 64 if self.rows % 64 == 0 else 48

        @pl.loop(0, self.rows // step)
        def _(i):
            r = pl.ds(pl.multiple_of(i * step, step), step)
            self.sum[block[0], block[1], r, :] = (
                self.sum[block[0], block[1], r, :] + other[r, :]
            )

    def after_swap(self):
        a, _ = self.axes()
        self.swap().wait_recv()

        @pl.loop(0, 4)
        def _(j):
            first = lax.rem(1 - a + j // 2, 2)
            y, x = self.block(first, lax.rem(j, 2))
            total = self.term(4 * y + 2 * x + self.core) + self.pair[y, x].astype(F32)
            self.sum[y, x] = total.astype(BF)

        self.stage(1).start()

    def after_one(self):
        a, b = self.axes()
        self.stage(1).wait()
        self.add(self.block(a, 1 - b), self.one.at[1 - b])
        self.stage(2).start()
        self.add(self.block(a, b), self.one.at[b])

    def after_two(self):
        a, b = self.axes()
        self.stage(2).wait()
        self.add(self.block(a, b), self.two)

    def result(self):
        return self.sum.at[self.y, self.x]


class Half:
    def __init__(self, me, kept, came, x_first, bufs, sems, k):
        self.n, self.w, self.y, self.x, self.core = me
        self.kept, self.came, self.x_first = kept, came, x_first
        self.sum, self.one, self.two = bufs
        self.sems, self.k = sems, k
        self.rows = kept.shape[1]
        self.next = flip(self.n, 4) if x_first else flip(self.n, 2)
        self.here = self.y if x_first else self.x

    def loads(self):
        return [
            pltpu.make_async_copy(self.kept, self.sum, self.sems[0].at[2 * self.k]),
            pltpu.make_async_copy(self.came, self.one, self.sems[0].at[2 * self.k + 1]),
        ]

    def stage(self):
        return send(
            self.sum.at[1 - self.here],
            self.two,
            self.sems[1].at[self.k],
            self.sems[2].at[self.k],
            self.next,
            self.w,
        )

    def add(self, block, other):
        @pl.loop(0, self.rows // 64)
        def _(i):
            r = pl.ds(pl.multiple_of(i * 64, 64), 64)
            self.sum[block, r, :] = self.sum[block, r, :] + other[r, :]

    def after_one(self):
        for cp in self.loads():
            cp.wait()
        self.add(1 - self.here, self.one.at[1 - self.here])
        self.stage().start()
        self.add(self.here, self.one.at[self.here])

    def after_two(self):
        self.stage().wait()
        self.add(self.here, self.two)

    def result(self):
        return self.sum.at[self.here]


class Spread:
    def __init__(self, item, region, sems, k):
        self.item, self.region, self.sems, self.k = item, region, sems, k
        n = item.n
        self.blocks = (n, flip(n, 2), flip(n, 4), flip(flip(n, 2), 4))

    def copy(self, kind, src, block, peer):
        k = 7 * self.k + kind
        return send(
            src, self.region(block), self.sems[0].at[k], self.sems[1].at[k], peer, self.item.w
        )

    def own(self, kind):
        n = self.item.n
        return self.copy(kind, self.item.result(), n, (flip(n, 2), flip(n, 4), flip(n, 1))[kind])

    def corner(self):
        n, b = self.item.n, self.blocks
        if self.item.x_first:
            return self.copy(3, self.region(b[2]), b[2], flip(n, 2))
        return self.copy(3, self.region(b[1]), b[1], flip(n, 4))

    def to_core(self, which):
        block = self.blocks[which]
        return self.copy(3 + which, self.region(block), block, flip(self.item.n, 1))

    def keep(self):
        return pltpu.make_async_copy(
            self.item.result(), self.region(self.item.n), self.sems[2].at[self.k]
        )

    def start(self):
        order = (1, 0, 2) if self.item.x_first else (0, 1, 2)
        for kind in order:
            self.own(kind).start()
        self.keep().start()

    def relay(self):
        first, second = (1, 0) if self.item.x_first else (0, 1)
        self.own(first).wait_recv()
        self.corner().start()
        self.to_core(1 + first).start()
        self.own(second).wait_recv()
        self.to_core(1 + second).start()

    def last(self):
        self.corner().wait_recv()
        self.to_core(3).start()

    def finish(self):
        for kind in range(2):
            self.own(kind).wait_send()
        self.own(2).wait()
        self.corner().wait_send()
        for which in range(1, 4):
            self.to_core(which).wait()
        self.keep().wait()


class Rows:
    def __init__(self, ref):
        self.ref = ref
        self.shape = (4, ref.shape[0] // 4, ref.shape[1])

    @property
    def at(self):
        return self

    def __getitem__(self, index):
        d, r, _ = index
        start = pl.multiple_of(d * self.shape[1] + r.start, r.size)
        return self.ref.at[pl.ds(start, r.size), :]


def last_kernel(items, *refs):
    refs = list(refs)

    def take(count):
        out = refs[:count]
        del refs[:count]
        return out

    factors = take(4)
    stays, comes = take(4), take(4)
    feed_terms, gain_parts = take(2)
    outs = take(4)
    gate_full, up_full, down_full = take(3)
    feed_out, gain_out = take(2)
    attn_bufs = [take(5) for _ in range(4)]
    ffn_bufs = [take(3) for _ in range(4)]
    line_bufs = [take(3) for _ in range(4)]
    feed_v, feed_left, feed_right = take(3)
    gain_in, gain_sum, gain_line = take(3)
    factor_bufs = take(4)
    load_sem, swap_s, swap_r, st_s, st_r = take(5)
    half_sems = take(3)
    sp_sems = take(3)
    lr_s, lr_r, lg_s, lg_r, lg_l = take(5)
    fd_s, fd_r, fd_l = take(3)
    gn_s, gn_r, gz_s, gz_r = take(4)

    n, w = lax.axis_index("narrow"), lax.axis_index("wide")
    me = (n, w, n // 4, lax.rem(n // 2, 2), lax.rem(n, 2))
    attn = [
        Reduce(
            me,
            factor_bufs[2 * p : 2 * p + 2],
            cols,
            xf,
            attn_bufs[k],
            (swap_s, swap_r, st_s, st_r),
            k,
        )
        for k, (p, cols, xf) in enumerate(items)
    ]
    ffn = [
        Half(me, stays[k], comes[k], k % 2 == 0, ffn_bufs[k], half_sems, k) for k in range(4)
    ]
    cut, eighth = stays[2].shape[1], stays[2].shape[2]

    def down_region(k):
        return lambda block: down_full.at[
            pl.ds(k * cut, cut), pl.ds(pl.multiple_of(block * eighth, eighth), eighth)
        ]

    regions = (
        lambda block: gate_full.at[block],
        lambda block: up_full.at[block],
        down_region(0),
        down_region(1),
    )
    spread = [Spread(ffn[k], regions[k], sp_sems, k) for k in range(4)]
    for item in ffn:
        for cp in item.loads():
            cp.start()
    factor_loads = [
        pltpu.make_async_copy(src, dst, load_sem.at[k])
        for k, (src, dst) in enumerate(zip(factors, factor_bufs))
    ]
    for cp in factor_loads:
        cp.start()
    feed_load = pltpu.make_async_copy(feed_terms, feed_v, fd_l)
    feed_load.start()

    barrier = pltpu.get_barrier_semaphore()
    narrow_peers = [lax.rem(n + i, 8) for i in range(1, 8)]
    wide_peers = [lax.rem(w + i, 4) for i in range(1, 4)]
    for peer in narrow_peers:
        pl.semaphore_signal(
            barrier, inc=1, device_id=at(peer, w), device_id_type=pl.DeviceIdType.MESH
        )
    for peer in wide_peers:
        pl.semaphore_signal(
            barrier, inc=1, device_id=at(n, peer), device_id_type=pl.DeviceIdType.MESH
        )
    pl.semaphore_wait(barrier, 10)

    feed_load.wait()
    feed = LineScatter(n, w, feed_v, (feed_left, feed_right), fd_s, fd_r, 4)
    for i in range(4):
        feed.begin(i)

    def gain_narrow(i):
        peer = narrow_peers[i]
        return send(gain_parts.at[peer], gain_in.at[i], gn_s.at[i], gn_r.at[i], peer, w)

    def gain_wide(i):
        return send(gain_sum, gain_line.at[i], gz_s.at[i], gz_r.at[i], n, wide_peers[i])

    for i in range(7):
        gain_narrow(i).start()

    for item in ffn:
        item.after_one()
    for cp in factor_loads:
        cp.wait()
    for item in attn:
        item.before_swap()
    feed.pass_on(0)
    for item in attn:
        item.after_swap()
    feed.pass_on(1)
    feed.pass_end(0)
    for i in range(7):
        gain_narrow(i).wait()
    total = gain_parts[n]
    for i in range(7):
        total = total + gain_in[i]
    gain_sum[...] = total
    for i in range(3):
        gain_wide(i).start()
    feed.pass_on(2)
    feed.pass_end(1)
    for item in attn[:2]:
        item.after_one()
    feed.pass_on(3)
    feed.pass_end(2)
    for item in attn[2:]:
        item.after_one()
    feed.pass_end(3)
    for k in range(4):
        ffn[k].after_two()
        spread[k].start()

    scatters, gathers = [], []
    for k, item in enumerate(attn):
        left, right, own = line_bufs[k]
        scatters.append(
            LineScatter(n, w, Rows(item.result()), (left, right), lr_s.at[k], lr_r.at[k], 1)
        )
        gathers.append(LineGather(n, w, own, outs[k], lg_s.at[k], lg_r.at[k], 1))

    def keep(k):
        return pltpu.make_async_copy(line_bufs[k][2], outs[k].at[w], lg_l.at[k])

    def line_turn(k):
        scatters[k].finish(0, line_bufs[k][2])
        gathers[k].start()
        keep(k).start()

    for k in (0, 1):
        attn[k].after_two()
        scatters[k].begin(0)
    for i in range(4):
        feed.finish(i, feed_out)
    for k in (2, 3):
        attn[k].after_two()
        scatters[k].begin(0)
    for k in (0, 1, 2, 3):
        scatters[k].pass_on(0)
    for k in (0, 1, 2, 3):
        scatters[k].pass_end(0)
    for k in (0, 1, 2, 3):
        line_turn(k)
    for s in spread[:2]:
        s.relay()
    for k in (0, 1, 2, 3):
        gathers[k].near(0)
    for k in (0, 1, 2, 3):
        gathers[k].far(0)
    for s in spread[2:]:
        s.relay()
    for i in range(3):
        gain_wide(i).wait()
    gain_out[...] = (gain_sum[...] + gain_line[0]) + (gain_line[1] + gain_line[2])
    for s in spread:
        s.last()
    for s in spread:
        s.finish()
    for item in attn:
        item.swap().wait_send()
    for k in range(4):
        scatters[k].drain()
        gathers[k].finish()
        keep(k).wait()
    feed.drain()


def reduce_last(factors, stays, comes, feed_terms, gain_parts):
    rows = factors[0].shape[1] // 8
    q_cols, k_cols = HEADS * HEAD_DIM, KV_HEADS * HEAD_DIM
    items = [
        (0, (0, q_cols), True),
        (0, (q_cols, 2 * k_cols), False),
        (1, (0, k_cols), True),
        (1, (k_cols, q_cols - k_cols), False),
    ]
    scratch = []
    for _, (_, cols), _ in items:
        scratch += [
            pltpu.VMEM((2, 2, rows, cols), BF),
            pltpu.VMEM((2, 2, rows, cols), BF),
            pltpu.VMEM((2, 2, rows, cols), BF),
            pltpu.VMEM((2, rows, cols), BF),
            pltpu.VMEM((rows, cols), BF),
        ]
    for stay in stays:
        scratch += [
            pltpu.VMEM(stay.shape, BF),
            pltpu.VMEM(stay.shape, BF),
            pltpu.VMEM(stay.shape[1:], BF),
        ]
    outs = []
    for _, (_, cols), _ in items:
        scratch += [pltpu.VMEM((3, rows // 4, cols), BF)] * 2 + [pltpu.VMEM((rows // 4, cols), BF)]
        outs.append(jax.ShapeDtypeStruct((4, rows // 4, cols), BF))
    outs.append(jax.ShapeDtypeStruct((8,) + stays[0].shape[1:], BF))
    outs.append(jax.ShapeDtypeStruct((8,) + stays[1].shape[1:], BF))
    outs.append(jax.ShapeDtypeStruct((2 * stays[2].shape[1], 8 * stays[2].shape[2]), BF))
    outs.append(jax.ShapeDtypeStruct(feed_terms.shape[1:], F32))
    outs.append(jax.ShapeDtypeStruct(gain_parts.shape[1:], F32))
    scratch += [pltpu.VMEM(feed_terms.shape, BF)]
    scratch += [pltpu.VMEM((3,) + feed_terms.shape[1:], BF)] * 2
    scratch += [
        pltpu.VMEM((7,) + gain_parts.shape[1:], F32),
        pltpu.VMEM(gain_parts.shape[1:], F32),
        pltpu.VMEM((3,) + gain_parts.shape[1:], F32),
    ]
    scratch += [pltpu.VMEM(f.shape, BF) for f in factors]
    dma = pltpu.SemaphoreType.DMA
    scratch += [dma((4,)), dma((4,)), dma((4,)), dma((8,)), dma((8,))]
    scratch += [dma((8,)), dma((4,)), dma((4,))]
    scratch += [dma((28,)), dma((28,)), dma((4,))]
    scratch += [dma((4, 6)), dma((4, 6)), dma((4, 8)), dma((4, 4)), dma((4,))]
    scratch += [dma((24,)), dma((24,)), dma]
    scratch += [dma((7,)), dma((7,)), dma((3,)), dma((3,))]
    hbm, vmem = pl.BlockSpec(memory_space=pl.ANY), pl.BlockSpec(memory_space=pltpu.VMEM)
    out = pl.pallas_call(
        functools.partial(last_kernel, items),
        name="reduce_last",
        out_shape=tuple(outs),
        in_specs=[hbm] * 13 + [vmem],
        out_specs=[hbm] * 7 + [vmem] * 2,
        scratch_shapes=scratch,
        compiler_params=pltpu.CompilerParams(
            collective_id=4, has_side_effects=True, vmem_limit_bytes=64 * 1024 * 1024 - 65536
        ),
    )(*factors, *stays, *comes, feed_terms, gain_parts)
    qkv = out[0].reshape(rows, -1), out[1].reshape(rows, -1)
    project = jnp.concatenate([out[2].reshape(rows, -1), out[3].reshape(rows, -1)], axis=1)
    width = out[4].shape[2]
    ffn = [out[4].reshape(-1, width), out[5].reshape(-1, width), out[6]]
    return qkv, project, ffn, out[7], out[8]


def per_device(
    fast,
    block_input,
    cotangent,
    query_weight,
    key_weight,
    value_weight,
    project_weight,
    prenorm_gain,
    midnorm_gain,
    gate_weight,
    up_weight,
    down_weight,
    doc_lengths,
    tile_counts,
):
    tokens_here, model = block_input.shape
    group = HEADS // KV_HEADS
    scale = HEAD_DIM ** (-0.5)
    q_cols, k_cols = HEADS * HEAD_DIM, KV_HEADS * HEAD_DIM
    inputs_f = block_input.astype(jnp.float32)
    ends = jnp.cumsum(doc_lengths[0])
    position = jnp.arange(tokens_here, dtype=jnp.int32)
    segment = jnp.sum((position[:, None] >= ends[None, :]).astype(jnp.int32), axis=1)
    allowed = (segment[:, None] == segment[None, :]) & (position[None, :] <= position[:, None])
    if fast:
        gains = jnp.stack([prenorm_gain, midnorm_gain]).astype(F32).reshape(1, -1)
        qkv_full, project_full, grad_rows, normed, qkv, attended, *small = gather_first(
            block_input,
            query_weight,
            key_weight,
            value_weight,
            project_weight,
            gains,
            cotangent,
            doc_lengths,
        )
        first_gain, second_gain, bias, logs = small
        first_gain, second_gain = first_gain.reshape(-1), second_gain.reshape(-1)
    else:
        qkv_full = jnp.concatenate(
            [
                lax.all_gather(query_weight, "narrow", axis=0, tiled=True),
                lax.all_gather(key_weight, "narrow", axis=0, tiled=True),
                lax.all_gather(value_weight, "narrow", axis=0, tiled=True),
            ],
            axis=1,
        )
        project_full = lax.all_gather(project_weight, "narrow", axis=1, tiled=True)
        first_gain = lax.all_gather(prenorm_gain, "narrow", axis=0, tiled=True).astype(F32)
        second_gain = lax.all_gather(midnorm_gain, "narrow", axis=0, tiled=True).astype(F32)
        grad_rows = lax.all_gather(cotangent, "wide", axis=0, tiled=True)
        normed = rms_scale(inputs_f, first_gain).astype(jnp.bfloat16)
        qkv = jnp.dot(normed, qkv_full, preferred_element_type=jnp.float32).astype(jnp.bfloat16)
    if not fast:
        query_rows = qkv[:, :q_cols].reshape(tokens_here, KV_HEADS, group, HEAD_DIM)
        key_rows = qkv[:, q_cols : q_cols + k_cols].reshape(tokens_here, KV_HEADS, HEAD_DIM)
        value_rows = qkv[:, q_cols + k_cols :].reshape(tokens_here, KV_HEADS, HEAD_DIM)
        scores = (
            jnp.einsum("qcgd,kcd->cgqk", query_rows, key_rows, preferred_element_type=jnp.float32)
            * scale
        )
        masked = jnp.where(allowed, scores, -1e30)
        peak = jnp.max(masked, axis=-1, keepdims=True)
        expo = jnp.exp(masked - peak)
        total = jnp.sum(expo, axis=-1, keepdims=True)
        probs_low = (expo / total).astype(jnp.bfloat16)
        logsum = peak + jnp.log(total)
        attended = (
            jnp.einsum("cgqk,kcd->qcgd", probs_low, value_rows, preferred_element_type=jnp.float32)
            .astype(jnp.bfloat16)
            .reshape(tokens_here, HEADS * HEAD_DIM)
        )
    branch = jnp.dot(attended, project_full, preferred_element_type=jnp.float32)
    middle = inputs_f + branch
    mixed_in = rms_scale(middle, second_gain).astype(jnp.bfloat16)
    width = gate_weight.shape[1]
    wide_index = lax.axis_index("wide")
    my_count = jnp.sum(
        jnp.where(jnp.arange(tile_counts.shape[0], dtype=jnp.int32) == wide_index, tile_counts, 0)
    )
    live = (jnp.arange(width, dtype=jnp.int32) // TILE < my_count).astype(jnp.float32)
    if fast:
        mixed_back, feed_terms, *pieces = feed_forward(
            mixed_in, grad_rows, gate_weight, up_weight, down_weight, tile_counts.reshape(1, -1)
        )
        stays = pieces[1::2]
        comes = [
            lax.ppermute(piece, "narrow", [(i, i ^ bit) for i in range(8)])
            for piece, bit in zip(pieces[0::2], (2, 4, 2, 4))
        ]
    else:
        gathered = lax.all_gather(mixed_in, "wide", axis=0, tiled=True)
        gate_pre = jnp.dot(gathered, gate_weight, preferred_element_type=jnp.float32)
        up_pre = jnp.dot(gathered, up_weight, preferred_element_type=jnp.float32)
        hidden_back = contract_cols(grad_rows, down_weight)
        sigma = jax.nn.sigmoid(gate_pre)
        hidden = (gate_pre * sigma * up_pre * live).astype(BF)
        gate_back = (
            hidden_back * up_pre * live * sigma * (1.0 + gate_pre * (1.0 - sigma))
        ).astype(BF)
        up_back = (hidden_back * gate_pre * sigma * live).astype(BF)
        mixed_terms = (
            contract_cols(gate_back, gate_weight) + contract_cols(up_back, up_weight)
        ).astype(BF)
        mixed_back = lax.psum_scatter(
            mixed_terms, "wide", scatter_dimension=0, tiled=True
        ).astype(F32)
        partial_rows = jnp.dot(hidden, down_weight, preferred_element_type=jnp.float32)
        down_part = contract_rows(hidden, grad_rows)
        gate_part = contract_rows(gathered, gate_back)
        up_part = contract_rows(gathered, up_back)
    out_grad = cotangent.astype(jnp.float32)
    unused_second, second_backward = jax.vjp(rms_scale, middle, second_gain)
    middle_norm_back, second_gain_part = second_backward(mixed_back)
    middle_back = out_grad + middle_norm_back
    branch_back = middle_back.astype(jnp.bfloat16)
    attended_back = contract_cols(branch_back, project_full).astype(jnp.bfloat16)
    if fast:
        qkv_back = attention_back(qkv, attended_back, logs, bias)
    else:
        attended_back = attended_back.reshape(tokens_here, KV_HEADS, group, HEAD_DIM)
        scores_again = (
            jnp.einsum("qcgd,kcd->cgqk", query_rows, key_rows, preferred_element_type=jnp.float32)
            * scale
        )
        probs_again = jnp.where(allowed, jnp.exp(scores_again - logsum), 0.0)
        probs_again_low = probs_again.astype(jnp.bfloat16)
        value_back = (
            jnp.einsum(
                "cgqk,qcgd->kcd", probs_again_low, attended_back, preferred_element_type=jnp.float32
            )
            .astype(jnp.bfloat16)
            .reshape(tokens_here, KV_HEADS * HEAD_DIM)
        )
        probs_back = jnp.einsum(
            "qcgd,kcd->cgqk", attended_back, value_rows, preferred_element_type=jnp.float32
        )
        scores_back = (
            probs_again * (probs_back - jnp.sum(probs_again * probs_back, axis=-1, keepdims=True))
        ).astype(jnp.bfloat16)
        query_back = (
            (
                jnp.einsum("cgqk,kcd->qcgd", scores_back, key_rows, preferred_element_type=jnp.float32)
                * scale
            )
            .astype(jnp.bfloat16)
            .reshape(tokens_here, HEADS * HEAD_DIM)
        )
        key_back = (
            (
                jnp.einsum(
                    "cgqk,qcgd->kcd", scores_back, query_rows, preferred_element_type=jnp.float32
                )
                * scale
            )
            .astype(jnp.bfloat16)
            .reshape(tokens_here, KV_HEADS * HEAD_DIM)
        )
        qkv_back = jnp.concatenate([query_back, key_back, value_back], axis=1)
    normed_back = contract_cols(qkv_back, qkv_full)
    unused_first, first_backward = jax.vjp(rms_scale, inputs_f, first_gain)
    input_norm_back, first_gain_part = first_backward(normed_back)
    input_grad = (middle_back + input_norm_back).astype(jnp.bfloat16)

    if fast:
        gain_parts = jnp.stack(
            [first_gain_part.reshape(8, -1), second_gain_part.reshape(8, -1)], axis=1
        ).reshape(8, 1, -1)
        input_grad, qkv_back = lax.optimization_barrier((input_grad, qkv_back))
        qkv_total, project_total, ffn_totals, feed, gain_total = reduce_last(
            (normed, qkv_back, branch_back, attended),
            stays,
            comes,
            feed_terms,
            gain_parts,
        )
        gain_total = gain_total.reshape(2, -1)
        first_total, second_total = gain_total[0], gain_total[1]
        query_total = qkv_total[0].astype(F32)
        key_total = qkv_total[1][:, :k_cols].astype(F32)
        value_total = qkv_total[1][:, k_cols:].astype(F32)
        project_total = project_total.T.astype(F32)
        gate_total, up_total, down_total = [t.astype(F32) for t in ffn_totals]
    else:

        def owned(part):
            share = lax.psum_scatter(part.astype(BF), "narrow", scatter_dimension=0, tiled=True)
            return lax.psum(share, "wide").astype(F32)

        qkv_total = owned(contract_rows(normed, qkv_back))
        query_total = qkv_total[:, :q_cols]
        key_total = qkv_total[:, q_cols : q_cols + k_cols]
        value_total = qkv_total[:, q_cols + k_cols :]
        project_total = owned(contract_rows(branch_back, attended)).T
        first_total = owned(first_gain_part)
        second_total = owned(second_gain_part)
        gate_total, up_total, down_total = (
            lax.psum(gate_part.astype(BF), "narrow").astype(F32),
            lax.psum(up_part.astype(BF), "narrow").astype(F32),
            lax.psum(down_part.astype(BF), "narrow").astype(F32),
        )
        feed = lax.psum_scatter(
            partial_rows.astype(BF), "wide", scatter_dimension=0, tiled=True
        ).astype(F32)
    block_output = (middle + feed).astype(BF)
    return (
        block_output,
        input_grad,
        query_total,
        key_total,
        value_total,
        project_total,
        first_total,
        second_total,
        gate_total,
        up_total,
        down_total,
    )


def solution(mesh):
    fast = mesh.shape["narrow"] == 8 and mesh.shape["wide"] == 4
    placed = (
        P(("narrow", "wide"), None),
        P(("narrow", "wide"), None),
        P("narrow", None),
        P("narrow", None),
        P("narrow", None),
        P(None, "narrow"),
        P("narrow"),
        P("narrow"),
        P(None, "wide"),
        P(None, "wide"),
        P("wide", None),
        P(("narrow", "wide"), None),
        P(),
    )
    return jax.shard_map(
        functools.partial(per_device, fast),
        mesh=mesh,
        in_specs=placed,
        out_specs=(
            P(("narrow", "wide"), None),
            P(("narrow", "wide"), None),
            P("narrow", None),
            P("narrow", None),
            P("narrow", None),
            P(None, "narrow"),
            P("narrow"),
            P("narrow"),
            P(None, "wide"),
            P(None, "wide"),
            P("wide", None),
        ),
        check_vma=False,
    )
```

```python
import functools

import jax
import jax.numpy as jnp
from jax import lax
from jax.experimental import pallas as pl
from jax.experimental.pallas import tpu as pltpu
from jax.sharding import PartitionSpec as P

HEADS = 24
KV_HEADS = 6
HEAD_DIM = 64
TILE = 128


EPSILON = 1e-06

BF = jnp.bfloat16
F32 = jnp.float32


def rms_scale(rows, gain):
    factor = lax.rsqrt(jnp.mean(rows * rows, axis=-1, keepdims=True) + EPSILON)
    return rows * factor * gain


def scale_back(back, rows, gain, factor):
    scaled = back * gain
    inner = jnp.mean(scaled * rows, axis=-1, keepdims=True)
    return factor * scaled - rows * (factor**3 * inner), jnp.sum(back * rows * factor, axis=0)


def contract_rows(left, right):
    return lax.dot_general(
        left, right, (((0,), (0,)), ((), ())), preferred_element_type=jnp.float32
    )


def contract_cols(left, right):
    return lax.dot_general(
        left, right, (((1,), (1,)), ((), ())), preferred_element_type=jnp.float32
    )


def flip(n, bit):
    return n + bit - 2 * bit * lax.rem(n // bit, 2)


def at(n, w):
    return {"narrow": n, "wide": w}


def send(src, dst, ssem, rsem, n, w):
    return pltpu.make_async_remote_copy(
        src_ref=src,
        dst_ref=dst,
        send_sem=ssem,
        recv_sem=rsem,
        device_id=at(n, w),
        device_id_type=pl.DeviceIdType.MESH,
    )


def greet(narrow_peers, n, w, line):
    barrier = pltpu.get_barrier_semaphore()
    for peer in narrow_peers:
        pl.semaphore_signal(
            barrier, inc=1, device_id=at(peer, w), device_id_type=pl.DeviceIdType.MESH
        )
    if not line:
        pl.semaphore_wait(barrier, len(narrow_peers))
    if line:

        @pl.when(w > 0)
        def _():
            pl.semaphore_signal(
                barrier, inc=1, device_id=at(n, w - 1), device_id_type=pl.DeviceIdType.MESH
            )

        @pl.when(w < 3)
        def _():
            pl.semaphore_signal(
                barrier, inc=1, device_id=at(n, w + 1), device_id_type=pl.DeviceIdType.MESH
            )

        @pl.when((w == 0) | (w == 3))
        def _():
            pl.semaphore_wait(barrier, len(narrow_peers) + 1)

        @pl.when((w == 1) | (w == 2))
        def _():
            pl.semaphore_wait(barrier, len(narrow_peers) + 2)


class LineGather:
    def __init__(self, n, w, own, whole, ssem, rsem, chunks):
        self.n, self.w, self.own, self.whole = n, w, own, whole
        self.ssem, self.rsem, self.chunks = ssem, rsem, chunks
        self.rows = own.shape[0] // chunks

    def span(self, i):
        return pl.ds(pl.multiple_of(i * self.rows, self.rows), self.rows)

    def part(self, shard, i):
        return self.whole.at[shard, self.span(i), :]

    def put(self, way, here, shard, i):
        src = self.own.at[self.span(i), :] if shard is here else self.part(shard, i)
        to = here + 1 - 2 * way
        s = (way * 4 + shard) * self.chunks + i
        r = shard * self.chunks + i
        return send(src, self.part(shard, i), self.ssem.at[s], self.rsem.at[r], self.n, to)

    def came(self, shard, i):
        self.put(0, 0, shard, i).wait_recv()

    def start_chunk(self, i):
        @pl.when(self.w < 3)
        def _():
            self.put(0, self.w, self.w, i).start()

        @pl.when(self.w > 0)
        def _():
            self.put(1, self.w, self.w, i).start()

    def start(self):
        for i in range(self.chunks):
            self.start_chunk(i)

    def near(self, i):
        @pl.when(self.w == 1)
        def _():
            self.came(0, i)
            self.put(0, 1, 0, i).start()
            self.came(2, i)
            self.put(1, 1, 2, i).start()

        @pl.when(self.w == 2)
        def _():
            self.came(3, i)
            self.put(1, 2, 3, i).start()
            self.came(1, i)
            self.put(0, 2, 1, i).start()

    def far(self, i):
        @pl.when(self.w == 1)
        def _():
            self.came(3, i)
            self.put(1, 1, 3, i).start()

        @pl.when(self.w == 2)
        def _():
            self.came(0, i)
            self.put(0, 2, 0, i).start()

    def ready(self, i):
        @pl.when(self.w == 0)
        def _():
            for shard in (1, 2, 3):
                self.came(shard, i)

        @pl.when(self.w == 3)
        def _():
            for shard in (2, 1, 0):
                self.came(shard, i)

    def finish_sends(self):
        for here in range(4):

            @pl.when(self.w == here)
            def _():
                for i in range(self.chunks):
                    if here < 3:
                        for shard in range(here + 1):
                            self.put(0, here, shard, i).wait_send()
                    if here > 0:
                        for shard in range(here, 4):
                            self.put(1, here, shard, i).wait_send()

    def finish(self):
        for i in range(self.chunks):
            self.ready(i)
        self.finish_sends()


def first_kernel(
    x_ref,
    q_ref,
    k_ref,
    v_ref,
    p_ref,
    g_ref,
    c_ref,
    docs_ref,
    qkv_out,
    p_out,
    c_full,
    normed_out,
    rows_out,
    att_out,
    middle_out,
    mixed_out,
    gain_row,
    gain_late,
    bias_ref,
    log_out,
    g_full,
    qkv_full,
    p_full,
    c_buf,
    x_buf,
    normed,
    middle,
    mixed,
    qkv,
    att,
    in_sem,
    out_sem,
    ssem,
    rsem,
    gs_sem,
    gr_sem,
    zs_sem,
    zr_sem,
):
    n, w = lax.axis_index("narrow"), lax.axis_index("wide")
    x, y, c, d = flip(n, 2), flip(n, 4), flip(n, 1), flip(flip(n, 2), 4)
    others = [lax.rem(n + i, 8) for i in range(1, 8)]
    rows = q_ref.shape[0]
    half = rows // 2
    depth = p_ref.shape[0]
    qc, kc = q_ref.shape[1], k_ref.shape[1]
    cols = ((0, qc), (qc, kc), (qc + kc, kc))

    def region(t, block, h):
        if t == 3:
            r = pl.ds(0, depth) if h == 2 else pl.ds(h * (depth // 2), depth // 2)
            return p_full.at[r, pl.ds(pl.multiple_of(block * rows, rows), rows)]
        start = pl.multiple_of(block * rows, rows)
        r = pl.ds(start, rows) if h == 2 else pl.ds(start + h * half, half)
        return qkv_full.at[r, pl.ds(cols[t][0], cols[t][1])]

    locals_in = []
    for i, (src, dst) in enumerate(
        (
            (g_ref, g_full.at[n]),
            (x_ref, x_buf),
            (p_ref, region(3, n, 2)),
            (c_ref, c_buf),
            (q_ref, region(0, n, 2)),
            (k_ref, region(1, n, 2)),
            (v_ref, region(2, n, 2)),
        )
    ):
        cp = pltpu.make_async_copy(src, dst, in_sem.at[i])
        cp.start()
        locals_in.append(cp)

    greet(others, n, w, True)

    def own(t, h):
        ref = (q_ref, k_ref, v_ref, p_ref)[t]
        if h == 2:
            return ref
        size = ref.shape[0] // 2
        return ref.at[pl.ds(h * size, size), :]

    def msg(t, kind, src, block, h, peer):
        k = t * 10 + kind
        return send(src, region(t, block, h), ssem.at[k], rsem.at[k], peer, w)

    def to_x(t, h):
        return msg(t, h, own(t, h), n, h, x)

    def to_y(t, h):
        return msg(t, 2 + h, own(t, h), n, h, y)

    def on_x(t):
        return msg(t, 4, region(t, y, 0), y, 0, x)

    def on_y(t):
        return msg(t, 5, region(t, x, 1), x, 1, y)

    def to_c(t, which):
        block = (n, x, y, d)[which]
        src = own(t, 2) if which == 0 else region(t, block, 2)
        return msg(t, 6 + which, src, block, 2, c)

    def start_own(t):
        to_x(t, 1).start()
        to_y(t, 0).start()
        to_x(t, 0).start()
        to_y(t, 1).start()

    def gain(i):
        return send(g_ref, g_full.at[n], gs_sem.at[i], gr_sem.at[i], others[i], w)

    line = LineGather(n, w, c_ref, c_full, zs_sem, zr_sem, 4)
    for i in range(7):
        gain(i).start()
    start_own(0)
    line.start()
    for t in (1, 2):
        start_own(t)
    for t in range(3):
        to_c(t, 0).start()

    locals_out = []

    def put(src, dst):
        cp = pltpu.make_async_copy(src, dst, out_sem.at[len(locals_out)])
        cp.start()
        locals_out.append(cp)

    for i in range(7):
        gain(i).wait()
    for cp in locals_in:
        cp.wait()
    put(c_buf, c_full.at[w])
    for k in range(8):
        gain_row[:, pl.ds(k * rows, rows)] = g_full[k, :, :rows]
        gain_late[:, pl.ds(k * rows, rows)] = g_full[k, :, rows:]
    strip = 16

    def scaled(rows_f, gain_ref, s, kept, others_f):
        factor = lax.rsqrt(jnp.mean(rows_f * rows_f, axis=-1, keepdims=True) + EPSILON)
        lane = lax.broadcasted_iota(jnp.int32, (strip, log_out.shape[1]), 1)
        log_out[s, :] = jnp.where(lane == kept, factor, others_f)
        return (rows_f * factor * gain_ref[...]).astype(BF)

    @pl.loop(0, x_buf.shape[0] // strip)
    def _(i):
        s = pl.ds(pl.multiple_of(i * strip, strip), strip)
        normed[s, :] = scaled(x_buf[s, :].astype(F32), gain_row, s, 127, 0.0)

    put(normed, normed_out)

    docs = docs_ref[...]
    late = lax.broadcasted_iota(jnp.int32, bias_ref.shape, 0)
    early = lax.broadcasted_iota(jnp.int32, bias_ref.shape, 1)
    end = docs[:, :1]
    late_doc = jnp.where(late >= end, 1, 0)
    early_doc = jnp.where(early >= end, 1, 0)
    for k in range(1, docs.shape[1]):
        end = end + docs[:, k : k + 1]
        late_doc = late_doc + jnp.where(late >= end, 1, 0)
        early_doc = early_doc + jnp.where(early >= end, 1, 0)
    allowed = (late_doc == early_doc) & (early <= late)
    bias_ref[...] = jnp.where(allowed, 0.0, -1e30)

    def relay(t):
        to_y(t, 0).wait_recv()
        on_x(t).start()
        to_x(t, 1).wait_recv()
        on_y(t).start()
        to_x(t, 0).wait_recv()
        to_c(t, 1).start()
        to_y(t, 1).wait_recv()
        to_c(t, 2).start()

    def corner(t):
        on_x(t).wait_recv()
        on_y(t).wait_recv()
        to_c(t, 3).start()

    line.near(0)
    relay(0)
    line.near(1)
    relay(1)
    line.near(2)
    relay(2)
    start_own(3)
    to_c(3, 0).start()
    line.near(3)
    line.far(0)
    line.far(1)
    for t in range(3):
        corner(t)
    line.far(2)
    for t in range(3):
        for which in range(4):
            to_c(t, which).wait_recv()
    put(qkv_full, qkv_out)
    tile = 256

    @pl.loop(0, qkv.shape[1] // tile)
    def _(i):
        s = pl.ds(pl.multiple_of(i * tile, tile), tile)
        qkv[:, s] = jnp.dot(normed[...], qkv_full[:, s], preferred_element_type=F32).astype(BF)

    put(qkv, rows_out)
    line.far(3)

    pair = 2 * HEAD_DIM
    group = HEADS // KV_HEADS

    @pl.loop(0, KV_HEADS // 2)
    def _(i):
        keys = qkv[:, pl.ds(pl.multiple_of(qc + i * pair, pair), pair)]
        values = qkv[:, pl.ds(pl.multiple_of(qc + kc + i * pair, pair), pair)]
        lane = lax.broadcasted_iota(jnp.int32, log_out.shape, 1)
        for b in range(group):
            at_cols = pl.ds(pl.multiple_of((i * group + b) * pair, pair), pair)
            queries = qkv[:, at_cols]
            side = (2 * b) // group
            key = keys[:, side * HEAD_DIM : (side + 1) * HEAD_DIM]
            value = values[:, side * HEAD_DIM : (side + 1) * HEAD_DIM]
            heads = []
            for e in range(2):
                query = queries[:, e * HEAD_DIM : (e + 1) * HEAD_DIM]
                masked = contract_cols(query, key) * (HEAD_DIM**-0.5) + bias_ref[...]
                peak = jnp.max(masked, axis=-1, keepdims=True)
                expo = jnp.exp(masked - peak)
                total = jnp.sum(expo, axis=-1, keepdims=True)
                probs = (expo * (1.0 / total)).astype(BF)
                heads.append(jnp.dot(probs, value, preferred_element_type=F32))
                log_out[...] = jnp.where(
                    lane == 2 * (i * group + b) + e, peak + jnp.log(total), log_out[...]
                )
            att[:, at_cols] = jnp.concatenate(heads, axis=1).astype(BF)

    put(att, att_out)
    relay(3)
    corner(3)
    for which in range(4):
        to_c(3, which).wait_recv()
    put(p_full, p_out)

    @pl.loop(0, x_buf.shape[1] // tile)
    def _(i):
        s = pl.ds(pl.multiple_of(i * tile, tile), tile)
        middle[:, s] = x_buf[:, s].astype(F32) + jnp.dot(
            att[...], p_full[:, s], preferred_element_type=F32
        )

    put(middle, middle_out)

    @pl.loop(0, x_buf.shape[0] // strip)
    def _(i):
        s = pl.ds(pl.multiple_of(i * strip, strip), strip)
        mixed[s, :] = scaled(middle[s, :], gain_late, s, 126, log_out[s, :])

    put(mixed, mixed_out)
    for t in range(4):
        for h in range(2):
            to_x(t, h).wait_send()
            to_y(t, h).wait_send()
        on_x(t).wait_send()
        on_y(t).wait_send()
        for which in range(4):
            to_c(t, which).wait_send()
    line.finish()
    for cp in locals_out:
        cp.wait()


def gather_first(rows_in, query, key, value, project, gains, cotangent, docs):
    rows = query.shape[0]
    width = query.shape[1] + 2 * key.shape[1]
    tokens_here, model = rows_in.shape
    hbm, vmem = pl.BlockSpec(memory_space=pl.ANY), pl.BlockSpec(memory_space=pltpu.VMEM)
    return pl.pallas_call(
        first_kernel,
        name="gather_first",
        out_shape=(
            jax.ShapeDtypeStruct((8 * rows, width), BF),
            jax.ShapeDtypeStruct((project.shape[0], 8 * rows), BF),
            jax.ShapeDtypeStruct((4,) + cotangent.shape, BF),
            jax.ShapeDtypeStruct((tokens_here, model), BF),
            jax.ShapeDtypeStruct((tokens_here, width), BF),
            jax.ShapeDtypeStruct((tokens_here, query.shape[1]), BF),
            jax.ShapeDtypeStruct((tokens_here, model), F32),
            jax.ShapeDtypeStruct((tokens_here, model), BF),
            jax.ShapeDtypeStruct((1, model), F32),
            jax.ShapeDtypeStruct((1, model), F32),
            jax.ShapeDtypeStruct((tokens_here, tokens_here), F32),
            jax.ShapeDtypeStruct((tokens_here, 128), F32),
        ),
        in_specs=[hbm] * 7 + [vmem],
        out_specs=[hbm] * 8 + [vmem] * 4,
        scratch_shapes=[
            pltpu.VMEM((8,) + gains.shape, gains.dtype),
            pltpu.VMEM((8 * rows, width), BF),
            pltpu.VMEM((project.shape[0], 8 * rows), BF),
            pltpu.VMEM(cotangent.shape, BF),
            pltpu.VMEM((tokens_here, model), BF),
            pltpu.VMEM((tokens_here, model), BF),
            pltpu.VMEM((tokens_here, model), F32),
            pltpu.VMEM((tokens_here, model), BF),
            pltpu.VMEM((tokens_here, width), BF),
            pltpu.VMEM((tokens_here, query.shape[1]), BF),
            pltpu.SemaphoreType.DMA((7,)),
            pltpu.SemaphoreType.DMA((8,)),
            pltpu.SemaphoreType.DMA((40,)),
            pltpu.SemaphoreType.DMA((40,)),
            pltpu.SemaphoreType.DMA((7,)),
            pltpu.SemaphoreType.DMA((7,)),
            pltpu.SemaphoreType.DMA((32,)),
            pltpu.SemaphoreType.DMA((16,)),
        ],
        compiler_params=pltpu.CompilerParams(collective_id=1, has_side_effects=True),
    )(rows_in, query, key, value, project, gains, cotangent, docs)


def attention_back_kernel(qkv, back, logs, bias, out):
    q_cols, k_cols = HEADS * HEAD_DIM, KV_HEADS * HEAD_DIM
    pair = 2 * HEAD_DIM
    group = HEADS // KV_HEADS
    scale = HEAD_DIM**-0.5

    @pl.loop(0, KV_HEADS // 2)
    def _(i):
        key_at = pl.ds(pl.multiple_of(q_cols + i * pair, pair), pair)
        value_at = pl.ds(pl.multiple_of(q_cols + k_cols + i * pair, pair), pair)
        keys, values = qkv[:, key_at], qkv[:, value_at]
        lane = lax.broadcasted_iota(jnp.int32, logs.shape, 1)
        key_backs, value_backs = [], []
        for side in range(2):
            key = keys[:, side * HEAD_DIM : (side + 1) * HEAD_DIM]
            value = values[:, side * HEAD_DIM : (side + 1) * HEAD_DIM]
            key_back = jnp.zeros(key.shape, F32)
            value_back = jnp.zeros(key.shape, F32)
            for b in range(side * group // 2, (side + 1) * group // 2):
                at_cols = pl.ds(pl.multiple_of((i * group + b) * pair, pair), pair)
                queries, backs = qkv[:, at_cols], back[:, at_cols]
                heads = []
                for e in range(2):
                    query = queries[:, e * HEAD_DIM : (e + 1) * HEAD_DIM]
                    given = backs[:, e * HEAD_DIM : (e + 1) * HEAD_DIM]
                    logsum = jnp.sum(
                        jnp.where(lane == 2 * (i * group + b) + e, logs[...], 0.0),
                        axis=-1,
                        keepdims=True,
                    )
                    probs = jnp.exp(contract_cols(query, key) * scale + bias[...] - logsum)
                    value_back = value_back + contract_rows(probs.astype(BF), given)
                    probs_back = contract_cols(given, value)
                    inner = jnp.sum(probs * probs_back, axis=-1, keepdims=True)
                    scores_back = (probs * (probs_back - inner)).astype(BF)
                    heads.append(jnp.dot(scores_back, key, preferred_element_type=F32) * scale)
                    key_back = key_back + contract_rows(scores_back, query)
                out[:, at_cols] = jnp.concatenate(heads, axis=1).astype(BF)
            key_backs.append(key_back * scale)
            value_backs.append(value_back)
        out[:, key_at] = jnp.concatenate(key_backs, axis=1).astype(BF)
        out[:, value_at] = jnp.concatenate(value_backs, axis=1).astype(BF)


def attention_back(qkv, back, logs, bias):
    vmem = pl.BlockSpec(memory_space=pltpu.VMEM)
    heads = HEADS * qkv.shape[0] * qkv.shape[0]
    return pl.pallas_call(
        attention_back_kernel,
        name="attention_back",
        out_shape=jax.ShapeDtypeStruct(qkv.shape, BF),
        in_specs=[vmem] * 4,
        out_specs=vmem,
        cost_estimate=pl.CostEstimate(
            flops=10 * heads * HEAD_DIM, bytes_accessed=8 * qkv.size, transcendentals=heads
        ),
    )(qkv, back, logs, bias)


class LineScatter:
    def __init__(self, n, w, terms, bufs, ssem, rsem, chunks):
        self.n, self.w, self.terms, self.bufs = n, w, terms, bufs
        self.ssem, self.rsem, self.chunks = ssem, rsem, chunks
        self.rows = terms.shape[1] // chunks

    def span(self, i):
        return pl.ds(pl.multiple_of(i * self.rows, self.rows), self.rows)

    def term(self, d, i):
        return self.terms.at[d, self.span(i), :]

    def slot(self, way, slot, i):
        return self.bufs[way].at[slot, self.span(i), :]

    def put(self, way, here, d, i, src):
        slot = d - here - 1 if way == 0 else here - 1 - d
        k = (way * 3 + slot) * self.chunks + i
        to = here + 1 - 2 * way
        return send(src, self.slot(way, slot, i), self.ssem.at[k], self.rsem.at[k], self.n, to)

    def came(self, way, slot, i):
        k = (way * 3 + slot) * self.chunks + i
        ref = self.slot(way, slot, i)
        send(ref, ref, self.ssem.at[k], self.rsem.at[k], self.n, 1).wait_recv()

    def begin(self, i):
        for here, way in ((0, 0), (3, 1)):

            @pl.when(self.w == here)
            def _():
                for d in (3, 2, 1) if way == 0 else (0, 1, 2):
                    self.put(way, here, d, i, self.term(d, i)).start()

    def join(self, way, here, d, i):
        slot = d - here if way == 0 else here - d
        self.came(way, slot, i)
        mine, sum_ = self.term(d, i), self.slot(way, slot, i)
        sum_[...] = (mine[...].astype(F32) + sum_[...].astype(F32)).astype(BF)
        self.put(way, here, d, i, sum_).start()

    def pass_on(self, i):
        @pl.when(self.w == 1)
        def _():
            self.join(0, 1, 3, i)
            self.join(0, 1, 2, i)

        @pl.when(self.w == 2)
        def _():
            self.join(1, 2, 0, i)
            self.join(1, 2, 1, i)

    def pass_end(self, i):
        @pl.when(self.w == 1)
        def _():
            self.join(1, 1, 0, i)

        @pl.when(self.w == 2)
        def _():
            self.join(0, 2, 3, i)

    def finish(self, i, out):
        for here, ways in ((0, (1,)), (1, (0, 1)), (2, (0, 1)), (3, (0,))):

            @pl.when(self.w == here)
            def _():
                for way in ways:
                    self.came(way, 0, i)
                total = self.term(here, i)[...].astype(F32)
                for way in ways:
                    total = total + self.slot(way, 0, i)[...].astype(F32)
                out[self.span(i), :] = total.astype(out.dtype)

    def drain(self):
        sent = {
            0: ((0, 3), (0, 2), (0, 1)),
            1: ((0, 3), (0, 2), (1, 0)),
            2: ((1, 0), (1, 1), (0, 3)),
            3: ((1, 0), (1, 1), (1, 2)),
        }
        for here in range(4):

            @pl.when(self.w == here)
            def _():
                for i in range(self.chunks):
                    for way, d in sent[here]:
                        self.put(way, here, d, i, self.term(d, i)).wait_send()


def middle_kernel(
    mixed,
    cot,
    wg,
    wu,
    wd,
    counts,
    back_out,
    partial_out,
    gate_go,
    gate_stay,
    up_go,
    up_stay,
    low_go,
    low_stay,
    high_go,
    high_stay,
    x_all,
    cot_v,
    wg_v,
    wu_v,
    wd_v,
    gate_f,
    up_f,
    back_f,
    hid,
    gb,
    ub,
    terms,
    from_left,
    from_right,
    part_buf,
    gate_k,
    up_k,
    down_k,
    in_sem,
    ag_s,
    ag_r,
    rs_s,
    rs_r,
    part_sem,
    sw_s,
    sw_r,
    out_sem,
    ready,
    live,
):
    n, w = lax.axis_index("narrow"), lax.axis_index("wide")
    y, x, core = n // 4, lax.rem(n // 2, 2), lax.rem(n, 2)
    mate = flip(n, 1)
    chunks = 4
    rows = mixed.shape[0] // chunks
    tokens, model = 4 * mixed.shape[0], mixed.shape[1]
    width = wg.shape[1]
    batch = 4 * rows
    loads = [
        pltpu.make_async_copy(src, dst, in_sem.at[k])
        for k, (src, dst) in enumerate(
            ((mixed, x_all.at[w]), (wg, wg_v), (wu, wu_v), (cot, cot_v), (wd, wd_v))
        )
    ]
    for cp in loads:
        cp.start()
    greet([mate], n, w, True)

    gather = LineGather(n, w, mixed, x_all, ag_s, ag_r, chunks)
    scatter = LineScatter(n, w, terms, (from_left, from_right), rs_s, rs_r, chunks)
    gather.start_chunk(0)
    gather.start_chunk(1)
    here = lax.broadcasted_iota(jnp.int32, counts.shape, 1) == w
    count = jnp.sum(jnp.where(here, counts[...].astype(F32), 0.0), axis=-1, keepdims=True)
    slot = lax.broadcasted_iota(jnp.int32, live.shape, 1) // TILE
    live[...] = jnp.where(slot.astype(F32) < count, 1.0, 0.0)
    gather.near(0)
    gather.far(0)
    for cp in loads:
        cp.wait()

    def rows_of(ref, i):
        r = pl.ds(pl.multiple_of(i * rows, rows), rows)
        return ref[:, r, :].reshape(batch, ref.shape[2])

    def store(i):
        return pltpu.make_async_copy(
            part_buf.at[lax.rem(i, 2)],
            partial_out.at[:, pl.ds(pl.multiple_of(i * rows, rows), rows), :],
            part_sem.at[lax.rem(i, 2)],
        )

    @pl.loop(0, chunks)
    def _(i):
        r = pl.ds(pl.multiple_of(i * rows, rows), rows)
        gather.ready(i)
        xs = rows_of(x_all, i)
        gate_f[...] = jnp.dot(xs, wg_v[...], preferred_element_type=F32)
        up_f[...] = jnp.dot(xs, wu_v[...], preferred_element_type=F32)

        @pl.when(i < chunks - 1)
        def _():
            gather.near(i + 1)

        @pl.when(i < chunks - 2)
        def _():
            gather.start_chunk(i + 2)

        back_f[...] = contract_cols(rows_of(cot_v, i), wd_v[...])
        step = 16

        @pl.loop(0, batch // step)
        def _(t):
            s = pl.ds(pl.multiple_of(t * step, step), step)
            d = t // (rows // step)
            into = pl.ds(
                pl.multiple_of(i * rows + lax.rem(t, rows // step) * step, step), step
            )
            gate, up = gate_f[s, :], up_f[s, :] * live[...]
            sigma = jax.nn.sigmoid(gate)
            silu = gate * sigma
            hid[d, into, :] = (silu * up).astype(BF)
            back = back_f[s, :]
            gb[d, into, :] = (back * up * sigma * (1.0 + gate * (1.0 - sigma))).astype(BF)
            ub[d, into, :] = (back * silu * live[...]).astype(BF)

        @pl.when(i > 0)
        def _():
            scatter.pass_on(i - 1)

        @pl.when(i < chunks - 1)
        def _():
            gather.far(i + 1)

        terms[:, r, :] = (
            (contract_cols(rows_of(gb, i), wg_v[...]) + contract_cols(rows_of(ub, i), wu_v[...]))
            .astype(BF)
            .reshape(4, rows, model)
        )
        scatter.begin(i)

        @pl.when(i > 1)
        def _():
            store(i - 2).wait()

        part_buf[lax.rem(i, 2)] = (
            jnp.dot(rows_of(hid, i), wd_v[...], preferred_element_type=F32)
            .astype(BF)
            .reshape(4, rows, model)
        )
        store(i).start()

        @pl.when(i > 0)
        def _():
            scatter.pass_end(i - 1)

    pl.semaphore_signal(
        ready, inc=1, device_id=at(mate, w), device_id_type=pl.DeviceIdType.MESH
    )

    def row_grad(back, block):
        cols = pl.ds(pl.multiple_of(block * (model // 8), model // 8), model // 8)
        return contract_rows(
            x_all[:, :, cols].reshape(tokens, model // 8), back[...].reshape(tokens, width)
        )

    def col_grad(block):
        cols = pl.ds(pl.multiple_of(block * (model // 8), model // 8), model // 8)
        return contract_rows(
            hid[...].reshape(tokens, width), cot_v[:, :, cols].reshape(tokens, model // 8)
        )

    eighth, half = model // 8, model // 2

    def place(j, base):
        return pl.ds(pl.multiple_of(base + j * eighth, eighth), eighth)

    swaps = [
        send(buf.at[pl.ds(half, half), :], buf.at[pl.ds(0, half), :], sw_s.at[k], sw_r.at[k], mate, w)
        for k, buf in enumerate((wg_v, wu_v))
    ]
    swaps.append(
        send(
            wd_v.at[:, pl.ds(half, half)], wd_v.at[:, pl.ds(0, half)], sw_s.at[2], sw_r.at[2], mate, w
        )
    )

    @pl.loop(0, 4)
    def _(j):
        wg_v[place(j, half), :] = row_grad(gb, 2 * j + 1 - core).astype(BF)

    scatter.pass_on(chunks - 1)
    pl.semaphore_wait(ready, 1)
    swaps[0].start()

    @pl.loop(0, 4)
    def _(j):
        wu_v[place(j, half), :] = row_grad(ub, 2 * j + 1 - core).astype(BF)

    swaps[1].start()

    @pl.loop(0, 4)
    def _(j):
        wd_v[:, place(j, half)] = col_grad(2 * j + 1 - core).astype(BF)

    swaps[2].start()
    swaps[0].wait_recv()

    @pl.loop(0, 4)
    def _(j):
        gate_k[j // 2, lax.rem(j, 2)] = (
            row_grad(gb, 2 * j + core) + wg_v[place(j, 0), :].astype(F32)
        ).astype(BF)

    cut = width // 2
    pieces = (
        (gate_k.at[:, 1 - x], gate_go),
        (gate_k.at[:, x], gate_stay),
        (up_k.at[1 - y], up_go),
        (up_k.at[y], up_stay),
        (down_k.at[:, 1 - x, pl.ds(0, cut), :], low_go),
        (down_k.at[:, x, pl.ds(0, cut), :], low_stay),
        (down_k.at[1 - y, :, pl.ds(cut, cut), :], high_go),
        (down_k.at[y, :, pl.ds(cut, cut), :], high_stay),
    )
    puts = [
        pltpu.make_async_copy(src, dst, out_sem.at[k]) for k, (src, dst) in enumerate(pieces)
    ]
    for k in (0, 1):
        puts[k].start()
    scatter.pass_end(chunks - 1)
    swaps[1].wait_recv()

    @pl.loop(0, 4)
    def _(j):
        up_k[j // 2, lax.rem(j, 2)] = (
            row_grad(ub, 2 * j + core) + wu_v[place(j, 0), :].astype(F32)
        ).astype(BF)

    for k in (2, 3):
        puts[k].start()
    swaps[2].wait_recv()

    @pl.loop(0, 4)
    def _(j):
        down_k[j // 2, lax.rem(j, 2)] = (
            col_grad(2 * j + core) + wd_v[:, place(j, 0)].astype(F32)
        ).astype(BF)

    for k in (4, 5, 6, 7):
        puts[k].start()
    for i in range(chunks):
        scatter.finish(i, back_out)
    scatter.drain()
    gather.finish_sends()
    for k in range(3):
        swaps[k].wait_send()
    store(chunks - 2).wait()
    store(chunks - 1).wait()
    for cp in puts:
        cp.wait()


def feed_forward(mixed, cot, gate_weight, up_weight, down_weight, counts):
    tokens_here, model = mixed.shape
    width = gate_weight.shape[1]
    rows, eighth, cut = tokens_here // 4, model // 8, width // 2
    hbm, vmem = pl.BlockSpec(memory_space=pl.ANY), pl.BlockSpec(memory_space=pltpu.VMEM)
    row_piece = jax.ShapeDtypeStruct((2, eighth, width), BF)
    col_piece = jax.ShapeDtypeStruct((2, cut, eighth), BF)
    dma = pltpu.SemaphoreType.DMA
    acc = pltpu.VMEM((4 * rows, width), F32)
    act = pltpu.VMEM((4, tokens_here, width), BF)
    tok = pltpu.VMEM((4, tokens_here, model), BF)
    three = pltpu.VMEM((3, tokens_here, model), BF)
    return pl.pallas_call(
        middle_kernel,
        name="feed_forward",
        out_shape=(
            jax.ShapeDtypeStruct(mixed.shape, F32),
            jax.ShapeDtypeStruct((4,) + mixed.shape, BF),
        )
        + (row_piece,) * 4
        + (col_piece,) * 4,
        in_specs=[hbm] * 5 + [vmem],
        out_specs=[vmem] + [hbm] * 9,
        scratch_shapes=[
            tok,
            tok,
            pltpu.VMEM(gate_weight.shape, BF),
            pltpu.VMEM(up_weight.shape, BF),
            pltpu.VMEM(down_weight.shape, BF),
            acc,
            acc,
            acc,
            act,
            act,
            act,
            tok,
            three,
            three,
            pltpu.VMEM((2, 4, rows, model), BF),
            pltpu.VMEM((2, 2, eighth, width), BF),
            pltpu.VMEM((2, 2, eighth, width), BF),
            pltpu.VMEM((2, 2, width, eighth), BF),
            dma((5,)),
            dma((32,)),
            dma((16,)),
            dma((24,)),
            dma((24,)),
            dma((2,)),
            dma((3,)),
            dma((3,)),
            dma((8,)),
            pltpu.SemaphoreType.REGULAR,
            pltpu.VMEM((1, width), F32),
        ],
        compiler_params=pltpu.CompilerParams(
            collective_id=5, has_side_effects=True, vmem_limit_bytes=64 * 1024 * 1024 - 65536
        ),
    )(mixed, cot, gate_weight, up_weight, down_weight, counts)


class Reduce:
    def __init__(self, me, factors, cols, x_first, bufs, sems, k):
        self.n, self.w, self.y, self.x, self.core = me
        self.left, self.right = factors
        self.cols, self.x_first = pl.ds(*cols), x_first
        self.away, self.sum, self.pair, self.one, self.two = bufs
        self.sems, self.k = sems, k
        self.rows = self.sum.shape[2]
        self.near = flip(self.n, 2) if x_first else flip(self.n, 4)
        self.next = flip(self.n, 4) if x_first else flip(self.n, 2)

    def term(self, block):
        own = pl.ds(pl.multiple_of(block * self.rows, self.rows), self.rows)
        return contract_rows(self.left[:, own], self.right[:, self.cols])

    def swap(self):
        return send(
            self.away,
            self.pair,
            self.sems[0].at[self.k],
            self.sems[1].at[self.k],
            flip(self.n, 1),
            self.w,
        )

    def before_swap(self):
        @pl.loop(0, 4)
        def _(j):
            self.away[j // 2, lax.rem(j, 2)] = self.term(2 * j + 1 - self.core).astype(BF)

        self.swap().start()

    def block(self, first, second):
        return (second, first) if self.x_first else (first, second)

    def axes(self):
        return (self.x, self.y) if self.x_first else (self.y, self.x)

    def stage(self, s):
        a, b = self.axes()
        if s == 1:
            src = self.sum.at[:, 1 - a] if self.x_first else self.sum.at[1 - a]
            dst, peer = self.one, self.near
        else:
            src = self.sum.at[self.block(a, 1 - b)]
            dst, peer = self.two, self.next
        k = 2 * self.k + s - 1
        return send(src, dst, self.sems[2].at[k], self.sems[3].at[k], peer, self.w)

    def add(self, block, other):
        step = 64 if self.rows % 64 == 0 else 48

        @pl.loop(0, self.rows // step)
        def _(i):
            r = pl.ds(pl.multiple_of(i * step, step), step)
            self.sum[block[0], block[1], r, :] = (
                self.sum[block[0], block[1], r, :] + other[r, :]
            )

    def after_swap(self):
        a, _ = self.axes()
        self.swap().wait_recv()

        @pl.loop(0, 4)
        def _(j):
            first = lax.rem(1 - a + j // 2, 2)
            y, x = self.block(first, lax.rem(j, 2))
            total = self.term(4 * y + 2 * x + self.core) + self.pair[y, x].astype(F32)
            self.sum[y, x] = total.astype(BF)

        self.stage(1).start()

    def after_one(self):
        a, b = self.axes()
        self.stage(1).wait()
        self.add(self.block(a, 1 - b), self.one.at[1 - b])
        self.stage(2).start()
        self.add(self.block(a, b), self.one.at[b])

    def after_two(self):
        a, b = self.axes()
        self.stage(2).wait()
        self.add(self.block(a, b), self.two)

    def result(self):
        return self.sum.at[self.y, self.x]


class Half:
    def __init__(self, me, kept, came, x_first, bufs, sems, k):
        self.n, self.w, self.y, self.x, self.core = me
        self.kept, self.came, self.x_first = kept, came, x_first
        self.sum, self.one, self.two = bufs
        self.sems, self.k = sems, k
        self.rows = kept.shape[1]
        self.next = flip(self.n, 4) if x_first else flip(self.n, 2)
        self.here = self.y if x_first else self.x

    def loads(self):
        return [
            pltpu.make_async_copy(self.kept, self.sum, self.sems[0].at[2 * self.k]),
            pltpu.make_async_copy(self.came, self.one, self.sems[0].at[2 * self.k + 1]),
        ]

    def stage(self):
        return send(
            self.sum.at[1 - self.here],
            self.two,
            self.sems[1].at[self.k],
            self.sems[2].at[self.k],
            self.next,
            self.w,
        )

    def add(self, block, other):
        @pl.loop(0, self.rows // 64)
        def _(i):
            r = pl.ds(pl.multiple_of(i * 64, 64), 64)
            self.sum[block, r, :] = self.sum[block, r, :] + other[r, :]

    def after_one(self):
        for cp in self.loads():
            cp.wait()
        self.add(1 - self.here, self.one.at[1 - self.here])
        self.stage().start()
        self.add(self.here, self.one.at[self.here])

    def after_two(self):
        self.stage().wait()
        self.add(self.here, self.two)

    def result(self):
        return self.sum.at[self.here]


class Spread:
    def __init__(self, item, region, sems, k):
        self.item, self.region, self.sems, self.k = item, region, sems, k
        n = item.n
        self.blocks = (n, flip(n, 2), flip(n, 4), flip(flip(n, 2), 4))

    def copy(self, kind, src, block, peer):
        k = 7 * self.k + kind
        return send(
            src, self.region(block), self.sems[0].at[k], self.sems[1].at[k], peer, self.item.w
        )

    def own(self, kind):
        n = self.item.n
        return self.copy(kind, self.item.result(), n, (flip(n, 2), flip(n, 4), flip(n, 1))[kind])

    def corner(self):
        n, b = self.item.n, self.blocks
        if self.item.x_first:
            return self.copy(3, self.region(b[2]), b[2], flip(n, 2))
        return self.copy(3, self.region(b[1]), b[1], flip(n, 4))

    def to_core(self, which):
        block = self.blocks[which]
        return self.copy(3 + which, self.region(block), block, flip(self.item.n, 1))

    def keep(self):
        return pltpu.make_async_copy(
            self.item.result(), self.region(self.item.n), self.sems[2].at[self.k]
        )

    def start(self):
        order = (1, 0, 2) if self.item.x_first else (0, 1, 2)
        for kind in order:
            self.own(kind).start()
        self.keep().start()

    def relay(self):
        first, second = (1, 0) if self.item.x_first else (0, 1)
        self.own(first).wait_recv()
        self.corner().start()
        self.to_core(1 + first).start()
        self.own(second).wait_recv()
        self.to_core(1 + second).start()

    def last(self):
        self.corner().wait_recv()
        self.to_core(3).start()

    def finish(self):
        for kind in range(2):
            self.own(kind).wait_send()
        self.own(2).wait()
        self.corner().wait_send()
        for which in range(1, 4):
            self.to_core(which).wait()
        self.keep().wait()


class Rows:
    def __init__(self, ref):
        self.ref = ref
        self.shape = (4, ref.shape[0] // 4, ref.shape[1])

    @property
    def at(self):
        return self

    def __getitem__(self, index):
        d, r, _ = index
        start = pl.multiple_of(d * self.shape[1] + r.start, r.size)
        return self.ref.at[pl.ds(start, r.size), :]


def last_kernel(items, *refs):
    refs = list(refs)

    def take(count):
        out = refs[:count]
        del refs[:count]
        return out

    factors = take(4)
    stays, comes = take(4), take(4)
    feed_terms, gain_parts = take(2)
    outs = take(4)
    gate_full, up_full, down_full = take(3)
    feed_out, gain_out = take(2)
    attn_bufs = [take(5) for _ in range(4)]
    ffn_bufs = [take(3) for _ in range(4)]
    line_bufs = [take(3) for _ in range(4)]
    feed_v, feed_left, feed_right = take(3)
    gain_in, gain_sum, gain_line = take(3)
    factor_bufs = take(4)
    load_sem, swap_s, swap_r, st_s, st_r = take(5)
    half_sems = take(3)
    sp_sems = take(3)
    lr_s, lr_r, lg_s, lg_r, lg_l = take(5)
    fd_s, fd_r, fd_l = take(3)
    gn_s, gn_r, gz_s, gz_r = take(4)

    n, w = lax.axis_index("narrow"), lax.axis_index("wide")
    me = (n, w, n // 4, lax.rem(n // 2, 2), lax.rem(n, 2))
    attn = [
        Reduce(
            me,
            factor_bufs[2 * p : 2 * p + 2],
            cols,
            xf,
            attn_bufs[k],
            (swap_s, swap_r, st_s, st_r),
            k,
        )
        for k, (p, cols, xf) in enumerate(items)
    ]
    ffn = [
        Half(me, stays[k], comes[k], k % 2 == 0, ffn_bufs[k], half_sems, k) for k in range(4)
    ]
    cut, eighth = stays[2].shape[1], stays[2].shape[2]

    def down_region(k):
        return lambda block: down_full.at[
            pl.ds(k * cut, cut), pl.ds(pl.multiple_of(block * eighth, eighth), eighth)
        ]

    regions = (
        lambda block: gate_full.at[block],
        lambda block: up_full.at[block],
        down_region(0),
        down_region(1),
    )
    spread = [Spread(ffn[k], regions[k], sp_sems, k) for k in range(4)]
    for item in ffn:
        for cp in item.loads():
            cp.start()
    factor_loads = [
        pltpu.make_async_copy(src, dst, load_sem.at[k])
        for k, (src, dst) in enumerate(zip(factors, factor_bufs))
    ]
    for cp in factor_loads:
        cp.start()
    feed_load = pltpu.make_async_copy(feed_terms, feed_v, fd_l)
    feed_load.start()

    barrier = pltpu.get_barrier_semaphore()
    narrow_peers = [lax.rem(n + i, 8) for i in range(1, 8)]
    wide_peers = [lax.rem(w + i, 4) for i in range(1, 4)]
    for peer in narrow_peers:
        pl.semaphore_signal(
            barrier, inc=1, device_id=at(peer, w), device_id_type=pl.DeviceIdType.MESH
        )
    for peer in wide_peers:
        pl.semaphore_signal(
            barrier, inc=1, device_id=at(n, peer), device_id_type=pl.DeviceIdType.MESH
        )
    pl.semaphore_wait(barrier, 10)

    feed_load.wait()
    feed = LineScatter(n, w, feed_v, (feed_left, feed_right), fd_s, fd_r, 4)
    for i in range(4):
        feed.begin(i)

    def gain_narrow(i):
        peer = narrow_peers[i]
        return send(gain_parts.at[peer], gain_in.at[i], gn_s.at[i], gn_r.at[i], peer, w)

    def gain_wide(i):
        return send(gain_sum, gain_line.at[i], gz_s.at[i], gz_r.at[i], n, wide_peers[i])

    for i in range(7):
        gain_narrow(i).start()

    for item in ffn:
        item.after_one()
    for cp in factor_loads:
        cp.wait()
    for item in attn:
        item.before_swap()
    feed.pass_on(0)
    for item in attn:
        item.after_swap()
    feed.pass_on(1)
    feed.pass_end(0)
    for i in range(7):
        gain_narrow(i).wait()
    total = gain_parts[n]
    for i in range(7):
        total = total + gain_in[i]
    gain_sum[...] = total
    for i in range(3):
        gain_wide(i).start()
    feed.pass_on(2)
    feed.pass_end(1)
    for item in attn[:2]:
        item.after_one()
    feed.pass_on(3)
    feed.pass_end(2)
    for item in attn[2:]:
        item.after_one()
    feed.pass_end(3)
    for k in range(4):
        ffn[k].after_two()
        spread[k].start()

    scatters, gathers = [], []
    for k, item in enumerate(attn):
        left, right, own = line_bufs[k]
        scatters.append(
            LineScatter(n, w, Rows(item.result()), (left, right), lr_s.at[k], lr_r.at[k], 1)
        )
        gathers.append(LineGather(n, w, own, outs[k], lg_s.at[k], lg_r.at[k], 1))

    def keep(k):
        return pltpu.make_async_copy(line_bufs[k][2], outs[k].at[w], lg_l.at[k])

    def line_turn(k):
        scatters[k].finish(0, line_bufs[k][2])
        gathers[k].start()
        keep(k).start()

    for k in (0, 1):
        attn[k].after_two()
        scatters[k].begin(0)
    for i in range(4):
        feed.finish(i, feed_out)
    for k in (2, 3):
        attn[k].after_two()
        scatters[k].begin(0)
    for k in (0, 1, 2, 3):
        scatters[k].pass_on(0)
    for k in (0, 1, 2, 3):
        scatters[k].pass_end(0)
    for k in (0, 1, 2, 3):
        line_turn(k)
    for s in spread[:2]:
        s.relay()
    for k in (0, 1, 2, 3):
        gathers[k].near(0)
    for k in (0, 1, 2, 3):
        gathers[k].far(0)
    for s in spread[2:]:
        s.relay()
    for i in range(3):
        gain_wide(i).wait()
    gain_out[...] = (gain_sum[...] + gain_line[0]) + (gain_line[1] + gain_line[2])
    for s in spread:
        s.last()
    for s in spread:
        s.finish()
    for item in attn:
        item.swap().wait_send()
    for k in range(4):
        scatters[k].drain()
        gathers[k].finish()
        keep(k).wait()
    feed.drain()


def reduce_last(factors, stays, comes, feed_terms, gain_parts):
    rows = factors[0].shape[1] // 8
    q_cols, k_cols = HEADS * HEAD_DIM, KV_HEADS * HEAD_DIM
    items = [
        (0, (0, q_cols), True),
        (0, (q_cols, 2 * k_cols), False),
        (1, (0, k_cols), True),
        (1, (k_cols, q_cols - k_cols), False),
    ]
    scratch = []
    for _, (_, cols), _ in items:
        scratch += [
            pltpu.VMEM((2, 2, rows, cols), BF),
            pltpu.VMEM((2, 2, rows, cols), BF),
            pltpu.VMEM((2, 2, rows, cols), BF),
            pltpu.VMEM((2, rows, cols), BF),
            pltpu.VMEM((rows, cols), BF),
        ]
    for stay in stays:
        scratch += [
            pltpu.VMEM(stay.shape, BF),
            pltpu.VMEM(stay.shape, BF),
            pltpu.VMEM(stay.shape[1:], BF),
        ]
    outs = []
    for _, (_, cols), _ in items:
        scratch += [pltpu.VMEM((3, rows // 4, cols), BF)] * 2 + [pltpu.VMEM((rows // 4, cols), BF)]
        outs.append(jax.ShapeDtypeStruct((4, rows // 4, cols), BF))
    outs.append(jax.ShapeDtypeStruct((8,) + stays[0].shape[1:], BF))
    outs.append(jax.ShapeDtypeStruct((8,) + stays[1].shape[1:], BF))
    outs.append(jax.ShapeDtypeStruct((2 * stays[2].shape[1], 8 * stays[2].shape[2]), BF))
    outs.append(jax.ShapeDtypeStruct(feed_terms.shape[1:], F32))
    outs.append(jax.ShapeDtypeStruct(gain_parts.shape[1:], F32))
    scratch += [pltpu.VMEM(feed_terms.shape, BF)]
    scratch += [pltpu.VMEM((3,) + feed_terms.shape[1:], BF)] * 2
    scratch += [
        pltpu.VMEM((7,) + gain_parts.shape[1:], F32),
        pltpu.VMEM(gain_parts.shape[1:], F32),
        pltpu.VMEM((3,) + gain_parts.shape[1:], F32),
    ]
    scratch += [pltpu.VMEM(f.shape, BF) for f in factors]
    dma = pltpu.SemaphoreType.DMA
    scratch += [dma((4,)), dma((4,)), dma((4,)), dma((8,)), dma((8,))]
    scratch += [dma((8,)), dma((4,)), dma((4,))]
    scratch += [dma((28,)), dma((28,)), dma((4,))]
    scratch += [dma((4, 6)), dma((4, 6)), dma((4, 8)), dma((4, 4)), dma((4,))]
    scratch += [dma((24,)), dma((24,)), dma]
    scratch += [dma((7,)), dma((7,)), dma((3,)), dma((3,))]
    hbm, vmem = pl.BlockSpec(memory_space=pl.ANY), pl.BlockSpec(memory_space=pltpu.VMEM)
    out = pl.pallas_call(
        functools.partial(last_kernel, items),
        name="reduce_last",
        out_shape=tuple(outs),
        in_specs=[hbm] * 13 + [vmem],
        out_specs=[hbm] * 7 + [vmem] * 2,
        scratch_shapes=scratch,
        compiler_params=pltpu.CompilerParams(
            collective_id=4, has_side_effects=True, vmem_limit_bytes=64 * 1024 * 1024 - 65536
        ),
    )(*factors, *stays, *comes, feed_terms, gain_parts)
    qkv = out[0].reshape(rows, -1), out[1].reshape(rows, -1)
    project = jnp.concatenate([out[2].reshape(rows, -1), out[3].reshape(rows, -1)], axis=1)
    width = out[4].shape[2]
    ffn = [out[4].reshape(-1, width), out[5].reshape(-1, width), out[6]]
    return qkv, project, ffn, out[7], out[8]


def per_device(
    fast,
    block_input,
    cotangent,
    query_weight,
    key_weight,
    value_weight,
    project_weight,
    prenorm_gain,
    midnorm_gain,
    gate_weight,
    up_weight,
    down_weight,
    doc_lengths,
    tile_counts,
):
    tokens_here, model = block_input.shape
    group = HEADS // KV_HEADS
    scale = HEAD_DIM ** (-0.5)
    q_cols, k_cols = HEADS * HEAD_DIM, KV_HEADS * HEAD_DIM
    inputs_f = block_input.astype(jnp.float32)
    ends = jnp.cumsum(doc_lengths[0])
    position = jnp.arange(tokens_here, dtype=jnp.int32)
    segment = jnp.sum((position[:, None] >= ends[None, :]).astype(jnp.int32), axis=1)
    allowed = (segment[:, None] == segment[None, :]) & (position[None, :] <= position[:, None])
    if fast:
        gains = jnp.stack([prenorm_gain, midnorm_gain]).astype(F32).reshape(1, -1)
        qkv_full, project_full, grad_rows, normed, qkv, attended, *rest = gather_first(
            block_input,
            query_weight,
            key_weight,
            value_weight,
            project_weight,
            gains,
            cotangent,
            doc_lengths,
        )
        middle, mixed_in, first_gain, second_gain, bias, logs = rest
        first_gain, second_gain = first_gain.reshape(-1), second_gain.reshape(-1)
    else:
        qkv_full = jnp.concatenate(
            [
                lax.all_gather(query_weight, "narrow", axis=0, tiled=True),
                lax.all_gather(key_weight, "narrow", axis=0, tiled=True),
                lax.all_gather(value_weight, "narrow", axis=0, tiled=True),
            ],
            axis=1,
        )
        project_full = lax.all_gather(project_weight, "narrow", axis=1, tiled=True)
        first_gain = lax.all_gather(prenorm_gain, "narrow", axis=0, tiled=True).astype(F32)
        second_gain = lax.all_gather(midnorm_gain, "narrow", axis=0, tiled=True).astype(F32)
        grad_rows = lax.all_gather(cotangent, "wide", axis=0, tiled=True)
        normed = rms_scale(inputs_f, first_gain).astype(jnp.bfloat16)
        qkv = jnp.dot(normed, qkv_full, preferred_element_type=jnp.float32).astype(jnp.bfloat16)
    if not fast:
        query_rows = qkv[:, :q_cols].reshape(tokens_here, KV_HEADS, group, HEAD_DIM)
        key_rows = qkv[:, q_cols : q_cols + k_cols].reshape(tokens_here, KV_HEADS, HEAD_DIM)
        value_rows = qkv[:, q_cols + k_cols :].reshape(tokens_here, KV_HEADS, HEAD_DIM)
        scores = (
            jnp.einsum("qcgd,kcd->cgqk", query_rows, key_rows, preferred_element_type=jnp.float32)
            * scale
        )
        masked = jnp.where(allowed, scores, -1e30)
        peak = jnp.max(masked, axis=-1, keepdims=True)
        expo = jnp.exp(masked - peak)
        total = jnp.sum(expo, axis=-1, keepdims=True)
        probs_low = (expo / total).astype(jnp.bfloat16)
        logsum = peak + jnp.log(total)
        attended = (
            jnp.einsum("cgqk,kcd->qcgd", probs_low, value_rows, preferred_element_type=jnp.float32)
            .astype(jnp.bfloat16)
            .reshape(tokens_here, HEADS * HEAD_DIM)
        )
        branch = jnp.dot(attended, project_full, preferred_element_type=jnp.float32)
        middle = inputs_f + branch
        mixed_in = rms_scale(middle, second_gain).astype(jnp.bfloat16)
    width = gate_weight.shape[1]
    wide_index = lax.axis_index("wide")
    my_count = jnp.sum(
        jnp.where(jnp.arange(tile_counts.shape[0], dtype=jnp.int32) == wide_index, tile_counts, 0)
    )
    live = (jnp.arange(width, dtype=jnp.int32) // TILE < my_count).astype(jnp.float32)
    if fast:
        mixed_back, feed_terms, *pieces = feed_forward(
            mixed_in, grad_rows, gate_weight, up_weight, down_weight, tile_counts.reshape(1, -1)
        )
        stays = pieces[1::2]
        comes = [
            lax.ppermute(piece, "narrow", [(i, i ^ bit) for i in range(8)])
            for piece, bit in zip(pieces[0::2], (2, 4, 2, 4))
        ]
    else:
        gathered = lax.all_gather(mixed_in, "wide", axis=0, tiled=True)
        gate_pre = jnp.dot(gathered, gate_weight, preferred_element_type=jnp.float32)
        up_pre = jnp.dot(gathered, up_weight, preferred_element_type=jnp.float32)
        hidden_back = contract_cols(grad_rows, down_weight)
        sigma = jax.nn.sigmoid(gate_pre)
        hidden = (gate_pre * sigma * up_pre * live).astype(BF)
        gate_back = (
            hidden_back * up_pre * live * sigma * (1.0 + gate_pre * (1.0 - sigma))
        ).astype(BF)
        up_back = (hidden_back * gate_pre * sigma * live).astype(BF)
        mixed_terms = (
            contract_cols(gate_back, gate_weight) + contract_cols(up_back, up_weight)
        ).astype(BF)
        mixed_back = lax.psum_scatter(
            mixed_terms, "wide", scatter_dimension=0, tiled=True
        ).astype(F32)
        partial_rows = jnp.dot(hidden, down_weight, preferred_element_type=jnp.float32)
        down_part = contract_rows(hidden, grad_rows)
        gate_part = contract_rows(gathered, gate_back)
        up_part = contract_rows(gathered, up_back)
    out_grad = cotangent.astype(jnp.float32)
    if fast:
        middle_norm_back, second_gain_part = scale_back(
            mixed_back, middle, second_gain, logs[:, 126:127]
        )
    else:
        unused_second, second_backward = jax.vjp(rms_scale, middle, second_gain)
        middle_norm_back, second_gain_part = second_backward(mixed_back)
    middle_back = out_grad + middle_norm_back
    branch_back = middle_back.astype(jnp.bfloat16)
    attended_back = contract_cols(branch_back, project_full).astype(jnp.bfloat16)
    if fast:
        qkv_back = attention_back(qkv, attended_back, logs, bias)
    else:
        attended_back = attended_back.reshape(tokens_here, KV_HEADS, group, HEAD_DIM)
        scores_again = (
            jnp.einsum("qcgd,kcd->cgqk", query_rows, key_rows, preferred_element_type=jnp.float32)
            * scale
        )
        probs_again = jnp.where(allowed, jnp.exp(scores_again - logsum), 0.0)
        probs_again_low = probs_again.astype(jnp.bfloat16)
        value_back = (
            jnp.einsum(
                "cgqk,qcgd->kcd", probs_again_low, attended_back, preferred_element_type=jnp.float32
            )
            .astype(jnp.bfloat16)
            .reshape(tokens_here, KV_HEADS * HEAD_DIM)
        )
        probs_back = jnp.einsum(
            "qcgd,kcd->cgqk", attended_back, value_rows, preferred_element_type=jnp.float32
        )
        scores_back = (
            probs_again * (probs_back - jnp.sum(probs_again * probs_back, axis=-1, keepdims=True))
        ).astype(jnp.bfloat16)
        query_back = (
            (
                jnp.einsum("cgqk,kcd->qcgd", scores_back, key_rows, preferred_element_type=jnp.float32)
                * scale
            )
            .astype(jnp.bfloat16)
            .reshape(tokens_here, HEADS * HEAD_DIM)
        )
        key_back = (
            (
                jnp.einsum(
                    "cgqk,qcgd->kcd", scores_back, query_rows, preferred_element_type=jnp.float32
                )
                * scale
            )
            .astype(jnp.bfloat16)
            .reshape(tokens_here, KV_HEADS * HEAD_DIM)
        )
        qkv_back = jnp.concatenate([query_back, key_back, value_back], axis=1)
    normed_back = contract_cols(qkv_back, qkv_full)
    if fast:
        input_norm_back, first_gain_part = scale_back(
            normed_back, inputs_f, first_gain, logs[:, 127:128]
        )
    else:
        unused_first, first_backward = jax.vjp(rms_scale, inputs_f, first_gain)
        input_norm_back, first_gain_part = first_backward(normed_back)
    input_grad = (middle_back + input_norm_back).astype(jnp.bfloat16)

    if fast:
        gain_parts = jnp.stack(
            [first_gain_part.reshape(8, -1), second_gain_part.reshape(8, -1)], axis=1
        ).reshape(8, 1, -1)
        input_grad, qkv_back = lax.optimization_barrier((input_grad, qkv_back))
        qkv_total, project_total, ffn_totals, feed, gain_total = reduce_last(
            (normed, qkv_back, branch_back, attended),
            stays,
            comes,
            feed_terms,
            gain_parts,
        )
        gain_total = gain_total.reshape(2, -1)
        first_total, second_total = gain_total[0], gain_total[1]
        query_total = qkv_total[0].astype(F32)
        key_total = qkv_total[1][:, :k_cols].astype(F32)
        value_total = qkv_total[1][:, k_cols:].astype(F32)
        project_total = project_total.T.astype(F32)
        gate_total, up_total, down_total = [t.astype(F32) for t in ffn_totals]
    else:

        def owned(part):
            share = lax.psum_scatter(part.astype(BF), "narrow", scatter_dimension=0, tiled=True)
            return lax.psum(share, "wide").astype(F32)

        qkv_total = owned(contract_rows(normed, qkv_back))
        query_total = qkv_total[:, :q_cols]
        key_total = qkv_total[:, q_cols : q_cols + k_cols]
        value_total = qkv_total[:, q_cols + k_cols :]
        project_total = owned(contract_rows(branch_back, attended)).T
        first_total = owned(first_gain_part)
        second_total = owned(second_gain_part)
        gate_total, up_total, down_total = (
            lax.psum(gate_part.astype(BF), "narrow").astype(F32),
            lax.psum(up_part.astype(BF), "narrow").astype(F32),
            lax.psum(down_part.astype(BF), "narrow").astype(F32),
        )
        feed = lax.psum_scatter(
            partial_rows.astype(BF), "wide", scatter_dimension=0, tiled=True
        ).astype(F32)
    block_output = (middle + feed).astype(BF)
    return (
        block_output,
        input_grad,
        query_total,
        key_total,
        value_total,
        project_total,
        first_total,
        second_total,
        gate_total,
        up_total,
        down_total,
    )


def solution(mesh):
    fast = mesh.shape["narrow"] == 8 and mesh.shape["wide"] == 4
    placed = (
        P(("narrow", "wide"), None),
        P(("narrow", "wide"), None),
        P("narrow", None),
        P("narrow", None),
        P("narrow", None),
        P(None, "narrow"),
        P("narrow"),
        P("narrow"),
        P(None, "wide"),
        P(None, "wide"),
        P("wide", None),
        P(("narrow", "wide"), None),
        P(),
    )
    return jax.shard_map(
        functools.partial(per_device, fast),
        mesh=mesh,
        in_specs=placed,
        out_specs=(
            P(("narrow", "wide"), None),
            P(("narrow", "wide"), None),
            P("narrow", None),
            P("narrow", None),
            P("narrow", None),
            P(None, "narrow"),
            P("narrow"),
            P("narrow"),
            P(None, "wide"),
            P(None, "wide"),
            P("wide", None),
        ),
        check_vma=False,
    )
```

```python
import functools

import jax
import jax.numpy as jnp
from jax import lax
from jax.experimental import pallas as pl
from jax.experimental.pallas import tpu as pltpu
from jax.sharding import PartitionSpec as P

HEADS = 24
KV_HEADS = 6
HEAD_DIM = 64
TILE = 128


EPSILON = 1e-06

BF = jnp.bfloat16
F32 = jnp.float32


def rms_scale(rows, gain):
    factor = lax.rsqrt(jnp.mean(rows * rows, axis=-1, keepdims=True) + EPSILON)
    return rows * factor * gain


def scale_back(back, rows, gain, factor):
    scaled = back * gain
    inner = jnp.mean(scaled * rows, axis=-1, keepdims=True)
    return factor * scaled - rows * (factor**3 * inner), jnp.sum(back * rows * factor, axis=0)


def contract_rows(left, right):
    return lax.dot_general(
        left, right, (((0,), (0,)), ((), ())), preferred_element_type=jnp.float32
    )


def contract_cols(left, right):
    return lax.dot_general(
        left, right, (((1,), (1,)), ((), ())), preferred_element_type=jnp.float32
    )


def flip(n, bit):
    return n + bit - 2 * bit * lax.rem(n // bit, 2)


def at(n, w):
    return {"narrow": n, "wide": w}


def send(src, dst, ssem, rsem, n, w):
    return pltpu.make_async_remote_copy(
        src_ref=src,
        dst_ref=dst,
        send_sem=ssem,
        recv_sem=rsem,
        device_id=at(n, w),
        device_id_type=pl.DeviceIdType.MESH,
    )


def greet(narrow_peers, n, w, line):
    barrier = pltpu.get_barrier_semaphore()
    for peer in narrow_peers:
        pl.semaphore_signal(
            barrier, inc=1, device_id=at(peer, w), device_id_type=pl.DeviceIdType.MESH
        )
    if not line:
        pl.semaphore_wait(barrier, len(narrow_peers))
    if line:

        @pl.when(w > 0)
        def _():
            pl.semaphore_signal(
                barrier, inc=1, device_id=at(n, w - 1), device_id_type=pl.DeviceIdType.MESH
            )

        @pl.when(w < 3)
        def _():
            pl.semaphore_signal(
                barrier, inc=1, device_id=at(n, w + 1), device_id_type=pl.DeviceIdType.MESH
            )

        @pl.when((w == 0) | (w == 3))
        def _():
            pl.semaphore_wait(barrier, len(narrow_peers) + 1)

        @pl.when((w == 1) | (w == 2))
        def _():
            pl.semaphore_wait(barrier, len(narrow_peers) + 2)


class LineGather:
    def __init__(self, n, w, own, whole, ssem, rsem, chunks):
        self.n, self.w, self.own, self.whole = n, w, own, whole
        self.ssem, self.rsem, self.chunks = ssem, rsem, chunks
        self.rows = own.shape[0] // chunks

    def span(self, i):
        return pl.ds(pl.multiple_of(i * self.rows, self.rows), self.rows)

    def part(self, shard, i):
        return self.whole.at[shard, self.span(i), :]

    def put(self, way, here, shard, i):
        src = self.own.at[self.span(i), :] if shard is here else self.part(shard, i)
        to = here + 1 - 2 * way
        s = (way * 4 + shard) * self.chunks + i
        r = shard * self.chunks + i
        return send(src, self.part(shard, i), self.ssem.at[s], self.rsem.at[r], self.n, to)

    def came(self, shard, i):
        self.put(0, 0, shard, i).wait_recv()

    def start_chunk(self, i):
        @pl.when(self.w < 3)
        def _():
            self.put(0, self.w, self.w, i).start()

        @pl.when(self.w > 0)
        def _():
            self.put(1, self.w, self.w, i).start()

    def start(self):
        for i in range(self.chunks):
            self.start_chunk(i)

    def near(self, i):
        @pl.when(self.w == 1)
        def _():
            self.came(0, i)
            self.put(0, 1, 0, i).start()
            self.came(2, i)
            self.put(1, 1, 2, i).start()

        @pl.when(self.w == 2)
        def _():
            self.came(3, i)
            self.put(1, 2, 3, i).start()
            self.came(1, i)
            self.put(0, 2, 1, i).start()

    def far(self, i):
        @pl.when(self.w == 1)
        def _():
            self.came(3, i)
            self.put(1, 1, 3, i).start()

        @pl.when(self.w == 2)
        def _():
            self.came(0, i)
            self.put(0, 2, 0, i).start()

    def ready(self, i):
        @pl.when(self.w == 0)
        def _():
            for shard in (1, 2, 3):
                self.came(shard, i)

        @pl.when(self.w == 3)
        def _():
            for shard in (2, 1, 0):
                self.came(shard, i)

    def finish_sends(self):
        for here in range(4):

            @pl.when(self.w == here)
            def _():
                for i in range(self.chunks):
                    if here < 3:
                        for shard in range(here + 1):
                            self.put(0, here, shard, i).wait_send()
                    if here > 0:
                        for shard in range(here, 4):
                            self.put(1, here, shard, i).wait_send()

    def finish(self):
        for i in range(self.chunks):
            self.ready(i)
        self.finish_sends()


def first_kernel(
    x_ref,
    q_ref,
    k_ref,
    v_ref,
    p_ref,
    g_ref,
    c_ref,
    docs_ref,
    qkv_out,
    p_out,
    c_full,
    normed_out,
    rows_out,
    att_out,
    middle_out,
    mixed_out,
    gain_row,
    gain_late,
    bias_ref,
    log_out,
    g_full,
    qkv_full,
    p_full,
    c_buf,
    x_buf,
    normed,
    middle,
    mixed,
    qkv,
    att,
    in_sem,
    out_sem,
    ssem,
    rsem,
    gs_sem,
    gr_sem,
    zs_sem,
    zr_sem,
):
    n, w = lax.axis_index("narrow"), lax.axis_index("wide")
    x, y, c, d = flip(n, 2), flip(n, 4), flip(n, 1), flip(flip(n, 2), 4)
    others = [lax.rem(n + i, 8) for i in range(1, 8)]
    rows = q_ref.shape[0]
    half = rows // 2
    depth = p_ref.shape[0]
    qc, kc = q_ref.shape[1], k_ref.shape[1]
    cols = ((0, qc), (qc, kc), (qc + kc, kc))

    def region(t, block, h):
        if t == 3:
            r = pl.ds(0, depth) if h == 2 else pl.ds(h * (depth // 2), depth // 2)
            return p_full.at[r, pl.ds(pl.multiple_of(block * rows, rows), rows)]
        start = pl.multiple_of(block * rows, rows)
        r = pl.ds(start, rows) if h == 2 else pl.ds(start + h * half, half)
        return qkv_full.at[r, pl.ds(cols[t][0], cols[t][1])]

    locals_in = []
    for i, (src, dst) in enumerate(
        (
            (g_ref, g_full.at[n]),
            (x_ref, x_buf),
            (p_ref, region(3, n, 2)),
            (c_ref, c_buf),
            (q_ref, region(0, n, 2)),
            (k_ref, region(1, n, 2)),
            (v_ref, region(2, n, 2)),
        )
    ):
        cp = pltpu.make_async_copy(src, dst, in_sem.at[i])
        cp.start()
        locals_in.append(cp)

    greet(others, n, w, True)

    def own(t, h):
        ref = (q_ref, k_ref, v_ref, p_ref)[t]
        if h == 2:
            return ref
        size = ref.shape[0] // 2
        return ref.at[pl.ds(h * size, size), :]

    def msg(t, kind, src, block, h, peer):
        k = t * 10 + kind
        return send(src, region(t, block, h), ssem.at[k], rsem.at[k], peer, w)

    def to_x(t, h):
        return msg(t, h, own(t, h), n, h, x)

    def to_y(t, h):
        return msg(t, 2 + h, own(t, h), n, h, y)

    def on_x(t):
        return msg(t, 4, region(t, y, 0), y, 0, x)

    def on_y(t):
        return msg(t, 5, region(t, x, 1), x, 1, y)

    def to_c(t, which):
        block = (n, x, y, d)[which]
        src = own(t, 2) if which == 0 else region(t, block, 2)
        return msg(t, 6 + which, src, block, 2, c)

    def start_own(t):
        to_x(t, 1).start()
        to_y(t, 0).start()
        to_x(t, 0).start()
        to_y(t, 1).start()

    def gain(i):
        return send(g_ref, g_full.at[n], gs_sem.at[i], gr_sem.at[i], others[i], w)

    line = LineGather(n, w, c_ref, c_full, zs_sem, zr_sem, 4)
    for i in range(7):
        gain(i).start()
    start_own(0)
    line.start()
    for t in (1, 2):
        start_own(t)
    for t in range(3):
        to_c(t, 0).start()

    locals_out = []

    def put(src, dst):
        cp = pltpu.make_async_copy(src, dst, out_sem.at[len(locals_out)])
        cp.start()
        locals_out.append(cp)

    for i in range(7):
        gain(i).wait()
    for cp in locals_in:
        cp.wait()
    put(c_buf, c_full.at[w])
    for k in range(8):
        gain_row[:, pl.ds(k * rows, rows)] = g_full[k, :, :rows]
        gain_late[:, pl.ds(k * rows, rows)] = g_full[k, :, rows:]
    strip = 16

    def scaled(rows_f, gain_ref, s, kept, others_f):
        factor = lax.rsqrt(jnp.mean(rows_f * rows_f, axis=-1, keepdims=True) + EPSILON)
        lane = lax.broadcasted_iota(jnp.int32, (strip, log_out.shape[1]), 1)
        log_out[s, :] = jnp.where(lane == kept, factor, others_f)
        return (rows_f * factor * gain_ref[...]).astype(BF)

    @pl.loop(0, x_buf.shape[0] // strip)
    def _(i):
        s = pl.ds(pl.multiple_of(i * strip, strip), strip)
        normed[s, :] = scaled(x_buf[s, :].astype(F32), gain_row, s, 127, 0.0)

    put(normed, normed_out)

    docs = docs_ref[...]
    late = lax.broadcasted_iota(jnp.int32, bias_ref.shape, 0)
    early = lax.broadcasted_iota(jnp.int32, bias_ref.shape, 1)
    end = docs[:, :1]
    late_doc = jnp.where(late >= end, 1, 0)
    early_doc = jnp.where(early >= end, 1, 0)
    for k in range(1, docs.shape[1]):
        end = end + docs[:, k : k + 1]
        late_doc = late_doc + jnp.where(late >= end, 1, 0)
        early_doc = early_doc + jnp.where(early >= end, 1, 0)
    allowed = (late_doc == early_doc) & (early <= late)
    bias_ref[...] = jnp.where(allowed, 0.0, -1e30)

    def relay(t):
        to_y(t, 0).wait_recv()
        on_x(t).start()
        to_x(t, 1).wait_recv()
        on_y(t).start()
        to_x(t, 0).wait_recv()
        to_c(t, 1).start()
        to_y(t, 1).wait_recv()
        to_c(t, 2).start()

    def corner(t):
        on_x(t).wait_recv()
        on_y(t).wait_recv()
        to_c(t, 3).start()

    line.near(0)
    relay(0)
    line.near(1)
    relay(1)
    line.near(2)
    relay(2)
    start_own(3)
    to_c(3, 0).start()
    line.near(3)
    line.far(0)
    line.far(1)
    for t in range(3):
        corner(t)
    line.far(2)
    for t in range(3):
        for which in range(4):
            to_c(t, which).wait_recv()
    put(qkv_full, qkv_out)
    tile = 256

    @pl.loop(0, qkv.shape[1] // tile)
    def _(i):
        s = pl.ds(pl.multiple_of(i * tile, tile), tile)
        qkv[:, s] = jnp.dot(normed[...], qkv_full[:, s], preferred_element_type=F32).astype(BF)

    put(qkv, rows_out)
    line.far(3)

    pair = 2 * HEAD_DIM
    group = HEADS // KV_HEADS

    @pl.loop(0, KV_HEADS // 2)
    def _(i):
        keys = qkv[:, pl.ds(pl.multiple_of(qc + i * pair, pair), pair)]
        values = qkv[:, pl.ds(pl.multiple_of(qc + kc + i * pair, pair), pair)]
        lane = lax.broadcasted_iota(jnp.int32, log_out.shape, 1)
        for b in range(group):
            at_cols = pl.ds(pl.multiple_of((i * group + b) * pair, pair), pair)
            queries = qkv[:, at_cols]
            side = (2 * b) // group
            key = keys[:, side * HEAD_DIM : (side + 1) * HEAD_DIM]
            value = values[:, side * HEAD_DIM : (side + 1) * HEAD_DIM]
            heads = []
            for e in range(2):
                query = queries[:, e * HEAD_DIM : (e + 1) * HEAD_DIM]
                masked = contract_cols(query, key) * (HEAD_DIM**-0.5) + bias_ref[...]
                peak = jnp.max(masked, axis=-1, keepdims=True)
                expo = jnp.exp(masked - peak)
                total = jnp.sum(expo, axis=-1, keepdims=True)
                probs = (expo * (1.0 / total)).astype(BF)
                heads.append(jnp.dot(probs, value, preferred_element_type=F32))
                log_out[...] = jnp.where(
                    lane == 2 * (i * group + b) + e, peak + jnp.log(total), log_out[...]
                )
            att[:, at_cols] = jnp.concatenate(heads, axis=1).astype(BF)

    put(att, att_out)
    relay(3)
    corner(3)
    for which in range(4):
        to_c(3, which).wait_recv()
    put(p_full, p_out)

    @pl.loop(0, x_buf.shape[1] // tile)
    def _(i):
        s = pl.ds(pl.multiple_of(i * tile, tile), tile)
        middle[:, s] = x_buf[:, s].astype(F32) + jnp.dot(
            att[...], p_full[:, s], preferred_element_type=F32
        )

    put(middle, middle_out)

    @pl.loop(0, x_buf.shape[0] // strip)
    def _(i):
        s = pl.ds(pl.multiple_of(i * strip, strip), strip)
        mixed[s, :] = scaled(middle[s, :], gain_late, s, 126, log_out[s, :])

    put(mixed, mixed_out)
    for t in range(4):
        for h in range(2):
            to_x(t, h).wait_send()
            to_y(t, h).wait_send()
        on_x(t).wait_send()
        on_y(t).wait_send()
        for which in range(4):
            to_c(t, which).wait_send()
    line.finish()
    for cp in locals_out:
        cp.wait()


def gather_first(rows_in, query, key, value, project, gains, cotangent, docs):
    rows = query.shape[0]
    width = query.shape[1] + 2 * key.shape[1]
    tokens_here, model = rows_in.shape
    hbm, vmem = pl.BlockSpec(memory_space=pl.ANY), pl.BlockSpec(memory_space=pltpu.VMEM)
    return pl.pallas_call(
        first_kernel,
        name="gather_first",
        out_shape=(
            jax.ShapeDtypeStruct((8 * rows, width), BF),
            jax.ShapeDtypeStruct((project.shape[0], 8 * rows), BF),
            jax.ShapeDtypeStruct((4,) + cotangent.shape, BF),
            jax.ShapeDtypeStruct((tokens_here, model), BF),
            jax.ShapeDtypeStruct((tokens_here, width), BF),
            jax.ShapeDtypeStruct((tokens_here, query.shape[1]), BF),
            jax.ShapeDtypeStruct((tokens_here, model), F32),
            jax.ShapeDtypeStruct((tokens_here, model), BF),
            jax.ShapeDtypeStruct((1, model), F32),
            jax.ShapeDtypeStruct((1, model), F32),
            jax.ShapeDtypeStruct((tokens_here, tokens_here), F32),
            jax.ShapeDtypeStruct((tokens_here, 128), F32),
        ),
        in_specs=[hbm] * 7 + [vmem],
        out_specs=[hbm] * 8 + [vmem] * 4,
        scratch_shapes=[
            pltpu.VMEM((8,) + gains.shape, gains.dtype),
            pltpu.VMEM((8 * rows, width), BF),
            pltpu.VMEM((project.shape[0], 8 * rows), BF),
            pltpu.VMEM(cotangent.shape, BF),
            pltpu.VMEM((tokens_here, model), BF),
            pltpu.VMEM((tokens_here, model), BF),
            pltpu.VMEM((tokens_here, model), F32),
            pltpu.VMEM((tokens_here, model), BF),
            pltpu.VMEM((tokens_here, width), BF),
            pltpu.VMEM((tokens_here, query.shape[1]), BF),
            pltpu.SemaphoreType.DMA((7,)),
            pltpu.SemaphoreType.DMA((8,)),
            pltpu.SemaphoreType.DMA((40,)),
            pltpu.SemaphoreType.DMA((40,)),
            pltpu.SemaphoreType.DMA((7,)),
            pltpu.SemaphoreType.DMA((7,)),
            pltpu.SemaphoreType.DMA((32,)),
            pltpu.SemaphoreType.DMA((16,)),
        ],
        compiler_params=pltpu.CompilerParams(collective_id=1, has_side_effects=True),
    )(rows_in, query, key, value, project, gains, cotangent, docs)


def attention_back_kernel(qkv, back, logs, bias, out):
    q_cols, k_cols = HEADS * HEAD_DIM, KV_HEADS * HEAD_DIM
    pair = 2 * HEAD_DIM
    group = HEADS // KV_HEADS
    scale = HEAD_DIM**-0.5

    @pl.loop(0, KV_HEADS // 2)
    def _(i):
        key_at = pl.ds(pl.multiple_of(q_cols + i * pair, pair), pair)
        value_at = pl.ds(pl.multiple_of(q_cols + k_cols + i * pair, pair), pair)
        keys, values = qkv[:, key_at], qkv[:, value_at]
        lane = lax.broadcasted_iota(jnp.int32, logs.shape, 1)
        key_backs, value_backs = [], []
        for side in range(2):
            key = keys[:, side * HEAD_DIM : (side + 1) * HEAD_DIM]
            value = values[:, side * HEAD_DIM : (side + 1) * HEAD_DIM]
            key_back = jnp.zeros(key.shape, F32)
            value_back = jnp.zeros(key.shape, F32)
            for b in range(side * group // 2, (side + 1) * group // 2):
                at_cols = pl.ds(pl.multiple_of((i * group + b) * pair, pair), pair)
                queries, backs = qkv[:, at_cols], back[:, at_cols]
                heads = []
                for e in range(2):
                    query = queries[:, e * HEAD_DIM : (e + 1) * HEAD_DIM]
                    given = backs[:, e * HEAD_DIM : (e + 1) * HEAD_DIM]
                    logsum = jnp.sum(
                        jnp.where(lane == 2 * (i * group + b) + e, logs[...], 0.0),
                        axis=-1,
                        keepdims=True,
                    )
                    probs = jnp.exp(contract_cols(query, key) * scale + bias[...] - logsum)
                    value_back = value_back + contract_rows(probs.astype(BF), given)
                    probs_back = contract_cols(given, value)
                    inner = jnp.sum(probs * probs_back, axis=-1, keepdims=True)
                    scores_back = (probs * (probs_back - inner)).astype(BF)
                    heads.append(jnp.dot(scores_back, key, preferred_element_type=F32) * scale)
                    key_back = key_back + contract_rows(scores_back, query)
                out[:, at_cols] = jnp.concatenate(heads, axis=1).astype(BF)
            key_backs.append(key_back * scale)
            value_backs.append(value_back)
        out[:, key_at] = jnp.concatenate(key_backs, axis=1).astype(BF)
        out[:, value_at] = jnp.concatenate(value_backs, axis=1).astype(BF)


def attention_back(qkv, back, logs, bias):
    vmem = pl.BlockSpec(memory_space=pltpu.VMEM)
    heads = HEADS * qkv.shape[0] * qkv.shape[0]
    return pl.pallas_call(
        attention_back_kernel,
        name="attention_back",
        out_shape=jax.ShapeDtypeStruct(qkv.shape, BF),
        in_specs=[vmem] * 4,
        out_specs=vmem,
        cost_estimate=pl.CostEstimate(
            flops=10 * heads * HEAD_DIM, bytes_accessed=8 * qkv.size, transcendentals=heads
        ),
    )(qkv, back, logs, bias)


class LineScatter:
    def __init__(self, n, w, terms, bufs, ssem, rsem, chunks):
        self.n, self.w, self.terms, self.bufs = n, w, terms, bufs
        self.ssem, self.rsem, self.chunks = ssem, rsem, chunks
        self.rows = terms.shape[1] // chunks

    def span(self, i):
        return pl.ds(pl.multiple_of(i * self.rows, self.rows), self.rows)

    def term(self, d, i):
        return self.terms.at[d, self.span(i), :]

    def slot(self, way, slot, i):
        return self.bufs[way].at[slot, self.span(i), :]

    def put(self, way, here, d, i, src):
        slot = d - here - 1 if way == 0 else here - 1 - d
        k = (way * 3 + slot) * self.chunks + i
        to = here + 1 - 2 * way
        return send(src, self.slot(way, slot, i), self.ssem.at[k], self.rsem.at[k], self.n, to)

    def came(self, way, slot, i):
        k = (way * 3 + slot) * self.chunks + i
        ref = self.slot(way, slot, i)
        send(ref, ref, self.ssem.at[k], self.rsem.at[k], self.n, 1).wait_recv()

    def begin(self, i):
        for here, way in ((0, 0), (3, 1)):

            @pl.when(self.w == here)
            def _():
                for d in (3, 2, 1) if way == 0 else (0, 1, 2):
                    self.put(way, here, d, i, self.term(d, i)).start()

    def join(self, way, here, d, i):
        slot = d - here if way == 0 else here - d
        self.came(way, slot, i)
        mine, sum_ = self.term(d, i), self.slot(way, slot, i)
        sum_[...] = (mine[...].astype(F32) + sum_[...].astype(F32)).astype(BF)
        self.put(way, here, d, i, sum_).start()

    def pass_on(self, i):
        @pl.when(self.w == 1)
        def _():
            self.join(0, 1, 3, i)
            self.join(0, 1, 2, i)

        @pl.when(self.w == 2)
        def _():
            self.join(1, 2, 0, i)
            self.join(1, 2, 1, i)

    def pass_end(self, i):
        @pl.when(self.w == 1)
        def _():
            self.join(1, 1, 0, i)

        @pl.when(self.w == 2)
        def _():
            self.join(0, 2, 3, i)

    def finish(self, i, out):
        for here, ways in ((0, (1,)), (1, (0, 1)), (2, (0, 1)), (3, (0,))):

            @pl.when(self.w == here)
            def _():
                for way in ways:
                    self.came(way, 0, i)
                total = self.term(here, i)[...].astype(F32)
                for way in ways:
                    total = total + self.slot(way, 0, i)[...].astype(F32)
                out[self.span(i), :] = total.astype(out.dtype)

    def drain(self):
        sent = {
            0: ((0, 3), (0, 2), (0, 1)),
            1: ((0, 3), (0, 2), (1, 0)),
            2: ((1, 0), (1, 1), (0, 3)),
            3: ((1, 0), (1, 1), (1, 2)),
        }
        for here in range(4):

            @pl.when(self.w == here)
            def _():
                for i in range(self.chunks):
                    for way, d in sent[here]:
                        self.put(way, here, d, i, self.term(d, i)).wait_send()


def middle_kernel(
    mixed,
    cot,
    wg,
    wu,
    wd,
    counts,
    back_out,
    partial_out,
    gate_go,
    gate_stay,
    up_go,
    up_stay,
    low_go,
    low_stay,
    high_go,
    high_stay,
    x_all,
    cot_v,
    wg_v,
    wu_v,
    wd_v,
    gate_f,
    up_f,
    back_f,
    hid,
    gb,
    ub,
    terms,
    from_left,
    from_right,
    part_buf,
    gate_k,
    up_k,
    down_k,
    in_sem,
    ag_s,
    ag_r,
    rs_s,
    rs_r,
    part_sem,
    sw_s,
    sw_r,
    out_sem,
    ready,
    live,
):
    n, w = lax.axis_index("narrow"), lax.axis_index("wide")
    y, x, core = n // 4, lax.rem(n // 2, 2), lax.rem(n, 2)
    mate = flip(n, 1)
    chunks = 4
    rows = mixed.shape[0] // chunks
    tokens, model = 4 * mixed.shape[0], mixed.shape[1]
    width = wg.shape[1]
    batch = 4 * rows
    loads = [
        pltpu.make_async_copy(src, dst, in_sem.at[k])
        for k, (src, dst) in enumerate(
            ((mixed, x_all.at[w]), (wg, wg_v), (wu, wu_v), (cot, cot_v), (wd, wd_v))
        )
    ]
    for cp in loads:
        cp.start()
    greet([mate], n, w, True)

    gather = LineGather(n, w, mixed, x_all, ag_s, ag_r, chunks)
    scatter = LineScatter(n, w, terms, (from_left, from_right), rs_s, rs_r, chunks)
    gather.start_chunk(0)
    gather.start_chunk(1)
    here = lax.broadcasted_iota(jnp.int32, counts.shape, 1) == w
    count = jnp.sum(jnp.where(here, counts[...].astype(F32), 0.0), axis=-1, keepdims=True)
    slot = lax.broadcasted_iota(jnp.int32, live.shape, 1) // TILE
    live[...] = jnp.where(slot.astype(F32) < count, 1.0, 0.0)
    gather.near(0)
    gather.far(0)
    for cp in loads:
        cp.wait()

    def rows_of(ref, i):
        r = pl.ds(pl.multiple_of(i * rows, rows), rows)
        return ref[:, r, :].reshape(batch, ref.shape[2])

    def store(i):
        return pltpu.make_async_copy(
            part_buf.at[lax.rem(i, 2)],
            partial_out.at[:, pl.ds(pl.multiple_of(i * rows, rows), rows), :],
            part_sem.at[lax.rem(i, 2)],
        )

    @pl.loop(0, chunks)
    def _(i):
        r = pl.ds(pl.multiple_of(i * rows, rows), rows)
        gather.ready(i)
        xs = rows_of(x_all, i)
        gate_f[...] = jnp.dot(xs, wg_v[...], preferred_element_type=F32)
        up_f[...] = jnp.dot(xs, wu_v[...], preferred_element_type=F32)

        @pl.when(i < chunks - 1)
        def _():
            gather.near(i + 1)

        @pl.when(i < chunks - 2)
        def _():
            gather.start_chunk(i + 2)

        back_f[...] = contract_cols(rows_of(cot_v, i), wd_v[...])
        step = 16

        @pl.loop(0, batch // step)
        def _(t):
            s = pl.ds(pl.multiple_of(t * step, step), step)
            d = t // (rows // step)
            into = pl.ds(
                pl.multiple_of(i * rows + lax.rem(t, rows // step) * step, step), step
            )
            gate, up = gate_f[s, :], up_f[s, :] * live[...]
            sigma = jax.nn.sigmoid(gate)
            silu = gate * sigma
            hid[d, into, :] = (silu * up).astype(BF)
            back = back_f[s, :]
            gb[d, into, :] = (back * up * sigma * (1.0 + gate * (1.0 - sigma))).astype(BF)
            ub[d, into, :] = (back * silu * live[...]).astype(BF)

        @pl.when(i > 0)
        def _():
            scatter.pass_on(i - 1)

        @pl.when(i < chunks - 1)
        def _():
            gather.far(i + 1)

        terms[:, r, :] = (
            (contract_cols(rows_of(gb, i), wg_v[...]) + contract_cols(rows_of(ub, i), wu_v[...]))
            .astype(BF)
            .reshape(4, rows, model)
        )
        scatter.begin(i)

        @pl.when(i > 1)
        def _():
            store(i - 2).wait()

        part_buf[lax.rem(i, 2)] = (
            jnp.dot(rows_of(hid, i), wd_v[...], preferred_element_type=F32)
            .astype(BF)
            .reshape(4, rows, model)
        )
        store(i).start()

        @pl.when(i > 0)
        def _():
            scatter.pass_end(i - 1)

    pl.semaphore_signal(
        ready, inc=1, device_id=at(mate, w), device_id_type=pl.DeviceIdType.MESH
    )

    def row_grad(back, block):
        cols = pl.ds(pl.multiple_of(block * (model // 8), model // 8), model // 8)
        return contract_rows(
            x_all[:, :, cols].reshape(tokens, model // 8), back[...].reshape(tokens, width)
        )

    def col_grad(block):
        cols = pl.ds(pl.multiple_of(block * (model // 8), model // 8), model // 8)
        return contract_rows(
            hid[...].reshape(tokens, width), cot_v[:, :, cols].reshape(tokens, model // 8)
        )

    eighth, half = model // 8, model // 2

    def place(j, base):
        return pl.ds(pl.multiple_of(base + j * eighth, eighth), eighth)

    swaps = [
        send(buf.at[pl.ds(half, half), :], buf.at[pl.ds(0, half), :], sw_s.at[k], sw_r.at[k], mate, w)
        for k, buf in enumerate((wg_v, wu_v))
    ]
    swaps.append(
        send(
            wd_v.at[:, pl.ds(half, half)], wd_v.at[:, pl.ds(0, half)], sw_s.at[2], sw_r.at[2], mate, w
        )
    )

    @pl.loop(0, 4)
    def _(j):
        wg_v[place(j, half), :] = row_grad(gb, 2 * j + 1 - core).astype(BF)

    pl.semaphore_wait(ready, 1)
    swaps[0].start()

    @pl.loop(0, 4)
    def _(j):
        wu_v[place(j, half), :] = row_grad(ub, 2 * j + 1 - core).astype(BF)

    swaps[1].start()
    scatter.pass_on(chunks - 1)

    @pl.loop(0, 4)
    def _(j):
        wd_v[:, place(j, half)] = col_grad(2 * j + 1 - core).astype(BF)

    swaps[2].start()
    swaps[0].wait_recv()

    @pl.loop(0, 4)
    def _(j):
        gate_k[j // 2, lax.rem(j, 2)] = (
            row_grad(gb, 2 * j + core) + wg_v[place(j, 0), :].astype(F32)
        ).astype(BF)

    cut = width // 2
    pieces = (
        (gate_k.at[:, 1 - x], gate_go),
        (gate_k.at[:, x], gate_stay),
        (up_k.at[1 - y], up_go),
        (up_k.at[y], up_stay),
        (down_k.at[:, 1 - x, pl.ds(0, cut), :], low_go),
        (down_k.at[:, x, pl.ds(0, cut), :], low_stay),
        (down_k.at[1 - y, :, pl.ds(cut, cut), :], high_go),
        (down_k.at[y, :, pl.ds(cut, cut), :], high_stay),
    )
    puts = [
        pltpu.make_async_copy(src, dst, out_sem.at[k]) for k, (src, dst) in enumerate(pieces)
    ]
    for k in (0, 1):
        puts[k].start()
    scatter.pass_end(chunks - 1)
    swaps[1].wait_recv()

    @pl.loop(0, 4)
    def _(j):
        up_k[j // 2, lax.rem(j, 2)] = (
            row_grad(ub, 2 * j + core) + wu_v[place(j, 0), :].astype(F32)
        ).astype(BF)

    for k in (2, 3):
        puts[k].start()
    swaps[2].wait_recv()

    @pl.loop(0, 4)
    def _(j):
        down_k[j // 2, lax.rem(j, 2)] = (
            col_grad(2 * j + core) + wd_v[:, place(j, 0)].astype(F32)
        ).astype(BF)

    for k in (4, 5, 6, 7):
        puts[k].start()
    for i in range(chunks):
        scatter.finish(i, back_out)
    scatter.drain()
    gather.finish_sends()
    for k in range(3):
        swaps[k].wait_send()
    store(chunks - 2).wait()
    store(chunks - 1).wait()
    for cp in puts:
        cp.wait()


def feed_forward(mixed, cot, gate_weight, up_weight, down_weight, counts):
    tokens_here, model = mixed.shape
    width = gate_weight.shape[1]
    rows, eighth, cut = tokens_here // 4, model // 8, width // 2
    hbm, vmem = pl.BlockSpec(memory_space=pl.ANY), pl.BlockSpec(memory_space=pltpu.VMEM)
    row_piece = jax.ShapeDtypeStruct((2, eighth, width), BF)
    col_piece = jax.ShapeDtypeStruct((2, cut, eighth), BF)
    dma = pltpu.SemaphoreType.DMA
    acc = pltpu.VMEM((4 * rows, width), F32)
    act = pltpu.VMEM((4, tokens_here, width), BF)
    tok = pltpu.VMEM((4, tokens_here, model), BF)
    three = pltpu.VMEM((3, tokens_here, model), BF)
    return pl.pallas_call(
        middle_kernel,
        name="feed_forward",
        out_shape=(
            jax.ShapeDtypeStruct(mixed.shape, F32),
            jax.ShapeDtypeStruct((4,) + mixed.shape, BF),
        )
        + (row_piece,) * 4
        + (col_piece,) * 4,
        in_specs=[hbm] * 5 + [vmem],
        out_specs=[vmem] + [hbm] * 9,
        scratch_shapes=[
            tok,
            tok,
            pltpu.VMEM(gate_weight.shape, BF),
            pltpu.VMEM(up_weight.shape, BF),
            pltpu.VMEM(down_weight.shape, BF),
            acc,
            acc,
            acc,
            act,
            act,
            act,
            tok,
            three,
            three,
            pltpu.VMEM((2, 4, rows, model), BF),
            pltpu.VMEM((2, 2, eighth, width), BF),
            pltpu.VMEM((2, 2, eighth, width), BF),
            pltpu.VMEM((2, 2, width, eighth), BF),
            dma((5,)),
            dma((32,)),
            dma((16,)),
            dma((24,)),
            dma((24,)),
            dma((2,)),
            dma((3,)),
            dma((3,)),
            dma((8,)),
            pltpu.SemaphoreType.REGULAR,
            pltpu.VMEM((1, width), F32),
        ],
        compiler_params=pltpu.CompilerParams(
            collective_id=5, has_side_effects=True, vmem_limit_bytes=64 * 1024 * 1024 - 65536
        ),
    )(mixed, cot, gate_weight, up_weight, down_weight, counts)


class Reduce:
    def __init__(self, me, factors, cols, x_first, bufs, sems, k):
        self.n, self.w, self.y, self.x, self.core = me
        self.left, self.right = factors
        self.cols, self.x_first = pl.ds(*cols), x_first
        self.away, self.sum, self.pair, self.one, self.two = bufs
        self.sems, self.k = sems, k
        self.rows = self.sum.shape[2]
        self.near = flip(self.n, 2) if x_first else flip(self.n, 4)
        self.next = flip(self.n, 4) if x_first else flip(self.n, 2)

    def term(self, block):
        own = pl.ds(pl.multiple_of(block * self.rows, self.rows), self.rows)
        return contract_rows(self.left[:, own], self.right[:, self.cols])

    def swap(self):
        return send(
            self.away,
            self.pair,
            self.sems[0].at[self.k],
            self.sems[1].at[self.k],
            flip(self.n, 1),
            self.w,
        )

    def before_swap(self):
        @pl.loop(0, 4)
        def _(j):
            self.away[j // 2, lax.rem(j, 2)] = self.term(2 * j + 1 - self.core).astype(BF)

        self.swap().start()

    def block(self, first, second):
        return (second, first) if self.x_first else (first, second)

    def axes(self):
        return (self.x, self.y) if self.x_first else (self.y, self.x)

    def stage(self, s):
        a, b = self.axes()
        if s == 1:
            src = self.sum.at[:, 1 - a] if self.x_first else self.sum.at[1 - a]
            dst, peer = self.one, self.near
        else:
            src = self.sum.at[self.block(a, 1 - b)]
            dst, peer = self.two, self.next
        k = 2 * self.k + s - 1
        return send(src, dst, self.sems[2].at[k], self.sems[3].at[k], peer, self.w)

    def add(self, block, other):
        step = 64 if self.rows % 64 == 0 else 48

        @pl.loop(0, self.rows // step)
        def _(i):
            r = pl.ds(pl.multiple_of(i * step, step), step)
            self.sum[block[0], block[1], r, :] = (
                self.sum[block[0], block[1], r, :] + other[r, :]
            )

    def after_swap(self):
        a, _ = self.axes()
        self.swap().wait_recv()

        @pl.loop(0, 4)
        def _(j):
            first = lax.rem(1 - a + j // 2, 2)
            y, x = self.block(first, lax.rem(j, 2))
            total = self.term(4 * y + 2 * x + self.core) + self.pair[y, x].astype(F32)
            self.sum[y, x] = total.astype(BF)

        self.stage(1).start()

    def after_one(self):
        a, b = self.axes()
        self.stage(1).wait()
        self.add(self.block(a, 1 - b), self.one.at[1 - b])
        self.stage(2).start()
        self.add(self.block(a, b), self.one.at[b])

    def after_two(self):
        a, b = self.axes()
        self.stage(2).wait()
        self.add(self.block(a, b), self.two)

    def result(self):
        return self.sum.at[self.y, self.x]


class Half:
    def __init__(self, me, kept, came, x_first, bufs, sems, k):
        self.n, self.w, self.y, self.x, self.core = me
        self.kept, self.came, self.x_first = kept, came, x_first
        self.sum, self.one, self.two = bufs
        self.sems, self.k = sems, k
        self.rows = kept.shape[1]
        self.next = flip(self.n, 4) if x_first else flip(self.n, 2)
        self.here = self.y if x_first else self.x

    def loads(self):
        return [
            pltpu.make_async_copy(self.kept, self.sum, self.sems[0].at[2 * self.k]),
            pltpu.make_async_copy(self.came, self.one, self.sems[0].at[2 * self.k + 1]),
        ]

    def stage(self):
        return send(
            self.sum.at[1 - self.here],
            self.two,
            self.sems[1].at[self.k],
            self.sems[2].at[self.k],
            self.next,
            self.w,
        )

    def add(self, block, other):
        @pl.loop(0, self.rows // 64)
        def _(i):
            r = pl.ds(pl.multiple_of(i * 64, 64), 64)
            self.sum[block, r, :] = self.sum[block, r, :] + other[r, :]

    def after_one(self):
        for cp in self.loads():
            cp.wait()
        self.add(1 - self.here, self.one.at[1 - self.here])
        self.stage().start()
        self.add(self.here, self.one.at[self.here])

    def after_two(self):
        self.stage().wait()
        self.add(self.here, self.two)

    def result(self):
        return self.sum.at[self.here]


class Spread:
    def __init__(self, item, region, sems, k):
        self.item, self.region, self.sems, self.k = item, region, sems, k
        n = item.n
        self.blocks = (n, flip(n, 2), flip(n, 4), flip(flip(n, 2), 4))

    def copy(self, kind, src, block, peer):
        k = 7 * self.k + kind
        return send(
            src, self.region(block), self.sems[0].at[k], self.sems[1].at[k], peer, self.item.w
        )

    def own(self, kind):
        n = self.item.n
        return self.copy(kind, self.item.result(), n, (flip(n, 2), flip(n, 4), flip(n, 1))[kind])

    def corner(self):
        n, b = self.item.n, self.blocks
        if self.item.x_first:
            return self.copy(3, self.region(b[2]), b[2], flip(n, 2))
        return self.copy(3, self.region(b[1]), b[1], flip(n, 4))

    def to_core(self, which):
        block = self.blocks[which]
        return self.copy(3 + which, self.region(block), block, flip(self.item.n, 1))

    def keep(self):
        return pltpu.make_async_copy(
            self.item.result(), self.region(self.item.n), self.sems[2].at[self.k]
        )

    def start(self):
        order = (1, 0, 2) if self.item.x_first else (0, 1, 2)
        for kind in order:
            self.own(kind).start()
        self.keep().start()

    def relay(self):
        first, second = (1, 0) if self.item.x_first else (0, 1)
        self.own(first).wait_recv()
        self.corner().start()
        self.to_core(1 + first).start()
        self.own(second).wait_recv()
        self.to_core(1 + second).start()

    def last(self):
        self.corner().wait_recv()
        self.to_core(3).start()

    def finish(self):
        for kind in range(2):
            self.own(kind).wait_send()
        self.own(2).wait()
        self.corner().wait_send()
        for which in range(1, 4):
            self.to_core(which).wait()
        self.keep().wait()


class Rows:
    def __init__(self, ref):
        self.ref = ref
        self.shape = (4, ref.shape[0] // 4, ref.shape[1])

    @property
    def at(self):
        return self

    def __getitem__(self, index):
        d, r, _ = index
        start = pl.multiple_of(d * self.shape[1] + r.start, r.size)
        return self.ref.at[pl.ds(start, r.size), :]


def last_kernel(items, *refs):
    refs = list(refs)

    def take(count):
        out = refs[:count]
        del refs[:count]
        return out

    factors = take(4)
    stays, comes = take(4), take(4)
    feed_terms, gain_parts = take(2)
    outs = take(4)
    gate_full, up_full, down_full = take(3)
    feed_out, gain_out = take(2)
    attn_bufs = [take(5) for _ in range(4)]
    ffn_bufs = [take(3) for _ in range(4)]
    line_bufs = [take(3) for _ in range(4)]
    feed_v, feed_left, feed_right = take(3)
    gain_in, gain_sum, gain_line = take(3)
    factor_bufs = take(4)
    load_sem, swap_s, swap_r, st_s, st_r = take(5)
    half_sems = take(3)
    sp_sems = take(3)
    lr_s, lr_r, lg_s, lg_r, lg_l = take(5)
    fd_s, fd_r, fd_l = take(3)
    gn_s, gn_r, gz_s, gz_r = take(4)

    n, w = lax.axis_index("narrow"), lax.axis_index("wide")
    me = (n, w, n // 4, lax.rem(n // 2, 2), lax.rem(n, 2))
    attn = [
        Reduce(
            me,
            factor_bufs[2 * p : 2 * p + 2],
            cols,
            xf,
            attn_bufs[k],
            (swap_s, swap_r, st_s, st_r),
            k,
        )
        for k, (p, cols, xf) in enumerate(items)
    ]
    ffn = [
        Half(me, stays[k], comes[k], k % 2 == 0, ffn_bufs[k], half_sems, k) for k in range(4)
    ]
    cut, eighth = stays[2].shape[1], stays[2].shape[2]

    def down_region(k):
        return lambda block: down_full.at[
            pl.ds(k * cut, cut), pl.ds(pl.multiple_of(block * eighth, eighth), eighth)
        ]

    regions = (
        lambda block: gate_full.at[block],
        lambda block: up_full.at[block],
        down_region(0),
        down_region(1),
    )
    spread = [Spread(ffn[k], regions[k], sp_sems, k) for k in range(4)]
    for item in ffn:
        for cp in item.loads():
            cp.start()
    factor_loads = [
        pltpu.make_async_copy(src, dst, load_sem.at[k])
        for k, (src, dst) in enumerate(zip(factors, factor_bufs))
    ]
    for cp in factor_loads:
        cp.start()
    feed_load = pltpu.make_async_copy(feed_terms, feed_v, fd_l)
    feed_load.start()

    barrier = pltpu.get_barrier_semaphore()
    narrow_peers = [lax.rem(n + i, 8) for i in range(1, 8)]
    wide_peers = [lax.rem(w + i, 4) for i in range(1, 4)]
    for peer in narrow_peers:
        pl.semaphore_signal(
            barrier, inc=1, device_id=at(peer, w), device_id_type=pl.DeviceIdType.MESH
        )
    for peer in wide_peers:
        pl.semaphore_signal(
            barrier, inc=1, device_id=at(n, peer), device_id_type=pl.DeviceIdType.MESH
        )
    pl.semaphore_wait(barrier, 10)

    feed_load.wait()
    feed = LineScatter(n, w, feed_v, (feed_left, feed_right), fd_s, fd_r, 4)
    for i in range(4):
        feed.begin(i)

    def gain_narrow(i):
        peer = narrow_peers[i]
        return send(gain_parts.at[peer], gain_in.at[i], gn_s.at[i], gn_r.at[i], peer, w)

    def gain_wide(i):
        return send(gain_sum, gain_line.at[i], gz_s.at[i], gz_r.at[i], n, wide_peers[i])

    for i in range(7):
        gain_narrow(i).start()

    for item in ffn:
        item.after_one()
    for cp in factor_loads:
        cp.wait()
    for item in attn:
        item.before_swap()
    feed.pass_on(0)
    for item in attn:
        item.after_swap()
    feed.pass_on(1)
    feed.pass_end(0)
    for i in range(7):
        gain_narrow(i).wait()
    total = gain_parts[n]
    for i in range(7):
        total = total + gain_in[i]
    gain_sum[...] = total
    for i in range(3):
        gain_wide(i).start()
    feed.pass_on(2)
    feed.pass_end(1)
    for item in attn[:2]:
        item.after_one()
    feed.pass_on(3)
    feed.pass_end(2)
    for item in attn[2:]:
        item.after_one()
    feed.pass_end(3)
    for k in range(4):
        ffn[k].after_two()
        spread[k].start()

    scatters, gathers = [], []
    for k, item in enumerate(attn):
        left, right, own = line_bufs[k]
        scatters.append(
            LineScatter(n, w, Rows(item.result()), (left, right), lr_s.at[k], lr_r.at[k], 1)
        )
        gathers.append(LineGather(n, w, own, outs[k], lg_s.at[k], lg_r.at[k], 1))

    def keep(k):
        return pltpu.make_async_copy(line_bufs[k][2], outs[k].at[w], lg_l.at[k])

    def line_turn(k):
        scatters[k].finish(0, line_bufs[k][2])
        gathers[k].start()
        keep(k).start()

    for k in (0, 1):
        attn[k].after_two()
        scatters[k].begin(0)
    for i in range(4):
        feed.finish(i, feed_out)
    for k in (2, 3):
        attn[k].after_two()
        scatters[k].begin(0)
    for k in (0, 1, 2, 3):
        scatters[k].pass_on(0)
    for k in (0, 1, 2, 3):
        scatters[k].pass_end(0)
    for k in (0, 1, 2, 3):
        line_turn(k)
    for s in spread[:2]:
        s.relay()
    for k in (0, 1, 2, 3):
        gathers[k].near(0)
    for k in (0, 1, 2, 3):
        gathers[k].far(0)
    for s in spread[2:]:
        s.relay()
    for i in range(3):
        gain_wide(i).wait()
    gain_out[...] = (gain_sum[...] + gain_line[0]) + (gain_line[1] + gain_line[2])
    for s in spread:
        s.last()
    for s in spread:
        s.finish()
    for item in attn:
        item.swap().wait_send()
    for k in range(4):
        scatters[k].drain()
        gathers[k].finish()
        keep(k).wait()
    feed.drain()


def reduce_last(factors, stays, comes, feed_terms, gain_parts):
    rows = factors[0].shape[1] // 8
    q_cols, k_cols = HEADS * HEAD_DIM, KV_HEADS * HEAD_DIM
    items = [
        (0, (0, q_cols), True),
        (0, (q_cols, 2 * k_cols), False),
        (1, (0, k_cols), True),
        (1, (k_cols, q_cols - k_cols), False),
    ]
    scratch = []
    for _, (_, cols), _ in items:
        scratch += [
            pltpu.VMEM((2, 2, rows, cols), BF),
            pltpu.VMEM((2, 2, rows, cols), BF),
            pltpu.VMEM((2, 2, rows, cols), BF),
            pltpu.VMEM((2, rows, cols), BF),
            pltpu.VMEM((rows, cols), BF),
        ]
    for stay in stays:
        scratch += [
            pltpu.VMEM(stay.shape, BF),
            pltpu.VMEM(stay.shape, BF),
            pltpu.VMEM(stay.shape[1:], BF),
        ]
    outs = []
    for _, (_, cols), _ in items:
        scratch += [pltpu.VMEM((3, rows // 4, cols), BF)] * 2 + [pltpu.VMEM((rows // 4, cols), BF)]
        outs.append(jax.ShapeDtypeStruct((4, rows // 4, cols), BF))
    outs.append(jax.ShapeDtypeStruct((8,) + stays[0].shape[1:], BF))
    outs.append(jax.ShapeDtypeStruct((8,) + stays[1].shape[1:], BF))
    outs.append(jax.ShapeDtypeStruct((2 * stays[2].shape[1], 8 * stays[2].shape[2]), BF))
    outs.append(jax.ShapeDtypeStruct(feed_terms.shape[1:], F32))
    outs.append(jax.ShapeDtypeStruct(gain_parts.shape[1:], F32))
    scratch += [pltpu.VMEM(feed_terms.shape, BF)]
    scratch += [pltpu.VMEM((3,) + feed_terms.shape[1:], BF)] * 2
    scratch += [
        pltpu.VMEM((7,) + gain_parts.shape[1:], F32),
        pltpu.VMEM(gain_parts.shape[1:], F32),
        pltpu.VMEM((3,) + gain_parts.shape[1:], F32),
    ]
    scratch += [pltpu.VMEM(f.shape, BF) for f in factors]
    dma = pltpu.SemaphoreType.DMA
    scratch += [dma((4,)), dma((4,)), dma((4,)), dma((8,)), dma((8,))]
    scratch += [dma((8,)), dma((4,)), dma((4,))]
    scratch += [dma((28,)), dma((28,)), dma((4,))]
    scratch += [dma((4, 6)), dma((4, 6)), dma((4, 8)), dma((4, 4)), dma((4,))]
    scratch += [dma((24,)), dma((24,)), dma]
    scratch += [dma((7,)), dma((7,)), dma((3,)), dma((3,))]
    hbm, vmem = pl.BlockSpec(memory_space=pl.ANY), pl.BlockSpec(memory_space=pltpu.VMEM)
    out = pl.pallas_call(
        functools.partial(last_kernel, items),
        name="reduce_last",
        out_shape=tuple(outs),
        in_specs=[hbm] * 13 + [vmem],
        out_specs=[hbm] * 7 + [vmem] * 2,
        scratch_shapes=scratch,
        compiler_params=pltpu.CompilerParams(
            collective_id=4, has_side_effects=True, vmem_limit_bytes=64 * 1024 * 1024 - 65536
        ),
    )(*factors, *stays, *comes, feed_terms, gain_parts)
    qkv = out[0].reshape(rows, -1), out[1].reshape(rows, -1)
    project = jnp.concatenate([out[2].reshape(rows, -1), out[3].reshape(rows, -1)], axis=1)
    width = out[4].shape[2]
    ffn = [out[4].reshape(-1, width), out[5].reshape(-1, width), out[6]]
    return qkv, project, ffn, out[7], out[8]


def per_device(
    fast,
    block_input,
    cotangent,
    query_weight,
    key_weight,
    value_weight,
    project_weight,
    prenorm_gain,
    midnorm_gain,
    gate_weight,
    up_weight,
    down_weight,
    doc_lengths,
    tile_counts,
):
    tokens_here, model = block_input.shape
    group = HEADS // KV_HEADS
    scale = HEAD_DIM ** (-0.5)
    q_cols, k_cols = HEADS * HEAD_DIM, KV_HEADS * HEAD_DIM
    inputs_f = block_input.astype(jnp.float32)
    ends = jnp.cumsum(doc_lengths[0])
    position = jnp.arange(tokens_here, dtype=jnp.int32)
    segment = jnp.sum((position[:, None] >= ends[None, :]).astype(jnp.int32), axis=1)
    allowed = (segment[:, None] == segment[None, :]) & (position[None, :] <= position[:, None])
    if fast:
        gains = jnp.stack([prenorm_gain, midnorm_gain]).astype(F32).reshape(1, -1)
        qkv_full, project_full, grad_rows, normed, qkv, attended, *rest = gather_first(
            block_input,
            query_weight,
            key_weight,
            value_weight,
            project_weight,
            gains,
            cotangent,
            doc_lengths,
        )
        middle, mixed_in, first_gain, second_gain, bias, logs = rest
        first_gain, second_gain = first_gain.reshape(-1), second_gain.reshape(-1)
    else:
        qkv_full = jnp.concatenate(
            [
                lax.all_gather(query_weight, "narrow", axis=0, tiled=True),
                lax.all_gather(key_weight, "narrow", axis=0, tiled=True),
                lax.all_gather(value_weight, "narrow", axis=0, tiled=True),
            ],
            axis=1,
        )
        project_full = lax.all_gather(project_weight, "narrow", axis=1, tiled=True)
        first_gain = lax.all_gather(prenorm_gain, "narrow", axis=0, tiled=True).astype(F32)
        second_gain = lax.all_gather(midnorm_gain, "narrow", axis=0, tiled=True).astype(F32)
        grad_rows = lax.all_gather(cotangent, "wide", axis=0, tiled=True)
        normed = rms_scale(inputs_f, first_gain).astype(jnp.bfloat16)
        qkv = jnp.dot(normed, qkv_full, preferred_element_type=jnp.float32).astype(jnp.bfloat16)
    if not fast:
        query_rows = qkv[:, :q_cols].reshape(tokens_here, KV_HEADS, group, HEAD_DIM)
        key_rows = qkv[:, q_cols : q_cols + k_cols].reshape(tokens_here, KV_HEADS, HEAD_DIM)
        value_rows = qkv[:, q_cols + k_cols :].reshape(tokens_here, KV_HEADS, HEAD_DIM)
        scores = (
            jnp.einsum("qcgd,kcd->cgqk", query_rows, key_rows, preferred_element_type=jnp.float32)
            * scale
        )
        masked = jnp.where(allowed, scores, -1e30)
        peak = jnp.max(masked, axis=-1, keepdims=True)
        expo = jnp.exp(masked - peak)
        total = jnp.sum(expo, axis=-1, keepdims=True)
        probs_low = (expo / total).astype(jnp.bfloat16)
        logsum = peak + jnp.log(total)
        attended = (
            jnp.einsum("cgqk,kcd->qcgd", probs_low, value_rows, preferred_element_type=jnp.float32)
            .astype(jnp.bfloat16)
            .reshape(tokens_here, HEADS * HEAD_DIM)
        )
        branch = jnp.dot(attended, project_full, preferred_element_type=jnp.float32)
        middle = inputs_f + branch
        mixed_in = rms_scale(middle, second_gain).astype(jnp.bfloat16)
    width = gate_weight.shape[1]
    wide_index = lax.axis_index("wide")
    my_count = jnp.sum(
        jnp.where(jnp.arange(tile_counts.shape[0], dtype=jnp.int32) == wide_index, tile_counts, 0)
    )
    live = (jnp.arange(width, dtype=jnp.int32) // TILE < my_count).astype(jnp.float32)
    if fast:
        mixed_back, feed_terms, *pieces = feed_forward(
            mixed_in, grad_rows, gate_weight, up_weight, down_weight, tile_counts.reshape(1, -1)
        )
        stays = pieces[1::2]
        comes = [
            lax.ppermute(piece, "narrow", [(i, i ^ bit) for i in range(8)])
            for piece, bit in zip(pieces[0::2], (2, 4, 2, 4))
        ]
    else:
        gathered = lax.all_gather(mixed_in, "wide", axis=0, tiled=True)
        gate_pre = jnp.dot(gathered, gate_weight, preferred_element_type=jnp.float32)
        up_pre = jnp.dot(gathered, up_weight, preferred_element_type=jnp.float32)
        hidden_back = contract_cols(grad_rows, down_weight)
        sigma = jax.nn.sigmoid(gate_pre)
        hidden = (gate_pre * sigma * up_pre * live).astype(BF)
        gate_back = (
            hidden_back * up_pre * live * sigma * (1.0 + gate_pre * (1.0 - sigma))
        ).astype(BF)
        up_back = (hidden_back * gate_pre * sigma * live).astype(BF)
        mixed_terms = (
            contract_cols(gate_back, gate_weight) + contract_cols(up_back, up_weight)
        ).astype(BF)
        mixed_back = lax.psum_scatter(
            mixed_terms, "wide", scatter_dimension=0, tiled=True
        ).astype(F32)
        partial_rows = jnp.dot(hidden, down_weight, preferred_element_type=jnp.float32)
        down_part = contract_rows(hidden, grad_rows)
        gate_part = contract_rows(gathered, gate_back)
        up_part = contract_rows(gathered, up_back)
    out_grad = cotangent.astype(jnp.float32)
    if fast:
        middle_norm_back, second_gain_part = scale_back(
            mixed_back, middle, second_gain, logs[:, 126:127]
        )
    else:
        unused_second, second_backward = jax.vjp(rms_scale, middle, second_gain)
        middle_norm_back, second_gain_part = second_backward(mixed_back)
    middle_back = out_grad + middle_norm_back
    branch_back = middle_back.astype(jnp.bfloat16)
    attended_back = contract_cols(branch_back, project_full).astype(jnp.bfloat16)
    if fast:
        qkv_back = attention_back(qkv, attended_back, logs, bias)
    else:
        attended_back = attended_back.reshape(tokens_here, KV_HEADS, group, HEAD_DIM)
        scores_again = (
            jnp.einsum("qcgd,kcd->cgqk", query_rows, key_rows, preferred_element_type=jnp.float32)
            * scale
        )
        probs_again = jnp.where(allowed, jnp.exp(scores_again - logsum), 0.0)
        probs_again_low = probs_again.astype(jnp.bfloat16)
        value_back = (
            jnp.einsum(
                "cgqk,qcgd->kcd", probs_again_low, attended_back, preferred_element_type=jnp.float32
            )
            .astype(jnp.bfloat16)
            .reshape(tokens_here, KV_HEADS * HEAD_DIM)
        )
        probs_back = jnp.einsum(
            "qcgd,kcd->cgqk", attended_back, value_rows, preferred_element_type=jnp.float32
        )
        scores_back = (
            probs_again * (probs_back - jnp.sum(probs_again * probs_back, axis=-1, keepdims=True))
        ).astype(jnp.bfloat16)
        query_back = (
            (
                jnp.einsum("cgqk,kcd->qcgd", scores_back, key_rows, preferred_element_type=jnp.float32)
                * scale
            )
            .astype(jnp.bfloat16)
            .reshape(tokens_here, HEADS * HEAD_DIM)
        )
        key_back = (
            (
                jnp.einsum(
                    "cgqk,qcgd->kcd", scores_back, query_rows, preferred_element_type=jnp.float32
                )
                * scale
            )
            .astype(jnp.bfloat16)
            .reshape(tokens_here, KV_HEADS * HEAD_DIM)
        )
        qkv_back = jnp.concatenate([query_back, key_back, value_back], axis=1)
    normed_back = contract_cols(qkv_back, qkv_full)
    if fast:
        input_norm_back, first_gain_part = scale_back(
            normed_back, inputs_f, first_gain, logs[:, 127:128]
        )
    else:
        unused_first, first_backward = jax.vjp(rms_scale, inputs_f, first_gain)
        input_norm_back, first_gain_part = first_backward(normed_back)
    input_grad = (middle_back + input_norm_back).astype(jnp.bfloat16)

    if fast:
        gain_parts = jnp.stack(
            [first_gain_part.reshape(8, -1), second_gain_part.reshape(8, -1)], axis=1
        ).reshape(8, 1, -1)
        input_grad, qkv_back = lax.optimization_barrier((input_grad, qkv_back))
        qkv_total, project_total, ffn_totals, feed, gain_total = reduce_last(
            (normed, qkv_back, branch_back, attended),
            stays,
            comes,
            feed_terms,
            gain_parts,
        )
        gain_total = gain_total.reshape(2, -1)
        first_total, second_total = gain_total[0], gain_total[1]
        query_total = qkv_total[0].astype(F32)
        key_total = qkv_total[1][:, :k_cols].astype(F32)
        value_total = qkv_total[1][:, k_cols:].astype(F32)
        project_total = project_total.T.astype(F32)
        gate_total, up_total, down_total = [t.astype(F32) for t in ffn_totals]
    else:

        def owned(part):
            share = lax.psum_scatter(part.astype(BF), "narrow", scatter_dimension=0, tiled=True)
            return lax.psum(share, "wide").astype(F32)

        qkv_total = owned(contract_rows(normed, qkv_back))
        query_total = qkv_total[:, :q_cols]
        key_total = qkv_total[:, q_cols : q_cols + k_cols]
        value_total = qkv_total[:, q_cols + k_cols :]
        project_total = owned(contract_rows(branch_back, attended)).T
        first_total = owned(first_gain_part)
        second_total = owned(second_gain_part)
        gate_total, up_total, down_total = (
            lax.psum(gate_part.astype(BF), "narrow").astype(F32),
            lax.psum(up_part.astype(BF), "narrow").astype(F32),
            lax.psum(down_part.astype(BF), "narrow").astype(F32),
        )
        feed = lax.psum_scatter(
            partial_rows.astype(BF), "wide", scatter_dimension=0, tiled=True
        ).astype(F32)
    block_output = (middle + feed).astype(BF)
    return (
        block_output,
        input_grad,
        query_total,
        key_total,
        value_total,
        project_total,
        first_total,
        second_total,
        gate_total,
        up_total,
        down_total,
    )


def solution(mesh):
    fast = mesh.shape["narrow"] == 8 and mesh.shape["wide"] == 4
    placed = (
        P(("narrow", "wide"), None),
        P(("narrow", "wide"), None),
        P("narrow", None),
        P("narrow", None),
        P("narrow", None),
        P(None, "narrow"),
        P("narrow"),
        P("narrow"),
        P(None, "wide"),
        P(None, "wide"),
        P("wide", None),
        P(("narrow", "wide"), None),
        P(),
    )
    return jax.shard_map(
        functools.partial(per_device, fast),
        mesh=mesh,
        in_specs=placed,
        out_specs=(
            P(("narrow", "wide"), None),
            P(("narrow", "wide"), None),
            P("narrow", None),
            P("narrow", None),
            P("narrow", None),
            P(None, "narrow"),
            P("narrow"),
            P("narrow"),
            P(None, "wide"),
            P(None, "wide"),
            P("wide", None),
        ),
        check_vma=False,
    )
```
